32 devices in a mesh: seq: 4 (over y, x), fsdp: 8 (over z, core).
Axes of the slice: x: 2, y: 2, z: 4, core: 2. Of those that a mesh axis runs over, the one named last changes fastest.
Arguments:
- tokens: bfloat16 [8, 1024, 1280], P('fsdp', 'seq'), may hold values from -6 to 6
- picture_ids: int32 [8, 1024], P('fsdp', 'seq'), may hold values from -1 to 10, as said below
- patch_rows: int32 [8, 1024], P('fsdp', 'seq'), may hold values from 0 to 31, as said below
- patch_cols: int32 [8, 1024], P('fsdp', 'seq'), may hold values from 0 to 31, as said below
- norm1_gain: bfloat16 [1280], P('fsdp'), may hold values from 0.099609375 to 1.8984375
- norm1_bias: bfloat16 [1280], P('fsdp'), may hold values from -3 to 3
- qkv_weight: bfloat16 [1280, 3840], P('fsdp'), may hold values from -0.15625 to 0.15625
- qkv_bias: bfloat16 [3840], P('fsdp'), may hold values from -3 to 3
- proj_weight: bfloat16 [1280, 1280], P('fsdp'), may hold values from -2 to 2
- proj_bias: bfloat16 [1280], P('fsdp'), may hold values from -3 to 3
- norm2_gain: bfloat16 [1280], P('fsdp'), may hold values from 0.099609375 to 1.8984375
- norm2_bias: bfloat16 [1280], P('fsdp'), may hold values from -3 to 3
- fc1_weight: bfloat16 [1280, 5120], P('fsdp'), may hold values from -0.15625 to 0.15625
- fc1_bias: bfloat16 [5120], P('fsdp'), may hold values from -3 to 3
- fc2_weight: bfloat16 [5120, 1280], P('fsdp'), may hold values from -0.078125 to 0.078125
- fc2_bias: bfloat16 [1280], P('fsdp'), may hold values from -3 to 3
- cotangent: bfloat16 [8, 1024, 1280], P('fsdp', 'seq'), may hold values from -6 to 6
Outputs:
- block_out: bfloat16 [8, 1024, 1280], P('fsdp', 'seq')
- tokens_grad: float32 [8, 1024, 1280], P('fsdp', 'seq')
- norm1_gain_grad: float32 [1280], P('fsdp')
- norm1_bias_grad: float32 [1280], P('fsdp')
- qkv_weight_grad: float32 [1280, 3840], P('fsdp')
- qkv_bias_grad: float32 [3840], P('fsdp')
- proj_weight_grad: float32 [1280, 1280], P('fsdp')
- proj_bias_grad: float32 [1280], P('fsdp')
- norm2_gain_grad: float32 [1280], P('fsdp')
- norm2_bias_grad: float32 [1280], P('fsdp')
- fc1_weight_grad: float32 [1280, 5120], P('fsdp')
- fc1_bias_grad: float32 [5120], P('fsdp')
- fc2_weight_grad: float32 [5120, 1280], P('fsdp')
- fc2_bias_grad: float32 [1280], P('fsdp')
The draws below stay inside these ranges and needn't reach their ends.
Inputs may be any that keep to these rules, and one draw needn't show every extreme that they name: `picture_ids`: each sequence holds whole pictures in turn from its first token: picture number p (0, 1, 2, ...) of h x w patches, h and w from 10 to 32, takes h * w consecutive tokens with id p; only the last picture of a sequence may have fewer than h rows of patches; the tokens after it, fewer than 32, are padding with id -1. The first sequence holds only pictures of 10 x 10 patches. `patch_rows`: the row of a token's patch within its picture, the picture's tokens going row after row; 0 on padding. The last sequence begins with a picture of 32 x 32 patches. `patch_cols`: the column of a token's patch within its picture; 0 on padding.
All inputs are finite; a program needn't handle non-finite values.
Results may differ from the reference program's by a relative error of at most 0.018.
Values may be sent and summed in bfloat16 or wider, within the bound.
A program may use at most 256 MiB of HBM per device.

```python
import jax
import jax.numpy as jnp
from jax import lax

D = 1280
HEADS = 16
HD = 80
FF = 5120
SIDE_LO = 10
SIDE_HI = 32
SEQS = 8
LEN = 1024


def picture_layout(key):
    candidates = LEN // (SIDE_LO * SIDE_LO) + 1

    def one_row(row_key, row_index):
        height_key, width_key = jax.random.split(row_key)
        heights = jax.random.randint(height_key, (candidates,), SIDE_LO, SIDE_HI + 1)
        widths = jax.random.randint(width_key, (candidates,), SIDE_LO, SIDE_HI + 1)
        slots = jnp.arange(candidates)
        smallest = row_index == 0
        largest_first = (row_index == SEQS - 1) & (slots == 0)
        heights = jnp.where(smallest, SIDE_LO, jnp.where(largest_first, SIDE_HI, heights))
        widths = jnp.where(smallest, SIDE_LO, jnp.where(largest_first, SIDE_HI, widths))
        area_of = heights * widths
        starts = jnp.cumsum(area_of) - area_of
        room_left = jnp.clip(LEN - starts, 0, None)
        taken_len = jnp.minimum(area_of, room_left // widths * widths)
        places = jnp.arange(LEN)
        inside = (places[None, :] >= starts[:, None]) & (places[None, :] < (starts + taken_len)[:, None])
        labels = jnp.sum(jnp.where(inside, slots[:, None] + 1, 0), axis=0) - 1
        offsets = places - jnp.sum(jnp.where(inside, starts[:, None], 0), axis=0)
        row_width = jnp.maximum(jnp.sum(jnp.where(inside, widths[:, None], 0), axis=0), 1)
        present = labels >= 0
        return (labels, jnp.where(present, offsets // row_width, 0), jnp.where(present, offsets % row_width, 0))
    row_keys = jax.random.split(jax.random.fold_in(key, 11), SEQS)
    return jax.vmap(one_row)(row_keys, jnp.arange(SEQS))


def draw_picture_ids(key, part):
    return picture_layout(key)[0].astype(jnp.int32)


def draw_patch_rows(key, part):
    return picture_layout(key)[1].astype(jnp.int32)


def draw_patch_cols(key, part):
    return picture_layout(key)[2].astype(jnp.int32)


def shard_levels(rng, dims, cuts, least, top_value):
    def one(dim, parts):
        steps = jax.random.uniform(jax.random.fold_in(jax.random.fold_in(rng, 6), dim), (parts,), jnp.float32, least / len(cuts), top_value / len(cuts))
        return jnp.repeat(jnp.exp(steps), dims[dim] // parts).reshape((-1,) + (1,) * (len(dims) - dim - 1))

    level = one(*cuts[0])
    for cut in cuts[1:]:
        level = level * one(*cut)
    return level


def normal_values(rng, dims, scale, reach, shards=(), held_as=jnp.bfloat16):
    values = jax.random.normal(rng, dims, jnp.float32) * scale
    if len(shards) > 0:
        values = shard_levels(rng, dims, shards, -0.22, 0.18) * values
    return jnp.clip(values, min=-reach, max=reach).astype(held_as)


def setup_inputs(seed: int = 0) -> dict:
    key_of = jax.random.split(jax.random.key(seed), 18)
    tokens = normal_values(key_of[0], (SEQS, LEN, D), 1.0, 6.0, ((0, 8), (1, 4)))
    picture_ids = draw_picture_ids(jax.random.fold_in(key_of[17], 71), 0)
    patch_rows = draw_patch_rows(jax.random.fold_in(key_of[17], 71), 0)
    patch_cols = draw_patch_cols(jax.random.fold_in(key_of[17], 71), 0)
    norm1_gain = jnp.clip(1.0 + 0.18 * jax.random.normal(key_of[4], (D,), jnp.float32), 0.099609375, 1.8984375).astype(jnp.bfloat16)
    norm1_bias = normal_values(key_of[5], (D,), 0.3, 3.0, ((0, 8),))
    qkv_weight = normal_values(key_of[6], (D, 3 * D), D ** -0.5, 0.15625, ((0, 8),))
    qkv_bias = normal_values(key_of[7], (3 * D,), 0.5, 3.0, ((0, 8),))
    proj_weight = normal_values(key_of[8], (D, D), (max(D // 160, 2)) ** -0.5, 2.0, ((0, 8),))
    proj_bias = normal_values(key_of[9], (D,), 0.5, 3.0, ((0, 8),))
    norm2_gain = jnp.clip(1.0 + 0.18 * jax.random.normal(key_of[10], (D,), jnp.float32), 0.099609375, 1.8984375).astype(jnp.bfloat16)
    norm2_bias = normal_values(key_of[11], (D,), 0.3, 3.0, ((0, 8),))
    fc1_weight = normal_values(key_of[12], (D, FF), D ** -0.5, 0.15625, ((0, 8),))
    fc1_bias = normal_values(key_of[13], (FF,), 0.5, 3.0, ((0, 8),))
    fc2_weight = normal_values(key_of[14], (FF, D), FF ** -0.5, 0.078125, ((0, 8),))
    fc2_bias = normal_values(key_of[15], (D,), 0.5, 3.0, ((0, 8),))
    cotangent = normal_values(key_of[16], (SEQS, LEN, D), 1.0, 6.0, ((0, 8), (1, 4)))
    return {"tokens": tokens, "picture_ids": picture_ids, "patch_rows": patch_rows, "patch_cols": patch_cols, "norm1_gain": norm1_gain, "norm1_bias": norm1_bias, "qkv_weight": qkv_weight, "qkv_bias": qkv_bias, "proj_weight": proj_weight, "proj_bias": proj_bias, "norm2_gain": norm2_gain, "norm2_bias": norm2_bias, "fc1_weight": fc1_weight, "fc1_bias": fc1_bias, "fc2_weight": fc2_weight, "fc2_bias": fc2_bias, "cotangent": cotangent}


@jax.custom_vjp
def low(v):
    return lax.optimization_barrier(v.astype(jnp.bfloat16)).astype(jnp.float32)

@jax.custom_vjp
def low_back(v):
    return v

def low_keep(v):
    return (low(v), None)

def low_pass(kept, grad):
    return (grad,)

def back_keep(v):
    return (v, None)

def back_low(kept, grad):
    return (low(grad),)
low.defvjp(low_keep, low_pass)
low_back.defvjp(back_keep, back_low)
NORM_EPSILON = 1e-06
PRECISE = lax.Precision.HIGHEST

def matmul(left, right):
    return jnp.dot(left, right, precision=PRECISE, preferred_element_type=jnp.float32)

def rounded(value):
    return low(low_back(value))

def layer_norm(inputs, gain, offset):
    centre = lax.optimization_barrier(jnp.mean(inputs, axis=-1, keepdims=True))
    spread = lax.optimization_barrier(jnp.mean((inputs - centre) ** 2, axis=-1, keepdims=True))
    return (inputs - centre) * lax.rsqrt(spread + NORM_EPSILON) * gain + offset

def rotary_tables(patch_row, patch_col):
    quarter = HD // 4
    inverse = jnp.power(10000.0, -jnp.arange(quarter).astype(jnp.float32) / quarter)
    half_angles = jnp.concatenate([patch_row.astype(jnp.float32)[:, None] * inverse[None, :], patch_col.astype(jnp.float32)[:, None] * inverse[None, :]], axis=-1)
    angles = jnp.concatenate([half_angles, half_angles], axis=-1)
    return (jnp.cos(angles)[:, None, :], jnp.sin(angles)[:, None, :])

def rotate(values_in, cosine, sine):
    half_size = values_in.shape[-1] // 2
    turned = jnp.concatenate([-values_in[..., half_size:], values_in[..., :half_size]], axis=-1)
    return values_in * cosine + turned * sine

def attend(queries, keys, values, picture):
    length = queries.shape[0]
    block_len = min(512, length)
    block_count = length // block_len
    factor = HD ** (-0.5)
    places = jnp.arange(length).astype(jnp.int32)

    def one_block(pieces):
        query_block, picture_block, place_block = pieces
        scores = low_back(jnp.einsum('qhd,khd->hqk', query_block, keys, precision=PRECISE) * factor)
        allowed = (picture_block[:, None] == picture[None, :]) & ((picture[None, :] >= 0) | (place_block[:, None] == places[None, :]))
        scores = jnp.where(allowed[None, :, :], scores, -1e+30)
        row_max = lax.optimization_barrier(jnp.max(scores, axis=-1, keepdims=True))
        powers = jnp.exp(scores - row_max)
        weights = low(powers / lax.optimization_barrier(jnp.sum(powers, axis=-1, keepdims=True)))
        return jnp.einsum('hqk,khd->qhd', weights, values, precision=PRECISE)
    pieces = (queries.reshape(block_count, block_len, HEADS, HD), picture.reshape(block_count, block_len), places.reshape(block_count, block_len))
    outputs = lax.map(jax.checkpoint(one_block), pieces)
    return outputs.reshape(length, HEADS, HD)

def forward(inputs, params, picture, patch_row, patch_col):
    gain_one, bias_one, weight_qkv, bias_qkv, weight_proj, bias_proj, gain_two, bias_two, weight_up, bias_up, weight_down, bias_down = params
    length = inputs.shape[0]
    attn_input = low(layer_norm(inputs, gain_one, bias_one))
    projected = low_back(matmul(attn_input, weight_qkv) + bias_qkv).reshape(length, 3, HEADS, HD)
    cosine, sine = rotary_tables(patch_row, patch_col)
    queries = rounded(rotate(projected[:, 0], cosine, sine))
    keys = rounded(rotate(projected[:, 1], cosine, sine))
    values = rounded(projected[:, 2])
    mixed = rounded(attend(queries, keys, values, picture).reshape(length, D))
    branch = low_back(matmul(mixed, weight_proj) + bias_proj)
    middle = inputs + branch
    mlp_input = low(layer_norm(middle, gain_two, bias_two))
    before = low_back(matmul(mlp_input, weight_up) + bias_up)
    activated = low(before * jax.nn.sigmoid(1.702 * before))
    return middle + matmul(activated, weight_down) + bias_down

def reference(tokens, picture_ids, patch_rows, patch_cols, norm1_gain, norm1_bias, qkv_weight, qkv_bias, proj_weight, proj_bias, norm2_gain, norm2_bias, fc1_weight, fc1_bias, fc2_weight, fc2_bias, cotangent):
    params = tuple((weight.astype(jnp.float32) for weight in (norm1_gain, norm1_bias, qkv_weight, qkv_bias, proj_weight, proj_bias, norm2_gain, norm2_bias, fc1_weight, fc1_bias, fc2_weight, fc2_bias)))

    def one_sequence(sums, pieces):
        inputs, picture, patch_row, patch_col, upstream = pieces

        def apply(block_in, weights_in):
            return forward(block_in, weights_in, picture, patch_row, patch_col)
        result, pull = jax.vjp(apply, inputs.astype(jnp.float32), params)
        input_grad, weight_grads = pull(upstream.astype(jnp.float32))
        sums = tuple((so_far + fresh for so_far, fresh in zip(sums, weight_grads)))
        return (sums, (result.astype(jnp.bfloat16), input_grad))
    zeros = tuple((jnp.zeros_like(weight) for weight in params))
    sums, (block_out, tokens_grad) = lax.scan(one_sequence, zeros, (tokens, picture_ids, patch_rows, patch_cols, cotangent))
    return (block_out, tokens_grad, sums[0], sums[1], sums[2], sums[3], sums[4], sums[5], sums[6], sums[7], sums[8], sums[9], sums[10], sums[11])
```

```python
import jax
import jax.numpy as jnp
from jax import lax
from jax.sharding import PartitionSpec as P

HD = 80
NORM_EPSILON = 1e-06
MASKED = -1e30
BF = jnp.bfloat16
F32 = jnp.float32


def standardize(values_in):
    centre = jnp.mean(values_in, axis=-1, keepdims=True)
    shifted = values_in - centre
    factor = lax.rsqrt(jnp.mean(shifted * shifted, axis=-1, keepdims=True) + NORM_EPSILON)
    return (shifted * factor, factor)


def norm_back(grad_out, normed, factor, gain):
    scaled = grad_out * gain
    return factor * (
        scaled
        - jnp.mean(scaled, axis=-1, keepdims=True)
        - normed * jnp.mean(scaled * normed, axis=-1, keepdims=True)
    )


def rotary_tables(patch_row, patch_col, head_size):
    quarter = head_size // 4
    inverse = jnp.power(10000.0, -jnp.arange(quarter, dtype=F32) / quarter)
    half_angles = jnp.concatenate(
        [
            patch_row.astype(F32)[..., None] * inverse,
            patch_col.astype(F32)[..., None] * inverse,
        ],
        axis=-1,
    )
    angles = jnp.concatenate([half_angles, half_angles], axis=-1)
    return (jnp.cos(angles)[..., None, :], jnp.sin(angles)[..., None, :])


def rotate(values_in, cosine, sine):
    half_size = values_in.shape[-1] // 2
    turned = jnp.concatenate([-values_in[..., half_size:], values_in[..., :half_size]], axis=-1)
    return values_in * cosine + turned * sine


def unrotate(grad_in, cosine, sine):
    half_size = grad_in.shape[-1] // 2
    moved = grad_in * sine
    return grad_in * cosine + jnp.concatenate(
        [moved[..., half_size:], -moved[..., :half_size]], axis=-1
    )


def masked_scores(queries, keys, picture, factor):
    places = jnp.arange(picture.shape[0], dtype=jnp.int32)
    scores = jnp.einsum("qhd,khd->hqk", queries, keys, preferred_element_type=F32) * factor
    allowed = (picture[:, None] == picture[None, :]) & (
        (picture[None, :] >= 0) | (places[:, None] == places[None, :])
    )
    return jnp.where(allowed[None, :, :], scores, MASKED)


def attend(queries, keys, values, picture):
    scores = masked_scores(queries, keys, picture, HD**-0.5)
    row_max = jnp.max(scores, axis=-1, keepdims=True)
    powers = jnp.exp(scores - row_max)
    totals = jnp.sum(powers, axis=-1, keepdims=True)
    weights = (powers / totals).astype(BF)
    mixed = jnp.einsum("hqk,khd->qhd", weights, values, preferred_element_type=F32)
    return mixed.astype(BF), row_max + jnp.log(totals)


def attend_back(queries, keys, values, picture, grad_mixed, log_total):
    factor = HD**-0.5
    scores = masked_scores(queries, keys, picture, factor)
    probs = jnp.exp(scores - log_total)
    weights = probs.astype(BF)
    grad_values = jnp.einsum("hqk,qhd->khd", weights, grad_mixed, preferred_element_type=F32)
    grad_weights = jnp.einsum("qhd,khd->hqk", grad_mixed, values, preferred_element_type=F32)
    centre = jnp.sum(probs * grad_weights, axis=-1, keepdims=True)
    grad_scores = (probs * (grad_weights - centre)).astype(BF)
    grad_queries = jnp.einsum("hqk,khd->qhd", grad_scores, keys, preferred_element_type=F32) * factor
    grad_keys = jnp.einsum("hqk,qhd->khd", grad_scores, queries, preferred_element_type=F32) * factor
    return grad_queries.astype(BF), grad_keys.astype(BF), grad_values.astype(BF)


def dot(left, right):
    return jnp.dot(left, right, preferred_element_type=F32)


def rows_term(left, right):
    return lax.dot_general(left, right, (((0,), (0,)), ((), ())), preferred_element_type=F32)


def contract_back(grad_out, weight):
    return lax.dot_general(grad_out, weight, (((1,), (1,)), ((), ())), preferred_element_type=F32)


def gather(value, axis_name, axis=0):
    return lax.all_gather(value, axis_name, axis=axis, tiled=True)


def scatter_sum(value, axis_name, axis=0):
    return lax.psum_scatter(value, axis_name, scatter_dimension=axis, tiled=True)


def shards(
    tokens,
    picture_ids,
    patch_rows,
    patch_cols,
    norm1_gain,
    norm1_bias,
    qkv_weight,
    qkv_bias,
    proj_weight,
    proj_bias,
    norm2_gain,
    norm2_bias,
    fc1_weight,
    fc1_bias,
    fc2_weight,
    fc2_bias,
    cotangent,
):
    n = lax.axis_size("seq")
    me = lax.axis_index("seq")
    stores = lax.axis_size("fsdp")
    _, own, width = tokens.shape
    heads = width // HD
    local_heads = heads // n
    hw = local_heads * HD
    rows = qkv_weight.shape[0]
    hidden = fc1_weight.shape[1]
    part = hidden // (stores * n)

    def pick(value, axis):
        return lax.dynamic_index_in_dim(value, me, axis, keepdims=False)

    own_qkv = pick(qkv_weight.reshape(rows, 3, n, hw), 2).reshape(rows, 3 * hw)
    own_up = pick(fc1_weight.reshape(rows, stores, n, part), 2).reshape(rows, stores * part)
    own_down = pick(fc2_weight.reshape(n, part, width), 0)
    small = (norm1_gain, norm1_bias, proj_bias, norm2_gain, norm2_bias, fc2_bias, qkv_bias, fc1_bias)
    sizes = [item.shape[0] for item in small]
    packed = gather(jnp.concatenate(small)[None], "fsdp")
    weight_qkv = gather(own_qkv, "fsdp")
    weight_proj = gather(proj_weight, "fsdp")
    weight_up = gather(own_up, "fsdp")
    weight_down = gather(own_down, "fsdp")
    params = []
    start = 0
    for size in sizes:
        params.append(packed[:, start : start + size].reshape(-1).astype(F32))
        start += size
    gain_one, bias_one, bias_proj, gain_two, bias_two, bias_down, bias_qkv, bias_up = params
    bias_qkv = pick(bias_qkv.reshape(3, n, hw), 1).reshape(3 * hw)
    bias_up = pick(bias_up.reshape(stores, n, part), 1).reshape(stores * part)

    places = jnp.stack([picture_ids[0], patch_rows[0], patch_cols[0]])
    places = gather(places, "seq", 1)
    picture = places[0]
    all_tokens = gather(tokens[0], "seq").astype(F32)
    upstream = gather(cotangent[0], "seq")
    length = all_tokens.shape[0]

    def mine(value):
        return lax.dynamic_slice_in_dim(value, me * own, own, 0)

    normed_one, factor_one = standardize(all_tokens)
    attn_input = (normed_one * gain_one + bias_one).astype(BF)
    projected = (dot(attn_input, weight_qkv) + bias_qkv).reshape(length, 3, local_heads, HD)
    cosine, sine = rotary_tables(places[1], places[2], HD)
    queries = rotate(projected[:, 0], cosine, sine).astype(BF)
    keys = rotate(projected[:, 1], cosine, sine).astype(BF)
    values = projected[:, 2].astype(BF)
    mixed_own, log_total = attend(queries, keys, values, picture)
    mixed = gather(mixed_own.reshape(length, hw), "seq", 1)
    middle = all_tokens + dot(mixed, weight_proj) + bias_proj
    normed_two, factor_two = standardize(middle)
    mlp_input = (normed_two * gain_two + bias_two).astype(BF)
    before = dot(mlp_input, weight_up) + bias_up
    gate = jax.nn.sigmoid(1.702 * before)
    activated = (before * gate).astype(BF)
    out_part = dot(activated, weight_down).astype(BF)
    block_out = (mine(middle) + scatter_sum(out_part, "seq").astype(F32) + bias_down).astype(BF)

    grad_down = scatter_sum(rows_term(activated, upstream).astype(BF), "fsdp")
    grad_activated = contract_back(upstream, weight_down)
    grad_before = (grad_activated * (gate + 1.702 * before * gate * (1.0 - gate))).astype(BF)
    grad_up = scatter_sum(rows_term(mlp_input, grad_before).astype(BF), "fsdp")
    grad_mlp_input = scatter_sum(contract_back(grad_before, weight_up).astype(BF), "seq").astype(F32)
    own_upstream = cotangent[0].astype(F32)
    own_two = mine(normed_two)
    grad_middle = own_upstream + norm_back(grad_mlp_input, own_two, mine(factor_two), gain_two)
    grad_branch = grad_middle.astype(BF)
    grad_mixed = contract_back(grad_branch, weight_proj).astype(BF)
    grad_heads = lax.all_to_all(grad_mixed, "seq", split_axis=1, concat_axis=0, tiled=True)
    branch_part = lax.all_to_all(grad_branch, "seq", split_axis=1, concat_axis=0, tiled=True)
    grad_proj = scatter_sum(rows_term(mixed, branch_part).astype(BF), "fsdp")
    grad_queries, grad_keys, grad_values = attend_back(
        queries, keys, values, picture, grad_heads.reshape(length, local_heads, HD), log_total
    )
    grad_projected = jnp.stack(
        [
            unrotate(grad_queries.astype(F32), cosine, sine).astype(BF),
            unrotate(grad_keys.astype(F32), cosine, sine).astype(BF),
            grad_values,
        ],
        axis=1,
    ).reshape(length, 3 * hw)
    grad_qkv = scatter_sum(rows_term(attn_input, grad_projected).astype(BF), "fsdp")
    grad_attn_input = scatter_sum(contract_back(grad_projected, weight_qkv).astype(BF), "seq").astype(F32)
    own_one = mine(normed_one)
    tokens_grad = grad_middle + norm_back(grad_attn_input, own_one, mine(factor_one), gain_one)

    def spread(value, groups):
        empty = jnp.zeros((groups, n, value.shape[0] // groups), F32)
        return lax.dynamic_update_slice_in_dim(
            empty, value.reshape(groups, 1, -1), me, 1
        ).reshape(stores, -1)

    sums = [
        jnp.sum(grad_attn_input * own_one, axis=0).reshape(stores, -1),
        jnp.sum(grad_attn_input, axis=0).reshape(stores, -1),
        jnp.sum(grad_branch.astype(F32), axis=0).reshape(stores, -1),
        jnp.sum(grad_mlp_input * own_two, axis=0).reshape(stores, -1),
        jnp.sum(grad_mlp_input, axis=0).reshape(stores, -1),
        jnp.sum(own_upstream, axis=0).reshape(stores, -1),
        spread(jnp.sum(grad_projected.astype(F32), axis=0), 3),
        spread(jnp.sum(grad_before.astype(F32), axis=0), stores),
    ]
    summed = lax.psum(scatter_sum(jnp.concatenate(sums, axis=1), "fsdp"), "seq")[0]
    finals = []
    start = 0
    for size in sizes:
        finals.append(summed[start : start + size])
        start += size
    full_down = gather(grad_down, "seq").astype(F32)
    full_up = gather(grad_up[None], "seq").reshape(n, rows, stores, part)
    full_up = full_up.transpose(1, 2, 0, 3).reshape(rows, hidden).astype(F32)
    full_proj = gather(grad_proj, "seq", 1).astype(F32)
    full_qkv = gather(grad_qkv[None], "seq").reshape(n, rows, 3, hw)
    full_qkv = full_qkv.transpose(1, 2, 0, 3).reshape(rows, 3 * width).astype(F32)
    return (
        block_out[None],
        tokens_grad[None],
        finals[0],
        finals[1],
        full_qkv,
        finals[6],
        full_proj,
        finals[2],
        finals[3],
        finals[4],
        full_up,
        finals[7],
        full_down,
        finals[5],
    )


def solution(mesh):
    token = P("fsdp", "seq", None)
    place = P("fsdp", "seq")
    vector = P("fsdp")
    matrix = P("fsdp", None)
    in_specs = (
        token,
        place,
        place,
        place,
        vector,
        vector,
        matrix,
        vector,
        matrix,
        vector,
        vector,
        vector,
        matrix,
        vector,
        matrix,
        vector,
        token,
    )
    out_specs = (
        token,
        token,
        vector,
        vector,
        matrix,
        vector,
        matrix,
        vector,
        vector,
        vector,
        matrix,
        vector,
        matrix,
        vector,
    )
    return jax.shard_map(shards, mesh=mesh, in_specs=in_specs, out_specs=out_specs, check_vma=False)
```

```python
import functools

import jax
import jax.numpy as jnp
import numpy as np
from jax import lax
from jax.experimental import pallas as pl
from jax.experimental.pallas import tpu as pltpu
from jax.sharding import PartitionSpec as P

HD = 80
NORM_EPSILON = 1e-06
MASKED = -1e30
BF = jnp.bfloat16
F32 = jnp.float32


def standardize(values_in):
    centre = jnp.mean(values_in, axis=-1, keepdims=True)
    shifted = values_in - centre
    factor = lax.rsqrt(jnp.mean(shifted * shifted, axis=-1, keepdims=True) + NORM_EPSILON)
    return (shifted * factor, factor)


def norm_back(grad_out, normed, factor, gain):
    scaled = grad_out * gain
    return factor * (
        scaled
        - jnp.mean(scaled, axis=-1, keepdims=True)
        - normed * jnp.mean(scaled * normed, axis=-1, keepdims=True)
    )


def rotary_tables(patch_row, patch_col, head_size):
    quarter = head_size // 4
    inverse = jnp.power(10000.0, -jnp.arange(quarter, dtype=F32) / quarter)
    half_angles = jnp.concatenate(
        [
            patch_row.astype(F32)[..., None] * inverse,
            patch_col.astype(F32)[..., None] * inverse,
        ],
        axis=-1,
    )
    angles = jnp.concatenate([half_angles, half_angles], axis=-1)
    return (jnp.cos(angles)[..., None, :], jnp.sin(angles)[..., None, :])


def rotate(values_in, cosine, sine):
    half_size = values_in.shape[-1] // 2
    turned = jnp.concatenate([-values_in[..., half_size:], values_in[..., :half_size]], axis=-1)
    return values_in * cosine + turned * sine


def unrotate(grad_in, cosine, sine):
    half_size = grad_in.shape[-1] // 2
    moved = grad_in * sine
    return grad_in * cosine + jnp.concatenate(
        [moved[..., half_size:], -moved[..., :half_size]], axis=-1
    )


def masked_scores(queries, keys, picture, factor):
    places = jnp.arange(picture.shape[0], dtype=jnp.int32)
    scores = jnp.einsum("qhd,khd->hqk", queries, keys, preferred_element_type=F32) * factor
    allowed = (picture[:, None] == picture[None, :]) & (
        (picture[None, :] >= 0) | (places[:, None] == places[None, :])
    )
    return jnp.where(allowed[None, :, :], scores, MASKED)


def attend(queries, keys, values, picture):
    scores = masked_scores(queries, keys, picture, HD**-0.5)
    row_max = jnp.max(scores, axis=-1, keepdims=True)
    powers = jnp.exp(scores - row_max)
    totals = jnp.sum(powers, axis=-1, keepdims=True)
    weights = (powers / totals).astype(BF)
    mixed = jnp.einsum("hqk,khd->qhd", weights, values, preferred_element_type=F32)
    return mixed.astype(BF), row_max + jnp.log(totals)


def attend_back(queries, keys, values, picture, grad_mixed, log_total):
    factor = HD**-0.5
    scores = masked_scores(queries, keys, picture, factor)
    probs = jnp.exp(scores - log_total)
    weights = probs.astype(BF)
    grad_values = jnp.einsum("hqk,qhd->khd", weights, grad_mixed, preferred_element_type=F32)
    grad_weights = jnp.einsum("qhd,khd->hqk", grad_mixed, values, preferred_element_type=F32)
    centre = jnp.sum(probs * grad_weights, axis=-1, keepdims=True)
    grad_scores = (probs * (grad_weights - centre)).astype(BF)
    grad_queries = jnp.einsum("hqk,khd->qhd", grad_scores, keys, preferred_element_type=F32) * factor
    grad_keys = jnp.einsum("hqk,qhd->khd", grad_scores, queries, preferred_element_type=F32) * factor
    return grad_queries.astype(BF), grad_keys.astype(BF), grad_values.astype(BF)


def dot(left, right):
    return jnp.dot(left, right, preferred_element_type=F32)


def rows_term(left, right):
    return lax.dot_general(left, right, (((0,), (0,)), ((), ())), preferred_element_type=F32)


def contract_back(grad_out, weight):
    return lax.dot_general(grad_out, weight, (((1,), (1,)), ((), ())), preferred_element_type=F32)


def gather(value, axis_name, axis=0):
    return lax.all_gather(value, axis_name, axis=axis, tiled=True)


def scatter_sum(value, axis_name, axis=0):
    return lax.psum_scatter(value, axis_name, scatter_dimension=axis, tiled=True)

MESH = pl.DeviceIdType.MESH


def mm(left, right):
    return jnp.dot(left, right, preferred_element_type=F32)


def mm_nt(left, right):
    return lax.dot_general(left, right, (((1,), (1,)), ((), ())), preferred_element_type=F32)


def mm_tn(left, right):
    return lax.dot_general(left, right, (((0,), (0,)), ((), ())), preferred_element_type=F32)


def lane_pad(value, lanes):
    gap = lanes - value.shape[1]
    if gap == 0:
        return value
    return jnp.concatenate([value, jnp.zeros((value.shape[0], gap), value.dtype)], axis=1)


def moments(value):
    centre = jnp.mean(value, axis=-1, keepdims=True)
    shifted = value - centre
    factor = lax.rsqrt(jnp.mean(shifted * shifted, axis=-1, keepdims=True) + NORM_EPSILON)
    return shifted * factor, factor


def block_kernel(
    dims,
    tok_in,
    cot_in,
    plc_in,
    small_in,
    wave_in,
    wq_in,
    wp_in,
    w1_in,
    w2_in,
    out_ref,
    tgrad_ref,
    rq_ref,
    rp_ref,
    r1_ref,
    r2_ref,
    sums_ref,
    tokb,
    ain,
    cotb,
    plb,
    plt,
    smb,
    vec,
    bqkv,
    cosb,
    sinb,
    wqc,
    wq,
    wp,
    w1,
    w2,
    qkv,
    lse,
    mixc,
    mix,
    mid,
    mlp,
    act,
    dge,
    snd,
    rsr,
    gmd,
    gp,
    dq4,
    dp4,
    d14,
    d24,
    zq3,
    zp3,
    z13,
    z23,
    dkv,
    smg,
    sg8,
    sems,
    local_sems,
):
    n, T, L, D, F, R, hl, P1, CQ, HP = dims
    J = F // 2
    hw = hl * HD
    W = 128
    QW = hl * W
    scale = HD**-0.5
    tile = 256 if D % 256 == 0 else 128
    me = lax.axis_index("seq")
    f = lax.axis_index("fsdp")
    k = f % 2
    j = f // 2
    partner = f + 1 - 2 * k
    seq_to = [(me + o) % n for o in range(n)]
    seq_from = [(me + n - o) % n for o in range(n)]
    z_to = [2 * ((j + d) % J) + k for d in range(J)]
    z_from = [2 * ((j + J - d) % J) + k for d in range(J)]
    used = {"remote": 0, "local": 0}
    leftover = []

    def take(count=1):
        used["remote"] += count
        return used["remote"] - count

    def send(src, dst, where, recv, late=True):
        copy = pltpu.make_async_remote_copy(
            src_ref=src,
            dst_ref=dst,
            send_sem=sems.at[take()],
            recv_sem=sems.at[recv],
            device_id=where,
            device_id_type=MESH,
        )
        copy.start()
        if late:
            leftover.append(copy)
        return copy

    def load(src, dst):
        used["local"] += 1
        copy = pltpu.make_async_copy(src, dst, local_sems.at[used["local"] - 1])
        copy.start()
        return copy

    def band(ref, index, size):
        return ref.at[pl.ds(pl.multiple_of(index * size, size), size)]

    def rows_of(index, size):
        return pl.ds(pl.multiple_of(index * size, size), size)

    def strips(total, step, body):
        def run(s, carry):
            body(rows_of(s, step))
            return carry

        lax.fori_loop(0, total // step, run, 0)

    strip = 32

    barrier = pltpu.get_barrier_semaphore()
    for o in range(1, n):
        pl.semaphore_signal(barrier, inc=1, device_id={"seq": seq_to[o]}, device_id_type=MESH)
    for o in range(1, F):
        pl.semaphore_signal(barrier, inc=1, device_id={"fsdp": (f + o) % F}, device_id_type=MESH)
    pl.semaphore_wait(barrier, n - 1 + F - 1)

    tok_copies = []
    for o in range(1, n):
        where = {"seq": seq_to[o]}
        c1 = send(plc_in, plb.at[me], where, take())
        c2 = send(tok_in, tokb.at[me], where, take())
        tok_copies.append((c1, c2))
    own_tok = load(tok_in, tokb.at[me])
    own_plc = load(plc_in, plb.at[me])
    own_small = load(small_in, smb.at[f])

    class Weight:
        def __init__(self, src, buf, rows):
            self.buf, self.rows = buf, rows
            self.own = load(src, band(buf, f, rows))
            self.near = send(src, band(buf, f, rows), {"fsdp": partner}, take())
            self.far = [
                send(src, band(buf, f, rows), {"fsdp": z_to[d]}, take()) for d in range(1, J)
            ]
            self.relayed = []

        def relay(self):
            for d in range(1, J):
                self.far[d - 1].wait_recv()
                part = band(self.buf, z_from[d], self.rows)
                self.relayed.append(send(part, part, {"fsdp": partner}, take(), late=False))

        def finish(self):
            self.own.wait()
            self.near.wait_recv()
            for copy in self.relayed:
                copy.wait_recv()

        def drain(self):
            for copy in self.relayed:
                copy.wait_send()

    weight_q = Weight(wq_in, wqc, R)
    small_copies = [
        send(small_in, smb.at[f], {"fsdp": (f + o) % F}, take()) for o in range(1, F)
    ]
    weight_p = Weight(wp_in, wp, R)
    weight_1 = Weight(w1_in, w1, R)
    weight_2 = Weight(w2_in, w2, R)
    own_cot = load(cot_in, cotb.at[me])

    own_small.wait()
    for copy in small_copies:
        copy.wait_recv()
    for row in range(7):
        vec[row : row + 1, :] = jnp.concatenate(
            [smb[s, row : row + 1, :R] for s in range(F)], axis=1
        )
    groups = 3 * D // R // 3
    heads = []
    for t in range(3):
        start = t * groups + me * (hw // R)
        line = jnp.concatenate(
            [
                smb[(start + b) // 3, pl.ds(7 + (start + b) % 3, 1), :][:, :R]
                for b in range(hw // R)
            ],
            axis=1,
        )
        for h in range(hl):
            heads.append(lane_pad(line[:, h * HD : (h + 1) * HD], W))
    bqkv[...] = jnp.broadcast_to(jnp.concatenate(heads, axis=1), bqkv.shape)

    def vector(row):
        return vec[row : row + 1, :]

    own_plc.wait()
    for c1, _ in tok_copies:
        c1.wait_recv()

    def table(i, carry):
        rows = rows_of(i, T)
        turned = jnp.transpose(plb[i], (1, 0))
        plt[rows, :] = turned
        angle = turned[:, 1:2] * wave_in[0:1, :] + turned[:, 2:3] * wave_in[1:2, :]
        cosb[rows, :] = jnp.cos(angle)
        sinb[rows, :] = jnp.sin(angle) * wave_in[2:3, :]
        return carry

    lax.fori_loop(0, n, table, 0)
    lane = lax.broadcasted_iota(jnp.int32, (1, W), 1)
    low_half = lane < HD // 2

    def swap(value):
        return jnp.where(
            low_half, pltpu.roll(value, W - HD // 2, 1), pltpu.roll(value, HD // 2, 1)
        )

    def norm_one(i):
        def body(rows):
            normed, _ = moments(tokb[i, rows, :].astype(F32))
            ain[rows_of_block(i, rows), :] = (normed * vector(0) + vector(1)).astype(BF)

        strips(T, strip, body)

    def rows_of_block(i, rows):
        return pl.ds(pl.multiple_of(i * T + rows.start, strip), strip)

    own_tok.wait()
    norm_one(me)
    for o in range(1, n):
        tok_copies[o - 1][1].wait_recv()
        norm_one(seq_from[o])

    weight_q.relay()
    weight_q.finish()

    def spread_heads(rows):
        line = wqc[rows, :]
        for h in range(3 * hl):
            wq[rows, h * W : (h + 1) * W] = lane_pad(line[:, h * HD : (h + 1) * HD], W)

    strips(D, R, spread_heads)

    def project(i, carry):
        rows = rows_of(i, T)
        line = ain[rows, :]
        cosine = cosb[rows, :]
        sine = sinb[rows, :]
        for t in range(3):
            part = mm(line, wq[:, t * QW : (t + 1) * QW]) + bqkv[0:1, t * QW : (t + 1) * QW]
            for h in range(hl):
                u = part[:, h * W : (h + 1) * W]
                if t < 2:
                    u = u * cosine + swap(u) * sine
                qkv[rows, t * QW + h * W : t * QW + (h + 1) * W] = u.astype(BF)
        return carry

    lax.fori_loop(0, n, project, 0)

    def masked(scores, i):
        ids = jnp.concatenate([plb[b, 3:4, :] for b in range(n)], axis=1)
        own_ids = plt[rows_of(i, T), 3:4]
        return jnp.where(own_ids == ids, scores * scale, MASKED)

    mix_send, mix_recv = take(n * (n - 1)), take(n * (n - 1))

    def mix_copy(i, o, peer, source):
        return pltpu.make_async_remote_copy(
            src_ref=mixc.at[source, i],
            dst_ref=mixc.at[source, i],
            send_sem=sems.at[mix_send + i * (n - 1) + o - 1],
            recv_sem=sems.at[mix_recv + i * (n - 1) + o - 1],
            device_id={"seq": peer},
            device_id_type=MESH,
        )

    def attend_block(i, carry):
        rows = rows_of(i, T)
        outs = []
        logs = jnp.zeros((T, W), F32)
        for h in range(hl):
            q = qkv[rows, h * W : (h + 1) * W]
            kk = qkv[:, QW + h * W : QW + (h + 1) * W]
            v = qkv[:, 2 * QW + h * W : 2 * QW + (h + 1) * W]
            s = masked(mm_nt(q, kk), i)
            top = jnp.max(s, axis=-1, keepdims=True)
            p = jnp.exp(s - top)
            total = jnp.sum(p, axis=-1, keepdims=True)
            outs.append((mm(p.astype(BF), v) / total)[:, :HD].astype(BF))
            logs = jnp.where(lane == h, top + jnp.log(total), logs)
        lse[rows, :] = logs
        mixc[me, i] = lane_pad(jnp.concatenate(outs, axis=1), HP)
        for o in range(1, n):
            mix_copy(i, o, seq_to[o], me).start()
        return carry

    lax.fori_loop(0, n, attend_block, 0)
    cot_copies = [
        send(cot_in, cotb.at[me], {"seq": seq_to[o]}, take()) for o in range(1, n)
    ]

    weight_p.relay()
    weight_p.finish()

    def branch(t, carry):
        i = (me + 1 + t) % n
        rows = rows_of(i, T)
        for o in range(1, n):
            mix_copy(i, o, seq_to[o], seq_from[o]).wait_recv()
        mix[rows, :] = jnp.concatenate([mixc[c, i][:, :hw] for c in range(n)], axis=1)
        mid[...] = mm(mix[rows, :], wp[...])

        def body(part):
            whole = rows_of_block(i, part)
            value = mid[part, :] + tokb[i, part, :].astype(F32) + vector(2)
            mid[part, :] = value
            normed, _ = moments(value)
            mlp[whole, :] = (normed * vector(3) + vector(4)).astype(BF)

        strips(T, strip, body)
        return carry

    lax.fori_loop(0, n, branch, 0)

    weight_1.relay()
    weight_1.finish()

    def up(i, carry):
        rows = rows_of(i, T)
        before = mm(mlp[rows, :], w1[...]) + vector(6)
        gate = jax.nn.sigmoid(1.702 * before)
        act[rows, :] = (before * gate).astype(BF)
        dge[rows, :] = (gate + 1.702 * before * gate * (1.0 - gate)).astype(BF)
        return carry

    lax.fori_loop(0, n, up, 0)

    own_cot.wait()
    for copy in cot_copies:
        copy.wait_recv()
    weight_2.relay()
    weight_2.finish()

    class Scatter:
        def __init__(self, stage):
            self.stage = stage
            self.out, self.into = take(n - 1), take(n - 1)

        def copy(self, t, to):
            return pltpu.make_async_remote_copy(
                src_ref=band(self.stage, to, T),
                dst_ref=rsr.at[t],
                send_sem=sems.at[self.out + t],
                recv_sem=sems.at[self.into + t],
                device_id={"seq": to},
                device_id_type=MESH,
            )

        def start(self, t, i):
            @pl.when(t < n - 1)
            def _():
                self.copy(t, i).start()

        def wait_recv(self):
            for t in range(n - 1):
                self.copy(t, seq_to[t + 1]).wait_recv()

        def wait_send(self):
            for t in range(n - 1):
                self.copy(t, seq_to[t + 1]).wait_send()

    for i in range(n):
        for o in range(1, n):
            mix_copy(i, o, seq_to[o], me).wait_send()
    scatter_mlp = Scatter(snd)

    def back(t, carry):
        i = (me + 1 + t) % n
        rows = rows_of(i, T)
        grad = (mm_nt(cotb[i], w2[...]) * dge[rows, :].astype(F32)).astype(BF)
        dge[rows, :] = grad
        snd[rows, :] = mm_nt(grad, w1[...]).astype(BF)
        scatter_mlp.start(t, i)
        return carry

    lax.fori_loop(0, n, back, 0)

    class Gradient:
        def __init__(self, grad, other, far, result, lanes):
            self.grad, self.other, self.far, self.result = grad, other, far, result
            self.lanes = lanes

        def exchange(self):
            self.near = []
            for c in range(J):
                self.near.append(
                    send(
                        band(self.grad, 2 * c + 1 - k, R),
                        self.other.at[c],
                        {"fsdp": partner},
                        take(),
                    )
                )

        def add_near(self):
            for copy in self.near:
                copy.wait_recv()

            def chip(c, carry):
                rows = rows_of(2 * c + k, R)
                self.grad[rows, :] = (
                    self.grad[rows, :].astype(F32) + self.other[c].astype(F32)
                ).astype(BF)
                return carry

            lax.fori_loop(0, J, chip, 0)
            self.across = [
                send(
                    band(self.grad, z_to[d], R),
                    self.far.at[d - 1],
                    {"fsdp": z_to[d]},
                    take(),
                )
                for d in range(1, J)
            ]

        def add_far(self):
            for copy in self.across:
                copy.wait_recv()
            rows = rows_of(f, R)
            total = self.grad[rows, :].astype(F32)
            for d in range(J - 1):
                total = total + self.far[d].astype(F32)
            self.other[0] = total.astype(BF)
            mine = self.other.at[0]
            self.keep = load(mine, self.result.at[me])
            self.share = [
                send(mine, self.result.at[me], {"seq": seq_to[o]}, take()) for o in range(1, n)
            ]

        def finish(self):
            self.keep.wait()
            for copy in self.share:
                copy.wait_recv()

    grad_up = Gradient(w1, d14, z13, r1_ref, P1)
    grad_down = Gradient(w2, d24, z23, r2_ref, D)
    grad_proj = Gradient(gp, dp4, zp3, rp_ref, HP)
    grad_qkv = Gradient(wqc, dq4, zq3, rq_ref, CQ)

    weight_1.drain()
    weight_2.drain()
    weight_q.drain()

    def up_grad(t, carry):
        w1[rows_of(t, tile), :] = mm_tn(mlp[:, rows_of(t, tile)], dge[...]).astype(BF)
        return carry

    lax.fori_loop(0, D // tile, up_grad, 0)
    grad_up.exchange()

    def down(i, carry):
        rows = rows_of(i, T)
        mlp[rows, :] = mm(act[rows, :], w2[...]).astype(BF)
        return carry

    lax.fori_loop(0, n, down, 0)

    def down_grad(t, carry):
        lanes = rows_of(t, tile)
        total = mm_tn(act[0:T, lanes], cotb[0])
        for b in range(1, n):
            total = total + mm_tn(act[b * T : (b + 1) * T, lanes], cotb[b])
        w2[lanes, :] = total.astype(BF)
        return carry

    lax.fori_loop(0, P1 // tile, down_grad, 0)
    grad_down.exchange()

    smg[...] = jnp.zeros(smg.shape, F32)
    scatter_mlp.wait_recv()

    def gather_parts(part):
        whole = rows_of_block(me, part)
        total = snd[whole, :].astype(F32)
        for t in range(n - 1):
            total = total + rsr[t, part, :].astype(F32)
        return total

    def add_sum(row, value):
        smg[row : row + 1, :] = smg[row : row + 1, :] + jnp.sum(value, axis=0, keepdims=True)

    def norm_two_back(part):
        upstream = cotb[me, part, :].astype(F32)
        grad = gather_parts(part)
        normed, factor = moments(mid[part, :])
        scaled = grad * vector(3)
        value = upstream + factor * (
            scaled
            - jnp.mean(scaled, axis=-1, keepdims=True)
            - normed * jnp.mean(scaled * normed, axis=-1, keepdims=True)
        )
        gmd[part, :] = value
        low = value.astype(BF)
        snd[rows_of_block(me, part), :] = low
        add_sum(2, low.astype(F32))
        add_sum(3, grad * normed)
        add_sum(4, grad)
        add_sum(5, upstream)

    strips(T, strip, norm_two_back)
    own_rows = rows_of(me, T)
    low_branch = snd[own_rows, :]
    grad_mixed = mm_nt(low_branch, wp[...]).astype(BF)
    for c in range(n):
        mixc[0, c] = lane_pad(grad_mixed[:, c * hw : (c + 1) * hw], HP)
        mixc[2, c] = lane_pad(low_branch[:, c * hw : (c + 1) * hw], HP)
    head_copies = [
        send(mixc.at[0, seq_to[o]], mixc.at[1, me], {"seq": seq_to[o]}, take()) for o in range(1, n)
    ]
    branch_copies = [
        send(mixc.at[2, seq_to[o]], mixc.at[3, me], {"seq": seq_to[o]}, take()) for o in range(1, n)
    ]
    mixc[1, me] = mixc[0, me]
    mixc[3, me] = mixc[2, me]

    grad_up.add_near()
    grad_down.add_near()

    for copy in head_copies:
        copy.wait_recv()
    out_copies = [
        send(band(mlp, seq_to[o], T), tokb.at[me], {"seq": seq_to[o]}, take()) for o in range(1, n)
    ]

    for h in range(hl):
        q_at = slice(h * W, (h + 1) * W)
        k_at = slice(QW + h * W, QW + (h + 1) * W)
        v_at = slice(2 * QW + h * W, 2 * QW + (h + 1) * W)
        dkv[...] = jnp.zeros(dkv.shape, F32)

        def attend_back_block(i, carry):
            rows = rows_of(i, T)
            q = qkv[rows, q_at]
            kk = qkv[:, k_at]
            g = lane_pad(mixc[1, i][:, h * HD : (h + 1) * HD], W)
            p = jnp.exp(masked(mm_nt(q, kk), i) - lse[rows, h : h + 1])
            dp = mm_nt(g, qkv[:, v_at])
            dkv[:, W:] = dkv[:, W:] + mm_tn(p.astype(BF), g)
            centre = jnp.sum(p * dp, axis=-1, keepdims=True)
            ds = (p * (dp - centre)).astype(BF)
            dq = (mm(ds, kk) * scale).astype(BF).astype(F32)
            dkv[:, :W] = dkv[:, :W] + mm_tn(ds, q)
            qkv[rows, q_at] = (dq * cosb[rows, :] - swap(dq) * sinb[rows, :]).astype(BF)
            return carry

        lax.fori_loop(0, n, attend_back_block, 0)

        def turn_back(i, carry):
            rows = rows_of(i, T)
            dk = (dkv[rows, :W] * scale).astype(BF).astype(F32)
            qkv[rows, k_at] = (dk * cosb[rows, :] - swap(dk) * sinb[rows, :]).astype(BF)
            qkv[rows, v_at] = dkv[rows, W:].astype(BF)
            return carry

        lax.fori_loop(0, n, turn_back, 0)

    scatter_mlp.wait_send()
    scatter_attn = Scatter(snd)

    def attn_back(t, carry):
        i = (me + 1 + t) % n
        rows = rows_of(i, T)
        snd[rows, :] = mm_nt(qkv[rows, :], wq[...]).astype(BF)
        scatter_attn.start(t, i)
        return carry

    lax.fori_loop(0, n, attn_back, 0)

    def qkv_grad(t, carry):
        rows = rows_of(t, tile)
        total = mm_tn(ain[:, rows], qkv[...])
        wqc[rows, :] = lane_pad(
            jnp.concatenate([total[:, h * W : h * W + HD].astype(BF) for h in range(3 * hl)], axis=1),
            CQ,
        )
        return carry

    lax.fori_loop(0, D // tile, qkv_grad, 0)
    grad_qkv.exchange()

    for copy in branch_copies:
        copy.wait_recv()

    def proj_grad(t, carry):
        lanes = rows_of(t, tile)
        total = mm_tn(mix[0:T, lanes], mixc[3, 0])
        for b in range(1, n):
            total = total + mm_tn(mix[b * T : (b + 1) * T, lanes], mixc[3, b])
        gp[lanes, :] = total.astype(BF)
        return carry

    lax.fori_loop(0, D // tile, proj_grad, 0)
    grad_proj.exchange()
    grad_qkv.add_near()
    grad_proj.add_near()
    grad_up.add_far()
    grad_down.add_far()

    def bias_sums(part):
        smg[6:7, :] = smg[6:7, :] + jnp.sum(dge[part, :].astype(F32), axis=0, keepdims=True)
        line = jnp.sum(qkv[part, :].astype(F32), axis=0, keepdims=True)
        line = lane_pad(
            jnp.concatenate([line[:, h * W : h * W + HD] for h in range(3 * hl)], axis=1), D
        )
        smg[7:8, :] = smg[7:8, :] + line

    strips(L, 64, bias_sums)

    scatter_attn.wait_recv()

    def norm_one_back(part):
        grad = gather_parts(part)
        normed, factor = moments(tokb[me, part, :].astype(F32))
        scaled = grad * vector(0)
        gmd[part, :] = gmd[part, :] + factor * (
            scaled
            - jnp.mean(scaled, axis=-1, keepdims=True)
            - normed * jnp.mean(scaled * normed, axis=-1, keepdims=True)
        )
        add_sum(0, grad * normed)
        add_sum(1, grad)

    strips(T, strip, norm_one_back)
    tokens_out = load(gmd, tgrad_ref)
    sum_copies = [
        send(smg, sg8.at[f], {"fsdp": (f + o) % F}, take()) for o in range(1, F)
    ]
    sg8[f] = smg[...]

    for copy in out_copies:
        copy.wait_recv()

    def write_out(part):
        whole = rows_of_block(me, part)
        total = mid[part, :] + mlp[whole, :].astype(F32) + vector(5)
        for o in range(1, n):
            total = total + tokb[seq_from[o], part, :].astype(F32)
        bias_rows = rows_of_block(me, part)
        ain[bias_rows, :] = total.astype(BF)

    strips(T, strip, write_out)
    block_out = load(band(ain, me, T), out_ref)

    for copy in sum_copies:
        copy.wait_recv()
    total = sg8[0]
    for s in range(1, F):
        total = total + sg8[s]
    plain = lax.broadcasted_iota(jnp.int32, total.shape, 0)
    vec[...] = jnp.where(plain < 8, total, 0.0)
    sums_keep = load(vec, sums_ref.at[me])
    sums_share = [
        send(vec, sums_ref.at[me], {"seq": seq_to[o]}, take()) for o in range(1, n)
    ]

    grad_qkv.add_far()
    grad_proj.add_far()
    for item in (grad_up, grad_down, grad_proj, grad_qkv):
        item.finish()
    for copy in sums_share:
        copy.wait_recv()
    sums_keep.wait()
    tokens_out.wait()
    block_out.wait()
    weight_p.drain()
    scatter_attn.wait_send()
    for copy in leftover:
        copy.wait_send()


def round_up(value, step):
    return -(-value // step) * step


def shards_kernel(
    tokens,
    picture_ids,
    patch_rows,
    patch_cols,
    norm1_gain,
    norm1_bias,
    qkv_weight,
    qkv_bias,
    proj_weight,
    proj_bias,
    norm2_gain,
    norm2_bias,
    fc1_weight,
    fc1_bias,
    fc2_weight,
    fc2_bias,
    cotangent,
):
    n = lax.axis_size("seq")
    me = lax.axis_index("seq")
    F = lax.axis_size("fsdp")
    f = lax.axis_index("fsdp")
    _, T, D = tokens.shape
    L = n * T
    hl = D // HD // n
    hw = hl * HD
    R = D // F
    hidden = fc1_weight.shape[1]
    P1 = hidden // n
    part = hidden // (F * n)
    CQ = round_up(3 * hw, 128)
    HP = round_up(hw, 128)
    J = F // 2
    W = 128

    def pick(value, axis):
        return lax.dynamic_index_in_dim(value, me, axis, keepdims=False)

    own_qkv = pick(qkv_weight.reshape(R, 3, n, hw), 2).reshape(R, 3 * hw)
    own_qkv = jnp.pad(own_qkv, ((0, 0), (0, CQ - 3 * hw)))
    own_up = pick(fc1_weight.reshape(R, F, n, part), 2).reshape(R, P1)
    own_down = pick(fc2_weight.reshape(n, part, D), 0)
    small = jnp.concatenate(
        [
            norm1_gain,
            norm1_bias,
            proj_bias,
            norm2_gain,
            norm2_bias,
            fc2_bias,
            pick(fc1_bias.reshape(n, part), 0),
            qkv_bias,
        ]
    )
    small = jnp.pad(small.astype(F32).reshape(10, R), ((0, 6), (0, 0)))
    spot = jnp.arange(T, dtype=jnp.int32) + me * T
    ids = jnp.where(picture_ids[0] >= 0, picture_ids[0], -1 - spot)
    places = jnp.stack([picture_ids[0], patch_rows[0], patch_cols[0], ids]).astype(F32)
    places = jnp.pad(places, ((0, 4), (0, 0)))
    quarter = HD // 4
    inverse = jnp.power(10000.0, -jnp.arange(quarter, dtype=F32) / quarter)
    none = jnp.zeros((quarter,), F32)
    lanes = np.arange(W)
    sign = np.where(lanes < HD // 2, -1.0, 1.0).astype(np.float32)
    wave = jnp.stack(
        [
            jnp.pad(jnp.concatenate([inverse, none, inverse, none]), (0, W - HD)),
            jnp.pad(jnp.concatenate([none, inverse, none, inverse]), (0, W - HD)),
            jnp.asarray(sign),
        ]
    )
    wave = jnp.pad(wave, ((0, 5), (0, 0)))
    dims = (n, T, L, D, F, R, hl, P1, CQ, HP)
    anywhere = pl.BlockSpec(memory_space=pl.ANY)
    local = pl.BlockSpec(memory_space=pltpu.VMEM)

    def vmem(shape, dtype=BF):
        return pltpu.VMEM(shape, dtype)

    scratch = [
        vmem((n, T, D)),
        vmem((L, D)),
        vmem((n, T, D)),
        vmem((n, 8, T), F32),
        vmem((L, 8), F32),
        vmem((F, 16, R), F32),
        vmem((8, D), F32),
        vmem((8, 3 * hl * W), F32),
        vmem((L, W), F32),
        vmem((L, W), F32),
        vmem((D, CQ)),
        vmem((D, 3 * hl * W)),
        vmem((D, D)),
        vmem((D, P1)),
        vmem((P1, D)),
        vmem((L, 3 * hl * W)),
        vmem((L, W), F32),
        vmem((n, n, T, HP)),
        vmem((L, D)),
        vmem((T, D), F32),
        vmem((L, D)),
        vmem((L, P1)),
        vmem((L, P1)),
        vmem((L, D)),
        vmem((n - 1, T, D)),
        vmem((T, D), F32),
        vmem((D, HP)),
        vmem((J, R, CQ)),
        vmem((J, R, HP)),
        vmem((J, R, P1)),
        vmem((J, R, D)),
        vmem((J - 1, R, CQ)),
        vmem((J - 1, R, HP)),
        vmem((J - 1, R, P1)),
        vmem((J - 1, R, D)),
        vmem((L, 2 * W), F32),
        vmem((8, D), F32),
        vmem((F, 8, D), F32),
        pltpu.SemaphoreType.DMA((320,)),
        pltpu.SemaphoreType.DMA((24,)),
    ]
    shapes = (
        jax.ShapeDtypeStruct((T, D), BF),
        jax.ShapeDtypeStruct((T, D), F32),
        jax.ShapeDtypeStruct((n, R, CQ), BF),
        jax.ShapeDtypeStruct((n, R, HP), BF),
        jax.ShapeDtypeStruct((n, R, P1), BF),
        jax.ShapeDtypeStruct((n, R, D), BF),
        jax.ShapeDtypeStruct((n, 8, D), F32),
    )
    block_out, tokens_grad, rq, rp, r1, r2, sums = pl.pallas_call(
        functools.partial(block_kernel, dims),
        out_shape=shapes,
        in_specs=[anywhere] * 4 + [local] + [anywhere] * 4,
        out_specs=[anywhere] * 7,
        scratch_shapes=scratch,
        compiler_params=pltpu.CompilerParams(
            collective_id=0, has_side_effects=True, vmem_limit_bytes=67043328
        ),
    )(tokens[0], cotangent[0], places, small, wave, own_qkv, proj_weight, own_up, own_down)
    full_down = r2.reshape(n * R, D).astype(F32)
    full_up = r1.reshape(n, R, F, part).transpose(1, 2, 0, 3).reshape(R, hidden).astype(F32)
    full_proj = rp[:, :, :hw].transpose(1, 0, 2).reshape(R, D).astype(F32)
    full_qkv = rq[:, :, : 3 * hw].reshape(n, R, 3, hw).transpose(1, 2, 0, 3)
    full_qkv = full_qkv.reshape(R, 3 * D).astype(F32)
    own = lax.dynamic_slice_in_dim(sums, f * R, R, 2)
    whole = jnp.sum(own[:, :6], axis=0)
    up_bias = own[:, 6].reshape(n * R)
    qkv_sums = sums[:, 7, : 3 * hw].reshape(n, 3, hw).transpose(1, 0, 2).reshape(3 * D)
    qkv_sums = lax.dynamic_slice_in_dim(qkv_sums, f * 3 * R, 3 * R, 0)
    return (
        block_out[None],
        tokens_grad[None],
        whole[0],
        whole[1],
        full_qkv,
        qkv_sums,
        full_proj,
        whole[2],
        whole[3],
        whole[4],
        full_up,
        up_bias,
        full_down,
        whole[5],
    )


def fits_kernel(mesh):
    return dict(mesh.shape) == {"seq": 4, "fsdp": 8}


def shards_plain(
    tokens,
    picture_ids,
    patch_rows,
    patch_cols,
    norm1_gain,
    norm1_bias,
    qkv_weight,
    qkv_bias,
    proj_weight,
    proj_bias,
    norm2_gain,
    norm2_bias,
    fc1_weight,
    fc1_bias,
    fc2_weight,
    fc2_bias,
    cotangent,
):
    n = lax.axis_size("seq")
    me = lax.axis_index("seq")
    stores = lax.axis_size("fsdp")
    _, own, width = tokens.shape
    heads = width // HD
    local_heads = heads // n
    hw = local_heads * HD
    rows = qkv_weight.shape[0]
    hidden = fc1_weight.shape[1]
    part = hidden // (stores * n)

    def pick(value, axis):
        return lax.dynamic_index_in_dim(value, me, axis, keepdims=False)

    own_qkv = pick(qkv_weight.reshape(rows, 3, n, hw), 2).reshape(rows, 3 * hw)
    own_up = pick(fc1_weight.reshape(rows, stores, n, part), 2).reshape(rows, stores * part)
    own_down = pick(fc2_weight.reshape(n, part, width), 0)
    small = (norm1_gain, norm1_bias, proj_bias, norm2_gain, norm2_bias, fc2_bias, qkv_bias, fc1_bias)
    sizes = [item.shape[0] for item in small]
    packed = gather(jnp.concatenate(small)[None], "fsdp")
    weight_qkv = gather(own_qkv, "fsdp")
    weight_proj = gather(proj_weight, "fsdp")
    weight_up = gather(own_up, "fsdp")
    weight_down = gather(own_down, "fsdp")
    params = []
    start = 0
    for size in sizes:
        params.append(packed[:, start : start + size].reshape(-1).astype(F32))
        start += size
    gain_one, bias_one, bias_proj, gain_two, bias_two, bias_down, bias_qkv, bias_up = params
    bias_qkv = pick(bias_qkv.reshape(3, n, hw), 1).reshape(3 * hw)
    bias_up = pick(bias_up.reshape(stores, n, part), 1).reshape(stores * part)

    places = jnp.stack([picture_ids[0], patch_rows[0], patch_cols[0]])
    places = gather(places, "seq", 1)
    picture = places[0]
    all_tokens = gather(tokens[0], "seq").astype(F32)
    upstream = gather(cotangent[0], "seq")
    length = all_tokens.shape[0]

    def mine(value):
        return lax.dynamic_slice_in_dim(value, me * own, own, 0)

    normed_one, factor_one = standardize(all_tokens)
    attn_input = (normed_one * gain_one + bias_one).astype(BF)
    projected = (dot(attn_input, weight_qkv) + bias_qkv).reshape(length, 3, local_heads, HD)
    cosine, sine = rotary_tables(places[1], places[2], HD)
    queries = rotate(projected[:, 0], cosine, sine).astype(BF)
    keys = rotate(projected[:, 1], cosine, sine).astype(BF)
    values = projected[:, 2].astype(BF)
    mixed_own, log_total = attend(queries, keys, values, picture)
    mixed = gather(mixed_own.reshape(length, hw), "seq", 1)
    middle = all_tokens + dot(mixed, weight_proj) + bias_proj
    normed_two, factor_two = standardize(middle)
    mlp_input = (normed_two * gain_two + bias_two).astype(BF)
    before = dot(mlp_input, weight_up) + bias_up
    gate = jax.nn.sigmoid(1.702 * before)
    activated = (before * gate).astype(BF)
    out_part = dot(activated, weight_down).astype(BF)
    block_out = (mine(middle) + scatter_sum(out_part, "seq").astype(F32) + bias_down).astype(BF)

    grad_down = scatter_sum(rows_term(activated, upstream).astype(BF), "fsdp")
    grad_activated = contract_back(upstream, weight_down)
    grad_before = (grad_activated * (gate + 1.702 * before * gate * (1.0 - gate))).astype(BF)
    grad_up = scatter_sum(rows_term(mlp_input, grad_before).astype(BF), "fsdp")
    grad_mlp_input = scatter_sum(contract_back(grad_before, weight_up).astype(BF), "seq").astype(F32)
    own_upstream = cotangent[0].astype(F32)
    own_two = mine(normed_two)
    grad_middle = own_upstream + norm_back(grad_mlp_input, own_two, mine(factor_two), gain_two)
    grad_branch = grad_middle.astype(BF)
    grad_mixed = contract_back(grad_branch, weight_proj).astype(BF)
    grad_heads = lax.all_to_all(grad_mixed, "seq", split_axis=1, concat_axis=0, tiled=True)
    branch_part = lax.all_to_all(grad_branch, "seq", split_axis=1, concat_axis=0, tiled=True)
    grad_proj = scatter_sum(rows_term(mixed, branch_part).astype(BF), "fsdp")
    grad_queries, grad_keys, grad_values = attend_back(
        queries, keys, values, picture, grad_heads.reshape(length, local_heads, HD), log_total
    )
    grad_projected = jnp.stack(
        [
            unrotate(grad_queries.astype(F32), cosine, sine).astype(BF),
            unrotate(grad_keys.astype(F32), cosine, sine).astype(BF),
            grad_values,
        ],
        axis=1,
    ).reshape(length, 3 * hw)
    grad_qkv = scatter_sum(rows_term(attn_input, grad_projected).astype(BF), "fsdp")
    grad_attn_input = scatter_sum(contract_back(grad_projected, weight_qkv).astype(BF), "seq").astype(F32)
    own_one = mine(normed_one)
    tokens_grad = grad_middle + norm_back(grad_attn_input, own_one, mine(factor_one), gain_one)

    def spread(value, groups):
        empty = jnp.zeros((groups, n, value.shape[0] // groups), F32)
        return lax.dynamic_update_slice_in_dim(
            empty, value.reshape(groups, 1, -1), me, 1
        ).reshape(stores, -1)

    sums = [
        jnp.sum(grad_attn_input * own_one, axis=0).reshape(stores, -1),
        jnp.sum(grad_attn_input, axis=0).reshape(stores, -1),
        jnp.sum(grad_branch.astype(F32), axis=0).reshape(stores, -1),
        jnp.sum(grad_mlp_input * own_two, axis=0).reshape(stores, -1),
        jnp.sum(grad_mlp_input, axis=0).reshape(stores, -1),
        jnp.sum(own_upstream, axis=0).reshape(stores, -1),
        spread(jnp.sum(grad_projected.astype(F32), axis=0), 3),
        spread(jnp.sum(grad_before.astype(F32), axis=0), stores),
    ]
    summed = lax.psum(scatter_sum(jnp.concatenate(sums, axis=1), "fsdp"), "seq")[0]
    finals = []
    start = 0
    for size in sizes:
        finals.append(summed[start : start + size])
        start += size
    full_down = gather(grad_down, "seq").astype(F32)
    full_up = gather(grad_up[None], "seq").reshape(n, rows, stores, part)
    full_up = full_up.transpose(1, 2, 0, 3).reshape(rows, hidden).astype(F32)
    full_proj = gather(grad_proj, "seq", 1).astype(F32)
    full_qkv = gather(grad_qkv[None], "seq").reshape(n, rows, 3, hw)
    full_qkv = full_qkv.transpose(1, 2, 0, 3).reshape(rows, 3 * width).astype(F32)
    return (
        block_out[None],
        tokens_grad[None],
        finals[0],
        finals[1],
        full_qkv,
        finals[6],
        full_proj,
        finals[2],
        finals[3],
        finals[4],
        full_up,
        finals[7],
        full_down,
        finals[5],
    )


def solution(mesh):
    token = P("fsdp", "seq", None)
    place = P("fsdp", "seq")
    vector = P("fsdp")
    matrix = P("fsdp", None)
    in_specs = (
        token,
        place,
        place,
        place,
        vector,
        vector,
        matrix,
        vector,
        matrix,
        vector,
        vector,
        vector,
        matrix,
        vector,
        matrix,
        vector,
        token,
    )
    out_specs = (
        token,
        token,
        vector,
        vector,
        matrix,
        vector,
        matrix,
        vector,
        vector,
        vector,
        matrix,
        vector,
        matrix,
        vector,
    )
    shards = shards_kernel if fits_kernel(mesh) else shards_plain
    return jax.shard_map(shards, mesh=mesh, in_specs=in_specs, out_specs=out_specs, check_vma=False)
```

```python
import functools

import jax
import jax.numpy as jnp
import numpy as np
from jax import lax
from jax.experimental import pallas as pl
from jax.experimental.pallas import tpu as pltpu
from jax.sharding import PartitionSpec as P

HD = 80
NORM_EPSILON = 1e-06
MASKED = -1e30
BF = jnp.bfloat16
F32 = jnp.float32


def standardize(values_in):
    centre = jnp.mean(values_in, axis=-1, keepdims=True)
    shifted = values_in - centre
    factor = lax.rsqrt(jnp.mean(shifted * shifted, axis=-1, keepdims=True) + NORM_EPSILON)
    return (shifted * factor, factor)


def norm_back(grad_out, normed, factor, gain):
    scaled = grad_out * gain
    return factor * (
        scaled
        - jnp.mean(scaled, axis=-1, keepdims=True)
        - normed * jnp.mean(scaled * normed, axis=-1, keepdims=True)
    )


def rotary_tables(patch_row, patch_col, head_size):
    quarter = head_size // 4
    inverse = jnp.power(10000.0, -jnp.arange(quarter, dtype=F32) / quarter)
    half_angles = jnp.concatenate(
        [
            patch_row.astype(F32)[..., None] * inverse,
            patch_col.astype(F32)[..., None] * inverse,
        ],
        axis=-1,
    )
    angles = jnp.concatenate([half_angles, half_angles], axis=-1)
    return (jnp.cos(angles)[..., None, :], jnp.sin(angles)[..., None, :])


def rotate(values_in, cosine, sine):
    half_size = values_in.shape[-1] // 2
    turned = jnp.concatenate([-values_in[..., half_size:], values_in[..., :half_size]], axis=-1)
    return values_in * cosine + turned * sine


def unrotate(grad_in, cosine, sine):
    half_size = grad_in.shape[-1] // 2
    moved = grad_in * sine
    return grad_in * cosine + jnp.concatenate(
        [moved[..., half_size:], -moved[..., :half_size]], axis=-1
    )


def masked_scores(queries, keys, picture, factor):
    places = jnp.arange(picture.shape[0], dtype=jnp.int32)
    scores = jnp.einsum("qhd,khd->hqk", queries, keys, preferred_element_type=F32) * factor
    allowed = (picture[:, None] == picture[None, :]) & (
        (picture[None, :] >= 0) | (places[:, None] == places[None, :])
    )
    return jnp.where(allowed[None, :, :], scores, MASKED)


def attend(queries, keys, values, picture):
    scores = masked_scores(queries, keys, picture, HD**-0.5)
    row_max = jnp.max(scores, axis=-1, keepdims=True)
    powers = jnp.exp(scores - row_max)
    totals = jnp.sum(powers, axis=-1, keepdims=True)
    weights = (powers / totals).astype(BF)
    mixed = jnp.einsum("hqk,khd->qhd", weights, values, preferred_element_type=F32)
    return mixed.astype(BF), row_max + jnp.log(totals)


def attend_back(queries, keys, values, picture, grad_mixed, log_total):
    factor = HD**-0.5
    scores = masked_scores(queries, keys, picture, factor)
    probs = jnp.exp(scores - log_total)
    weights = probs.astype(BF)
    grad_values = jnp.einsum("hqk,qhd->khd", weights, grad_mixed, preferred_element_type=F32)
    grad_weights = jnp.einsum("qhd,khd->hqk", grad_mixed, values, preferred_element_type=F32)
    centre = jnp.sum(probs * grad_weights, axis=-1, keepdims=True)
    grad_scores = (probs * (grad_weights - centre)).astype(BF)
    grad_queries = jnp.einsum("hqk,khd->qhd", grad_scores, keys, preferred_element_type=F32) * factor
    grad_keys = jnp.einsum("hqk,qhd->khd", grad_scores, queries, preferred_element_type=F32) * factor
    return grad_queries.astype(BF), grad_keys.astype(BF), grad_values.astype(BF)


def dot(left, right):
    return jnp.dot(left, right, preferred_element_type=F32)


def rows_term(left, right):
    return lax.dot_general(left, right, (((0,), (0,)), ((), ())), preferred_element_type=F32)


def contract_back(grad_out, weight):
    return lax.dot_general(grad_out, weight, (((1,), (1,)), ((), ())), preferred_element_type=F32)


def gather(value, axis_name, axis=0):
    return lax.all_gather(value, axis_name, axis=axis, tiled=True)


def scatter_sum(value, axis_name, axis=0):
    return lax.psum_scatter(value, axis_name, scatter_dimension=axis, tiled=True)

MESH = pl.DeviceIdType.MESH


def mm(left, right):
    return jnp.dot(left, right, preferred_element_type=F32)


def mm_nt(left, right):
    return lax.dot_general(left, right, (((1,), (1,)), ((), ())), preferred_element_type=F32)


def mm_tn(left, right):
    return lax.dot_general(left, right, (((0,), (0,)), ((), ())), preferred_element_type=F32)


def lane_pad(value, lanes):
    gap = lanes - value.shape[1]
    if gap == 0:
        return value
    return jnp.concatenate([value, jnp.zeros((value.shape[0], gap), value.dtype)], axis=1)


def moments(value):
    centre = jnp.mean(value, axis=-1, keepdims=True)
    shifted = value - centre
    factor = lax.rsqrt(jnp.mean(shifted * shifted, axis=-1, keepdims=True) + NORM_EPSILON)
    return shifted * factor, factor


def block_kernel(
    dims,
    tok_in,
    cot_in,
    plc_in,
    small_in,
    wave_in,
    wq_in,
    wp_in,
    w1_in,
    w2_in,
    out_ref,
    tgrad_ref,
    rq_ref,
    rp_ref,
    r1_ref,
    r2_ref,
    sums_ref,
    tokb,
    ain,
    cotb,
    plb,
    plt,
    smb,
    vec,
    bqkv,
    cosb,
    sinb,
    wqc,
    wq,
    wp,
    w1,
    w2,
    qkv,
    lse,
    mixc,
    mix,
    mid,
    mlp,
    act,
    dge,
    snd,
    rsr,
    gmd,
    gp,
    dq4,
    dp4,
    d14,
    d24,
    zq3,
    zp3,
    z13,
    z23,
    dkv,
    smg,
    sg8,
    sems,
    local_sems,
):
    n, T, L, D, F, R, hl, P1, CQ, HP = dims
    J = F // 2
    hw = hl * HD
    W = 128
    QW = hl * W
    scale = HD**-0.5
    tile = 256 if D % 256 == 0 else 128
    me = lax.axis_index("seq")
    f = lax.axis_index("fsdp")
    k = f % 2
    j = f // 2
    partner = f + 1 - 2 * k
    seq_to = [(me + o) % n for o in range(n)]
    seq_from = [(me + n - o) % n for o in range(n)]
    z_to = [2 * ((j + d) % J) + k for d in range(J)]
    z_from = [2 * ((j + J - d) % J) + k for d in range(J)]
    used = {"remote": 0, "local": 0}
    leftover = []

    def take(count=1):
        used["remote"] += count
        return used["remote"] - count

    def send(src, dst, where, recv, late=True):
        copy = pltpu.make_async_remote_copy(
            src_ref=src,
            dst_ref=dst,
            send_sem=sems.at[take()],
            recv_sem=sems.at[recv],
            device_id=where,
            device_id_type=MESH,
        )
        copy.start()
        if late:
            leftover.append(copy)
        return copy

    def load(src, dst):
        used["local"] += 1
        copy = pltpu.make_async_copy(src, dst, local_sems.at[used["local"] - 1])
        copy.start()
        return copy

    def band(ref, index, size):
        return ref.at[pl.ds(pl.multiple_of(index * size, size), size)]

    def rows_of(index, size):
        return pl.ds(pl.multiple_of(index * size, size), size)

    def strips(total, step, body):
        def run(s, carry):
            body(rows_of(s, step))
            return carry

        lax.fori_loop(0, total // step, run, 0)

    strip = 32

    raw_q = [load(wq_in.at[:, t * D : (t + 1) * D], d24.at[t]) for t in range(3)]
    raw_1 = [load(w1_in.at[:, c * P1 : (c + 1) * P1], d14.at[c]) for c in range(n)]

    barrier = pltpu.get_barrier_semaphore()
    for o in range(1, n):
        pl.semaphore_signal(barrier, inc=1, device_id={"seq": seq_to[o]}, device_id_type=MESH)
    for o in range(1, F):
        pl.semaphore_signal(barrier, inc=1, device_id={"fsdp": (f + o) % F}, device_id_type=MESH)
    pl.semaphore_wait(barrier, n - 1 + F - 1)

    tok_copies = []
    for o in range(1, n):
        where = {"seq": seq_to[o]}
        c1 = send(plc_in, plb.at[me], where, take())
        c2 = send(tok_in, tokb.at[me], where, take())
        tok_copies.append((c1, c2))
    own_tok = load(tok_in, tokb.at[me])
    own_plc = load(plc_in, plb.at[me])
    own_small = load(small_in, smb.at[f])

    class Weight:
        def __init__(self, src, buf, rows):
            self.buf, self.rows = buf, rows
            self.own = None
            if src is None:
                src = band(buf, f, rows)
            else:
                self.own = load(src, band(buf, f, rows))
            self.near = send(src, band(buf, f, rows), {"fsdp": partner}, take(), late=False)
            self.far = [
                send(src, band(buf, f, rows), {"fsdp": z_to[d]}, take(), late=False)
                for d in range(1, J)
            ]
            self.relayed = []

        def relay(self):
            for d in range(1, J):
                self.far[d - 1].wait_recv()
                part = band(self.buf, z_from[d], self.rows)
                self.relayed.append(send(part, part, {"fsdp": partner}, take(), late=False))

        def finish(self):
            if self.own is not None:
                self.own.wait()
            self.near.wait_recv()
            for copy in self.relayed:
                copy.wait_recv()

        def drain(self):
            for copy in [self.near] + self.far + self.relayed:
                copy.wait_send()

    def cut_columns(target, lines):
        for m in range(n):

            @pl.when(me == m)
            def _():
                target[rows_of(f, R), :] = lane_pad(
                    jnp.concatenate(lines(m), axis=1), target.shape[1]
                )

    small_copies = [
        send(small_in, smb.at[f], {"fsdp": (f + o) % F}, take()) for o in range(1, F)
    ]
    for copy in raw_q:
        copy.wait()
    cut_columns(wqc, lambda m: [d24[t, :, m * hw : (m + 1) * hw] for t in range(3)])
    weight_q = Weight(None, wqc, R)
    weight_p = Weight(wp_in, wp, R)
    for copy in raw_1:
        copy.wait()
    cut_columns(
        w1,
        lambda m: [
            d14[b * n * R // P1, :, b * n * R % P1 + m * R : b * n * R % P1 + (m + 1) * R]
            for b in range(F)
        ],
    )
    weight_1 = Weight(None, w1, R)
    weight_2 = Weight(w2_in.at[rows_of(me, R)], w2, R)
    own_cot = load(cot_in, cotb.at[me])

    own_small.wait()
    for copy in small_copies:
        copy.wait_recv()
    for row in range(7):
        vec[row : row + 1, :] = jnp.concatenate(
            [smb[s, row : row + 1, :R] for s in range(F)], axis=1
        )
    groups = 3 * D // R // 3
    heads = []
    for t in range(3):
        start = t * groups + me * (hw // R)
        line = jnp.concatenate(
            [
                smb[(start + b) // 3, pl.ds(7 + (start + b) % 3, 1), :][:, :R]
                for b in range(hw // R)
            ],
            axis=1,
        )
        for h in range(hl):
            heads.append(lane_pad(line[:, h * HD : (h + 1) * HD], W))
    bqkv[...] = jnp.broadcast_to(jnp.concatenate(heads, axis=1), bqkv.shape)

    def vector(row):
        return vec[row : row + 1, :]

    own_plc.wait()
    for c1, _ in tok_copies:
        c1.wait_recv()

    def table(i, carry):
        rows = rows_of(i, T)
        turned = jnp.transpose(plb[i], (1, 0))
        plt[rows, :] = turned
        angle = turned[:, 1:2] * wave_in[0:1, :] + turned[:, 2:3] * wave_in[1:2, :]
        cosb[rows, :] = jnp.cos(angle)
        sinb[rows, :] = jnp.sin(angle) * wave_in[2:3, :]
        return carry

    lax.fori_loop(0, n, table, 0)
    lane = lax.broadcasted_iota(jnp.int32, (1, W), 1)
    low_half = lane < HD // 2

    def swap(value):
        return jnp.where(
            low_half, pltpu.roll(value, W - HD // 2, 1), pltpu.roll(value, HD // 2, 1)
        )

    def norm_one(i):
        def body(rows):
            normed, _ = moments(tokb[i, rows, :].astype(F32))
            ain[rows_of_block(i, rows), :] = (normed * vector(0) + vector(1)).astype(BF)

        strips(T, strip, body)

    def rows_of_block(i, rows):
        return pl.ds(pl.multiple_of(i * T + rows.start, strip), strip)

    own_tok.wait()
    norm_one(me)
    for o in range(1, n):
        tok_copies[o - 1][1].wait_recv()
        norm_one(seq_from[o])

    weight_q.relay()
    weight_q.finish()

    def spread_heads(rows):
        line = wqc[rows, :]
        for h in range(3 * hl):
            wq[rows, h * W : (h + 1) * W] = lane_pad(line[:, h * HD : (h + 1) * HD], W)

    strips(D, R, spread_heads)

    def project(i, carry):
        rows = rows_of(i, T)
        line = ain[rows, :]
        cosine = cosb[rows, :]
        sine = sinb[rows, :]
        for t in range(3):
            part = mm(line, wq[:, t * QW : (t + 1) * QW]) + bqkv[0:1, t * QW : (t + 1) * QW]
            for h in range(hl):
                u = part[:, h * W : (h + 1) * W]
                if t < 2:
                    u = u * cosine + swap(u) * sine
                qkv[rows, t * QW + h * W : t * QW + (h + 1) * W] = u.astype(BF)
        return carry

    lax.fori_loop(0, n, project, 0)

    def masked(scores, i):
        ids = jnp.concatenate([plb[b, 3:4, :] for b in range(n)], axis=1)
        own_ids = plt[rows_of(i, T), 3:4]
        return jnp.where(own_ids == ids, scores * scale, MASKED)

    mix_send, mix_recv = take(n * (n - 1)), take(n * (n - 1))

    def mix_copy(i, o, peer, source):
        return pltpu.make_async_remote_copy(
            src_ref=mixc.at[source, i],
            dst_ref=mixc.at[source, i],
            send_sem=sems.at[mix_send + i * (n - 1) + o - 1],
            recv_sem=sems.at[mix_recv + i * (n - 1) + o - 1],
            device_id={"seq": peer},
            device_id_type=MESH,
        )

    def attend_block(i, carry):
        rows = rows_of(i, T)
        outs = []
        logs = jnp.zeros((T, W), F32)
        for h in range(hl):
            q = qkv[rows, h * W : (h + 1) * W]
            kk = qkv[:, QW + h * W : QW + (h + 1) * W]
            v = qkv[:, 2 * QW + h * W : 2 * QW + (h + 1) * W]
            s = masked(mm_nt(q, kk), i)
            top = jnp.max(s, axis=-1, keepdims=True)
            p = jnp.exp(s - top)
            total = jnp.sum(p, axis=-1, keepdims=True)
            outs.append((mm(p.astype(BF), v) / total)[:, :HD].astype(BF))
            logs = jnp.where(lane == h, top + jnp.log(total), logs)
        lse[rows, :] = logs
        mixc[me, i] = lane_pad(jnp.concatenate(outs, axis=1), HP)
        for o in range(1, n):
            mix_copy(i, o, seq_to[o], me).start()
        return carry

    lax.fori_loop(0, n, attend_block, 0)
    cot_copies = [
        send(cot_in, cotb.at[me], {"seq": seq_to[o]}, take()) for o in range(1, n)
    ]

    weight_p.relay()
    weight_p.finish()

    def branch(t, carry):
        i = (me + 1 + t) % n
        rows = rows_of(i, T)
        for o in range(1, n):
            mix_copy(i, o, seq_to[o], seq_from[o]).wait_recv()
        mix[rows, :] = jnp.concatenate([mixc[c, i][:, :hw] for c in range(n)], axis=1)
        mid[...] = mm(mix[rows, :], wp[...])

        def body(part):
            whole = rows_of_block(i, part)
            value = mid[part, :] + tokb[i, part, :].astype(F32) + vector(2)
            mid[part, :] = value
            normed, _ = moments(value)
            mlp[whole, :] = (normed * vector(3) + vector(4)).astype(BF)

        strips(T, strip, body)
        return carry

    lax.fori_loop(0, n, branch, 0)

    weight_1.relay()
    weight_1.finish()

    def up(i, carry):
        rows = rows_of(i, T)
        before = mm(mlp[rows, :], w1[...]) + vector(6)
        gate = jax.nn.sigmoid(1.702 * before)
        act[rows, :] = (before * gate).astype(BF)
        dge[rows, :] = (gate + 1.702 * before * gate * (1.0 - gate)).astype(BF)
        return carry

    lax.fori_loop(0, n, up, 0)

    own_cot.wait()
    for copy in cot_copies:
        copy.wait_recv()
    weight_2.relay()
    weight_2.finish()

    class Scatter:
        def __init__(self, stage):
            self.stage = stage
            self.out, self.into = take(n - 1), take(n - 1)

        def copy(self, t, to):
            return pltpu.make_async_remote_copy(
                src_ref=band(self.stage, to, T),
                dst_ref=rsr.at[t],
                send_sem=sems.at[self.out + t],
                recv_sem=sems.at[self.into + t],
                device_id={"seq": to},
                device_id_type=MESH,
            )

        def start(self, t, i):
            @pl.when(t < n - 1)
            def _():
                self.copy(t, i).start()

        def wait_recv(self):
            for t in range(n - 1):
                self.copy(t, seq_to[t + 1]).wait_recv()

        def wait_send(self):
            for t in range(n - 1):
                self.copy(t, seq_to[t + 1]).wait_send()

    for i in range(n):
        for o in range(1, n):
            mix_copy(i, o, seq_to[o], me).wait_send()
    scatter_mlp = Scatter(snd)

    def back(t, carry):
        i = (me + 1 + t) % n
        rows = rows_of(i, T)
        grad = (mm_nt(cotb[i], w2[...]) * dge[rows, :].astype(F32)).astype(BF)
        dge[rows, :] = grad
        snd[rows, :] = mm_nt(grad, w1[...]).astype(BF)
        scatter_mlp.start(t, i)
        return carry

    lax.fori_loop(0, n, back, 0)

    class Gradient:
        def __init__(self, grad, other, far, result, lanes):
            self.grad, self.other, self.far, self.result = grad, other, far, result
            self.lanes = lanes

        def exchange(self):
            self.near = []
            for c in range(J):
                self.near.append(
                    send(
                        band(self.grad, 2 * c + 1 - k, R),
                        self.other.at[c],
                        {"fsdp": partner},
                        take(),
                    )
                )

        def add_near(self):
            for copy in self.near:
                copy.wait_recv()

            def chip(c, carry):
                rows = rows_of(2 * c + k, R)
                self.grad[rows, :] = (
                    self.grad[rows, :].astype(F32) + self.other[c].astype(F32)
                ).astype(BF)
                return carry

            lax.fori_loop(0, J, chip, 0)
            self.across = [
                send(
                    band(self.grad, z_to[d], R),
                    self.far.at[d - 1],
                    {"fsdp": z_to[d]},
                    take(),
                )
                for d in range(1, J)
            ]

        def add_far(self):
            for copy in self.across:
                copy.wait_recv()
            rows = rows_of(f, R)
            total = self.grad[rows, :].astype(F32)
            for d in range(J - 1):
                total = total + self.far[d].astype(F32)
            self.other[0] = total.astype(BF)
            mine = self.other.at[0]
            self.keep = load(mine, self.result.at[me])
            self.share = [
                send(mine, self.result.at[me], {"seq": seq_to[o]}, take()) for o in range(1, n)
            ]

        def finish(self):
            self.keep.wait()
            for copy in self.share:
                copy.wait_recv()

    grad_up = Gradient(w1, d14, z13, r1_ref, P1)
    grad_down = Gradient(w2, d24, z23, r2_ref, D)
    grad_proj = Gradient(gp, dp4, zp3, rp_ref, HP)
    grad_qkv = Gradient(wqc, dq4, zq3, rq_ref, CQ)

    weight_1.drain()
    weight_2.drain()
    weight_q.drain()

    def up_grad(t, carry):
        w1[rows_of(t, tile), :] = mm_tn(mlp[:, rows_of(t, tile)], dge[...]).astype(BF)
        return carry

    lax.fori_loop(0, D // tile, up_grad, 0)
    grad_up.exchange()

    def down(i, carry):
        rows = rows_of(i, T)
        mlp[rows, :] = mm(act[rows, :], w2[...]).astype(BF)
        return carry

    lax.fori_loop(0, n, down, 0)

    def down_grad(t, carry):
        lanes = rows_of(t, tile)
        total = mm_tn(act[0:T, lanes], cotb[0])
        for b in range(1, n):
            total = total + mm_tn(act[b * T : (b + 1) * T, lanes], cotb[b])
        w2[lanes, :] = total.astype(BF)
        return carry

    lax.fori_loop(0, P1 // tile, down_grad, 0)
    grad_down.exchange()

    smg[...] = jnp.zeros(smg.shape, F32)
    scatter_mlp.wait_recv()

    def gather_parts(part):
        whole = rows_of_block(me, part)
        total = snd[whole, :].astype(F32)
        for t in range(n - 1):
            total = total + rsr[t, part, :].astype(F32)
        return total

    def add_sum(row, value):
        smg[row : row + 1, :] = smg[row : row + 1, :] + jnp.sum(value, axis=0, keepdims=True)

    def norm_two_back(part):
        upstream = cotb[me, part, :].astype(F32)
        grad = gather_parts(part)
        normed, factor = moments(mid[part, :])
        scaled = grad * vector(3)
        value = upstream + factor * (
            scaled
            - jnp.mean(scaled, axis=-1, keepdims=True)
            - normed * jnp.mean(scaled * normed, axis=-1, keepdims=True)
        )
        gmd[part, :] = value
        low = value.astype(BF)
        snd[rows_of_block(me, part), :] = low
        add_sum(2, low.astype(F32))
        add_sum(3, grad * normed)
        add_sum(4, grad)
        add_sum(5, upstream)

    strips(T, strip, norm_two_back)
    own_rows = rows_of(me, T)
    low_branch = snd[own_rows, :]
    grad_mixed = mm_nt(low_branch, wp[...]).astype(BF)
    for c in range(n):
        mixc[0, c] = lane_pad(grad_mixed[:, c * hw : (c + 1) * hw], HP)
        mixc[2, c] = lane_pad(low_branch[:, c * hw : (c + 1) * hw], HP)
    head_copies = [
        send(mixc.at[0, seq_to[o]], mixc.at[1, me], {"seq": seq_to[o]}, take()) for o in range(1, n)
    ]
    branch_copies = [
        send(mixc.at[2, seq_to[o]], mixc.at[3, me], {"seq": seq_to[o]}, take()) for o in range(1, n)
    ]
    mixc[1, me] = mixc[0, me]
    mixc[3, me] = mixc[2, me]

    grad_up.add_near()
    grad_down.add_near()

    for copy in head_copies:
        copy.wait_recv()
    out_copies = [
        send(band(mlp, seq_to[o], T), tokb.at[me], {"seq": seq_to[o]}, take()) for o in range(1, n)
    ]

    for h in range(hl):
        q_at = slice(h * W, (h + 1) * W)
        k_at = slice(QW + h * W, QW + (h + 1) * W)
        v_at = slice(2 * QW + h * W, 2 * QW + (h + 1) * W)
        dkv[...] = jnp.zeros(dkv.shape, F32)

        def attend_back_block(i, carry):
            rows = rows_of(i, T)
            q = qkv[rows, q_at]
            kk = qkv[:, k_at]
            g = lane_pad(mixc[1, i][:, h * HD : (h + 1) * HD], W)
            p = jnp.exp(masked(mm_nt(q, kk), i) - lse[rows, h : h + 1])
            dp = mm_nt(g, qkv[:, v_at])
            dkv[:, W:] = dkv[:, W:] + mm_tn(p.astype(BF), g)
            centre = jnp.sum(p * dp, axis=-1, keepdims=True)
            ds = (p * (dp - centre)).astype(BF)
            dq = (mm(ds, kk) * scale).astype(BF).astype(F32)
            dkv[:, :W] = dkv[:, :W] + mm_tn(ds, q)
            qkv[rows, q_at] = (dq * cosb[rows, :] - swap(dq) * sinb[rows, :]).astype(BF)
            return carry

        lax.fori_loop(0, n, attend_back_block, 0)

        def turn_back(i, carry):
            rows = rows_of(i, T)
            dk = (dkv[rows, :W] * scale).astype(BF).astype(F32)
            qkv[rows, k_at] = (dk * cosb[rows, :] - swap(dk) * sinb[rows, :]).astype(BF)
            qkv[rows, v_at] = dkv[rows, W:].astype(BF)
            return carry

        lax.fori_loop(0, n, turn_back, 0)

    scatter_mlp.wait_send()
    scatter_attn = Scatter(snd)

    def attn_back(t, carry):
        i = (me + 1 + t) % n
        rows = rows_of(i, T)
        snd[rows, :] = mm_nt(qkv[rows, :], wq[...]).astype(BF)
        scatter_attn.start(t, i)
        return carry

    lax.fori_loop(0, n, attn_back, 0)

    def qkv_grad(t, carry):
        rows = rows_of(t, tile)
        total = mm_tn(ain[:, rows], qkv[...])
        wqc[rows, :] = lane_pad(
            jnp.concatenate([total[:, h * W : h * W + HD].astype(BF) for h in range(3 * hl)], axis=1),
            CQ,
        )
        return carry

    lax.fori_loop(0, D // tile, qkv_grad, 0)
    grad_qkv.exchange()

    for copy in branch_copies:
        copy.wait_recv()

    def proj_grad(t, carry):
        lanes = rows_of(t, tile)
        total = mm_tn(mix[0:T, lanes], mixc[3, 0])
        for b in range(1, n):
            total = total + mm_tn(mix[b * T : (b + 1) * T, lanes], mixc[3, b])
        gp[lanes, :] = total.astype(BF)
        return carry

    lax.fori_loop(0, D // tile, proj_grad, 0)
    grad_proj.exchange()
    grad_qkv.add_near()
    grad_proj.add_near()
    grad_up.add_far()
    grad_down.add_far()

    def bias_sums(part):
        smg[6:7, :] = smg[6:7, :] + jnp.sum(dge[part, :].astype(F32), axis=0, keepdims=True)
        line = jnp.sum(qkv[part, :].astype(F32), axis=0, keepdims=True)
        line = lane_pad(
            jnp.concatenate([line[:, h * W : h * W + HD] for h in range(3 * hl)], axis=1), D
        )
        smg[7:8, :] = smg[7:8, :] + line

    strips(L, 64, bias_sums)

    scatter_attn.wait_recv()

    def norm_one_back(part):
        grad = gather_parts(part)
        normed, factor = moments(tokb[me, part, :].astype(F32))
        scaled = grad * vector(0)
        gmd[part, :] = gmd[part, :] + factor * (
            scaled
            - jnp.mean(scaled, axis=-1, keepdims=True)
            - normed * jnp.mean(scaled * normed, axis=-1, keepdims=True)
        )
        add_sum(0, grad * normed)
        add_sum(1, grad)

    strips(T, strip, norm_one_back)
    tokens_out = load(gmd, tgrad_ref)
    sum_copies = [
        send(smg, sg8.at[f], {"fsdp": (f + o) % F}, take()) for o in range(1, F)
    ]
    sg8[f] = smg[...]

    for copy in out_copies:
        copy.wait_recv()

    def write_out(part):
        whole = rows_of_block(me, part)
        total = mid[part, :] + mlp[whole, :].astype(F32) + vector(5)
        for o in range(1, n):
            total = total + tokb[seq_from[o], part, :].astype(F32)
        bias_rows = rows_of_block(me, part)
        ain[bias_rows, :] = total.astype(BF)

    strips(T, strip, write_out)
    block_out = load(band(ain, me, T), out_ref)

    for copy in sum_copies:
        copy.wait_recv()
    total = sg8[0]
    for s in range(1, F):
        total = total + sg8[s]
    plain = lax.broadcasted_iota(jnp.int32, total.shape, 0)
    vec[...] = jnp.where(plain < 8, total, 0.0)
    sums_keep = load(vec, sums_ref.at[me])
    sums_share = [
        send(vec, sums_ref.at[me], {"seq": seq_to[o]}, take()) for o in range(1, n)
    ]

    grad_qkv.add_far()
    grad_proj.add_far()
    for item in (grad_up, grad_down, grad_proj, grad_qkv):
        item.finish()
    for copy in sums_share:
        copy.wait_recv()
    sums_keep.wait()
    tokens_out.wait()
    block_out.wait()
    weight_p.drain()
    scatter_attn.wait_send()
    for copy in leftover:
        copy.wait_send()


def unpack_kernel(
    dims,
    block_in,
    tokens_in,
    rq_in,
    rp_in,
    r1_in,
    r2_in,
    sums_in,
    block_ref,
    tokens_ref,
    qkv_ref,
    proj_ref,
    up_ref,
    down_ref,
    vec_ref,
    block,
    tokens,
    rq,
    rp,
    r1,
    r2,
    sums,
    stage,
    vec,
    in_sems,
    out_sems,
):
    n, T, L, D, F, R, hl, P1, CQ, HP = dims
    hw = hl * HD
    f = lax.axis_index("fsdp")
    loads = []
    for src, dst in (
        (r2_in, r2),
        (r1_in, r1),
        (rq_in, rq),
        (rp_in, rp),
        (tokens_in, tokens),
        (block_in, block),
        (sums_in, sums),
    ):
        copy = pltpu.make_async_copy(src, dst, in_sems.at[len(loads)])
        copy.start()
        loads.append(copy)
    stores = []

    def store(src, dst):
        copy = pltpu.make_async_copy(src, dst, out_sems.at[len(stores)])
        copy.start()
        stores.append(copy)

    loads[0].wait()
    for c in range(n):
        stage[c] = r2[c].astype(F32)
        store(stage.at[c], down_ref.at[c * R : (c + 1) * R])
    loads[1].wait()
    width = n * R
    for c in range(n):
        blocks = range(c * P1 // width, (c + 1) * P1 // width)
        stage[n + c] = jnp.concatenate(
            [r1[m, :, b * R : (b + 1) * R] for b in blocks for m in range(n)], axis=1
        ).astype(F32)
        store(stage.at[n + c], up_ref.at[:, c * P1 : (c + 1) * P1])
    loads[2].wait()
    for t in range(3):
        stage[2 * n + t] = jnp.concatenate(
            [rq[m, :, t * hw : (t + 1) * hw] for m in range(n)], axis=1
        ).astype(F32)
        store(stage.at[2 * n + t], qkv_ref.at[:, t * D : (t + 1) * D])
    loads[3].wait()
    stage[2 * n + 3] = jnp.concatenate([rp[m, :, :hw] for m in range(n)], axis=1).astype(F32)
    store(stage.at[2 * n + 3], proj_ref)
    loads[4].wait()
    store(tokens, tokens_ref)
    loads[5].wait()
    store(block, block_ref)
    loads[6].wait()
    per_part = hw // R
    for s in range(F):

        @pl.when(f == s)
        def _():
            own = slice(s * R, (s + 1) * R)
            total = sums[0, 0:6, own]
            for m in range(1, n):
                total = total + sums[m, 0:6, own]
            lines = [total] + [sums[m, 6:7, own] for m in range(n)]
            for b in range(3):
                spot = 3 * s + b
                third, rest = spot // (n * per_part), spot % (n * per_part)
                at = third * hw + rest % per_part * R
                lines.append(sums[rest // per_part, 7:8, at : at + R])
            lines.append(jnp.zeros((16 - 9 - n, R), F32))
            vec[...] = jnp.concatenate(lines, axis=0)

    store(vec, vec_ref)
    for copy in stores:
        copy.wait()


def round_up(value, step):
    return -(-value // step) * step


def shards_kernel(
    tokens,
    picture_ids,
    patch_rows,
    patch_cols,
    norm1_gain,
    norm1_bias,
    qkv_weight,
    qkv_bias,
    proj_weight,
    proj_bias,
    norm2_gain,
    norm2_bias,
    fc1_weight,
    fc1_bias,
    fc2_weight,
    fc2_bias,
    cotangent,
):
    n = lax.axis_size("seq")
    me = lax.axis_index("seq")
    F = lax.axis_size("fsdp")
    f = lax.axis_index("fsdp")
    _, T, D = tokens.shape
    L = n * T
    hl = D // HD // n
    hw = hl * HD
    R = D // F
    hidden = fc1_weight.shape[1]
    P1 = hidden // n
    part = hidden // (F * n)
    CQ = round_up(3 * hw, 128)
    HP = round_up(hw, 128)
    J = F // 2
    W = 128

    def pick(value, axis):
        return lax.dynamic_index_in_dim(value, me, axis, keepdims=False)

    small = jnp.concatenate(
        [
            norm1_gain,
            norm1_bias,
            proj_bias,
            norm2_gain,
            norm2_bias,
            fc2_bias,
            pick(fc1_bias.reshape(n, part), 0),
            qkv_bias,
        ]
    )
    small = jnp.pad(small.astype(F32).reshape(10, R), ((0, 6), (0, 0)))
    spot = jnp.arange(T, dtype=jnp.int32) + me * T
    ids = jnp.where(picture_ids[0] >= 0, picture_ids[0], -1 - spot)
    places = jnp.stack([picture_ids[0], patch_rows[0], patch_cols[0], ids]).astype(F32)
    places = jnp.pad(places, ((0, 4), (0, 0)))
    quarter = HD // 4
    inverse = 10000.0 ** (-np.arange(quarter) / quarter)
    wave = np.zeros((8, W), np.float32)
    for c in range(2):
        wave[0, 2 * c * quarter : (2 * c + 1) * quarter] = inverse
        wave[1, (2 * c + 1) * quarter : (2 * c + 2) * quarter] = inverse
    wave[2] = np.where(np.arange(W) < HD // 2, -1.0, 1.0)
    dims = (n, T, L, D, F, R, hl, P1, CQ, HP)
    anywhere = pl.BlockSpec(memory_space=pl.ANY)
    local = pl.BlockSpec(memory_space=pltpu.VMEM)

    def vmem(shape, dtype=BF):
        return pltpu.VMEM(shape, dtype)

    scratch = [
        vmem((n, T, D)),
        vmem((L, D)),
        vmem((n, T, D)),
        vmem((n, 8, T), F32),
        vmem((L, 8), F32),
        vmem((F, 16, R), F32),
        vmem((8, D), F32),
        vmem((8, 3 * hl * W), F32),
        vmem((L, W), F32),
        vmem((L, W), F32),
        vmem((D, CQ)),
        vmem((D, 3 * hl * W)),
        vmem((D, D)),
        vmem((D, P1)),
        vmem((P1, D)),
        vmem((L, 3 * hl * W)),
        vmem((L, W), F32),
        vmem((n, n, T, HP)),
        vmem((L, D)),
        vmem((T, D), F32),
        vmem((L, D)),
        vmem((L, P1)),
        vmem((L, P1)),
        vmem((L, D)),
        vmem((n - 1, T, D)),
        vmem((T, D), F32),
        vmem((D, HP)),
        vmem((J, R, CQ)),
        vmem((J, R, HP)),
        vmem((J, R, P1)),
        vmem((J, R, D)),
        vmem((J - 1, R, CQ)),
        vmem((J - 1, R, HP)),
        vmem((J - 1, R, P1)),
        vmem((J - 1, R, D)),
        vmem((L, 2 * W), F32),
        vmem((8, D), F32),
        vmem((F, 8, D), F32),
        pltpu.SemaphoreType.DMA((320,)),
        pltpu.SemaphoreType.DMA((24,)),
    ]
    shapes = (
        jax.ShapeDtypeStruct((T, D), BF),
        jax.ShapeDtypeStruct((T, D), F32),
        jax.ShapeDtypeStruct((n, R, CQ), BF),
        jax.ShapeDtypeStruct((n, R, HP), BF),
        jax.ShapeDtypeStruct((n, R, P1), BF),
        jax.ShapeDtypeStruct((n, R, D), BF),
        jax.ShapeDtypeStruct((n, 8, D), F32),
    )
    block_out, tokens_grad, rq, rp, r1, r2, sums = pl.pallas_call(
        functools.partial(block_kernel, dims),
        out_shape=shapes,
        in_specs=[anywhere] * 4 + [local] + [anywhere] * 4,
        out_specs=[anywhere] * 7,
        scratch_shapes=scratch,
        compiler_params=pltpu.CompilerParams(
            collective_id=0, has_side_effects=True, vmem_limit_bytes=67043328
        ),
    )(tokens[0], cotangent[0], places, small, wave, qkv_weight, proj_weight, fc1_weight, fc2_weight)
    stored = (
        jax.ShapeDtypeStruct((T, D), BF),
        jax.ShapeDtypeStruct((T, D), F32),
        jax.ShapeDtypeStruct((R, 3 * D), F32),
        jax.ShapeDtypeStruct((R, D), F32),
        jax.ShapeDtypeStruct((R, hidden), F32),
        jax.ShapeDtypeStruct((n * R, D), F32),
        jax.ShapeDtypeStruct((16, R), F32),
    )
    block_out, tokens_grad, full_qkv, full_proj, full_up, full_down, sums = pl.pallas_call(
        functools.partial(unpack_kernel, dims),
        out_shape=stored,
        in_specs=[anywhere] * 7,
        out_specs=[anywhere] * 7,
        scratch_shapes=[
            vmem((T, D)),
            vmem((T, D), F32),
            vmem((n, R, CQ)),
            vmem((n, R, HP)),
            vmem((n, R, P1)),
            vmem((n, R, D)),
            vmem((n, 8, D), F32),
            vmem((4 + 2 * n, R, D), F32),
            vmem((16, R), F32),
            pltpu.SemaphoreType.DMA((7,)),
            pltpu.SemaphoreType.DMA((7 + 2 * n,)),
        ],
        compiler_params=pltpu.CompilerParams(vmem_limit_bytes=40000000),
    )(block_out, tokens_grad, rq, rp, r1, r2, sums)
    return (
        block_out[None],
        tokens_grad[None],
        sums[0],
        sums[1],
        full_qkv,
        sums[6 + n : 9 + n].reshape(3 * R),
        full_proj,
        sums[2],
        sums[3],
        sums[4],
        full_up,
        sums[6 : 6 + n].reshape(n * R),
        full_down,
        sums[5],
    )


def fits_kernel(mesh):
    return dict(mesh.shape) == {"seq": 4, "fsdp": 8}


def shards_plain(
    tokens,
    picture_ids,
    patch_rows,
    patch_cols,
    norm1_gain,
    norm1_bias,
    qkv_weight,
    qkv_bias,
    proj_weight,
    proj_bias,
    norm2_gain,
    norm2_bias,
    fc1_weight,
    fc1_bias,
    fc2_weight,
    fc2_bias,
    cotangent,
):
    n = lax.axis_size("seq")
    me = lax.axis_index("seq")
    stores = lax.axis_size("fsdp")
    _, own, width = tokens.shape
    heads = width // HD
    local_heads = heads // n
    hw = local_heads * HD
    rows = qkv_weight.shape[0]
    hidden = fc1_weight.shape[1]
    part = hidden // (stores * n)

    def pick(value, axis):
        return lax.dynamic_index_in_dim(value, me, axis, keepdims=False)

    own_qkv = pick(qkv_weight.reshape(rows, 3, n, hw), 2).reshape(rows, 3 * hw)
    own_up = pick(fc1_weight.reshape(rows, stores, n, part), 2).reshape(rows, stores * part)
    own_down = pick(fc2_weight.reshape(n, part, width), 0)
    small = (norm1_gain, norm1_bias, proj_bias, norm2_gain, norm2_bias, fc2_bias, qkv_bias, fc1_bias)
    sizes = [item.shape[0] for item in small]
    packed = gather(jnp.concatenate(small)[None], "fsdp")
    weight_qkv = gather(own_qkv, "fsdp")
    weight_proj = gather(proj_weight, "fsdp")
    weight_up = gather(own_up, "fsdp")
    weight_down = gather(own_down, "fsdp")
    params = []
    start = 0
    for size in sizes:
        params.append(packed[:, start : start + size].reshape(-1).astype(F32))
        start += size
    gain_one, bias_one, bias_proj, gain_two, bias_two, bias_down, bias_qkv, bias_up = params
    bias_qkv = pick(bias_qkv.reshape(3, n, hw), 1).reshape(3 * hw)
    bias_up = pick(bias_up.reshape(stores, n, part), 1).reshape(stores * part)

    places = jnp.stack([picture_ids[0], patch_rows[0], patch_cols[0]])
    places = gather(places, "seq", 1)
    picture = places[0]
    all_tokens = gather(tokens[0], "seq").astype(F32)
    upstream = gather(cotangent[0], "seq")
    length = all_tokens.shape[0]

    def mine(value):
        return lax.dynamic_slice_in_dim(value, me * own, own, 0)

    normed_one, factor_one = standardize(all_tokens)
    attn_input = (normed_one * gain_one + bias_one).astype(BF)
    projected = (dot(attn_input, weight_qkv) + bias_qkv).reshape(length, 3, local_heads, HD)
    cosine, sine = rotary_tables(places[1], places[2], HD)
    queries = rotate(projected[:, 0], cosine, sine).astype(BF)
    keys = rotate(projected[:, 1], cosine, sine).astype(BF)
    values = projected[:, 2].astype(BF)
    mixed_own, log_total = attend(queries, keys, values, picture)
    mixed = gather(mixed_own.reshape(length, hw), "seq", 1)
    middle = all_tokens + dot(mixed, weight_proj) + bias_proj
    normed_two, factor_two = standardize(middle)
    mlp_input = (normed_two * gain_two + bias_two).astype(BF)
    before = dot(mlp_input, weight_up) + bias_up
    gate = jax.nn.sigmoid(1.702 * before)
    activated = (before * gate).astype(BF)
    out_part = dot(activated, weight_down).astype(BF)
    block_out = (mine(middle) + scatter_sum(out_part, "seq").astype(F32) + bias_down).astype(BF)

    grad_down = scatter_sum(rows_term(activated, upstream).astype(BF), "fsdp")
    grad_activated = contract_back(upstream, weight_down)
    grad_before = (grad_activated * (gate + 1.702 * before * gate * (1.0 - gate))).astype(BF)
    grad_up = scatter_sum(rows_term(mlp_input, grad_before).astype(BF), "fsdp")
    grad_mlp_input = scatter_sum(contract_back(grad_before, weight_up).astype(BF), "seq").astype(F32)
    own_upstream = cotangent[0].astype(F32)
    own_two = mine(normed_two)
    grad_middle = own_upstream + norm_back(grad_mlp_input, own_two, mine(factor_two), gain_two)
    grad_branch = grad_middle.astype(BF)
    grad_mixed = contract_back(grad_branch, weight_proj).astype(BF)
    grad_heads = lax.all_to_all(grad_mixed, "seq", split_axis=1, concat_axis=0, tiled=True)
    branch_part = lax.all_to_all(grad_branch, "seq", split_axis=1, concat_axis=0, tiled=True)
    grad_proj = scatter_sum(rows_term(mixed, branch_part).astype(BF), "fsdp")
    grad_queries, grad_keys, grad_values = attend_back(
        queries, keys, values, picture, grad_heads.reshape(length, local_heads, HD), log_total
    )
    grad_projected = jnp.stack(
        [
            unrotate(grad_queries.astype(F32), cosine, sine).astype(BF),
            unrotate(grad_keys.astype(F32), cosine, sine).astype(BF),
            grad_values,
        ],
        axis=1,
    ).reshape(length, 3 * hw)
    grad_qkv = scatter_sum(rows_term(attn_input, grad_projected).astype(BF), "fsdp")
    grad_attn_input = scatter_sum(contract_back(grad_projected, weight_qkv).astype(BF), "seq").astype(F32)
    own_one = mine(normed_one)
    tokens_grad = grad_middle + norm_back(grad_attn_input, own_one, mine(factor_one), gain_one)

    def spread(value, groups):
        empty = jnp.zeros((groups, n, value.shape[0] // groups), F32)
        return lax.dynamic_update_slice_in_dim(
            empty, value.reshape(groups, 1, -1), me, 1
        ).reshape(stores, -1)

    sums = [
        jnp.sum(grad_attn_input * own_one, axis=0).reshape(stores, -1),
        jnp.sum(grad_attn_input, axis=0).reshape(stores, -1),
        jnp.sum(grad_branch.astype(F32), axis=0).reshape(stores, -1),
        jnp.sum(grad_mlp_input * own_two, axis=0).reshape(stores, -1),
        jnp.sum(grad_mlp_input, axis=0).reshape(stores, -1),
        jnp.sum(own_upstream, axis=0).reshape(stores, -1),
        spread(jnp.sum(grad_projected.astype(F32), axis=0), 3),
        spread(jnp.sum(grad_before.astype(F32), axis=0), stores),
    ]
    summed = lax.psum(scatter_sum(jnp.concatenate(sums, axis=1), "fsdp"), "seq")[0]
    finals = []
    start = 0
    for size in sizes:
        finals.append(summed[start : start + size])
        start += size
    full_down = gather(grad_down, "seq").astype(F32)
    full_up = gather(grad_up[None], "seq").reshape(n, rows, stores, part)
    full_up = full_up.transpose(1, 2, 0, 3).reshape(rows, hidden).astype(F32)
    full_proj = gather(grad_proj, "seq", 1).astype(F32)
    full_qkv = gather(grad_qkv[None], "seq").reshape(n, rows, 3, hw)
    full_qkv = full_qkv.transpose(1, 2, 0, 3).reshape(rows, 3 * width).astype(F32)
    return (
        block_out[None],
        tokens_grad[None],
        finals[0],
        finals[1],
        full_qkv,
        finals[6],
        full_proj,
        finals[2],
        finals[3],
        finals[4],
        full_up,
        finals[7],
        full_down,
        finals[5],
    )


def solution(mesh):
    token = P("fsdp", "seq", None)
    place = P("fsdp", "seq")
    vector = P("fsdp")
    matrix = P("fsdp", None)
    in_specs = (
        token,
        place,
        place,
        place,
        vector,
        vector,
        matrix,
        vector,
        matrix,
        vector,
        vector,
        vector,
        matrix,
        vector,
        matrix,
        vector,
        token,
    )
    out_specs = (
        token,
        token,
        vector,
        vector,
        matrix,
        vector,
        matrix,
        vector,
        vector,
        vector,
        matrix,
        vector,
        matrix,
        vector,
    )
    shards = shards_kernel if fits_kernel(mesh) else shards_plain
    return jax.shard_map(shards, mesh=mesh, in_specs=in_specs, out_specs=out_specs, check_vma=False)
```

```python
import functools

import jax
import jax.numpy as jnp
import numpy as np
from jax import lax
from jax.experimental import pallas as pl
from jax.experimental.pallas import tpu as pltpu
from jax.sharding import PartitionSpec as P

HD = 80
NORM_EPSILON = 1e-06
MASKED = -1e30
BF = jnp.bfloat16
F32 = jnp.float32


def standardize(values_in):
    centre = jnp.mean(values_in, axis=-1, keepdims=True)
    shifted = values_in - centre
    factor = lax.rsqrt(jnp.mean(shifted * shifted, axis=-1, keepdims=True) + NORM_EPSILON)
    return (shifted * factor, factor)


def norm_back(grad_out, normed, factor, gain):
    scaled = grad_out * gain
    return factor * (
        scaled
        - jnp.mean(scaled, axis=-1, keepdims=True)
        - normed * jnp.mean(scaled * normed, axis=-1, keepdims=True)
    )


def rotary_tables(patch_row, patch_col, head_size):
    quarter = head_size // 4
    inverse = jnp.power(10000.0, -jnp.arange(quarter, dtype=F32) / quarter)
    half_angles = jnp.concatenate(
        [
            patch_row.astype(F32)[..., None] * inverse,
            patch_col.astype(F32)[..., None] * inverse,
        ],
        axis=-1,
    )
    angles = jnp.concatenate([half_angles, half_angles], axis=-1)
    return (jnp.cos(angles)[..., None, :], jnp.sin(angles)[..., None, :])


def rotate(values_in, cosine, sine):
    half_size = values_in.shape[-1] // 2
    turned = jnp.concatenate([-values_in[..., half_size:], values_in[..., :half_size]], axis=-1)
    return values_in * cosine + turned * sine


def unrotate(grad_in, cosine, sine):
    half_size = grad_in.shape[-1] // 2
    moved = grad_in * sine
    return grad_in * cosine + jnp.concatenate(
        [moved[..., half_size:], -moved[..., :half_size]], axis=-1
    )


def masked_scores(queries, keys, picture, factor):
    places = jnp.arange(picture.shape[0], dtype=jnp.int32)
    scores = jnp.einsum("qhd,khd->hqk", queries, keys, preferred_element_type=F32) * factor
    allowed = (picture[:, None] == picture[None, :]) & (
        (picture[None, :] >= 0) | (places[:, None] == places[None, :])
    )
    return jnp.where(allowed[None, :, :], scores, MASKED)


def attend(queries, keys, values, picture):
    scores = masked_scores(queries, keys, picture, HD**-0.5)
    row_max = jnp.max(scores, axis=-1, keepdims=True)
    powers = jnp.exp(scores - row_max)
    totals = jnp.sum(powers, axis=-1, keepdims=True)
    weights = (powers / totals).astype(BF)
    mixed = jnp.einsum("hqk,khd->qhd", weights, values, preferred_element_type=F32)
    return mixed.astype(BF), row_max + jnp.log(totals)


def attend_back(queries, keys, values, picture, grad_mixed, log_total):
    factor = HD**-0.5
    scores = masked_scores(queries, keys, picture, factor)
    probs = jnp.exp(scores - log_total)
    weights = probs.astype(BF)
    grad_values = jnp.einsum("hqk,qhd->khd", weights, grad_mixed, preferred_element_type=F32)
    grad_weights = jnp.einsum("qhd,khd->hqk", grad_mixed, values, preferred_element_type=F32)
    centre = jnp.sum(probs * grad_weights, axis=-1, keepdims=True)
    grad_scores = (probs * (grad_weights - centre)).astype(BF)
    grad_queries = jnp.einsum("hqk,khd->qhd", grad_scores, keys, preferred_element_type=F32) * factor
    grad_keys = jnp.einsum("hqk,qhd->khd", grad_scores, queries, preferred_element_type=F32) * factor
    return grad_queries.astype(BF), grad_keys.astype(BF), grad_values.astype(BF)


def dot(left, right):
    return jnp.dot(left, right, preferred_element_type=F32)


def rows_term(left, right):
    return lax.dot_general(left, right, (((0,), (0,)), ((), ())), preferred_element_type=F32)


def contract_back(grad_out, weight):
    return lax.dot_general(grad_out, weight, (((1,), (1,)), ((), ())), preferred_element_type=F32)


def gather(value, axis_name, axis=0):
    return lax.all_gather(value, axis_name, axis=axis, tiled=True)


def scatter_sum(value, axis_name, axis=0):
    return lax.psum_scatter(value, axis_name, scatter_dimension=axis, tiled=True)

MESH = pl.DeviceIdType.MESH


def mm(left, right):
    return jnp.dot(left, right, preferred_element_type=F32)


def mm_nt(left, right):
    return lax.dot_general(left, right, (((1,), (1,)), ((), ())), preferred_element_type=F32)


def mm_tn(left, right):
    return lax.dot_general(left, right, (((0,), (0,)), ((), ())), preferred_element_type=F32)


def lane_pad(value, lanes):
    gap = lanes - value.shape[1]
    if gap == 0:
        return value
    return jnp.concatenate([value, jnp.zeros((value.shape[0], gap), value.dtype)], axis=1)


def moments(value):
    centre = jnp.mean(value, axis=-1, keepdims=True)
    shifted = value - centre
    factor = lax.rsqrt(jnp.mean(shifted * shifted, axis=-1, keepdims=True) + NORM_EPSILON)
    return shifted * factor, factor


def block_kernel(
    dims,
    tok_in,
    cot_in,
    plc_in,
    small_in,
    wave_in,
    wq_in,
    wp_in,
    w1_in,
    w2_in,
    out_ref,
    tgrad_ref,
    rq_ref,
    rp_ref,
    r1_ref,
    r2_ref,
    sums_ref,
    tokb,
    ain,
    cotb,
    plb,
    smb,
    vec,
    bqkv,
    cosb,
    sinb,
    wqc,
    wq,
    wp,
    w1,
    w2,
    qkv,
    lse,
    mixc,
    mix,
    mid,
    mlp,
    act,
    dge,
    snd,
    rsr,
    gmd,
    gp,
    dq4,
    dp4,
    d14,
    d24,
    zq3,
    zp3,
    z13,
    z23,
    dkv,
    smg,
    sg8,
    hq,
    hp,
    h1,
    h2,
    sems,
    local_sems,
):
    n, T, L, D, F, R, hl, P1, CQ, HP = dims
    J = F // 2
    hw = hl * HD
    W = 128
    QW = hl * W
    scale = HD**-0.5
    tile = 256 if D % 256 == 0 else 128
    me = lax.axis_index("seq")
    f = lax.axis_index("fsdp")
    k = f % 2
    j = f // 2
    partner = f + 1 - 2 * k
    x = me % 2
    y = me // 2

    def peer(o):
        return (y + o // 2) % 2 * 2 + (x + o % 2) % 2

    seq_to = [peer(o) for o in range(n)]
    seq_from = seq_to
    near_x, near_y, across = seq_to[1], seq_to[2], seq_to[3]
    edge = (j == 0) | (j == J - 1)
    middle = (j > 0) & (j < J - 1)
    z_to = [2 * ((j + d) % J) + k for d in range(J)]
    z_from = [2 * ((j + J - d) % J) + k for d in range(J)]
    used = {"remote": 0, "local": 0}
    leftover = []

    def take(count=1):
        used["remote"] += count
        return used["remote"] - count

    def remote(src, dst, where, recv):
        return pltpu.make_async_remote_copy(
            src_ref=src,
            dst_ref=dst,
            send_sem=sems.at[take()],
            recv_sem=sems.at[recv],
            device_id=where,
            device_id_type=MESH,
        )

    def when(condition, action):
        pl.when(condition)(action)

    def send(src, dst, where, recv, late=True):
        copy = remote(src, dst, where, recv)
        copy.start()
        if late:
            leftover.append(copy)
        return copy

    def load(src, dst):
        used["local"] += 1
        copy = pltpu.make_async_copy(src, dst, local_sems.at[used["local"] - 1])
        copy.start()
        return copy

    def band(ref, index, size):
        return ref.at[pl.ds(pl.multiple_of(index * size, size), size)]

    def rows_of(index, size):
        return pl.ds(pl.multiple_of(index * size, size), size)

    def strips(total, step, body):
        def run(s, carry):
            body(rows_of(s, step))
            return carry

        lax.fori_loop(0, total // step, run, 0)

    strip = 32

    raw_q = [load(wq_in.at[:, t * D : (t + 1) * D], d24.at[t]) for t in range(3)]
    raw_1 = [load(w1_in.at[:, c * P1 : (c + 1) * P1], d14.at[c]) for c in range(n)]

    barrier = pltpu.get_barrier_semaphore()
    for o in range(1, n):
        pl.semaphore_signal(barrier, inc=1, device_id={"seq": seq_to[o]}, device_id_type=MESH)
    for o in range(1, F):
        pl.semaphore_signal(barrier, inc=1, device_id={"fsdp": (f + o) % F}, device_id_type=MESH)
    pl.semaphore_wait(barrier, n - 1 + F - 1)

    class Spread:
        def __init__(self, src, at, rows):
            self.at, self.rows = at, rows
            self.first = [
                send(src, at(me, 0, rows), {"seq": seq_to[o]}, take()) for o in (1, 2)
            ]

        def relay(self):
            half = self.rows // 2
            self.first[0].wait_recv()
            part = self.at(near_x, 0, half)
            one = send(part, part, {"seq": near_y}, take(), late=False)
            self.first[1].wait_recv()
            part = self.at(near_y, half, self.rows)
            self.second = [one, send(part, part, {"seq": near_x}, take(), late=False)]

        def finish(self):
            for copy in self.second:
                copy.wait_recv()

        def drain(self):
            for copy in self.second:
                copy.wait_send()

    def rows_in(ref):
        return lambda index, lo, hi: ref.at[index, lo:hi]

    plc_copies = [
        send(plc_in, plb.at[me], {"seq": seq_to[o]}, take()) for o in range(1, n)
    ]
    tok = Spread(tok_in, rows_in(tokb), T)
    own_tok = load(tok_in, tokb.at[me])
    own_plc = load(plc_in, plb.at[me])
    own_small = load(small_in, smb.at[f])

    class Weight:
        def __init__(self, src, buf, rows):
            self.buf, self.rows = buf, rows
            self.own = None
            mine = band(buf, f, rows)
            if src is None:
                src = mine
            else:
                self.own = load(src, mine)
            self.near = send(src, mine, {"fsdp": partner}, take(), late=False)
            landed = {d: take() for d in (1, 2, 3)}
            self.far = {d: remote(src, mine, {"fsdp": z_to[d]}, landed[d]) for d in (1, 2, 3)}
            when(j != J - 1, self.far[1].start)
            when(j != 0, self.far[3].start)
            self.far[2].start()
            part = band(buf, z_from[2], rows)
            self.down = remote(part, part, {"fsdp": k}, landed[1])
            self.up = remote(part, part, {"fsdp": 2 * (J - 1) + k}, landed[3])
            self.relayed = []

        def hop(self):
            self.far[2].wait_recv()
            when(j == 1, self.down.start)
            when(j == J - 2, self.up.start)

        def relay(self):
            for d in (2, 1, 3):
                if d != 2:
                    self.far[d].wait_recv()
                part = band(self.buf, z_from[d], self.rows)
                self.relayed.append(send(part, part, {"fsdp": partner}, take(), late=False))

        def finish(self):
            if self.own is not None:
                self.own.wait()
            self.near.wait_recv()
            for copy in self.relayed:
                copy.wait_recv()

        def drain(self):
            for copy in [self.near, self.far[2]] + self.relayed:
                copy.wait_send()
            when(j != J - 1, self.far[1].wait_send)
            when(j != 0, self.far[3].wait_send)
            when(j == 1, self.down.wait_send)
            when(j == J - 2, self.up.wait_send)

    def cut_columns(target, lines):
        for m in range(n):

            @pl.when(me == m)
            def _():
                target[rows_of(f, R), :] = lane_pad(
                    jnp.concatenate(lines(m), axis=1), target.shape[1]
                )

    small_copies = [
        send(small_in, smb.at[f], {"fsdp": (f + o) % F}, take()) for o in range(1, F)
    ]
    for copy in raw_q:
        copy.wait()
    cut_columns(wqc, lambda m: [d24[t, :, m * hw : (m + 1) * hw] for t in range(3)])
    weight_q = Weight(None, wqc, R)
    for copy in raw_1:
        copy.wait()
    cut_columns(
        w1,
        lambda m: [
            d14[b * n * R // P1, :, b * n * R % P1 + m * R : b * n * R % P1 + (m + 1) * R]
            for b in range(F)
        ],
    )

    own_small.wait()
    for copy in small_copies:
        copy.wait_recv()
    for row in range(7):
        vec[row : row + 1, :] = jnp.concatenate(
            [smb[s, row : row + 1, :R] for s in range(F)], axis=1
        )
    groups = 3 * D // R // 3
    heads = []
    for t in range(3):
        start = t * groups + me * (hw // R)
        line = jnp.concatenate(
            [
                smb[(start + b) // 3, pl.ds(7 + (start + b) % 3, 1), :][:, :R]
                for b in range(hw // R)
            ],
            axis=1,
        )
        for h in range(hl):
            heads.append(lane_pad(line[:, h * HD : (h + 1) * HD], W))
    bqkv[...] = jnp.broadcast_to(jnp.concatenate(heads, axis=1), bqkv.shape)

    def vector(row):
        return vec[row : row + 1, :]

    def rows_of_block(i, rows):
        return pl.ds(pl.multiple_of(i * T + rows.start, strip), strip)

    def norm_one(i):
        def body(rows):
            normed, _ = moments(tokb[i, rows, :].astype(F32))
            ain[rows_of_block(i, rows), :] = (normed * vector(0) + vector(1)).astype(BF)

        strips(T, strip, body)

    own_tok.wait()
    norm_one(me)
    tok.relay()
    weight_q.hop()
    weight_p = Weight(wp_in, wp, R)
    weight_1 = Weight(None, w1, R)
    own_cot = load(cot_in, cotb.at[me])
    cot = Spread(cot_in, rows_in(cotb), T)
    norm_one(near_x)
    norm_one(near_y)

    own_plc.wait()
    for copy in plc_copies:
        copy.wait_recv()

    def table(i, carry):
        rows = rows_of(i, T)
        turned = jnp.transpose(plb[i], (1, 0))
        lse[rows, hl : hl + 8] = turned
        angle = turned[:, 1:2] * wave_in[0:1, :] + turned[:, 2:3] * wave_in[1:2, :]
        cosb[rows, :] = jnp.cos(angle)
        sinb[rows, :] = jnp.sin(angle) * wave_in[2:3, :]
        return carry

    lax.fori_loop(0, n, table, 0)
    lane = lax.broadcasted_iota(jnp.int32, (1, W), 1)
    low_half = lane < HD // 2

    def swap(value):
        return jnp.where(
            low_half, pltpu.roll(value, W - HD // 2, 1), pltpu.roll(value, HD // 2, 1)
        )

    tok.finish()
    norm_one(across)

    weight_q.relay()
    weight_q.finish()

    def spread_heads(rows):
        line = wqc[rows, :]
        for h in range(3 * hl):
            wq[rows, h * W : (h + 1) * W] = lane_pad(line[:, h * HD : (h + 1) * HD], W)

    strips(D, R, spread_heads)

    def project(i, carry):
        rows = rows_of(i, T)
        line = ain[rows, :]
        cosine = cosb[rows, :]
        sine = sinb[rows, :]
        for t in range(3):
            part = mm(line, wq[:, t * QW : (t + 1) * QW]) + bqkv[0:1, t * QW : (t + 1) * QW]
            for h in range(hl):
                u = part[:, h * W : (h + 1) * W]
                if t < 2:
                    u = u * cosine + swap(u) * sine
                qkv[rows, t * QW + h * W : t * QW + (h + 1) * W] = u.astype(BF)
        return carry

    lax.fori_loop(0, n, project, 0)

    def masked(scores, i):
        ids = jnp.concatenate([plb[b, 3:4, :] for b in range(n)], axis=1)
        own_ids = lse[rows_of(i, T), hl + 3 : hl + 4]
        return jnp.where(own_ids == ids, scores * scale, MASKED)

    mix_send, mix_recv = take(n * (n - 1)), take(n * (n - 1))

    def mix_copy(i, o, peer, source):
        return pltpu.make_async_remote_copy(
            src_ref=mixc.at[source, i],
            dst_ref=mixc.at[source, i],
            send_sem=sems.at[mix_send + i * (n - 1) + o - 1],
            recv_sem=sems.at[mix_recv + i * (n - 1) + o - 1],
            device_id={"seq": peer},
            device_id_type=MESH,
        )

    def attend_block(i, carry):
        rows = rows_of(i, T)
        outs = []
        logs = lse[rows, :]
        for h in range(hl):
            q = qkv[rows, h * W : (h + 1) * W]
            kk = qkv[:, QW + h * W : QW + (h + 1) * W]
            v = qkv[:, 2 * QW + h * W : 2 * QW + (h + 1) * W]
            s = masked(mm_nt(q, kk), i)
            top = jnp.max(s, axis=-1, keepdims=True)
            p = jnp.exp(s - top)
            total = jnp.sum(p, axis=-1, keepdims=True)
            outs.append((mm(p.astype(BF), v) / total)[:, :HD].astype(BF))
            logs = jnp.where(lane == h, top + jnp.log(total), logs)
        lse[rows, :] = logs
        mixc[me, i] = lane_pad(jnp.concatenate(outs, axis=1), HP)
        for o in range(1, n):
            mix_copy(i, o, seq_to[o], me).start()
        return carry

    weight_p.hop()
    weight_2 = Weight(w2_in.at[rows_of(me, R)], w2, R)
    cot.relay()
    lax.fori_loop(0, n // 2, attend_block, 0)
    weight_p.relay()
    lax.fori_loop(n // 2, n, attend_block, 0)
    weight_1.hop()
    weight_p.finish()
    tok.drain()

    def branch(i, carry):
        rows = rows_of(i, T)
        for o in range(1, n):
            mix_copy(i, o, seq_to[o], seq_from[o]).wait_recv()
        mix[rows, :] = jnp.concatenate([mixc[c, i][:, :hw] for c in range(n)], axis=1)
        gmd[...] = mm(mix[rows, :], wp[...])

        def body(part):
            whole = rows_of_block(i, part)
            value = gmd[part, :] + tokb[i, part, :].astype(F32) + vector(2)

            @pl.when(i == me)
            def _():
                mid[part, :] = value

            normed, _ = moments(value)
            mlp[whole, :] = (normed * vector(3) + vector(4)).astype(BF)

        strips(T, strip, body)
        return carry

    lax.fori_loop(0, n, branch, 0)

    weight_2.hop()
    weight_1.relay()
    weight_1.finish()

    def up(i, carry):
        rows = rows_of(i, T)
        before = mm(mlp[rows, :], w1[...]) + vector(6)
        gate = jax.nn.sigmoid(1.702 * before)
        act[rows, :] = (before * gate).astype(BF)
        dge[rows, :] = (gate + 1.702 * before * gate * (1.0 - gate)).astype(BF)
        return carry

    lax.fori_loop(0, n, up, 0)

    own_cot.wait()
    cot.finish()
    cot.drain()
    weight_2.relay()
    weight_2.finish()

    class Scatter:
        def __init__(self, stage):
            self.stage = stage
            self.out, self.into = take(n - 1), take(n - 1)

        def copy(self, t, to):
            return pltpu.make_async_remote_copy(
                src_ref=band(self.stage, to, T),
                dst_ref=rsr.at[t],
                send_sem=sems.at[self.out + t],
                recv_sem=sems.at[self.into + t],
                device_id={"seq": to},
                device_id_type=MESH,
            )

        def start(self, t, i):
            @pl.when(t < n - 1)
            def _():
                self.copy(t, i).start()

        def wait_recv(self):
            for t in range(n - 1):
                self.copy(t, seq_to[t + 1]).wait_recv()

        def wait_send(self):
            for t in range(n - 1):
                self.copy(t, seq_to[t + 1]).wait_send()

    for i in range(n):
        for o in range(1, n):
            mix_copy(i, o, seq_to[o], me).wait_send()
    scatter_mlp = Scatter(snd)

    def back(t, carry):
        i = peer(t + 1)
        rows = rows_of(i, T)
        grad = (mm_nt(cotb[i], w2[...]) * dge[rows, :].astype(F32)).astype(BF)
        dge[rows, :] = grad
        snd[rows, :] = mm_nt(grad, w1[...]).astype(BF)
        scatter_mlp.start(t, i)
        return carry

    lax.fori_loop(0, n, back, 0)

    class Gradient:
        def __init__(self, grad, other, far, extra, result, lo, width):
            self.grad, self.other, self.far, self.extra = grad, other, far, extra
            self.result, self.lanes = result, slice(lo, lo + width)

        def of(self, index):
            return self.grad.at[rows_of(index, R), self.lanes]

        def exchange(self):
            self.near = [
                send(
                    self.of(2 * c + 1 - k),
                    self.other.at[c, :, self.lanes],
                    {"fsdp": partner},
                    take(),
                )
                for c in range(J)
            ]

        def add_near(self):
            for copy in self.near:
                copy.wait_recv()
            lanes = self.lanes

            def chip(c, carry):
                rows = rows_of(2 * c + k, R)
                self.grad[rows, lanes] = (
                    self.grad[rows, lanes].astype(F32) + self.other[c, :, lanes].astype(F32)
                ).astype(BF)
                return carry

            lax.fori_loop(0, J, chip, 0)
            self.pass_on = remote(
                self.of(2 * (J - 1 - j) + k),
                self.extra.at[:, lanes],
                {"fsdp": 2 * (1 + j // (J - 1)) + k},
                take(),
            )
            self.across = {
                d: remote(
                    self.of(z_to[d]), self.far.at[d - 1, :, lanes], {"fsdp": z_to[d]}, take()
                )
                for d in (1, 2, 3)
            }
            when(edge, self.pass_on.start)
            when(edge, self.across[2].start)
            when(j != J - 1, self.across[1].start)
            when(j != 0, self.across[3].start)

        def hop(self):
            @pl.when(middle)
            def _():
                self.pass_on.wait_recv()
                rows = rows_of(z_to[2], R)
                self.grad[rows, self.lanes] = (
                    self.grad[rows, self.lanes].astype(F32)
                    + self.extra[:, self.lanes].astype(F32)
                ).astype(BF)
                self.across[2].start()

        def add_far(self):
            def total_of(steps):
                def action():
                    for d in steps:
                        self.across[d].wait_recv()
                    total = self.grad[rows_of(f, R), self.lanes].astype(F32)
                    for d in steps:
                        total = total + self.far[d - 1, :, self.lanes].astype(F32)
                    self.other[0, :, self.lanes] = total.astype(BF)

                return action

            when(j == 0, total_of((2, 3)))
            when(middle, total_of((1, 2, 3)))
            when(j == J - 1, total_of((1, 2)))

        def share(self):
            mine = self.other.at[0, :, self.lanes]
            self.keep = load(mine, self.result.at[me, :, self.lanes])
            self.spread = Spread(
                mine, lambda index, lo, hi: self.result.at[index, lo:hi, self.lanes], R
            )

        def relay(self):
            self.spread.relay()

        def finish(self):
            self.keep.wait()
            self.spread.finish()
            self.spread.drain()
            self.across[2].wait_send()
            when(j != J - 1, self.across[1].wait_send)
            when(j != 0, self.across[3].wait_send)
            when(edge, self.pass_on.wait_send)

    CH = CQ // 2
    grad_up = Gradient(w1, d14, z13, h1, r1_ref, 0, P1)
    grad_down = Gradient(w2, d24, z23, h2, r2_ref, 0, D)
    grad_proj = Gradient(gp, dp4, zp3, hp, rp_ref, 0, HP)
    grad_qkv = [Gradient(wqc, dq4, zq3, hq, rq_ref, b * CH, CH) for b in range(2)]

    weight_1.drain()
    weight_2.drain()
    weight_q.drain()

    def up_grad(t, carry):
        w1[rows_of(t, tile), :] = mm_tn(mlp[:, rows_of(t, tile)], dge[...]).astype(BF)
        return carry

    lax.fori_loop(0, D // tile, up_grad, 0)
    grad_up.exchange()

    def down(i, carry):
        rows = rows_of(i, T)
        mlp[rows, :] = mm(act[rows, :], w2[...]).astype(BF)
        return carry

    lax.fori_loop(0, n, down, 0)

    def down_grad(t, carry):
        lanes = rows_of(t, tile)
        total = mm_tn(act[0:T, lanes], cotb[0])
        for b in range(1, n):
            total = total + mm_tn(act[b * T : (b + 1) * T, lanes], cotb[b])
        w2[lanes, :] = total.astype(BF)
        return carry

    lax.fori_loop(0, P1 // tile, down_grad, 0)
    grad_down.exchange()
    grad_up.add_near()

    smg[...] = jnp.zeros(smg.shape, F32)
    scatter_mlp.wait_recv()

    def gather_parts(part):
        whole = rows_of_block(me, part)
        total = snd[whole, :].astype(F32)
        for t in range(n - 1):
            total = total + rsr[t, part, :].astype(F32)
        return total

    def add_sum(row, value):
        smg[row : row + 1, :] = smg[row : row + 1, :] + jnp.sum(value, axis=0, keepdims=True)

    def norm_two_back(part):
        upstream = cotb[me, part, :].astype(F32)
        grad = gather_parts(part)
        normed, factor = moments(mid[part, :])
        scaled = grad * vector(3)
        value = upstream + factor * (
            scaled
            - jnp.mean(scaled, axis=-1, keepdims=True)
            - normed * jnp.mean(scaled * normed, axis=-1, keepdims=True)
        )
        gmd[part, :] = value
        low = value.astype(BF)
        snd[rows_of_block(me, part), :] = low
        add_sum(2, low.astype(F32))
        add_sum(3, grad * normed)
        add_sum(4, grad)
        add_sum(5, upstream)

    strips(T, strip, norm_two_back)
    own_rows = rows_of(me, T)
    low_branch = snd[own_rows, :]
    grad_mixed = mm_nt(low_branch, wp[...]).astype(BF)
    for c in range(n):
        mixc[0, c] = lane_pad(grad_mixed[:, c * hw : (c + 1) * hw], HP)
        mixc[2, c] = lane_pad(low_branch[:, c * hw : (c + 1) * hw], HP)
    head_copies = [
        send(mixc.at[0, seq_to[o]], mixc.at[1, me], {"seq": seq_to[o]}, take()) for o in range(1, n)
    ]
    branch_copies = [
        send(mixc.at[2, seq_to[o]], mixc.at[3, me], {"seq": seq_to[o]}, take()) for o in range(1, n)
    ]
    mixc[1, me] = mixc[0, me]
    mixc[3, me] = mixc[2, me]

    grad_down.add_near()
    grad_up.hop()

    for copy in head_copies:
        copy.wait_recv()
    out_copies = [
        send(band(mlp, seq_to[o], T), tokb.at[me], {"seq": seq_to[o]}, take()) for o in range(1, n)
    ]

    def proj_grad(t, carry):
        lanes = rows_of(t, tile)
        total = mm_tn(mix[0:T, lanes], mixc[3, 0])
        for b in range(1, n):
            total = total + mm_tn(mix[b * T : (b + 1) * T, lanes], mixc[3, b])
        gp[lanes, :] = total.astype(BF)
        return carry

    def qkv_grad(half):
        pair = hl // 2 * W

        def body(t, carry):
            rows = rows_of(t, tile)
            parts = []
            for third in range(3):
                at = third * QW + half * pair
                total = mm_tn(ain[:, rows], qkv[:, at : at + pair])
                parts += [total[:, h * W : h * W + HD].astype(BF) for h in range(hl // 2)]
            wqc[rows, half * CH : (half + 1) * CH] = lane_pad(jnp.concatenate(parts, axis=1), CH)
            return carry

        lax.fori_loop(0, D // tile, body, 0)
        grad_qkv[half].exchange()

    def between(h):
        if h == 0:
            grad_down.hop()
            for copy in branch_copies:
                copy.wait_recv()
            lax.fori_loop(0, D // tile, proj_grad, 0)
            grad_proj.exchange()
        if h == 1:
            grad_proj.add_near()
            qkv_grad(0)
            grad_up.add_far()
        if h == 2:
            grad_proj.hop()
            grad_qkv[0].add_near()
        if h == 3:
            grad_qkv[0].hop()
            grad_down.add_far()

    for h in range(hl):
        q_at = slice(h * W, (h + 1) * W)
        k_at = slice(QW + h * W, QW + (h + 1) * W)
        v_at = slice(2 * QW + h * W, 2 * QW + (h + 1) * W)
        dkv[...] = jnp.zeros(dkv.shape, F32)

        def attend_back_block(i, carry):
            rows = rows_of(i, T)
            q = qkv[rows, q_at]
            kk = qkv[:, k_at]
            g = lane_pad(mixc[1, i][:, h * HD : (h + 1) * HD], W)
            p = jnp.exp(masked(mm_nt(q, kk), i) - lse[rows, h : h + 1])
            dp = mm_nt(g, qkv[:, v_at])
            dkv[:, W:] = dkv[:, W:] + mm_tn(p.astype(BF), g)
            centre = jnp.sum(p * dp, axis=-1, keepdims=True)
            ds = (p * (dp - centre)).astype(BF)
            dq = (mm(ds, kk) * scale).astype(BF).astype(F32)
            dkv[:, :W] = dkv[:, :W] + mm_tn(ds, q)
            qkv[rows, q_at] = (dq * cosb[rows, :] - swap(dq) * sinb[rows, :]).astype(BF)
            return carry

        lax.fori_loop(0, n, attend_back_block, 0)

        def turn_back(i, carry):
            rows = rows_of(i, T)
            dk = (dkv[rows, :W] * scale).astype(BF).astype(F32)
            qkv[rows, k_at] = (dk * cosb[rows, :] - swap(dk) * sinb[rows, :]).astype(BF)
            qkv[rows, v_at] = dkv[rows, W:].astype(BF)
            return carry

        lax.fori_loop(0, n, turn_back, 0)
        between(h)

    scatter_mlp.wait_send()
    scatter_attn = Scatter(snd)

    def attn_back(t, carry):
        i = peer(t + 1)
        rows = rows_of(i, T)
        snd[rows, :] = mm_nt(qkv[rows, :], wq[...]).astype(BF)
        scatter_attn.start(t, i)
        return carry

    lax.fori_loop(0, n, attn_back, 0)

    grad_up.share()
    grad_down.share()
    qkv_grad(1)
    grad_proj.add_far()
    grad_proj.share()

    def bias_sums(part):
        smg[6:7, :] = smg[6:7, :] + jnp.sum(dge[part, :].astype(F32), axis=0, keepdims=True)
        line = jnp.sum(qkv[part, :].astype(F32), axis=0, keepdims=True)
        line = lane_pad(
            jnp.concatenate([line[:, h * W : h * W + HD] for h in range(3 * hl)], axis=1), D
        )
        smg[7:8, :] = smg[7:8, :] + line

    grad_qkv[1].add_near()
    strips(L, 64, bias_sums)
    grad_qkv[0].add_far()
    grad_qkv[0].share()
    grad_qkv[1].hop()

    scatter_attn.wait_recv()

    def norm_one_back(part):
        grad = gather_parts(part)
        normed, factor = moments(tokb[me, part, :].astype(F32))
        scaled = grad * vector(0)
        gmd[part, :] = gmd[part, :] + factor * (
            scaled
            - jnp.mean(scaled, axis=-1, keepdims=True)
            - normed * jnp.mean(scaled * normed, axis=-1, keepdims=True)
        )
        add_sum(0, grad * normed)
        add_sum(1, grad)

    strips(T, strip, norm_one_back)
    tokens_out = load(gmd, tgrad_ref)
    sum_copies = [
        send(smg, sg8.at[f], {"fsdp": (f + o) % F}, take()) for o in range(1, F)
    ]
    sg8[f] = smg[...]
    grad_up.relay()
    grad_down.relay()
    grad_qkv[1].add_far()
    grad_qkv[1].share()

    for copy in out_copies:
        copy.wait_recv()

    def write_out(part):
        whole = rows_of_block(me, part)
        total = mid[part, :] + mlp[whole, :].astype(F32) + vector(5)
        for o in range(1, n):
            total = total + tokb[seq_from[o], part, :].astype(F32)
        bias_rows = rows_of_block(me, part)
        ain[bias_rows, :] = total.astype(BF)

    strips(T, strip, write_out)
    block_out = load(band(ain, me, T), out_ref)

    for copy in sum_copies:
        copy.wait_recv()
    total = sg8[0]
    for s in range(1, F):
        total = total + sg8[s]
    plain = lax.broadcasted_iota(jnp.int32, total.shape, 0)
    vec[...] = jnp.where(plain < 8, total, 0.0)
    sums_keep = load(vec, sums_ref.at[me])
    sums_share = [
        send(vec, sums_ref.at[me], {"seq": seq_to[o]}, take()) for o in range(1, n)
    ]

    grads = [grad_up, grad_down, grad_proj] + grad_qkv
    for item in grads[2:]:
        item.relay()
    for item in grads:
        item.finish()
    for copy in sums_share:
        copy.wait_recv()
    sums_keep.wait()
    tokens_out.wait()
    block_out.wait()
    weight_p.drain()
    scatter_attn.wait_send()
    for copy in leftover:
        copy.wait_send()


def unpack_kernel(
    dims,
    block_in,
    tokens_in,
    rq_in,
    rp_in,
    r1_in,
    r2_in,
    sums_in,
    block_ref,
    tokens_ref,
    qkv_ref,
    proj_ref,
    up_ref,
    down_ref,
    vec_ref,
    block,
    tokens,
    rq,
    rp,
    r1,
    r2,
    sums,
    stage,
    vec,
    in_sems,
    out_sems,
):
    n, T, L, D, F, R, hl, P1, CQ, HP = dims
    hw = hl * HD
    f = lax.axis_index("fsdp")
    loads = []
    for src, dst in (
        (r2_in, r2),
        (r1_in, r1),
        (rq_in, rq),
        (rp_in, rp),
        (tokens_in, tokens),
        (block_in, block),
        (sums_in, sums),
    ):
        copy = pltpu.make_async_copy(src, dst, in_sems.at[len(loads)])
        copy.start()
        loads.append(copy)
    stores = []

    def store(src, dst):
        copy = pltpu.make_async_copy(src, dst, out_sems.at[len(stores)])
        copy.start()
        stores.append(copy)

    loads[0].wait()
    for c in range(n):
        stage[c] = r2[c].astype(F32)
        store(stage.at[c], down_ref.at[c * R : (c + 1) * R])
    loads[1].wait()
    width = n * R
    for c in range(n):
        blocks = range(c * P1 // width, (c + 1) * P1 // width)
        stage[n + c] = jnp.concatenate(
            [r1[m, :, b * R : (b + 1) * R] for b in blocks for m in range(n)], axis=1
        ).astype(F32)
        store(stage.at[n + c], up_ref.at[:, c * P1 : (c + 1) * P1])
    loads[2].wait()
    for t in range(3):
        stage[2 * n + t] = jnp.concatenate(
            [
                rq[m, :, b * CQ // 2 + t * hw // 2 : b * CQ // 2 + (t + 1) * hw // 2]
                for m in range(n)
                for b in range(2)
            ],
            axis=1,
        ).astype(F32)
        store(stage.at[2 * n + t], qkv_ref.at[:, t * D : (t + 1) * D])
    loads[3].wait()
    stage[2 * n + 3] = jnp.concatenate([rp[m, :, :hw] for m in range(n)], axis=1).astype(F32)
    store(stage.at[2 * n + 3], proj_ref)
    loads[4].wait()
    store(tokens, tokens_ref)
    loads[5].wait()
    store(block, block_ref)
    loads[6].wait()
    per_part = hw // R
    for s in range(F):

        @pl.when(f == s)
        def _():
            own = slice(s * R, (s + 1) * R)
            total = sums[0, 0:6, own]
            for m in range(1, n):
                total = total + sums[m, 0:6, own]
            lines = [total] + [sums[m, 6:7, own] for m in range(n)]
            for b in range(3):
                spot = 3 * s + b
                third, rest = spot // (n * per_part), spot % (n * per_part)
                at = third * hw + rest % per_part * R
                lines.append(sums[rest // per_part, 7:8, at : at + R])
            lines.append(jnp.zeros((16 - 9 - n, R), F32))
            vec[...] = jnp.concatenate(lines, axis=0)

    store(vec, vec_ref)
    for copy in stores:
        copy.wait()


def round_up(value, step):
    return -(-value // step) * step


def shards_kernel(
    tokens,
    picture_ids,
    patch_rows,
    patch_cols,
    norm1_gain,
    norm1_bias,
    qkv_weight,
    qkv_bias,
    proj_weight,
    proj_bias,
    norm2_gain,
    norm2_bias,
    fc1_weight,
    fc1_bias,
    fc2_weight,
    fc2_bias,
    cotangent,
):
    n = lax.axis_size("seq")
    me = lax.axis_index("seq")
    F = lax.axis_size("fsdp")
    f = lax.axis_index("fsdp")
    _, T, D = tokens.shape
    L = n * T
    hl = D // HD // n
    hw = hl * HD
    R = D // F
    hidden = fc1_weight.shape[1]
    P1 = hidden // n
    part = hidden // (F * n)
    CQ = round_up(3 * hw, 128)
    HP = round_up(hw, 128)
    J = F // 2
    W = 128

    def pick(value, axis):
        return lax.dynamic_index_in_dim(value, me, axis, keepdims=False)

    lines = (
        norm1_gain,
        norm1_bias,
        proj_bias,
        norm2_gain,
        norm2_bias,
        fc2_bias,
        pick(fc1_bias.reshape(n, part), 0),
        qkv_bias,
    )
    small = jnp.concatenate([item.astype(F32).reshape(-1, R) for item in lines])
    small = jnp.pad(small, ((0, 6), (0, 0)))
    spot = jnp.arange(T, dtype=jnp.int32) + me * T
    ids = jnp.where(picture_ids[0] >= 0, picture_ids[0], -1 - spot)
    places = jnp.stack([picture_ids[0], patch_rows[0], patch_cols[0], ids]).astype(F32)
    places = jnp.pad(places, ((0, 4), (0, 0)))
    quarter = HD // 4
    inverse = 10000.0 ** (-np.arange(quarter) / quarter)
    wave = np.zeros((8, W), np.float32)
    for c in range(2):
        wave[0, 2 * c * quarter : (2 * c + 1) * quarter] = inverse
        wave[1, (2 * c + 1) * quarter : (2 * c + 2) * quarter] = inverse
    wave[2] = np.where(np.arange(W) < HD // 2, -1.0, 1.0)
    dims = (n, T, L, D, F, R, hl, P1, CQ, HP)
    anywhere = pl.BlockSpec(memory_space=pl.ANY)
    local = pl.BlockSpec(memory_space=pltpu.VMEM)

    def vmem(shape, dtype=BF):
        return pltpu.VMEM(shape, dtype)

    scratch = [
        vmem((n, T, D)),
        vmem((L, D)),
        vmem((n, T, D)),
        vmem((n, 8, T), F32),
        vmem((F, 16, R), F32),
        vmem((8, D), F32),
        vmem((8, 3 * hl * W), F32),
        vmem((L, W), F32),
        vmem((L, W), F32),
        vmem((D, CQ)),
        vmem((D, 3 * hl * W)),
        vmem((D, D)),
        vmem((D, P1)),
        vmem((P1, D)),
        vmem((L, 3 * hl * W)),
        vmem((L, W), F32),
        vmem((n, n, T, HP)),
        vmem((L, D)),
        vmem((T, D), F32),
        vmem((L, D)),
        vmem((L, P1)),
        vmem((L, P1)),
        vmem((L, D)),
        vmem((n - 1, T, D)),
        vmem((T, D), F32),
        vmem((D, HP)),
        vmem((J, R, CQ)),
        vmem((J, R, HP)),
        vmem((J, R, P1)),
        vmem((J, R, D)),
        vmem((J - 1, R, CQ)),
        vmem((J - 1, R, HP)),
        vmem((J - 1, R, P1)),
        vmem((J - 1, R, D)),
        vmem((L, 2 * W), F32),
        vmem((8, D), F32),
        vmem((F, 8, D), F32),
        vmem((R, CQ)),
        vmem((R, HP)),
        vmem((R, P1)),
        vmem((R, D)),
        pltpu.SemaphoreType.DMA((448,)),
        pltpu.SemaphoreType.DMA((24,)),
    ]
    shapes = (
        jax.ShapeDtypeStruct((T, D), BF),
        jax.ShapeDtypeStruct((T, D), F32),
        jax.ShapeDtypeStruct((n, R, CQ), BF),
        jax.ShapeDtypeStruct((n, R, HP), BF),
        jax.ShapeDtypeStruct((n, R, P1), BF),
        jax.ShapeDtypeStruct((n, R, D), BF),
        jax.ShapeDtypeStruct((n, 8, D), F32),
    )
    block_out, tokens_grad, rq, rp, r1, r2, sums = pl.pallas_call(
        functools.partial(block_kernel, dims),
        out_shape=shapes,
        in_specs=[anywhere] * 4 + [local] + [anywhere] * 4,
        out_specs=[anywhere] * 7,
        scratch_shapes=scratch,
        compiler_params=pltpu.CompilerParams(
            collective_id=0, has_side_effects=True, vmem_limit_bytes=67043328
        ),
    )(tokens[0], cotangent[0], places, small, wave, qkv_weight, proj_weight, fc1_weight, fc2_weight)
    stored = (
        jax.ShapeDtypeStruct((T, D), BF),
        jax.ShapeDtypeStruct((T, D), F32),
        jax.ShapeDtypeStruct((R, 3 * D), F32),
        jax.ShapeDtypeStruct((R, D), F32),
        jax.ShapeDtypeStruct((R, hidden), F32),
        jax.ShapeDtypeStruct((n * R, D), F32),
        jax.ShapeDtypeStruct((16, R), F32),
    )
    block_out, tokens_grad, full_qkv, full_proj, full_up, full_down, sums = pl.pallas_call(
        functools.partial(unpack_kernel, dims),
        out_shape=stored,
        in_specs=[anywhere] * 7,
        out_specs=[anywhere] * 7,
        scratch_shapes=[
            vmem((T, D)),
            vmem((T, D), F32),
            vmem((n, R, CQ)),
            vmem((n, R, HP)),
            vmem((n, R, P1)),
            vmem((n, R, D)),
            vmem((n, 8, D), F32),
            vmem((4 + 2 * n, R, D), F32),
            vmem((16, R), F32),
            pltpu.SemaphoreType.DMA((7,)),
            pltpu.SemaphoreType.DMA((7 + 2 * n,)),
        ],
        compiler_params=pltpu.CompilerParams(vmem_limit_bytes=67043328),
    )(block_out, tokens_grad, rq, rp, r1, r2, sums)
    return (
        block_out[None],
        tokens_grad[None],
        sums[0],
        sums[1],
        full_qkv,
        sums[6 + n : 9 + n].reshape(3 * R),
        full_proj,
        sums[2],
        sums[3],
        sums[4],
        full_up,
        sums[6 : 6 + n].reshape(n * R),
        full_down,
        sums[5],
    )


def fits_kernel(mesh):
    return dict(mesh.shape) == {"seq": 4, "fsdp": 8}


def shards_plain(
    tokens,
    picture_ids,
    patch_rows,
    patch_cols,
    norm1_gain,
    norm1_bias,
    qkv_weight,
    qkv_bias,
    proj_weight,
    proj_bias,
    norm2_gain,
    norm2_bias,
    fc1_weight,
    fc1_bias,
    fc2_weight,
    fc2_bias,
    cotangent,
):
    n = lax.axis_size("seq")
    me = lax.axis_index("seq")
    stores = lax.axis_size("fsdp")
    _, own, width = tokens.shape
    heads = width // HD
    local_heads = heads // n
    hw = local_heads * HD
    rows = qkv_weight.shape[0]
    hidden = fc1_weight.shape[1]
    part = hidden // (stores * n)

    def pick(value, axis):
        return lax.dynamic_index_in_dim(value, me, axis, keepdims=False)

    own_qkv = pick(qkv_weight.reshape(rows, 3, n, hw), 2).reshape(rows, 3 * hw)
    own_up = pick(fc1_weight.reshape(rows, stores, n, part), 2).reshape(rows, stores * part)
    own_down = pick(fc2_weight.reshape(n, part, width), 0)
    small = (norm1_gain, norm1_bias, proj_bias, norm2_gain, norm2_bias, fc2_bias, qkv_bias, fc1_bias)
    sizes = [item.shape[0] for item in small]
    packed = gather(jnp.concatenate(small)[None], "fsdp")
    weight_qkv = gather(own_qkv, "fsdp")
    weight_proj = gather(proj_weight, "fsdp")
    weight_up = gather(own_up, "fsdp")
    weight_down = gather(own_down, "fsdp")
    params = []
    start = 0
    for size in sizes:
        params.append(packed[:, start : start + size].reshape(-1).astype(F32))
        start += size
    gain_one, bias_one, bias_proj, gain_two, bias_two, bias_down, bias_qkv, bias_up = params
    bias_qkv = pick(bias_qkv.reshape(3, n, hw), 1).reshape(3 * hw)
    bias_up = pick(bias_up.reshape(stores, n, part), 1).reshape(stores * part)

    places = jnp.stack([picture_ids[0], patch_rows[0], patch_cols[0]])
    places = gather(places, "seq", 1)
    picture = places[0]
    all_tokens = gather(tokens[0], "seq").astype(F32)
    upstream = gather(cotangent[0], "seq")
    length = all_tokens.shape[0]

    def mine(value):
        return lax.dynamic_slice_in_dim(value, me * own, own, 0)

    normed_one, factor_one = standardize(all_tokens)
    attn_input = (normed_one * gain_one + bias_one).astype(BF)
    projected = (dot(attn_input, weight_qkv) + bias_qkv).reshape(length, 3, local_heads, HD)
    cosine, sine = rotary_tables(places[1], places[2], HD)
    queries = rotate(projected[:, 0], cosine, sine).astype(BF)
    keys = rotate(projected[:, 1], cosine, sine).astype(BF)
    values = projected[:, 2].astype(BF)
    mixed_own, log_total = attend(queries, keys, values, picture)
    mixed = gather(mixed_own.reshape(length, hw), "seq", 1)
    middle = all_tokens + dot(mixed, weight_proj) + bias_proj
    normed_two, factor_two = standardize(middle)
    mlp_input = (normed_two * gain_two + bias_two).astype(BF)
    before = dot(mlp_input, weight_up) + bias_up
    gate = jax.nn.sigmoid(1.702 * before)
    activated = (before * gate).astype(BF)
    out_part = dot(activated, weight_down).astype(BF)
    block_out = (mine(middle) + scatter_sum(out_part, "seq").astype(F32) + bias_down).astype(BF)

    grad_down = scatter_sum(rows_term(activated, upstream).astype(BF), "fsdp")
    grad_activated = contract_back(upstream, weight_down)
    grad_before = (grad_activated * (gate + 1.702 * before * gate * (1.0 - gate))).astype(BF)
    grad_up = scatter_sum(rows_term(mlp_input, grad_before).astype(BF), "fsdp")
    grad_mlp_input = scatter_sum(contract_back(grad_before, weight_up).astype(BF), "seq").astype(F32)
    own_upstream = cotangent[0].astype(F32)
    own_two = mine(normed_two)
    grad_middle = own_upstream + norm_back(grad_mlp_input, own_two, mine(factor_two), gain_two)
    grad_branch = grad_middle.astype(BF)
    grad_mixed = contract_back(grad_branch, weight_proj).astype(BF)
    grad_heads = lax.all_to_all(grad_mixed, "seq", split_axis=1, concat_axis=0, tiled=True)
    branch_part = lax.all_to_all(grad_branch, "seq", split_axis=1, concat_axis=0, tiled=True)
    grad_proj = scatter_sum(rows_term(mixed, branch_part).astype(BF), "fsdp")
    grad_queries, grad_keys, grad_values = attend_back(
        queries, keys, values, picture, grad_heads.reshape(length, local_heads, HD), log_total
    )
    grad_projected = jnp.stack(
        [
            unrotate(grad_queries.astype(F32), cosine, sine).astype(BF),
            unrotate(grad_keys.astype(F32), cosine, sine).astype(BF),
            grad_values,
        ],
        axis=1,
    ).reshape(length, 3 * hw)
    grad_qkv = scatter_sum(rows_term(attn_input, grad_projected).astype(BF), "fsdp")
    grad_attn_input = scatter_sum(contract_back(grad_projected, weight_qkv).astype(BF), "seq").astype(F32)
    own_one = mine(normed_one)
    tokens_grad = grad_middle + norm_back(grad_attn_input, own_one, mine(factor_one), gain_one)

    def spread(value, groups):
        empty = jnp.zeros((groups, n, value.shape[0] // groups), F32)
        return lax.dynamic_update_slice_in_dim(
            empty, value.reshape(groups, 1, -1), me, 1
        ).reshape(stores, -1)

    sums = [
        jnp.sum(grad_attn_input * own_one, axis=0).reshape(stores, -1),
        jnp.sum(grad_attn_input, axis=0).reshape(stores, -1),
        jnp.sum(grad_branch.astype(F32), axis=0).reshape(stores, -1),
        jnp.sum(grad_mlp_input * own_two, axis=0).reshape(stores, -1),
        jnp.sum(grad_mlp_input, axis=0).reshape(stores, -1),
        jnp.sum(own_upstream, axis=0).reshape(stores, -1),
        spread(jnp.sum(grad_projected.astype(F32), axis=0), 3),
        spread(jnp.sum(grad_before.astype(F32), axis=0), stores),
    ]
    summed = lax.psum(scatter_sum(jnp.concatenate(sums, axis=1), "fsdp"), "seq")[0]
    finals = []
    start = 0
    for size in sizes:
        finals.append(summed[start : start + size])
        start += size
    full_down = gather(grad_down, "seq").astype(F32)
    full_up = gather(grad_up[None], "seq").reshape(n, rows, stores, part)
    full_up = full_up.transpose(1, 2, 0, 3).reshape(rows, hidden).astype(F32)
    full_proj = gather(grad_proj, "seq", 1).astype(F32)
    full_qkv = gather(grad_qkv[None], "seq").reshape(n, rows, 3, hw)
    full_qkv = full_qkv.transpose(1, 2, 0, 3).reshape(rows, 3 * width).astype(F32)
    return (
        block_out[None],
        tokens_grad[None],
        finals[0],
        finals[1],
        full_qkv,
        finals[6],
        full_proj,
        finals[2],
        finals[3],
        finals[4],
        full_up,
        finals[7],
        full_down,
        finals[5],
    )


def solution(mesh):
    token = P("fsdp", "seq", None)
    place = P("fsdp", "seq")
    vector = P("fsdp")
    matrix = P("fsdp", None)
    in_specs = (
        token,
        place,
        place,
        place,
        vector,
        vector,
        matrix,
        vector,
        matrix,
        vector,
        vector,
        vector,
        matrix,
        vector,
        matrix,
        vector,
        token,
    )
    out_specs = (
        token,
        token,
        vector,
        vector,
        matrix,
        vector,
        matrix,
        vector,
        vector,
        vector,
        matrix,
        vector,
        matrix,
        vector,
    )
    shards = shards_kernel if fits_kernel(mesh) else shards_plain
    return jax.shard_map(shards, mesh=mesh, in_specs=in_specs, out_specs=out_specs, check_vma=False)
```

```python
import functools

import jax
import jax.numpy as jnp
import numpy as np
from jax import lax
from jax.experimental import pallas as pl
from jax.experimental.pallas import tpu as pltpu
from jax.sharding import PartitionSpec as P

HD = 80
NORM_EPSILON = 1e-06
MASKED = -1e30
BF = jnp.bfloat16
F32 = jnp.float32


def standardize(values_in):
    centre = jnp.mean(values_in, axis=-1, keepdims=True)
    shifted = values_in - centre
    factor = lax.rsqrt(jnp.mean(shifted * shifted, axis=-1, keepdims=True) + NORM_EPSILON)
    return (shifted * factor, factor)


def norm_back(grad_out, normed, factor, gain):
    scaled = grad_out * gain
    return factor * (
        scaled
        - jnp.mean(scaled, axis=-1, keepdims=True)
        - normed * jnp.mean(scaled * normed, axis=-1, keepdims=True)
    )


def rotary_tables(patch_row, patch_col, head_size):
    quarter = head_size // 4
    inverse = jnp.power(10000.0, -jnp.arange(quarter, dtype=F32) / quarter)
    half_angles = jnp.concatenate(
        [
            patch_row.astype(F32)[..., None] * inverse,
            patch_col.astype(F32)[..., None] * inverse,
        ],
        axis=-1,
    )
    angles = jnp.concatenate([half_angles, half_angles], axis=-1)
    return (jnp.cos(angles)[..., None, :], jnp.sin(angles)[..., None, :])


def rotate(values_in, cosine, sine):
    half_size = values_in.shape[-1] // 2
    turned = jnp.concatenate([-values_in[..., half_size:], values_in[..., :half_size]], axis=-1)
    return values_in * cosine + turned * sine


def unrotate(grad_in, cosine, sine):
    half_size = grad_in.shape[-1] // 2
    moved = grad_in * sine
    return grad_in * cosine + jnp.concatenate(
        [moved[..., half_size:], -moved[..., :half_size]], axis=-1
    )


def masked_scores(queries, keys, picture, factor):
    places = jnp.arange(picture.shape[0], dtype=jnp.int32)
    scores = jnp.einsum("qhd,khd->hqk", queries, keys, preferred_element_type=F32) * factor
    allowed = (picture[:, None] == picture[None, :]) & (
        (picture[None, :] >= 0) | (places[:, None] == places[None, :])
    )
    return jnp.where(allowed[None, :, :], scores, MASKED)


def attend(queries, keys, values, picture):
    scores = masked_scores(queries, keys, picture, HD**-0.5)
    row_max = jnp.max(scores, axis=-1, keepdims=True)
    powers = jnp.exp(scores - row_max)
    totals = jnp.sum(powers, axis=-1, keepdims=True)
    weights = (powers / totals).astype(BF)
    mixed = jnp.einsum("hqk,khd->qhd", weights, values, preferred_element_type=F32)
    return mixed.astype(BF), row_max + jnp.log(totals)


def attend_back(queries, keys, values, picture, grad_mixed, log_total):
    factor = HD**-0.5
    scores = masked_scores(queries, keys, picture, factor)
    probs = jnp.exp(scores - log_total)
    weights = probs.astype(BF)
    grad_values = jnp.einsum("hqk,qhd->khd", weights, grad_mixed, preferred_element_type=F32)
    grad_weights = jnp.einsum("qhd,khd->hqk", grad_mixed, values, preferred_element_type=F32)
    centre = jnp.sum(probs * grad_weights, axis=-1, keepdims=True)
    grad_scores = (probs * (grad_weights - centre)).astype(BF)
    grad_queries = jnp.einsum("hqk,khd->qhd", grad_scores, keys, preferred_element_type=F32) * factor
    grad_keys = jnp.einsum("hqk,qhd->khd", grad_scores, queries, preferred_element_type=F32) * factor
    return grad_queries.astype(BF), grad_keys.astype(BF), grad_values.astype(BF)


def dot(left, right):
    return jnp.dot(left, right, preferred_element_type=F32)


def rows_term(left, right):
    return lax.dot_general(left, right, (((0,), (0,)), ((), ())), preferred_element_type=F32)


def contract_back(grad_out, weight):
    return lax.dot_general(grad_out, weight, (((1,), (1,)), ((), ())), preferred_element_type=F32)


def gather(value, axis_name, axis=0):
    return lax.all_gather(value, axis_name, axis=axis, tiled=True)


def scatter_sum(value, axis_name, axis=0):
    return lax.psum_scatter(value, axis_name, scatter_dimension=axis, tiled=True)

MESH = pl.DeviceIdType.MESH


def mm(left, right):
    return jnp.dot(left, right, preferred_element_type=F32)


def mm_nt(left, right):
    return lax.dot_general(left, right, (((1,), (1,)), ((), ())), preferred_element_type=F32)


def mm_tn(left, right):
    return lax.dot_general(left, right, (((0,), (0,)), ((), ())), preferred_element_type=F32)


def lane_pad(value, lanes):
    gap = lanes - value.shape[1]
    if gap == 0:
        return value
    return jnp.concatenate([value, jnp.zeros((value.shape[0], gap), value.dtype)], axis=1)


def moments(value):
    centre = jnp.mean(value, axis=-1, keepdims=True)
    shifted = value - centre
    factor = lax.rsqrt(jnp.mean(shifted * shifted, axis=-1, keepdims=True) + NORM_EPSILON)
    return shifted * factor, factor


def block_kernel(
    dims,
    tok_in,
    cot_in,
    plc_in,
    small_in,
    wave_in,
    wq_in,
    wp_in,
    w1_in,
    w2_in,
    out_ref,
    tgrad_ref,
    rq_ref,
    rp_ref,
    r1_ref,
    r2_ref,
    sums_ref,
    tokb,
    ain,
    cotb,
    plb,
    smb,
    vec,
    bqkv,
    cosb,
    sinb,
    wqc,
    wq,
    wp,
    w1,
    w2,
    qkv,
    lse,
    mixc,
    mix,
    mid,
    mlp,
    act,
    dge,
    snd,
    rsr,
    gmd,
    gp,
    dq4,
    dp4,
    d14,
    d24,
    zq3,
    zp3,
    z13,
    z23,
    dkv,
    smg,
    sg8,
    hq,
    hp,
    h1,
    h2,
    sems,
    local_sems,
):
    n, T, L, D, F, R, hl, P1, CQ, HP = dims
    J = F // 2
    hw = hl * HD
    W = 128
    QW = hl * W
    scale = HD**-0.5
    tile = 256 if D % 256 == 0 else 128
    me = lax.axis_index("seq")
    f = lax.axis_index("fsdp")
    k = f % 2
    j = f // 2
    partner = f + 1 - 2 * k
    x = me % 2
    y = me // 2

    def peer(o):
        return (y + o // 2) % 2 * 2 + (x + o % 2) % 2

    seq_to = [peer(o) for o in range(n)]
    seq_from = seq_to
    near_x, near_y, across = seq_to[1], seq_to[2], seq_to[3]
    edge = (j == 0) | (j == J - 1)
    middle = (j > 0) & (j < J - 1)
    z_to = [2 * ((j + d) % J) + k for d in range(J)]
    z_from = [2 * ((j + J - d) % J) + k for d in range(J)]
    used = {"remote": 0, "local": 0}
    leftover = []

    def take(count=1):
        used["remote"] += count
        return used["remote"] - count

    def remote(src, dst, where, recv):
        return pltpu.make_async_remote_copy(
            src_ref=src,
            dst_ref=dst,
            send_sem=sems.at[take()],
            recv_sem=sems.at[recv],
            device_id=where,
            device_id_type=MESH,
        )

    def when(condition, action):
        pl.when(condition)(action)

    def send(src, dst, where, recv, late=True):
        copy = remote(src, dst, where, recv)
        copy.start()
        if late:
            leftover.append(copy)
        return copy

    def load(src, dst):
        used["local"] += 1
        copy = pltpu.make_async_copy(src, dst, local_sems.at[used["local"] - 1])
        copy.start()
        return copy

    def band(ref, index, size):
        return ref.at[pl.ds(pl.multiple_of(index * size, size), size)]

    def rows_of(index, size):
        return pl.ds(pl.multiple_of(index * size, size), size)

    def strips(total, step, body):
        def run(s, carry):
            body(rows_of(s, step))
            return carry

        lax.fori_loop(0, total // step, run, 0)

    strip = 32

    raw_q = [load(wq_in.at[:, t * D : (t + 1) * D], d24.at[t]) for t in range(3)]
    raw_1 = [load(w1_in.at[:, c * P1 : (c + 1) * P1], d14.at[c]) for c in range(n)]

    barrier = pltpu.get_barrier_semaphore()
    for o in range(1, n):
        pl.semaphore_signal(barrier, inc=1, device_id={"seq": seq_to[o]}, device_id_type=MESH)
    for o in range(1, F):
        pl.semaphore_signal(barrier, inc=1, device_id={"fsdp": (f + o) % F}, device_id_type=MESH)
    pl.semaphore_wait(barrier, n - 1 + F - 1)

    class Spread:
        def __init__(self, src, at, rows):
            self.at, self.rows = at, rows
            self.first = [
                send(src, at(me, 0, rows), {"seq": seq_to[o]}, take()) for o in (1, 2)
            ]

        def relay(self):
            half = self.rows // 2
            self.first[0].wait_recv()
            part = self.at(near_x, 0, half)
            one = send(part, part, {"seq": near_y}, take(), late=False)
            self.first[1].wait_recv()
            part = self.at(near_y, half, self.rows)
            self.second = [one, send(part, part, {"seq": near_x}, take(), late=False)]

        def finish(self):
            for copy in self.second:
                copy.wait_recv()

        def drain(self):
            for copy in self.second:
                copy.wait_send()

    def rows_in(ref):
        return lambda index, lo, hi: ref.at[index, lo:hi]

    plc_copies = [
        send(plc_in, plb.at[me], {"seq": seq_to[o]}, take()) for o in range(1, n)
    ]
    tok = Spread(tok_in, rows_in(tokb), T)
    own_tok = load(tok_in, tokb.at[me])
    own_plc = load(plc_in, plb.at[me])
    own_small = load(small_in, smb.at[f])

    class Weight:
        def __init__(self, src, buf, rows):
            self.buf, self.rows = buf, rows
            self.own = None
            mine = band(buf, f, rows)
            if src is None:
                src = mine
            else:
                self.own = load(src, mine)
            self.near = send(src, mine, {"fsdp": partner}, take(), late=False)
            landed = {d: take() for d in (1, 2, 3)}
            self.far = {d: remote(src, mine, {"fsdp": z_to[d]}, landed[d]) for d in (1, 2, 3)}
            self.far[2].start()
            when(j != J - 1, self.far[1].start)
            when(j != 0, self.far[3].start)
            part = band(buf, z_from[2], rows)
            self.down = remote(part, part, {"fsdp": k}, landed[1])
            self.up = remote(part, part, {"fsdp": 2 * (J - 1) + k}, landed[3])
            self.relayed = []

        def hop(self):
            self.far[2].wait_recv()
            when(j == 1, self.down.start)
            when(j == J - 2, self.up.start)

        def relay(self):
            for d in (2, 1, 3):
                if d != 2:
                    self.far[d].wait_recv()
                part = band(self.buf, z_from[d], self.rows)
                self.relayed.append(send(part, part, {"fsdp": partner}, take(), late=False))

        def finish(self):
            if self.own is not None:
                self.own.wait()
            self.near.wait_recv()
            for copy in self.relayed:
                copy.wait_recv()

        def drain(self):
            for copy in [self.near, self.far[2]] + self.relayed:
                copy.wait_send()
            when(j != J - 1, self.far[1].wait_send)
            when(j != 0, self.far[3].wait_send)
            when(j == 1, self.down.wait_send)
            when(j == J - 2, self.up.wait_send)

    def cut_columns(target, lines):
        for m in range(n):

            @pl.when(me == m)
            def _():
                target[rows_of(f, R), :] = lane_pad(
                    jnp.concatenate(lines(m), axis=1), target.shape[1]
                )

    small_copies = [
        send(small_in, smb.at[f], {"fsdp": (f + o) % F}, take()) for o in range(1, F)
    ]
    for copy in raw_q:
        copy.wait()
    cut_columns(wqc, lambda m: [d24[t, :, m * hw : (m + 1) * hw] for t in range(3)])
    weight_q = Weight(None, wqc, R)
    for copy in raw_1:
        copy.wait()
    cut_columns(
        w1,
        lambda m: [
            d14[b * n * R // P1, :, b * n * R % P1 + m * R : b * n * R % P1 + (m + 1) * R]
            for b in range(F)
        ],
    )

    own_small.wait()
    for copy in small_copies:
        copy.wait_recv()
    for row in range(7):
        vec[row : row + 1, :] = jnp.concatenate(
            [smb[s, row : row + 1, :R] for s in range(F)], axis=1
        )
    groups = 3 * D // R // 3
    heads = []
    for t in range(3):
        start = t * groups + me * (hw // R)
        line = jnp.concatenate(
            [
                smb[(start + b) // 3, pl.ds(7 + (start + b) % 3, 1), :][:, :R]
                for b in range(hw // R)
            ],
            axis=1,
        )
        for h in range(hl):
            heads.append(lane_pad(line[:, h * HD : (h + 1) * HD], W))
    bqkv[...] = jnp.broadcast_to(jnp.concatenate(heads, axis=1), bqkv.shape)

    def vector(row):
        return vec[row : row + 1, :]

    def rows_of_block(i, rows):
        return pl.ds(pl.multiple_of(i * T + rows.start, strip), strip)

    def norm_one(i):
        def body(rows):
            normed, _ = moments(tokb[i, rows, :].astype(F32))
            ain[rows_of_block(i, rows), :] = (normed * vector(0) + vector(1)).astype(BF)

        strips(T, strip, body)

    own_tok.wait()
    norm_one(me)
    tok.relay()
    weight_q.hop()
    weight_p = Weight(wp_in, wp, R)
    weight_1 = Weight(None, w1, R)
    own_cot = load(cot_in, cotb.at[me])
    cot = Spread(cot_in, rows_in(cotb), T)
    norm_one(near_x)
    norm_one(near_y)

    own_plc.wait()
    for copy in plc_copies:
        copy.wait_recv()

    def table(i, carry):
        rows = rows_of(i, T)
        turned = jnp.transpose(plb[i], (1, 0))
        lse[rows, hl : hl + 8] = turned
        angle = turned[:, 1:2] * wave_in[0:1, :] + turned[:, 2:3] * wave_in[1:2, :]
        cosb[rows, :] = jnp.cos(angle)
        sinb[rows, :] = jnp.sin(angle) * wave_in[2:3, :]
        return carry

    lax.fori_loop(0, n, table, 0)
    lane = lax.broadcasted_iota(jnp.int32, (1, W), 1)
    low_half = lane < HD // 2

    def swap(value):
        return jnp.where(
            low_half, pltpu.roll(value, W - HD // 2, 1), pltpu.roll(value, HD // 2, 1)
        )

    tok.finish()
    norm_one(across)

    weight_q.relay()
    weight_q.finish()

    def spread_heads(rows):
        line = wqc[rows, :]
        for h in range(3 * hl):
            wq[rows, h * W : (h + 1) * W] = lane_pad(line[:, h * HD : (h + 1) * HD], W)

    strips(D, R, spread_heads)

    def project(i, carry):
        rows = rows_of(i, T)
        line = ain[rows, :]
        cosine = cosb[rows, :]
        sine = sinb[rows, :]
        for t in range(3):
            part = mm(line, wq[:, t * QW : (t + 1) * QW]) + bqkv[0:1, t * QW : (t + 1) * QW]
            for h in range(hl):
                u = part[:, h * W : (h + 1) * W]
                if t < 2:
                    u = u * cosine + swap(u) * sine
                qkv[rows, t * QW + h * W : t * QW + (h + 1) * W] = u.astype(BF)
        return carry

    lax.fori_loop(0, n, project, 0)

    def masked(scores, i):
        ids = jnp.concatenate([plb[b, 3:4, :] for b in range(n)], axis=1)
        own_ids = lse[rows_of(i, T), hl + 3 : hl + 4]
        return jnp.where(own_ids == ids, scores * scale, MASKED)

    mix_send, mix_recv = take(n * (n - 1)), take(n * (n - 1))

    def mix_copy(i, o, peer, source):
        return pltpu.make_async_remote_copy(
            src_ref=mixc.at[source, i],
            dst_ref=mixc.at[source, i],
            send_sem=sems.at[mix_send + i * (n - 1) + o - 1],
            recv_sem=sems.at[mix_recv + i * (n - 1) + o - 1],
            device_id={"seq": peer},
            device_id_type=MESH,
        )

    def attend_block(i, carry):
        rows = rows_of(i, T)
        outs = []
        logs = lse[rows, :]
        for h in range(hl):
            q = qkv[rows, h * W : (h + 1) * W]
            kk = qkv[:, QW + h * W : QW + (h + 1) * W]
            v = qkv[:, 2 * QW + h * W : 2 * QW + (h + 1) * W]
            s = masked(mm_nt(q, kk), i)
            top = jnp.max(s, axis=-1, keepdims=True)
            p = jnp.exp(s - top)
            total = jnp.sum(p, axis=-1, keepdims=True)
            outs.append((mm(p.astype(BF), v) / total)[:, :HD].astype(BF))
            logs = jnp.where(lane == h, top + jnp.log(total), logs)
        lse[rows, :] = logs
        mixc[me, i] = lane_pad(jnp.concatenate(outs, axis=1), HP)
        for o in range(1, n):
            mix_copy(i, o, seq_to[o], me).start()
        return carry

    weight_p.hop()
    weight_2 = Weight(w2_in.at[rows_of(me, R)], w2, R)
    cot.relay()
    lax.fori_loop(0, n // 2, attend_block, 0)
    weight_p.relay()
    lax.fori_loop(n // 2, n, attend_block, 0)
    weight_1.hop()
    weight_p.finish()
    tok.drain()

    def branch(i, carry):
        rows = rows_of(i, T)
        for o in range(1, n):
            mix_copy(i, o, seq_to[o], seq_from[o]).wait_recv()
        mix[rows, :] = jnp.concatenate([mixc[c, i][:, :hw] for c in range(n)], axis=1)
        gmd[...] = mm(mix[rows, :], wp[...])

        def body(part):
            whole = rows_of_block(i, part)
            value = gmd[part, :] + tokb[i, part, :].astype(F32) + vector(2)

            @pl.when(i == me)
            def _():
                mid[part, :] = value

            normed, _ = moments(value)
            mlp[whole, :] = (normed * vector(3) + vector(4)).astype(BF)

        strips(T, strip, body)
        return carry

    lax.fori_loop(0, n, branch, 0)

    weight_2.hop()
    weight_1.relay()
    weight_1.finish()

    def up(i, carry):
        rows = rows_of(i, T)
        before = mm(mlp[rows, :], w1[...]) + vector(6)
        gate = jax.nn.sigmoid(1.702 * before)
        act[rows, :] = (before * gate).astype(BF)
        dge[rows, :] = (gate + 1.702 * before * gate * (1.0 - gate)).astype(BF)
        return carry

    lax.fori_loop(0, n, up, 0)

    own_cot.wait()
    cot.finish()
    cot.drain()
    weight_2.relay()
    weight_2.finish()

    half = T // 2

    class Scatter:
        def __init__(self, stage, landing, slots):
            self.stage, self.landing = stage, landing
            slot_x, slot_y, pass_x, pass_y = slots
            to_x, to_y = {"seq": near_x}, {"seq": near_y}
            self.pass_a = self.make(across, 0, pass_x, to_x)
            self.pass_b = self.make(across, 1, pass_y, to_y)
            self.last_a = self.make(near_x, 0, slot_x, to_x)
            self.last_b = self.make(near_y, 1, slot_y, to_y)
            self.sum_a = self.make(near_y, 0, slot_y, to_y)
            self.sum_b = self.make(near_x, 1, slot_x, to_x)

        def make(self, block, part, slot, where):
            return remote(
                self.stage.at[self.rows(block, part)],
                self.landing.at[slot, part * half : (part + 1) * half],
                where,
                take(),
            )

        def rows(self, block, part):
            return pl.ds(pl.multiple_of(block * T + part * half, half), half)

        def start(self, t):
            @pl.when(t == 0)
            def _():
                self.pass_a.start()
                self.pass_b.start()

            when(t == 1, self.last_a.start)
            when(t == 2, self.last_b.start)

        def relay(self, slot):
            for part, into, out, block in (
                (0, self.pass_a, self.sum_a, near_y),
                (1, self.pass_b, self.sum_b, near_x),
            ):
                into.wait_recv()

                def body(rows):
                    at = pl.ds(pl.multiple_of(block * T + part * half + rows.start, strip), strip)
                    there = pl.ds(pl.multiple_of(part * half + rows.start, strip), strip)
                    self.stage[at, :] = (
                        self.stage[at, :].astype(F32) + self.landing[slot, there, :].astype(F32)
                    ).astype(BF)

                strips(half, strip, body)
                out.start()

        def wait_recv(self):
            for copy in (self.last_a, self.last_b, self.sum_a, self.sum_b):
                copy.wait_recv()

        def wait_send(self):
            for copy in (
                self.pass_a,
                self.pass_b,
                self.last_a,
                self.last_b,
                self.sum_a,
                self.sum_b,
            ):
                copy.wait_send()

    def block_at(t):
        return peer(((t + 2) % 3 + 1) * (1 - t // 3))

    for i in range(n):
        for o in range(1, n):
            mix_copy(i, o, seq_to[o], me).wait_send()
    scatter_mlp = Scatter(snd, rsr, (0, 1, 2, 2))

    def back(t, carry):
        i = block_at(t)
        rows = rows_of(i, T)
        grad = (mm_nt(cotb[i], w2[...]) * dge[rows, :].astype(F32)).astype(BF)
        dge[rows, :] = grad
        snd[rows, :] = mm_nt(grad, w1[...]).astype(BF)
        scatter_mlp.start(t)
        return carry

    lax.fori_loop(0, n, back, 0)

    class Gradient:
        def __init__(self, grad, other, far, extra, result, lo, width):
            self.grad, self.other, self.far, self.extra = grad, other, far, extra
            self.result, self.lanes = result, slice(lo, lo + width)

        def of(self, index):
            return self.grad.at[rows_of(index, R), self.lanes]

        def exchange(self):
            self.near = [
                send(
                    self.of(2 * c + 1 - k),
                    self.other.at[c, :, self.lanes],
                    {"fsdp": partner},
                    take(),
                )
                for c in range(J)
            ]

        def add_near(self):
            for copy in self.near:
                copy.wait_recv()
            lanes = self.lanes

            def chip(c, carry):
                rows = rows_of(2 * c + k, R)
                self.grad[rows, lanes] = (
                    self.grad[rows, lanes].astype(F32) + self.other[c, :, lanes].astype(F32)
                ).astype(BF)
                return carry

            lax.fori_loop(0, J, chip, 0)
            self.pass_on = remote(
                self.of(2 * (J - 1 - j) + k),
                self.extra.at[:, lanes],
                {"fsdp": 2 * (1 + j // (J - 1)) + k},
                take(),
            )
            self.across = {
                d: remote(
                    self.of(z_to[d]), self.far.at[d - 1, :, lanes], {"fsdp": z_to[d]}, take()
                )
                for d in (1, 2, 3)
            }
            when(edge, self.pass_on.start)
            when(edge, self.across[2].start)
            when(j != J - 1, self.across[1].start)
            when(j != 0, self.across[3].start)

        def hop(self):
            @pl.when(middle)
            def _():
                self.pass_on.wait_recv()
                rows = rows_of(z_to[2], R)
                self.grad[rows, self.lanes] = (
                    self.grad[rows, self.lanes].astype(F32)
                    + self.extra[:, self.lanes].astype(F32)
                ).astype(BF)
                self.across[2].start()

        def add_far(self):
            def total_of(steps):
                def action():
                    for d in steps:
                        self.across[d].wait_recv()
                    total = self.grad[rows_of(f, R), self.lanes].astype(F32)
                    for d in steps:
                        total = total + self.far[d - 1, :, self.lanes].astype(F32)
                    self.other[0, :, self.lanes] = total.astype(BF)

                return action

            when(j == 0, total_of((2, 3)))
            when(middle, total_of((1, 2, 3)))
            when(j == J - 1, total_of((1, 2)))

        def share(self):
            mine = self.other.at[0, :, self.lanes]
            self.keep = load(mine, self.result.at[me, :, self.lanes])
            self.spread = Spread(
                mine, lambda index, lo, hi: self.result.at[index, lo:hi, self.lanes], R
            )

        def relay(self):
            self.spread.relay()

        def finish(self):
            self.keep.wait()
            self.spread.finish()
            self.spread.drain()
            self.across[2].wait_send()
            when(j != J - 1, self.across[1].wait_send)
            when(j != 0, self.across[3].wait_send)
            when(edge, self.pass_on.wait_send)

    CH = CQ // 2
    grad_up = Gradient(w1, d14, z13, h1, r1_ref, 0, P1)
    grad_down = Gradient(w2, d24, z23, h2, r2_ref, 0, D)
    grad_proj = Gradient(gp, dp4, zp3, hp, rp_ref, 0, HP)
    grad_qkv = [Gradient(wqc, dq4, zq3, hq, rq_ref, b * CH, CH) for b in range(2)]

    weight_1.drain()
    weight_2.drain()
    weight_q.drain()

    def up_grad(t, carry):
        w1[rows_of(t, tile), :] = mm_tn(mlp[:, rows_of(t, tile)], dge[...]).astype(BF)
        return carry

    lax.fori_loop(0, D // tile, up_grad, 0)
    grad_up.exchange()
    scatter_mlp.relay(2)

    def down(i, carry):
        rows = rows_of(i, T)
        mlp[rows, :] = mm(act[rows, :], w2[...]).astype(BF)
        return carry

    lax.fori_loop(0, n, down, 0)
    grad_up.add_near()

    def down_grad(t, carry):
        lanes = rows_of(t, tile)
        total = mm_tn(act[0:T, lanes], cotb[0])
        for b in range(1, n):
            total = total + mm_tn(act[b * T : (b + 1) * T, lanes], cotb[b])
        w2[lanes, :] = total.astype(BF)
        return carry

    lax.fori_loop(0, P1 // tile, down_grad, 0)
    grad_down.exchange()

    smg[...] = jnp.zeros(smg.shape, F32)
    scatter_mlp.wait_recv()

    def gather_parts(part):
        whole = rows_of_block(me, part)
        total = snd[whole, :].astype(F32)
        return total + rsr[0, part, :].astype(F32) + rsr[1, part, :].astype(F32)

    def add_sum(row, value):
        smg[row : row + 1, :] = smg[row : row + 1, :] + jnp.sum(value, axis=0, keepdims=True)

    def norm_two_back(part):
        upstream = cotb[me, part, :].astype(F32)
        grad = gather_parts(part)
        normed, factor = moments(mid[part, :])
        scaled = grad * vector(3)
        value = upstream + factor * (
            scaled
            - jnp.mean(scaled, axis=-1, keepdims=True)
            - normed * jnp.mean(scaled * normed, axis=-1, keepdims=True)
        )
        gmd[part, :] = value
        low = value.astype(BF)
        snd[rows_of_block(me, part), :] = low
        add_sum(2, low.astype(F32))
        add_sum(3, grad * normed)
        add_sum(4, grad)
        add_sum(5, upstream)

    strips(T, strip, norm_two_back)
    own_rows = rows_of(me, T)
    low_branch = snd[own_rows, :]
    grad_mixed = mm_nt(low_branch, wp[...]).astype(BF)
    for c in range(n):
        mixc[0, c] = lane_pad(grad_mixed[:, c * hw : (c + 1) * hw], HP)
        mixc[2, c] = lane_pad(low_branch[:, c * hw : (c + 1) * hw], HP)
    head_copies = [
        send(mixc.at[0, seq_to[o]], mixc.at[1, me], {"seq": seq_to[o]}, take()) for o in range(1, n)
    ]
    branch_copies = [
        send(mixc.at[2, seq_to[o]], mixc.at[3, me], {"seq": seq_to[o]}, take()) for o in range(1, n)
    ]
    mixc[1, me] = mixc[0, me]
    mixc[3, me] = mixc[2, me]

    grad_down.add_near()
    grad_up.hop()

    for copy in head_copies:
        copy.wait_recv()
    scatter_out = Scatter(mlp, tokb, (me, me, near_y, near_x))
    for t in range(n - 1):
        scatter_out.start(t)

    def proj_grad(t, carry):
        lanes = rows_of(t, tile)
        total = mm_tn(mix[0:T, lanes], mixc[3, 0])
        for b in range(1, n):
            total = total + mm_tn(mix[b * T : (b + 1) * T, lanes], mixc[3, b])
        gp[lanes, :] = total.astype(BF)
        return carry

    def qkv_grad(half):
        pair = hl // 2 * W

        def body(t, carry):
            rows = rows_of(t, tile)
            parts = []
            for third in range(3):
                at = third * QW + half * pair
                total = mm_tn(ain[:, rows], qkv[:, at : at + pair])
                parts += [total[:, h * W : h * W + HD].astype(BF) for h in range(hl // 2)]
            wqc[rows, half * CH : (half + 1) * CH] = lane_pad(jnp.concatenate(parts, axis=1), CH)
            return carry

        lax.fori_loop(0, D // tile, body, 0)
        grad_qkv[half].exchange()

    def between(h):
        if h == 0:
            grad_down.hop()
            for copy in branch_copies:
                copy.wait_recv()
            lax.fori_loop(0, D // tile, proj_grad, 0)
            grad_proj.exchange()
            scatter_out.relay(across)
        if h == 1:
            grad_proj.add_near()
            qkv_grad(0)
            grad_up.add_far()
        if h == 2:
            grad_proj.hop()
            grad_qkv[0].add_near()
        if h == 3:
            grad_qkv[0].hop()
            grad_down.add_far()

    for h in range(hl):
        q_at = slice(h * W, (h + 1) * W)
        k_at = slice(QW + h * W, QW + (h + 1) * W)
        v_at = slice(2 * QW + h * W, 2 * QW + (h + 1) * W)
        dkv[...] = jnp.zeros(dkv.shape, F32)

        def attend_back_block(i, carry):
            rows = rows_of(i, T)
            q = qkv[rows, q_at]
            kk = qkv[:, k_at]
            g = lane_pad(mixc[1, i][:, h * HD : (h + 1) * HD], W)
            p = jnp.exp(masked(mm_nt(q, kk), i) - lse[rows, h : h + 1])
            dp = mm_nt(g, qkv[:, v_at])
            dkv[:, W:] = dkv[:, W:] + mm_tn(p.astype(BF), g)
            centre = jnp.sum(p * dp, axis=-1, keepdims=True)
            ds = (p * (dp - centre)).astype(BF)
            dq = (mm(ds, kk) * scale).astype(BF).astype(F32)
            dkv[:, :W] = dkv[:, :W] + mm_tn(ds, q)
            qkv[rows, q_at] = (dq * cosb[rows, :] - swap(dq) * sinb[rows, :]).astype(BF)
            return carry

        lax.fori_loop(0, n, attend_back_block, 0)

        def turn_back(i, carry):
            rows = rows_of(i, T)
            dk = (dkv[rows, :W] * scale).astype(BF).astype(F32)
            qkv[rows, k_at] = (dk * cosb[rows, :] - swap(dk) * sinb[rows, :]).astype(BF)
            qkv[rows, v_at] = dkv[rows, W:].astype(BF)
            return carry

        lax.fori_loop(0, n, turn_back, 0)
        between(h)

    scatter_mlp.wait_send()
    scatter_attn = Scatter(snd, rsr, (0, 1, 2, 2))

    def attn_back(t, carry):
        i = block_at(t)
        rows = rows_of(i, T)
        snd[rows, :] = mm_nt(qkv[rows, :], wq[...]).astype(BF)
        scatter_attn.start(t)
        return carry

    lax.fori_loop(0, n, attn_back, 0)

    qkv_grad(1)
    scatter_attn.relay(2)
    grad_up.share()
    grad_down.share()
    grad_proj.add_far()
    grad_proj.share()

    def bias_sums(part):
        smg[6:7, :] = smg[6:7, :] + jnp.sum(dge[part, :].astype(F32), axis=0, keepdims=True)
        line = jnp.sum(qkv[part, :].astype(F32), axis=0, keepdims=True)
        line = lane_pad(
            jnp.concatenate([line[:, h * W : h * W + HD] for h in range(3 * hl)], axis=1), D
        )
        smg[7:8, :] = smg[7:8, :] + line

    grad_qkv[1].add_near()
    strips(L, 64, bias_sums)
    grad_qkv[0].add_far()
    grad_qkv[0].share()
    grad_qkv[1].hop()

    scatter_attn.wait_recv()

    def norm_one_back(part):
        grad = gather_parts(part)
        normed, factor = moments(tokb[me, part, :].astype(F32))
        scaled = grad * vector(0)
        gmd[part, :] = gmd[part, :] + factor * (
            scaled
            - jnp.mean(scaled, axis=-1, keepdims=True)
            - normed * jnp.mean(scaled * normed, axis=-1, keepdims=True)
        )
        add_sum(0, grad * normed)
        add_sum(1, grad)

    strips(T, strip, norm_one_back)
    tokens_out = load(gmd, tgrad_ref)
    sum_copies = [
        send(smg, sg8.at[f], {"fsdp": (f + o) % F}, take()) for o in range(1, F)
    ]
    sg8[f] = smg[...]
    grad_up.relay()
    grad_down.relay()
    grad_qkv[1].add_far()
    grad_qkv[1].share()

    scatter_out.wait_recv()

    def write_out(part):
        whole = rows_of_block(me, part)
        total = mid[part, :] + mlp[whole, :].astype(F32) + vector(5)
        for slot in (near_x, near_y):
            total = total + tokb[slot, part, :].astype(F32)
        bias_rows = rows_of_block(me, part)
        ain[bias_rows, :] = total.astype(BF)

    strips(T, strip, write_out)
    block_out = load(band(ain, me, T), out_ref)

    for copy in sum_copies:
        copy.wait_recv()
    total = sg8[0]
    for s in range(1, F):
        total = total + sg8[s]
    plain = lax.broadcasted_iota(jnp.int32, total.shape, 0)
    vec[...] = jnp.where(plain < 8, total, 0.0)
    sums_keep = load(vec, sums_ref.at[me])
    sums_share = [
        send(vec, sums_ref.at[me], {"seq": seq_to[o]}, take()) for o in range(1, n)
    ]

    grads = [grad_up, grad_down, grad_proj] + grad_qkv
    for item in grads[2:]:
        item.relay()
    for item in grads:
        item.finish()
    for copy in sums_share:
        copy.wait_recv()
    sums_keep.wait()
    tokens_out.wait()
    block_out.wait()
    weight_p.drain()
    scatter_attn.wait_send()
    scatter_out.wait_send()
    for copy in leftover:
        copy.wait_send()
    assert used["remote"] <= sems.shape[0] and used["local"] <= local_sems.shape[0], used


def unpack_kernel(
    dims,
    block_in,
    tokens_in,
    rq_in,
    rp_in,
    r1_in,
    r2_in,
    sums_in,
    block_ref,
    tokens_ref,
    qkv_ref,
    proj_ref,
    up_ref,
    down_ref,
    vec_ref,
    block,
    tokens,
    rq,
    rp,
    r1,
    r2,
    sums,
    stage,
    vec,
    in_sems,
    out_sems,
):
    n, T, L, D, F, R, hl, P1, CQ, HP = dims
    hw = hl * HD
    f = lax.axis_index("fsdp")
    loads = []
    for src, dst in (
        (r2_in, r2),
        (r1_in, r1),
        (rq_in, rq),
        (rp_in, rp),
        (tokens_in, tokens),
        (block_in, block),
        (sums_in, sums),
    ):
        copy = pltpu.make_async_copy(src, dst, in_sems.at[len(loads)])
        copy.start()
        loads.append(copy)
    stores = []

    def store(src, dst):
        copy = pltpu.make_async_copy(src, dst, out_sems.at[len(stores)])
        copy.start()
        stores.append(copy)

    loads[0].wait()
    for c in range(n):
        stage[c] = r2[c].astype(F32)
        store(stage.at[c], down_ref.at[c * R : (c + 1) * R])
    loads[1].wait()
    width = n * R
    for c in range(n):
        blocks = range(c * P1 // width, (c + 1) * P1 // width)
        stage[n + c] = jnp.concatenate(
            [r1[m, :, b * R : (b + 1) * R] for b in blocks for m in range(n)], axis=1
        ).astype(F32)
        store(stage.at[n + c], up_ref.at[:, c * P1 : (c + 1) * P1])
    loads[2].wait()
    for t in range(3):
        stage[2 * n + t] = jnp.concatenate(
            [
                rq[m, :, b * CQ // 2 + t * hw // 2 : b * CQ // 2 + (t + 1) * hw // 2]
                for m in range(n)
                for b in range(2)
            ],
            axis=1,
        ).astype(F32)
        store(stage.at[2 * n + t], qkv_ref.at[:, t * D : (t + 1) * D])
    loads[3].wait()
    stage[2 * n + 3] = jnp.concatenate([rp[m, :, :hw] for m in range(n)], axis=1).astype(F32)
    store(stage.at[2 * n + 3], proj_ref)
    loads[4].wait()
    store(tokens, tokens_ref)
    loads[5].wait()
    store(block, block_ref)
    loads[6].wait()
    per_part = hw // R
    for s in range(F):

        @pl.when(f == s)
        def _():
            own = slice(s * R, (s + 1) * R)
            total = sums[0, 0:6, own]
            for m in range(1, n):
                total = total + sums[m, 0:6, own]
            lines = [total] + [sums[m, 6:7, own] for m in range(n)]
            for b in range(3):
                spot = 3 * s + b
                third, rest = spot // (n * per_part), spot % (n * per_part)
                at = third * hw + rest % per_part * R
                lines.append(sums[rest // per_part, 7:8, at : at + R])
            lines.append(jnp.zeros((16 - 9 - n, R), F32))
            vec[...] = jnp.concatenate(lines, axis=0)

    store(vec, vec_ref)
    for copy in stores:
        copy.wait()


def round_up(value, step):
    return -(-value // step) * step


def shards_kernel(
    tokens,
    picture_ids,
    patch_rows,
    patch_cols,
    norm1_gain,
    norm1_bias,
    qkv_weight,
    qkv_bias,
    proj_weight,
    proj_bias,
    norm2_gain,
    norm2_bias,
    fc1_weight,
    fc1_bias,
    fc2_weight,
    fc2_bias,
    cotangent,
):
    n = lax.axis_size("seq")
    me = lax.axis_index("seq")
    F = lax.axis_size("fsdp")
    f = lax.axis_index("fsdp")
    _, T, D = tokens.shape
    L = n * T
    hl = D // HD // n
    hw = hl * HD
    R = D // F
    hidden = fc1_weight.shape[1]
    P1 = hidden // n
    part = hidden // (F * n)
    CQ = round_up(3 * hw, 128)
    HP = round_up(hw, 128)
    J = F // 2
    W = 128

    def pick(value, axis):
        return lax.dynamic_index_in_dim(value, me, axis, keepdims=False)

    lines = (
        norm1_gain,
        norm1_bias,
        proj_bias,
        norm2_gain,
        norm2_bias,
        fc2_bias,
        pick(fc1_bias.reshape(n, part), 0),
        qkv_bias,
    )
    small = jnp.concatenate([item.astype(F32).reshape(-1, R) for item in lines])
    small = jnp.pad(small, ((0, 6), (0, 0)))
    spot = jnp.arange(T, dtype=jnp.int32) + me * T
    ids = jnp.where(picture_ids[0] >= 0, picture_ids[0], -1 - spot)
    places = jnp.stack([picture_ids[0], patch_rows[0], patch_cols[0], ids]).astype(F32)
    places = jnp.pad(places, ((0, 4), (0, 0)))
    quarter = HD // 4
    inverse = 10000.0 ** (-np.arange(quarter) / quarter)
    wave = np.zeros((8, W), np.float32)
    for c in range(2):
        wave[0, 2 * c * quarter : (2 * c + 1) * quarter] = inverse
        wave[1, (2 * c + 1) * quarter : (2 * c + 2) * quarter] = inverse
    wave[2] = np.where(np.arange(W) < HD // 2, -1.0, 1.0)
    dims = (n, T, L, D, F, R, hl, P1, CQ, HP)
    anywhere = pl.BlockSpec(memory_space=pl.ANY)
    local = pl.BlockSpec(memory_space=pltpu.VMEM)

    def vmem(shape, dtype=BF):
        return pltpu.VMEM(shape, dtype)

    scratch = [
        vmem((n, T, D)),
        vmem((L, D)),
        vmem((n, T, D)),
        vmem((n, 8, T), F32),
        vmem((F, 16, R), F32),
        vmem((8, D), F32),
        vmem((8, 3 * hl * W), F32),
        vmem((L, W), F32),
        vmem((L, W), F32),
        vmem((D, CQ)),
        vmem((D, 3 * hl * W)),
        vmem((D, D)),
        vmem((D, P1)),
        vmem((P1, D)),
        vmem((L, 3 * hl * W)),
        vmem((L, W), F32),
        vmem((n, n, T, HP)),
        vmem((L, D)),
        vmem((T, D), F32),
        vmem((L, D)),
        vmem((L, P1)),
        vmem((L, P1)),
        vmem((L, D)),
        vmem((n - 1, T, D)),
        vmem((T, D), F32),
        vmem((D, HP)),
        vmem((J, R, CQ)),
        vmem((J, R, HP)),
        vmem((J, R, P1)),
        vmem((J, R, D)),
        vmem((J - 1, R, CQ)),
        vmem((J - 1, R, HP)),
        vmem((J - 1, R, P1)),
        vmem((J - 1, R, D)),
        vmem((L, 2 * W), F32),
        vmem((8, D), F32),
        vmem((F, 8, D), F32),
        vmem((R, CQ)),
        vmem((R, HP)),
        vmem((R, P1)),
        vmem((R, D)),
        pltpu.SemaphoreType.DMA((448,)),
        pltpu.SemaphoreType.DMA((24,)),
    ]
    shapes = (
        jax.ShapeDtypeStruct((T, D), BF),
        jax.ShapeDtypeStruct((T, D), F32),
        jax.ShapeDtypeStruct((n, R, CQ), BF),
        jax.ShapeDtypeStruct((n, R, HP), BF),
        jax.ShapeDtypeStruct((n, R, P1), BF),
        jax.ShapeDtypeStruct((n, R, D), BF),
        jax.ShapeDtypeStruct((n, 8, D), F32),
    )
    block_out, tokens_grad, rq, rp, r1, r2, sums = pl.pallas_call(
        functools.partial(block_kernel, dims),
        out_shape=shapes,
        in_specs=[anywhere] * 4 + [local] + [anywhere] * 4,
        out_specs=[anywhere] * 7,
        scratch_shapes=scratch,
        compiler_params=pltpu.CompilerParams(
            collective_id=0, has_side_effects=True, vmem_limit_bytes=67043328
        ),
    )(tokens[0], cotangent[0], places, small, wave, qkv_weight, proj_weight, fc1_weight, fc2_weight)
    stored = (
        jax.ShapeDtypeStruct((T, D), BF),
        jax.ShapeDtypeStruct((T, D), F32),
        jax.ShapeDtypeStruct((R, 3 * D), F32),
        jax.ShapeDtypeStruct((R, D), F32),
        jax.ShapeDtypeStruct((R, hidden), F32),
        jax.ShapeDtypeStruct((n * R, D), F32),
        jax.ShapeDtypeStruct((16, R), F32),
    )
    block_out, tokens_grad, full_qkv, full_proj, full_up, full_down, sums = pl.pallas_call(
        functools.partial(unpack_kernel, dims),
        out_shape=stored,
        in_specs=[anywhere] * 7,
        out_specs=[anywhere] * 7,
        scratch_shapes=[
            vmem((T, D)),
            vmem((T, D), F32),
            vmem((n, R, CQ)),
            vmem((n, R, HP)),
            vmem((n, R, P1)),
            vmem((n, R, D)),
            vmem((n, 8, D), F32),
            vmem((4 + 2 * n, R, D), F32),
            vmem((16, R), F32),
            pltpu.SemaphoreType.DMA((7,)),
            pltpu.SemaphoreType.DMA((7 + 2 * n,)),
        ],
        compiler_params=pltpu.CompilerParams(vmem_limit_bytes=67043328),
    )(block_out, tokens_grad, rq, rp, r1, r2, sums)
    return (
        block_out[None],
        tokens_grad[None],
        sums[0],
        sums[1],
        full_qkv,
        sums[6 + n : 9 + n].reshape(3 * R),
        full_proj,
        sums[2],
        sums[3],
        sums[4],
        full_up,
        sums[6 : 6 + n].reshape(n * R),
        full_down,
        sums[5],
    )


def fits_kernel(mesh):
    return dict(mesh.shape) == {"seq": 4, "fsdp": 8}


def shards_plain(
    tokens,
    picture_ids,
    patch_rows,
    patch_cols,
    norm1_gain,
    norm1_bias,
    qkv_weight,
    qkv_bias,
    proj_weight,
    proj_bias,
    norm2_gain,
    norm2_bias,
    fc1_weight,
    fc1_bias,
    fc2_weight,
    fc2_bias,
    cotangent,
):
    n = lax.axis_size("seq")
    me = lax.axis_index("seq")
    stores = lax.axis_size("fsdp")
    _, own, width = tokens.shape
    heads = width // HD
    local_heads = heads // n
    hw = local_heads * HD
    rows = qkv_weight.shape[0]
    hidden = fc1_weight.shape[1]
    part = hidden // (stores * n)

    def pick(value, axis):
        return lax.dynamic_index_in_dim(value, me, axis, keepdims=False)

    own_qkv = pick(qkv_weight.reshape(rows, 3, n, hw), 2).reshape(rows, 3 * hw)
    own_up = pick(fc1_weight.reshape(rows, stores, n, part), 2).reshape(rows, stores * part)
    own_down = pick(fc2_weight.reshape(n, part, width), 0)
    small = (norm1_gain, norm1_bias, proj_bias, norm2_gain, norm2_bias, fc2_bias, qkv_bias, fc1_bias)
    sizes = [item.shape[0] for item in small]
    packed = gather(jnp.concatenate(small)[None], "fsdp")
    weight_qkv = gather(own_qkv, "fsdp")
    weight_proj = gather(proj_weight, "fsdp")
    weight_up = gather(own_up, "fsdp")
    weight_down = gather(own_down, "fsdp")
    params = []
    start = 0
    for size in sizes:
        params.append(packed[:, start : start + size].reshape(-1).astype(F32))
        start += size
    gain_one, bias_one, bias_proj, gain_two, bias_two, bias_down, bias_qkv, bias_up = params
    bias_qkv = pick(bias_qkv.reshape(3, n, hw), 1).reshape(3 * hw)
    bias_up = pick(bias_up.reshape(stores, n, part), 1).reshape(stores * part)

    places = jnp.stack([picture_ids[0], patch_rows[0], patch_cols[0]])
    places = gather(places, "seq", 1)
    picture = places[0]
    all_tokens = gather(tokens[0], "seq").astype(F32)
    upstream = gather(cotangent[0], "seq")
    length = all_tokens.shape[0]

    def mine(value):
        return lax.dynamic_slice_in_dim(value, me * own, own, 0)

    normed_one, factor_one = standardize(all_tokens)
    attn_input = (normed_one * gain_one + bias_one).astype(BF)
    projected = (dot(attn_input, weight_qkv) + bias_qkv).reshape(length, 3, local_heads, HD)
    cosine, sine = rotary_tables(places[1], places[2], HD)
    queries = rotate(projected[:, 0], cosine, sine).astype(BF)
    keys = rotate(projected[:, 1], cosine, sine).astype(BF)
    values = projected[:, 2].astype(BF)
    mixed_own, log_total = attend(queries, keys, values, picture)
    mixed = gather(mixed_own.reshape(length, hw), "seq", 1)
    middle = all_tokens + dot(mixed, weight_proj) + bias_proj
    normed_two, factor_two = standardize(middle)
    mlp_input = (normed_two * gain_two + bias_two).astype(BF)
    before = dot(mlp_input, weight_up) + bias_up
    gate = jax.nn.sigmoid(1.702 * before)
    activated = (before * gate).astype(BF)
    out_part = dot(activated, weight_down).astype(BF)
    block_out = (mine(middle) + scatter_sum(out_part, "seq").astype(F32) + bias_down).astype(BF)

    grad_down = scatter_sum(rows_term(activated, upstream).astype(BF), "fsdp")
    grad_activated = contract_back(upstream, weight_down)
    grad_before = (grad_activated * (gate + 1.702 * before * gate * (1.0 - gate))).astype(BF)
    grad_up = scatter_sum(rows_term(mlp_input, grad_before).astype(BF), "fsdp")
    grad_mlp_input = scatter_sum(contract_back(grad_before, weight_up).astype(BF), "seq").astype(F32)
    own_upstream = cotangent[0].astype(F32)
    own_two = mine(normed_two)
    grad_middle = own_upstream + norm_back(grad_mlp_input, own_two, mine(factor_two), gain_two)
    grad_branch = grad_middle.astype(BF)
    grad_mixed = contract_back(grad_branch, weight_proj).astype(BF)
    grad_heads = lax.all_to_all(grad_mixed, "seq", split_axis=1, concat_axis=0, tiled=True)
    branch_part = lax.all_to_all(grad_branch, "seq", split_axis=1, concat_axis=0, tiled=True)
    grad_proj = scatter_sum(rows_term(mixed, branch_part).astype(BF), "fsdp")
    grad_queries, grad_keys, grad_values = attend_back(
        queries, keys, values, picture, grad_heads.reshape(length, local_heads, HD), log_total
    )
    grad_projected = jnp.stack(
        [
            unrotate(grad_queries.astype(F32), cosine, sine).astype(BF),
            unrotate(grad_keys.astype(F32), cosine, sine).astype(BF),
            grad_values,
        ],
        axis=1,
    ).reshape(length, 3 * hw)
    grad_qkv = scatter_sum(rows_term(attn_input, grad_projected).astype(BF), "fsdp")
    grad_attn_input = scatter_sum(contract_back(grad_projected, weight_qkv).astype(BF), "seq").astype(F32)
    own_one = mine(normed_one)
    tokens_grad = grad_middle + norm_back(grad_attn_input, own_one, mine(factor_one), gain_one)

    def spread(value, groups):
        empty = jnp.zeros((groups, n, value.shape[0] // groups), F32)
        return lax.dynamic_update_slice_in_dim(
            empty, value.reshape(groups, 1, -1), me, 1
        ).reshape(stores, -1)

    sums = [
        jnp.sum(grad_attn_input * own_one, axis=0).reshape(stores, -1),
        jnp.sum(grad_attn_input, axis=0).reshape(stores, -1),
        jnp.sum(grad_branch.astype(F32), axis=0).reshape(stores, -1),
        jnp.sum(grad_mlp_input * own_two, axis=0).reshape(stores, -1),
        jnp.sum(grad_mlp_input, axis=0).reshape(stores, -1),
        jnp.sum(own_upstream, axis=0).reshape(stores, -1),
        spread(jnp.sum(grad_projected.astype(F32), axis=0), 3),
        spread(jnp.sum(grad_before.astype(F32), axis=0), stores),
    ]
    summed = lax.psum(scatter_sum(jnp.concatenate(sums, axis=1), "fsdp"), "seq")[0]
    finals = []
    start = 0
    for size in sizes:
        finals.append(summed[start : start + size])
        start += size
    full_down = gather(grad_down, "seq").astype(F32)
    full_up = gather(grad_up[None], "seq").reshape(n, rows, stores, part)
    full_up = full_up.transpose(1, 2, 0, 3).reshape(rows, hidden).astype(F32)
    full_proj = gather(grad_proj, "seq", 1).astype(F32)
    full_qkv = gather(grad_qkv[None], "seq").reshape(n, rows, 3, hw)
    full_qkv = full_qkv.transpose(1, 2, 0, 3).reshape(rows, 3 * width).astype(F32)
    return (
        block_out[None],
        tokens_grad[None],
        finals[0],
        finals[1],
        full_qkv,
        finals[6],
        full_proj,
        finals[2],
        finals[3],
        finals[4],
        full_up,
        finals[7],
        full_down,
        finals[5],
    )


def solution(mesh):
    token = P("fsdp", "seq", None)
    place = P("fsdp", "seq")
    vector = P("fsdp")
    matrix = P("fsdp", None)
    in_specs = (
        token,
        place,
        place,
        place,
        vector,
        vector,
        matrix,
        vector,
        matrix,
        vector,
        vector,
        vector,
        matrix,
        vector,
        matrix,
        vector,
        token,
    )
    out_specs = (
        token,
        token,
        vector,
        vector,
        matrix,
        vector,
        matrix,
        vector,
        vector,
        vector,
        matrix,
        vector,
        matrix,
        vector,
    )
    shards = shards_kernel if fits_kernel(mesh) else shards_plain
    return jax.shard_map(shards, mesh=mesh, in_specs=in_specs, out_specs=out_specs, check_vma=False)
```

```python
import functools

import jax
import jax.numpy as jnp
import numpy as np
from jax import lax
from jax.experimental import pallas as pl
from jax.experimental.pallas import tpu as pltpu
from jax.sharding import PartitionSpec as P

HD = 80
NORM_EPSILON = 1e-06
MASKED = -1e30
BF = jnp.bfloat16
F32 = jnp.float32


def standardize(values_in):
    centre = jnp.mean(values_in, axis=-1, keepdims=True)
    shifted = values_in - centre
    factor = lax.rsqrt(jnp.mean(shifted * shifted, axis=-1, keepdims=True) + NORM_EPSILON)
    return (shifted * factor, factor)


def norm_back(grad_out, normed, factor, gain):
    scaled = grad_out * gain
    return factor * (
        scaled
        - jnp.mean(scaled, axis=-1, keepdims=True)
        - normed * jnp.mean(scaled * normed, axis=-1, keepdims=True)
    )


def rotary_tables(patch_row, patch_col, head_size):
    quarter = head_size // 4
    inverse = jnp.power(10000.0, -jnp.arange(quarter, dtype=F32) / quarter)
    half_angles = jnp.concatenate(
        [
            patch_row.astype(F32)[..., None] * inverse,
            patch_col.astype(F32)[..., None] * inverse,
        ],
        axis=-1,
    )
    angles = jnp.concatenate([half_angles, half_angles], axis=-1)
    return (jnp.cos(angles)[..., None, :], jnp.sin(angles)[..., None, :])


def rotate(values_in, cosine, sine):
    half_size = values_in.shape[-1] // 2
    turned = jnp.concatenate([-values_in[..., half_size:], values_in[..., :half_size]], axis=-1)
    return values_in * cosine + turned * sine


def unrotate(grad_in, cosine, sine):
    half_size = grad_in.shape[-1] // 2
    moved = grad_in * sine
    return grad_in * cosine + jnp.concatenate(
        [moved[..., half_size:], -moved[..., :half_size]], axis=-1
    )


def masked_scores(queries, keys, picture, factor):
    places = jnp.arange(picture.shape[0], dtype=jnp.int32)
    scores = jnp.einsum("qhd,khd->hqk", queries, keys, preferred_element_type=F32) * factor
    allowed = (picture[:, None] == picture[None, :]) & (
        (picture[None, :] >= 0) | (places[:, None] == places[None, :])
    )
    return jnp.where(allowed[None, :, :], scores, MASKED)


def attend(queries, keys, values, picture):
    scores = masked_scores(queries, keys, picture, HD**-0.5)
    row_max = jnp.max(scores, axis=-1, keepdims=True)
    powers = jnp.exp(scores - row_max)
    totals = jnp.sum(powers, axis=-1, keepdims=True)
    weights = (powers / totals).astype(BF)
    mixed = jnp.einsum("hqk,khd->qhd", weights, values, preferred_element_type=F32)
    return mixed.astype(BF), row_max + jnp.log(totals)


def attend_back(queries, keys, values, picture, grad_mixed, log_total):
    factor = HD**-0.5
    scores = masked_scores(queries, keys, picture, factor)
    probs = jnp.exp(scores - log_total)
    weights = probs.astype(BF)
    grad_values = jnp.einsum("hqk,qhd->khd", weights, grad_mixed, preferred_element_type=F32)
    grad_weights = jnp.einsum("qhd,khd->hqk", grad_mixed, values, preferred_element_type=F32)
    centre = jnp.sum(probs * grad_weights, axis=-1, keepdims=True)
    grad_scores = (probs * (grad_weights - centre)).astype(BF)
    grad_queries = jnp.einsum("hqk,khd->qhd", grad_scores, keys, preferred_element_type=F32) * factor
    grad_keys = jnp.einsum("hqk,qhd->khd", grad_scores, queries, preferred_element_type=F32) * factor
    return grad_queries.astype(BF), grad_keys.astype(BF), grad_values.astype(BF)


def dot(left, right):
    return jnp.dot(left, right, preferred_element_type=F32)


def rows_term(left, right):
    return lax.dot_general(left, right, (((0,), (0,)), ((), ())), preferred_element_type=F32)


def contract_back(grad_out, weight):
    return lax.dot_general(grad_out, weight, (((1,), (1,)), ((), ())), preferred_element_type=F32)


def gather(value, axis_name, axis=0):
    return lax.all_gather(value, axis_name, axis=axis, tiled=True)


def scatter_sum(value, axis_name, axis=0):
    return lax.psum_scatter(value, axis_name, scatter_dimension=axis, tiled=True)

MESH = pl.DeviceIdType.MESH


def mm(left, right):
    return jnp.dot(left, right, preferred_element_type=F32)


def mm_nt(left, right):
    return lax.dot_general(left, right, (((1,), (1,)), ((), ())), preferred_element_type=F32)


def mm_tn(left, right):
    return lax.dot_general(left, right, (((0,), (0,)), ((), ())), preferred_element_type=F32)


def lane_pad(value, lanes):
    gap = lanes - value.shape[1]
    if gap == 0:
        return value
    return jnp.concatenate([value, jnp.zeros((value.shape[0], gap), value.dtype)], axis=1)


def moments(value):
    centre = jnp.mean(value, axis=-1, keepdims=True)
    shifted = value - centre
    factor = lax.rsqrt(jnp.mean(shifted * shifted, axis=-1, keepdims=True) + NORM_EPSILON)
    return shifted * factor, factor


def block_kernel(
    dims,
    tok_in,
    cot_in,
    ids_in,
    row_in,
    col_in,
    vec_ins,
    wave_in,
    wq_in,
    wp_in,
    w1_in,
    w2_in,
    out_ref,
    tgrad_ref,
    rq_ref,
    rp_ref,
    r1_ref,
    r2_ref,
    sums_ref,
    tokb,
    ain,
    cotb,
    plb,
    smb,
    vec,
    bqkv,
    cosb,
    sinb,
    wqc,
    wq,
    wp,
    w1,
    w2,
    qkv,
    lse,
    mixc,
    mix,
    mid,
    mlp,
    act,
    dge,
    snd,
    rsr,
    gmd,
    gp,
    dq4,
    dp4,
    d14,
    d24,
    zq3,
    zp3,
    z13,
    z23,
    dkv,
    smg,
    sg8,
    hq,
    hp,
    h1,
    h2,
    sems,
    local_sems,
):
    n, T, L, D, F, R, hl, P1, CQ, HP = dims
    J = F // 2
    hw = hl * HD
    W = 128
    QW = hl * W
    scale = HD**-0.5
    tile = 256 if D % 256 == 0 else 128
    me = lax.axis_index("seq")
    f = lax.axis_index("fsdp")
    k = f % 2
    j = f // 2
    partner = f + 1 - 2 * k
    x = me % 2
    y = me // 2

    def peer(o):
        return (y + o // 2) % 2 * 2 + (x + o % 2) % 2

    seq_to = [peer(o) for o in range(n)]
    seq_from = seq_to
    near_x, near_y, across = seq_to[1], seq_to[2], seq_to[3]
    edge = (j == 0) | (j == J - 1)
    middle = (j > 0) & (j < J - 1)
    z_to = [2 * ((j + d) % J) + k for d in range(J)]
    z_from = [2 * ((j + J - d) % J) + k for d in range(J)]
    used = {"remote": 0, "local": 0}
    leftover = []

    def take(count=1):
        used["remote"] += count
        return used["remote"] - count

    def remote(src, dst, where, recv):
        return pltpu.make_async_remote_copy(
            src_ref=src,
            dst_ref=dst,
            send_sem=sems.at[take()],
            recv_sem=sems.at[recv],
            device_id=where,
            device_id_type=MESH,
        )

    def when(condition, action):
        pl.when(condition)(action)

    def send(src, dst, where, recv, late=True):
        copy = remote(src, dst, where, recv)
        copy.start()
        if late:
            leftover.append(copy)
        return copy

    def load(src, dst):
        used["local"] += 1
        copy = pltpu.make_async_copy(src, dst, local_sems.at[used["local"] - 1])
        copy.start()
        return copy

    def band(ref, index, size):
        return ref.at[pl.ds(pl.multiple_of(index * size, size), size)]

    def rows_of(index, size):
        return pl.ds(pl.multiple_of(index * size, size), size)

    def strips(total, step, body):
        def run(s, carry):
            body(rows_of(s, step))
            return carry

        lax.fori_loop(0, total // step, run, 0)

    strip = 32

    spot = lax.broadcasted_iota(jnp.int32, (1, T), 1) + me * T
    ids = ids_in[...]
    plb[me, 0:4, :] = jnp.concatenate(
        [
            ids.astype(F32),
            row_in[...].astype(F32),
            col_in[...].astype(F32),
            jnp.where(ids >= 0, ids, -1 - spot).astype(F32),
        ],
        axis=0,
    )
    plb[me, 4:8, :] = jnp.zeros((4, T), F32)
    for row in range(6):
        smb[f, row : row + 1, :] = vec_ins[row][...].astype(F32).reshape(1, R)
    up_bias = vec_ins[6][...].astype(F32).reshape(1, n * R)
    for m in range(n):

        @pl.when(me == m)
        def _():
            smb[f, 6:7, :] = up_bias[:, m * R : (m + 1) * R]

    qkv_bias = vec_ins[7][...].astype(F32).reshape(1, 3 * R)
    for t in range(3):
        smb[f, 7 + t : 8 + t, :] = qkv_bias[:, t * R : (t + 1) * R]
    smb[f, 10:16, :] = jnp.zeros((6, R), F32)

    raw_q = [load(wq_in.at[:, t * D : (t + 1) * D], d24.at[t]) for t in range(3)]
    raw_1 = [load(w1_in.at[:, c * P1 : (c + 1) * P1], d14.at[c]) for c in range(n)]

    barrier = pltpu.get_barrier_semaphore()
    for o in range(1, n):
        pl.semaphore_signal(barrier, inc=1, device_id={"seq": seq_to[o]}, device_id_type=MESH)
    for o in range(1, F):
        pl.semaphore_signal(barrier, inc=1, device_id={"fsdp": (f + o) % F}, device_id_type=MESH)
    pl.semaphore_wait(barrier, n - 1 + F - 1)

    class Spread:
        def __init__(self, src, at, rows):
            self.at, self.rows = at, rows
            self.first = [
                send(src, at(me, 0, rows), {"seq": seq_to[o]}, take()) for o in (1, 2)
            ]

        def relay(self):
            half = self.rows // 2
            self.first[0].wait_recv()
            part = self.at(near_x, 0, half)
            one = send(part, part, {"seq": near_y}, take(), late=False)
            self.first[1].wait_recv()
            part = self.at(near_y, half, self.rows)
            self.second = [one, send(part, part, {"seq": near_x}, take(), late=False)]

        def finish(self):
            for copy in self.second:
                copy.wait_recv()

        def drain(self):
            for copy in self.second:
                copy.wait_send()

    def rows_in(ref):
        return lambda index, lo, hi: ref.at[index, lo:hi]

    plc_copies = [
        send(plb.at[me], plb.at[me], {"seq": seq_to[o]}, take()) for o in range(1, n)
    ]
    tok = Spread(tok_in, rows_in(tokb), T)
    own_tok = load(tok_in, tokb.at[me])

    class Weight:
        def __init__(self, src, buf, rows):
            self.buf, self.rows = buf, rows
            self.own = None
            mine = band(buf, f, rows)
            if src is None:
                src = mine
            else:
                self.own = load(src, mine)
            self.near = send(src, mine, {"fsdp": partner}, take(), late=False)
            landed = {d: take() for d in (1, 2, 3)}
            self.far = {d: remote(src, mine, {"fsdp": z_to[d]}, landed[d]) for d in (1, 2, 3)}
            self.far[2].start()
            when(j != J - 1, self.far[1].start)
            when(j != 0, self.far[3].start)
            part = band(buf, z_from[2], rows)
            self.down = remote(part, part, {"fsdp": k}, landed[1])
            self.up = remote(part, part, {"fsdp": 2 * (J - 1) + k}, landed[3])
            self.relayed = []

        def hop(self):
            self.far[2].wait_recv()
            when(j == 1, self.down.start)
            when(j == J - 2, self.up.start)

        def relay(self):
            for d in (2, 1, 3):
                if d != 2:
                    self.far[d].wait_recv()
                part = band(self.buf, z_from[d], self.rows)
                self.relayed.append(send(part, part, {"fsdp": partner}, take(), late=False))

        def finish(self):
            if self.own is not None:
                self.own.wait()
            self.near.wait_recv()
            for copy in self.relayed:
                copy.wait_recv()

        def drain(self):
            for copy in [self.near, self.far[2]] + self.relayed:
                copy.wait_send()
            when(j != J - 1, self.far[1].wait_send)
            when(j != 0, self.far[3].wait_send)
            when(j == 1, self.down.wait_send)
            when(j == J - 2, self.up.wait_send)

    class Quarter:
        def __init__(self):
            self.cols = pl.ds(pl.multiple_of(x * (D // 2), D // 2), D // 2)
            self.holder, self.other = y == k, y != k
            used["local"] += 1
            self.own = pltpu.make_async_copy(
                wp_in.at[:, self.cols],
                wp.at[j, k, :, self.cols],
                local_sems.at[used["local"] - 1],
            )
            when(self.holder, self.own.start)
            landed = {d: take() for d in (1, 2, 3)}
            mine = wp.at[j, k, :, self.cols]
            self.far = {
                d: remote(wp_in.at[:, self.cols], mine, {"fsdp": z_to[d]}, landed[d])
                for d in (1, 2, 3)
            }
            part = wp.at[z_from[2] // 2, k, :, self.cols]
            self.down = remote(part, part, {"fsdp": k}, landed[1])
            self.up = remote(part, part, {"fsdp": 2 * (J - 1) + k}, landed[3])
            when(self.holder, self.far[2].start)
            when(self.holder & (j != J - 1), self.far[1].start)
            when(self.holder & (j != 0), self.far[3].start)

            def quarter(device_y, device_x, lo, hi):
                cols = pl.ds(pl.multiple_of(device_x * (D // 2), D // 2), D // 2)
                return wp.at[lo:hi, device_y, :, cols]

            to_x, to_y, to_core = {"seq": near_x}, {"seq": near_y}, {"fsdp": partner}
            h = J // 2
            whole = quarter(y, x, 0, J)
            self.give = [remote(whole, whole, where, take()) for where in (to_x, to_y, to_core)]
            q = quarter(y, 1 - x, 0, J)
            self.along_x = remote(q, q, to_core, take())
            q = quarter(y, 1 - x, 0, h)
            self.on_y = remote(q, q, to_y, take())
            q = quarter(1 - y, x, 0, J)
            self.along_y = remote(q, q, to_core, take())
            q = quarter(1 - y, x, h, J)
            self.on_x = remote(q, q, to_x, take())
            q = quarter(1 - y, 1 - x, 0, J)
            self.last = remote(q, q, to_core, take())

        def hop(self):
            @pl.when(self.holder)
            def _():
                self.far[2].wait_recv()
                when(j == 1, self.down.start)
                when(j == J - 2, self.up.start)

        def start_give(self):
            @pl.when(self.holder)
            def _():
                self.own.wait()
                self.far[1].wait_recv()
                self.far[3].wait_recv()
                for copy in self.give:
                    copy.start()

        def relay(self):
            @pl.when(self.holder)
            def _():
                self.give[0].wait_recv()
                self.on_y.start()
                self.along_x.start()

            @pl.when(self.other)
            def _():
                self.give[1].wait_recv()
                self.on_x.start()
                self.along_y.start()

        def relay_last(self):
            @pl.when(self.other)
            def _():
                self.on_y.wait_recv()
                self.on_x.wait_recv()
                self.last.start()

        def finish(self):
            @pl.when(self.holder)
            def _():
                self.along_y.wait_recv()
                self.last.wait_recv()

            @pl.when(self.other)
            def _():
                self.give[2].wait_recv()
                self.along_x.wait_recv()

        def drain(self):
            @pl.when(self.holder)
            def _():
                for copy in self.give + [self.along_x, self.on_y, self.far[2]]:
                    copy.wait_send()
                when(j != J - 1, self.far[1].wait_send)
                when(j != 0, self.far[3].wait_send)
                when(j == 1, self.down.wait_send)
                when(j == J - 2, self.up.wait_send)

            @pl.when(self.other)
            def _():
                for copy in (self.along_y, self.on_x, self.last):
                    copy.wait_send()

    def cut_columns(target, lines):
        for m in range(n):

            @pl.when(me == m)
            def _():
                target[rows_of(f, R), :] = lane_pad(
                    jnp.concatenate(lines(m), axis=1), target.shape[1]
                )

    small_copies = [
        send(smb.at[f], smb.at[f], {"fsdp": (f + o) % F}, take()) for o in range(1, F)
    ]
    for copy in raw_q:
        copy.wait()
    cut_columns(wqc, lambda m: [d24[t, :, m * hw : (m + 1) * hw] for t in range(3)])
    weight_q = Weight(None, wqc, R)
    for copy in raw_1:
        copy.wait()
    cut_columns(
        w1,
        lambda m: [
            d14[b * n * R // P1, :, b * n * R % P1 + m * R : b * n * R % P1 + (m + 1) * R]
            for b in range(F)
        ],
    )

    for copy in small_copies:
        copy.wait_recv()
    for row in range(7):
        vec[row : row + 1, :] = jnp.concatenate(
            [smb[s, row : row + 1, :R] for s in range(F)], axis=1
        )
    groups = 3 * D // R // 3
    heads = []
    for t in range(3):
        start = t * groups + me * (hw // R)
        line = jnp.concatenate(
            [
                smb[(start + b) // 3, pl.ds(7 + (start + b) % 3, 1), :][:, :R]
                for b in range(hw // R)
            ],
            axis=1,
        )
        for h in range(hl):
            heads.append(lane_pad(line[:, h * HD : (h + 1) * HD], W))
    bqkv[...] = jnp.broadcast_to(jnp.concatenate(heads, axis=1), bqkv.shape)

    def vector(row):
        return vec[row : row + 1, :]

    def rows_of_block(i, rows):
        return pl.ds(pl.multiple_of(i * T + rows.start, strip), strip)

    def norm_one(i):
        def body(rows):
            normed, _ = moments(tokb[i, rows, :].astype(F32))
            ain[rows_of_block(i, rows), :] = (normed * vector(0) + vector(1)).astype(BF)

        strips(T, strip, body)

    own_tok.wait()
    norm_one(me)
    tok.relay()
    weight_q.hop()
    weight_p = Quarter()
    weight_1 = Weight(None, w1, R)
    own_cot = load(cot_in, cotb.at[me])
    cot = Spread(cot_in, rows_in(cotb), T)
    norm_one(near_x)
    norm_one(near_y)

    for copy in plc_copies:
        copy.wait_recv()

    def table(i, carry):
        rows = rows_of(i, T)
        turned = jnp.transpose(plb[i], (1, 0))
        lse[rows, hl : hl + 8] = turned
        angle = turned[:, 1:2] * wave_in[0:1, :] + turned[:, 2:3] * wave_in[1:2, :]
        cosb[rows, :] = jnp.cos(angle)
        sinb[rows, :] = jnp.sin(angle) * wave_in[2:3, :]
        return carry

    lax.fori_loop(0, n, table, 0)
    lane = lax.broadcasted_iota(jnp.int32, (1, W), 1)
    low_half = lane < HD // 2

    def swap(value):
        return jnp.where(
            low_half, pltpu.roll(value, W - HD // 2, 1), pltpu.roll(value, HD // 2, 1)
        )

    tok.finish()
    norm_one(across)

    weight_q.relay()
    weight_p.hop()
    weight_q.finish()

    def spread_heads(rows):
        line = wqc[rows, :]
        for h in range(3 * hl):
            wq[rows, h * W : (h + 1) * W] = lane_pad(line[:, h * HD : (h + 1) * HD], W)

    strips(D, R, spread_heads)

    def project(i, carry):
        rows = rows_of(i, T)
        line = ain[rows, :]
        cosine = cosb[rows, :]
        sine = sinb[rows, :]
        for t in range(3):
            part = mm(line, wq[:, t * QW : (t + 1) * QW]) + bqkv[0:1, t * QW : (t + 1) * QW]
            for h in range(hl):
                u = part[:, h * W : (h + 1) * W]
                if t < 2:
                    u = u * cosine + swap(u) * sine
                qkv[rows, t * QW + h * W : t * QW + (h + 1) * W] = u.astype(BF)
        return carry

    weight_p.start_give()
    lax.fori_loop(0, n, project, 0)

    def masked(scores, i):
        ids = jnp.concatenate([plb[b, 3:4, :] for b in range(n)], axis=1)
        own_ids = lse[rows_of(i, T), hl + 3 : hl + 4]
        return jnp.where(own_ids == ids, scores * scale, MASKED)

    mix_send, mix_recv = take(n * (n - 1)), take(n * (n - 1))

    def mix_copy(i, o, peer, source):
        return pltpu.make_async_remote_copy(
            src_ref=mixc.at[source, i],
            dst_ref=mixc.at[source, i],
            send_sem=sems.at[mix_send + i * (n - 1) + o - 1],
            recv_sem=sems.at[mix_recv + i * (n - 1) + o - 1],
            device_id={"seq": peer},
            device_id_type=MESH,
        )

    def attend_block(i, carry):
        rows = rows_of(i, T)
        outs = []
        logs = lse[rows, :]
        for h in range(hl):
            q = qkv[rows, h * W : (h + 1) * W]
            kk = qkv[:, QW + h * W : QW + (h + 1) * W]
            v = qkv[:, 2 * QW + h * W : 2 * QW + (h + 1) * W]
            s = masked(mm_nt(q, kk), i)
            top = jnp.max(s, axis=-1, keepdims=True)
            p = jnp.exp(s - top)
            total = jnp.sum(p, axis=-1, keepdims=True)
            outs.append((mm(p.astype(BF), v) / total)[:, :HD].astype(BF))
            logs = jnp.where(lane == h, top + jnp.log(total), logs)
        lse[rows, :] = logs
        mixc[me, i] = lane_pad(jnp.concatenate(outs, axis=1), HP)
        for o in range(1, n):
            mix_copy(i, o, seq_to[o], me).start()
        return carry

    weight_2 = Weight(w2_in.at[rows_of(me, R)], w2, R)
    cot.relay()
    lax.fori_loop(0, n // 2, attend_block, 0)
    weight_p.relay()
    weight_1.hop()
    lax.fori_loop(n // 2, n, attend_block, 0)
    weight_p.relay_last()
    weight_p.finish()
    tok.drain()

    def proj_weight():
        return wp[...].reshape(D, D)

    def branch(i, carry):
        rows = rows_of(i, T)
        for o in range(1, n):
            mix_copy(i, o, seq_to[o], seq_from[o]).wait_recv()
        mix[rows, :] = jnp.concatenate([mixc[c, i][:, :hw] for c in range(n)], axis=1)
        gmd[...] = mm(mix[rows, :], proj_weight())

        def body(part):
            whole = rows_of_block(i, part)
            value = gmd[part, :] + tokb[i, part, :].astype(F32) + vector(2)

            @pl.when(i == me)
            def _():
                mid[part, :] = value

            normed, _ = moments(value)
            mlp[whole, :] = (normed * vector(3) + vector(4)).astype(BF)

        strips(T, strip, body)
        return carry

    lax.fori_loop(0, n, branch, 0)

    weight_2.hop()
    weight_1.relay()
    weight_1.finish()

    def up(i, carry):
        rows = rows_of(i, T)
        before = mm(mlp[rows, :], w1[...]) + vector(6)
        gate = jax.nn.sigmoid(1.702 * before)
        act[rows, :] = (before * gate).astype(BF)
        dge[rows, :] = (gate + 1.702 * before * gate * (1.0 - gate)).astype(BF)
        return carry

    lax.fori_loop(0, n, up, 0)

    own_cot.wait()
    cot.finish()
    cot.drain()
    weight_2.relay()
    weight_2.finish()

    half = T // 2

    class Scatter:
        def __init__(self, stage, landing, slots):
            self.stage, self.landing = stage, landing
            slot_x, slot_y, pass_x, pass_y = slots
            to_x, to_y = {"seq": near_x}, {"seq": near_y}
            self.pass_a = self.make(across, 0, pass_x, to_x)
            self.pass_b = self.make(across, 1, pass_y, to_y)
            self.last_a = self.make(near_x, 0, slot_x, to_x)
            self.last_b = self.make(near_y, 1, slot_y, to_y)
            self.sum_a = self.make(near_y, 0, slot_y, to_y)
            self.sum_b = self.make(near_x, 1, slot_x, to_x)

        def make(self, block, part, slot, where):
            return remote(
                self.stage.at[self.rows(block, part)],
                self.landing.at[slot, part * half : (part + 1) * half],
                where,
                take(),
            )

        def rows(self, block, part):
            return pl.ds(pl.multiple_of(block * T + part * half, half), half)

        def start(self, t):
            @pl.when(t == 0)
            def _():
                self.pass_a.start()
                self.pass_b.start()

            when(t == 1, self.last_a.start)
            when(t == 2, self.last_b.start)

        def relay(self, slot):
            for part, into, out, block in (
                (0, self.pass_a, self.sum_a, near_y),
                (1, self.pass_b, self.sum_b, near_x),
            ):
                into.wait_recv()

                def body(rows):
                    at = pl.ds(pl.multiple_of(block * T + part * half + rows.start, strip), strip)
                    there = pl.ds(pl.multiple_of(part * half + rows.start, strip), strip)
                    self.stage[at, :] = (
                        self.stage[at, :].astype(F32) + self.landing[slot, there, :].astype(F32)
                    ).astype(BF)

                strips(half, strip, body)
                out.start()

        def wait_recv(self):
            for copy in (self.last_a, self.last_b, self.sum_a, self.sum_b):
                copy.wait_recv()

        def wait_send(self):
            for copy in (
                self.pass_a,
                self.pass_b,
                self.last_a,
                self.last_b,
                self.sum_a,
                self.sum_b,
            ):
                copy.wait_send()

    def block_at(t):
        return peer(((t + 2) % 3 + 1) * (1 - t // 3))

    for i in range(n):
        for o in range(1, n):
            mix_copy(i, o, seq_to[o], me).wait_send()
    scatter_mlp = Scatter(snd, rsr, (0, 1, 2, 2))

    def back(t, carry):
        i = block_at(t)
        rows = rows_of(i, T)
        grad = (mm_nt(cotb[i], w2[...]) * dge[rows, :].astype(F32)).astype(BF)
        dge[rows, :] = grad
        snd[rows, :] = mm_nt(grad, w1[...]).astype(BF)
        scatter_mlp.start(t)
        return carry

    lax.fori_loop(0, n, back, 0)

    class Gradient:
        def __init__(self, grad, other, far, extra, result, lo, width):
            self.grad, self.other, self.far, self.extra = grad, other, far, extra
            self.result, self.lanes = result, slice(lo, lo + width)

        def of(self, index):
            return self.grad.at[rows_of(index, R), self.lanes]

        def exchange(self):
            self.near = [
                send(
                    self.of(2 * c + 1 - k),
                    self.other.at[c, :, self.lanes],
                    {"fsdp": partner},
                    take(),
                )
                for c in range(J)
            ]

        def add_near(self):
            for copy in self.near:
                copy.wait_recv()
            lanes = self.lanes

            def chip(c, carry):
                rows = rows_of(2 * c + k, R)
                self.grad[rows, lanes] = (
                    self.grad[rows, lanes].astype(F32) + self.other[c, :, lanes].astype(F32)
                ).astype(BF)
                return carry

            lax.fori_loop(0, J, chip, 0)
            self.pass_on = remote(
                self.of(2 * (J - 1 - j) + k),
                self.extra.at[:, lanes],
                {"fsdp": 2 * (1 + j // (J - 1)) + k},
                take(),
            )
            self.across = {
                d: remote(
                    self.of(z_to[d]), self.far.at[d - 1, :, lanes], {"fsdp": z_to[d]}, take()
                )
                for d in (1, 2, 3)
            }
            when(edge, self.pass_on.start)
            when(edge, self.across[2].start)
            when(j != J - 1, self.across[1].start)
            when(j != 0, self.across[3].start)

        def hop(self):
            @pl.when(middle)
            def _():
                self.pass_on.wait_recv()
                rows = rows_of(z_to[2], R)
                self.grad[rows, self.lanes] = (
                    self.grad[rows, self.lanes].astype(F32)
                    + self.extra[:, self.lanes].astype(F32)
                ).astype(BF)
                self.across[2].start()

        def add_far(self):
            def total_of(steps):
                def action():
                    for d in steps:
                        self.across[d].wait_recv()
                    total = self.grad[rows_of(f, R), self.lanes].astype(F32)
                    for d in steps:
                        total = total + self.far[d - 1, :, self.lanes].astype(F32)
                    self.other[0, :, self.lanes] = total.astype(BF)

                return action

            when(j == 0, total_of((2, 3)))
            when(middle, total_of((1, 2, 3)))
            when(j == J - 1, total_of((1, 2)))

        def share(self):
            mine = self.other.at[0, :, self.lanes]
            self.keep = load(mine, self.result.at[me, :, self.lanes])
            self.spread = Spread(
                mine, lambda index, lo, hi: self.result.at[index, lo:hi, self.lanes], R
            )

        def relay(self):
            self.spread.relay()

        def finish(self):
            self.keep.wait()
            self.spread.finish()
            self.spread.drain()
            self.across[2].wait_send()
            when(j != J - 1, self.across[1].wait_send)
            when(j != 0, self.across[3].wait_send)
            when(edge, self.pass_on.wait_send)

    CH = CQ // 2
    grad_up = Gradient(w1, d14, z13, h1, r1_ref, 0, P1)
    grad_down = Gradient(w2, d24, z23, h2, r2_ref, 0, D)
    grad_proj = Gradient(gp, dp4, zp3, hp, rp_ref, 0, HP)
    grad_qkv = [Gradient(wqc, dq4, zq3, hq, rq_ref, b * CH, CH) for b in range(2)]

    weight_1.drain()
    weight_2.drain()
    weight_q.drain()

    def up_grad(t, carry):
        w1[rows_of(t, tile), :] = mm_tn(mlp[:, rows_of(t, tile)], dge[...]).astype(BF)
        return carry

    lax.fori_loop(0, D // tile, up_grad, 0)
    grad_up.exchange()
    scatter_mlp.relay(2)

    def down(i, carry):
        rows = rows_of(i, T)
        mlp[rows, :] = mm(act[rows, :], w2[...]).astype(BF)
        return carry

    lax.fori_loop(0, n, down, 0)
    grad_up.add_near()

    def down_grad(t, carry):
        lanes = rows_of(t, tile)
        total = mm_tn(act[0:T, lanes], cotb[0])
        for b in range(1, n):
            total = total + mm_tn(act[b * T : (b + 1) * T, lanes], cotb[b])
        w2[lanes, :] = total.astype(BF)
        return carry

    lax.fori_loop(0, P1 // tile, down_grad, 0)
    grad_down.exchange()

    smg[...] = jnp.zeros(smg.shape, F32)
    scatter_mlp.wait_recv()

    def gather_parts(part):
        whole = rows_of_block(me, part)
        total = snd[whole, :].astype(F32)
        return total + rsr[0, part, :].astype(F32) + rsr[1, part, :].astype(F32)

    def add_sum(row, value):
        smg[row : row + 1, :] = smg[row : row + 1, :] + jnp.sum(value, axis=0, keepdims=True)

    def norm_two_back(part):
        upstream = cotb[me, part, :].astype(F32)
        grad = gather_parts(part)
        normed, factor = moments(mid[part, :])
        scaled = grad * vector(3)
        value = upstream + factor * (
            scaled
            - jnp.mean(scaled, axis=-1, keepdims=True)
            - normed * jnp.mean(scaled * normed, axis=-1, keepdims=True)
        )
        gmd[part, :] = value
        low = value.astype(BF)
        snd[rows_of_block(me, part), :] = low
        add_sum(2, low.astype(F32))
        add_sum(3, grad * normed)
        add_sum(4, grad)
        add_sum(5, upstream)

    strips(T, strip, norm_two_back)
    own_rows = rows_of(me, T)
    low_branch = snd[own_rows, :]
    grad_mixed = mm_nt(low_branch, proj_weight()).astype(BF)
    for c in range(n):
        mixc[0, c] = lane_pad(grad_mixed[:, c * hw : (c + 1) * hw], HP)
        mixc[2, c] = lane_pad(low_branch[:, c * hw : (c + 1) * hw], HP)
    head_copies = [
        send(mixc.at[0, seq_to[o]], mixc.at[1, me], {"seq": seq_to[o]}, take()) for o in range(1, n)
    ]
    branch_copies = [
        send(mixc.at[2, seq_to[o]], mixc.at[3, me], {"seq": seq_to[o]}, take()) for o in range(1, n)
    ]
    mixc[1, me] = mixc[0, me]
    mixc[3, me] = mixc[2, me]

    grad_down.add_near()
    grad_up.hop()

    for copy in head_copies:
        copy.wait_recv()
    scatter_out = Scatter(mlp, tokb, (me, me, near_y, near_x))
    for t in range(n - 1):
        scatter_out.start(t)

    def proj_grad(t, carry):
        lanes = rows_of(t, tile)
        total = mm_tn(mix[0:T, lanes], mixc[3, 0])
        for b in range(1, n):
            total = total + mm_tn(mix[b * T : (b + 1) * T, lanes], mixc[3, b])
        gp[lanes, :] = total.astype(BF)
        return carry

    def qkv_grad(half):
        pair = hl // 2 * W

        def body(t, carry):
            rows = rows_of(t, tile)
            parts = []
            for third in range(3):
                at = third * QW + half * pair
                total = mm_tn(ain[:, rows], qkv[:, at : at + pair])
                parts += [total[:, h * W : h * W + HD].astype(BF) for h in range(hl // 2)]
            wqc[rows, half * CH : (half + 1) * CH] = lane_pad(jnp.concatenate(parts, axis=1), CH)
            return carry

        lax.fori_loop(0, D // tile, body, 0)
        grad_qkv[half].exchange()

    def between(h):
        if h == 0:
            grad_down.hop()
            for copy in branch_copies:
                copy.wait_recv()
            lax.fori_loop(0, D // tile, proj_grad, 0)
            grad_proj.exchange()
            scatter_out.relay(across)
        if h == 1:
            grad_proj.add_near()
            qkv_grad(0)
            grad_up.add_far()
        if h == 2:
            grad_proj.hop()
            grad_qkv[0].add_near()
        if h == 3:
            grad_qkv[0].hop()
            grad_down.add_far()

    for h in range(hl):
        q_at = slice(h * W, (h + 1) * W)
        k_at = slice(QW + h * W, QW + (h + 1) * W)
        v_at = slice(2 * QW + h * W, 2 * QW + (h + 1) * W)
        dkv[...] = jnp.zeros(dkv.shape, F32)

        def attend_back_block(i, carry):
            rows = rows_of(i, T)
            q = qkv[rows, q_at]
            kk = qkv[:, k_at]
            g = lane_pad(mixc[1, i][:, h * HD : (h + 1) * HD], W)
            p = jnp.exp(masked(mm_nt(q, kk), i) - lse[rows, h : h + 1])
            dp = mm_nt(g, qkv[:, v_at])
            dkv[:, W:] = dkv[:, W:] + mm_tn(p.astype(BF), g)
            centre = jnp.sum(p * dp, axis=-1, keepdims=True)
            ds = (p * (dp - centre)).astype(BF)
            dq = (mm(ds, kk) * scale).astype(BF).astype(F32)
            dkv[:, :W] = dkv[:, :W] + mm_tn(ds, q)
            qkv[rows, q_at] = (dq * cosb[rows, :] - swap(dq) * sinb[rows, :]).astype(BF)
            return carry

        lax.fori_loop(0, n, attend_back_block, 0)

        def turn_back(i, carry):
            rows = rows_of(i, T)
            dk = (dkv[rows, :W] * scale).astype(BF).astype(F32)
            qkv[rows, k_at] = (dk * cosb[rows, :] - swap(dk) * sinb[rows, :]).astype(BF)
            qkv[rows, v_at] = dkv[rows, W:].astype(BF)
            return carry

        lax.fori_loop(0, n, turn_back, 0)
        between(h)

    scatter_mlp.wait_send()
    scatter_attn = Scatter(snd, rsr, (0, 1, 2, 2))

    def attn_back(t, carry):
        i = block_at(t)
        rows = rows_of(i, T)
        snd[rows, :] = mm_nt(qkv[rows, :], wq[...]).astype(BF)
        scatter_attn.start(t)
        return carry

    lax.fori_loop(0, n, attn_back, 0)

    qkv_grad(1)
    scatter_attn.relay(2)
    grad_up.share()
    grad_down.share()
    grad_proj.add_far()
    grad_proj.share()

    def bias_sums(part):
        smg[6:7, :] = smg[6:7, :] + jnp.sum(dge[part, :].astype(F32), axis=0, keepdims=True)
        line = jnp.sum(qkv[part, :].astype(F32), axis=0, keepdims=True)
        line = lane_pad(
            jnp.concatenate([line[:, h * W : h * W + HD] for h in range(3 * hl)], axis=1), D
        )
        smg[7:8, :] = smg[7:8, :] + line

    grad_qkv[1].add_near()
    strips(L, 64, bias_sums)
    grad_qkv[0].add_far()
    grad_qkv[0].share()
    grad_qkv[1].hop()

    scatter_attn.wait_recv()

    def norm_one_back(part):
        grad = gather_parts(part)
        normed, factor = moments(tokb[me, part, :].astype(F32))
        scaled = grad * vector(0)
        gmd[part, :] = gmd[part, :] + factor * (
            scaled
            - jnp.mean(scaled, axis=-1, keepdims=True)
            - normed * jnp.mean(scaled * normed, axis=-1, keepdims=True)
        )
        add_sum(0, grad * normed)
        add_sum(1, grad)

    strips(T, strip, norm_one_back)
    tokens_out = load(gmd, tgrad_ref)
    sum_copies = [
        send(smg, sg8.at[f], {"fsdp": (f + o) % F}, take()) for o in range(1, F)
    ]
    sg8[f] = smg[...]
    grad_up.relay()
    grad_down.relay()
    grad_qkv[1].add_far()
    grad_qkv[1].share()

    scatter_out.wait_recv()

    def write_out(part):
        whole = rows_of_block(me, part)
        total = mid[part, :] + mlp[whole, :].astype(F32) + vector(5)
        for slot in (near_x, near_y):
            total = total + tokb[slot, part, :].astype(F32)
        bias_rows = rows_of_block(me, part)
        ain[bias_rows, :] = total.astype(BF)

    strips(T, strip, write_out)
    block_out = load(band(ain, me, T), out_ref)

    for copy in sum_copies:
        copy.wait_recv()
    total = sg8[0]
    for s in range(1, F):
        total = total + sg8[s]
    plain = lax.broadcasted_iota(jnp.int32, total.shape, 0)
    vec[...] = jnp.where(plain < 8, total, 0.0)
    sums_keep = load(vec, sums_ref.at[me])
    sums_share = [
        send(vec, sums_ref.at[me], {"seq": seq_to[o]}, take()) for o in range(1, n)
    ]

    grads = [grad_up, grad_down, grad_proj] + grad_qkv
    for item in grads[2:]:
        item.relay()
    for item in grads:
        item.finish()
    for copy in sums_share:
        copy.wait_recv()
    sums_keep.wait()
    tokens_out.wait()
    block_out.wait()
    weight_p.drain()
    scatter_attn.wait_send()
    scatter_out.wait_send()
    for copy in leftover:
        copy.wait_send()
    assert used["remote"] <= sems.shape[0] and used["local"] <= local_sems.shape[0], used


def unpack_kernel(
    dims,
    block_in,
    tokens_in,
    rq_in,
    rp_in,
    r1_in,
    r2_in,
    sums_in,
    block_ref,
    tokens_ref,
    qkv_ref,
    proj_ref,
    up_ref,
    down_ref,
    v0,
    v1,
    v2,
    v3,
    v4,
    v5,
    v6,
    v7,
    block,
    tokens,
    rq,
    rp,
    r1,
    r2,
    sums,
    stage,
    in_sems,
    out_sems,
):
    n, T, L, D, F, R, hl, P1, CQ, HP = dims
    hw = hl * HD
    f = lax.axis_index("fsdp")
    loads = []
    for src, dst in (
        (r2_in, r2),
        (r1_in, r1),
        (rq_in, rq),
        (rp_in, rp),
        (tokens_in, tokens),
        (block_in, block),
        (sums_in, sums),
    ):
        copy = pltpu.make_async_copy(src, dst, in_sems.at[len(loads)])
        copy.start()
        loads.append(copy)
    stores = []

    def store(src, dst):
        copy = pltpu.make_async_copy(src, dst, out_sems.at[len(stores)])
        copy.start()
        stores.append(copy)

    loads[0].wait()
    for c in range(n):
        stage[c] = r2[c].astype(F32)
        store(stage.at[c], down_ref.at[c * R : (c + 1) * R])
    loads[1].wait()
    width = n * R
    for c in range(n):
        blocks = range(c * P1 // width, (c + 1) * P1 // width)
        stage[n + c] = jnp.concatenate(
            [r1[m, :, b * R : (b + 1) * R] for b in blocks for m in range(n)], axis=1
        ).astype(F32)
        store(stage.at[n + c], up_ref.at[:, c * P1 : (c + 1) * P1])
    loads[2].wait()
    for t in range(3):
        stage[2 * n + t] = jnp.concatenate(
            [
                rq[m, :, b * CQ // 2 + t * hw // 2 : b * CQ // 2 + (t + 1) * hw // 2]
                for m in range(n)
                for b in range(2)
            ],
            axis=1,
        ).astype(F32)
        store(stage.at[2 * n + t], qkv_ref.at[:, t * D : (t + 1) * D])
    loads[3].wait()
    stage[2 * n + 3] = jnp.concatenate([rp[m, :, :hw] for m in range(n)], axis=1).astype(F32)
    store(stage.at[2 * n + 3], proj_ref)
    loads[4].wait()
    store(tokens, tokens_ref)
    loads[5].wait()
    store(block, block_ref)
    loads[6].wait()
    per_part = hw // R
    for s in range(F):

        @pl.when(f == s)
        def _():
            own = slice(s * R, (s + 1) * R)
            total = sums[0, 0:6, own]
            for m in range(1, n):
                total = total + sums[m, 0:6, own]
            for row, out in enumerate((v0, v1, v2, v3, v4, v5)):
                out[...] = total[row : row + 1, :].reshape(R)
            lines = [sums[m, 6:7, own] for m in range(n)]
            v6[...] = jnp.concatenate(lines, axis=1).reshape(n * R)
            lines = []
            for b in range(3):
                spot = 3 * s + b
                third, rest = spot // (n * per_part), spot % (n * per_part)
                at = third * hw + rest % per_part * R
                lines.append(sums[rest // per_part, 7:8, at : at + R])
            v7[...] = jnp.concatenate(lines, axis=1).reshape(3 * R)

    for copy in stores:
        copy.wait()


def round_up(value, step):
    return -(-value // step) * step


def shards_kernel(
    tokens,
    picture_ids,
    patch_rows,
    patch_cols,
    norm1_gain,
    norm1_bias,
    qkv_weight,
    qkv_bias,
    proj_weight,
    proj_bias,
    norm2_gain,
    norm2_bias,
    fc1_weight,
    fc1_bias,
    fc2_weight,
    fc2_bias,
    cotangent,
):
    n = lax.axis_size("seq")
    me = lax.axis_index("seq")
    F = lax.axis_size("fsdp")
    f = lax.axis_index("fsdp")
    _, T, D = tokens.shape
    L = n * T
    hl = D // HD // n
    hw = hl * HD
    R = D // F
    hidden = fc1_weight.shape[1]
    P1 = hidden // n
    part = hidden // (F * n)
    CQ = round_up(3 * hw, 128)
    HP = round_up(hw, 128)
    J = F // 2
    W = 128

    lines = (
        norm1_gain,
        norm1_bias,
        proj_bias,
        norm2_gain,
        norm2_bias,
        fc2_bias,
        fc1_bias,
        qkv_bias,
    )
    quarter = HD // 4
    inverse = 10000.0 ** (-np.arange(quarter) / quarter)
    wave = np.zeros((8, W), np.float32)
    for c in range(2):
        wave[0, 2 * c * quarter : (2 * c + 1) * quarter] = inverse
        wave[1, (2 * c + 1) * quarter : (2 * c + 2) * quarter] = inverse
    wave[2] = np.where(np.arange(W) < HD // 2, -1.0, 1.0)
    dims = (n, T, L, D, F, R, hl, P1, CQ, HP)
    anywhere = pl.BlockSpec(memory_space=pl.ANY)
    local = pl.BlockSpec(memory_space=pltpu.VMEM)

    def vmem(shape, dtype=BF):
        return pltpu.VMEM(shape, dtype)

    scratch = [
        vmem((n, T, D)),
        vmem((L, D)),
        vmem((n, T, D)),
        vmem((n, 8, T), F32),
        vmem((F, 16, R), F32),
        vmem((8, D), F32),
        vmem((8, 3 * hl * W), F32),
        vmem((L, W), F32),
        vmem((L, W), F32),
        vmem((D, CQ)),
        vmem((D, 3 * hl * W)),
        vmem((J, 2, R, D)),
        vmem((D, P1)),
        vmem((P1, D)),
        vmem((L, 3 * hl * W)),
        vmem((L, W), F32),
        vmem((n, n, T, HP)),
        vmem((L, D)),
        vmem((T, D), F32),
        vmem((L, D)),
        vmem((L, P1)),
        vmem((L, P1)),
        vmem((L, D)),
        vmem((n - 1, T, D)),
        vmem((T, D), F32),
        vmem((D, HP)),
        vmem((J, R, CQ)),
        vmem((J, R, HP)),
        vmem((J, R, P1)),
        vmem((J, R, D)),
        vmem((J - 1, R, CQ)),
        vmem((J - 1, R, HP)),
        vmem((J - 1, R, P1)),
        vmem((J - 1, R, D)),
        vmem((L, 2 * W), F32),
        vmem((8, D), F32),
        vmem((F, 8, D), F32),
        vmem((R, CQ)),
        vmem((R, HP)),
        vmem((R, P1)),
        vmem((R, D)),
        pltpu.SemaphoreType.DMA((448,)),
        pltpu.SemaphoreType.DMA((24,)),
    ]
    shapes = (
        jax.ShapeDtypeStruct((T, D), BF),
        jax.ShapeDtypeStruct((T, D), F32),
        jax.ShapeDtypeStruct((n, R, CQ), BF),
        jax.ShapeDtypeStruct((n, R, HP), BF),
        jax.ShapeDtypeStruct((n, R, P1), BF),
        jax.ShapeDtypeStruct((n, R, D), BF),
        jax.ShapeDtypeStruct((n, 8, D), F32),
    )
    block_out, tokens_grad, rq, rp, r1, r2, sums = pl.pallas_call(
        functools.partial(block_kernel, dims),
        out_shape=shapes,
        in_specs=[anywhere] * 2 + [local] * 3 + [(local,) * 8] + [local] + [anywhere] * 4,
        out_specs=[anywhere] * 7,
        scratch_shapes=scratch,
        compiler_params=pltpu.CompilerParams(
            collective_id=0, has_side_effects=True, vmem_limit_bytes=67043328
        ),
    )(
        tokens[0],
        cotangent[0],
        picture_ids,
        patch_rows,
        patch_cols,
        lines,
        wave,
        qkv_weight,
        proj_weight,
        fc1_weight,
        fc2_weight,
    )
    stored = (
        jax.ShapeDtypeStruct((T, D), BF),
        jax.ShapeDtypeStruct((T, D), F32),
        jax.ShapeDtypeStruct((R, 3 * D), F32),
        jax.ShapeDtypeStruct((R, D), F32),
        jax.ShapeDtypeStruct((R, hidden), F32),
        jax.ShapeDtypeStruct((n * R, D), F32),
    ) + tuple(jax.ShapeDtypeStruct((size,), F32) for size in [R] * 6 + [n * R, 3 * R])
    block_out, tokens_grad, full_qkv, full_proj, full_up, full_down, *vectors = pl.pallas_call(
        functools.partial(unpack_kernel, dims),
        out_shape=stored,
        in_specs=[anywhere] * 7,
        out_specs=[anywhere] * 6 + [local] * 8,
        scratch_shapes=[
            vmem((T, D)),
            vmem((T, D), F32),
            vmem((n, R, CQ)),
            vmem((n, R, HP)),
            vmem((n, R, P1)),
            vmem((n, R, D)),
            vmem((n, 8, D), F32),
            vmem((4 + 2 * n, R, D), F32),
            pltpu.SemaphoreType.DMA((7,)),
            pltpu.SemaphoreType.DMA((7 + 2 * n,)),
        ],
        compiler_params=pltpu.CompilerParams(vmem_limit_bytes=67043328),
    )(block_out, tokens_grad, rq, rp, r1, r2, sums)
    return (
        block_out[None],
        tokens_grad[None],
        vectors[0],
        vectors[1],
        full_qkv,
        vectors[7],
        full_proj,
        vectors[2],
        vectors[3],
        vectors[4],
        full_up,
        vectors[6],
        full_down,
        vectors[5],
    )


def fits_kernel(mesh):
    return dict(mesh.shape) == {"seq": 4, "fsdp": 8}


def shards_plain(
    tokens,
    picture_ids,
    patch_rows,
    patch_cols,
    norm1_gain,
    norm1_bias,
    qkv_weight,
    qkv_bias,
    proj_weight,
    proj_bias,
    norm2_gain,
    norm2_bias,
    fc1_weight,
    fc1_bias,
    fc2_weight,
    fc2_bias,
    cotangent,
):
    n = lax.axis_size("seq")
    me = lax.axis_index("seq")
    stores = lax.axis_size("fsdp")
    _, own, width = tokens.shape
    heads = width // HD
    local_heads = heads // n
    hw = local_heads * HD
    rows = qkv_weight.shape[0]
    hidden = fc1_weight.shape[1]
    part = hidden // (stores * n)

    def pick(value, axis):
        return lax.dynamic_index_in_dim(value, me, axis, keepdims=False)

    own_qkv = pick(qkv_weight.reshape(rows, 3, n, hw), 2).reshape(rows, 3 * hw)
    own_up = pick(fc1_weight.reshape(rows, stores, n, part), 2).reshape(rows, stores * part)
    own_down = pick(fc2_weight.reshape(n, part, width), 0)
    small = (norm1_gain, norm1_bias, proj_bias, norm2_gain, norm2_bias, fc2_bias, qkv_bias, fc1_bias)
    sizes = [item.shape[0] for item in small]
    packed = gather(jnp.concatenate(small)[None], "fsdp")
    weight_qkv = gather(own_qkv, "fsdp")
    weight_proj = gather(proj_weight, "fsdp")
    weight_up = gather(own_up, "fsdp")
    weight_down = gather(own_down, "fsdp")
    params = []
    start = 0
    for size in sizes:
        params.append(packed[:, start : start + size].reshape(-1).astype(F32))
        start += size
    gain_one, bias_one, bias_proj, gain_two, bias_two, bias_down, bias_qkv, bias_up = params
    bias_qkv = pick(bias_qkv.reshape(3, n, hw), 1).reshape(3 * hw)
    bias_up = pick(bias_up.reshape(stores, n, part), 1).reshape(stores * part)

    places = jnp.stack([picture_ids[0], patch_rows[0], patch_cols[0]])
    places = gather(places, "seq", 1)
    picture = places[0]
    all_tokens = gather(tokens[0], "seq").astype(F32)
    upstream = gather(cotangent[0], "seq")
    length = all_tokens.shape[0]

    def mine(value):
        return lax.dynamic_slice_in_dim(value, me * own, own, 0)

    normed_one, factor_one = standardize(all_tokens)
    attn_input = (normed_one * gain_one + bias_one).astype(BF)
    projected = (dot(attn_input, weight_qkv) + bias_qkv).reshape(length, 3, local_heads, HD)
    cosine, sine = rotary_tables(places[1], places[2], HD)
    queries = rotate(projected[:, 0], cosine, sine).astype(BF)
    keys = rotate(projected[:, 1], cosine, sine).astype(BF)
    values = projected[:, 2].astype(BF)
    mixed_own, log_total = attend(queries, keys, values, picture)
    mixed = gather(mixed_own.reshape(length, hw), "seq", 1)
    middle = all_tokens + dot(mixed, weight_proj) + bias_proj
    normed_two, factor_two = standardize(middle)
    mlp_input = (normed_two * gain_two + bias_two).astype(BF)
    before = dot(mlp_input, weight_up) + bias_up
    gate = jax.nn.sigmoid(1.702 * before)
    activated = (before * gate).astype(BF)
    out_part = dot(activated, weight_down).astype(BF)
    block_out = (mine(middle) + scatter_sum(out_part, "seq").astype(F32) + bias_down).astype(BF)

    grad_down = scatter_sum(rows_term(activated, upstream).astype(BF), "fsdp")
    grad_activated = contract_back(upstream, weight_down)
    grad_before = (grad_activated * (gate + 1.702 * before * gate * (1.0 - gate))).astype(BF)
    grad_up = scatter_sum(rows_term(mlp_input, grad_before).astype(BF), "fsdp")
    grad_mlp_input = scatter_sum(contract_back(grad_before, weight_up).astype(BF), "seq").astype(F32)
    own_upstream = cotangent[0].astype(F32)
    own_two = mine(normed_two)
    grad_middle = own_upstream + norm_back(grad_mlp_input, own_two, mine(factor_two), gain_two)
    grad_branch = grad_middle.astype(BF)
    grad_mixed = contract_back(grad_branch, weight_proj).astype(BF)
    grad_heads = lax.all_to_all(grad_mixed, "seq", split_axis=1, concat_axis=0, tiled=True)
    branch_part = lax.all_to_all(grad_branch, "seq", split_axis=1, concat_axis=0, tiled=True)
    grad_proj = scatter_sum(rows_term(mixed, branch_part).astype(BF), "fsdp")
    grad_queries, grad_keys, grad_values = attend_back(
        queries, keys, values, picture, grad_heads.reshape(length, local_heads, HD), log_total
    )
    grad_projected = jnp.stack(
        [
            unrotate(grad_queries.astype(F32), cosine, sine).astype(BF),
            unrotate(grad_keys.astype(F32), cosine, sine).astype(BF),
            grad_values,
        ],
        axis=1,
    ).reshape(length, 3 * hw)
    grad_qkv = scatter_sum(rows_term(attn_input, grad_projected).astype(BF), "fsdp")
    grad_attn_input = scatter_sum(contract_back(grad_projected, weight_qkv).astype(BF), "seq").astype(F32)
    own_one = mine(normed_one)
    tokens_grad = grad_middle + norm_back(grad_attn_input, own_one, mine(factor_one), gain_one)

    def spread(value, groups):
        empty = jnp.zeros((groups, n, value.shape[0] // groups), F32)
        return lax.dynamic_update_slice_in_dim(
            empty, value.reshape(groups, 1, -1), me, 1
        ).reshape(stores, -1)

    sums = [
        jnp.sum(grad_attn_input * own_one, axis=0).reshape(stores, -1),
        jnp.sum(grad_attn_input, axis=0).reshape(stores, -1),
        jnp.sum(grad_branch.astype(F32), axis=0).reshape(stores, -1),
        jnp.sum(grad_mlp_input * own_two, axis=0).reshape(stores, -1),
        jnp.sum(grad_mlp_input, axis=0).reshape(stores, -1),
        jnp.sum(own_upstream, axis=0).reshape(stores, -1),
        spread(jnp.sum(grad_projected.astype(F32), axis=0), 3),
        spread(jnp.sum(grad_before.astype(F32), axis=0), stores),
    ]
    summed = lax.psum(scatter_sum(jnp.concatenate(sums, axis=1), "fsdp"), "seq")[0]
    finals = []
    start = 0
    for size in sizes:
        finals.append(summed[start : start + size])
        start += size
    full_down = gather(grad_down, "seq").astype(F32)
    full_up = gather(grad_up[None], "seq").reshape(n, rows, stores, part)
    full_up = full_up.transpose(1, 2, 0, 3).reshape(rows, hidden).astype(F32)
    full_proj = gather(grad_proj, "seq", 1).astype(F32)
    full_qkv = gather(grad_qkv[None], "seq").reshape(n, rows, 3, hw)
    full_qkv = full_qkv.transpose(1, 2, 0, 3).reshape(rows, 3 * width).astype(F32)
    return (
        block_out[None],
        tokens_grad[None],
        finals[0],
        finals[1],
        full_qkv,
        finals[6],
        full_proj,
        finals[2],
        finals[3],
        finals[4],
        full_up,
        finals[7],
        full_down,
        finals[5],
    )


def solution(mesh):
    token = P("fsdp", "seq", None)
    place = P("fsdp", "seq")
    vector = P("fsdp")
    matrix = P("fsdp", None)
    in_specs = (
        token,
        place,
        place,
        place,
        vector,
        vector,
        matrix,
        vector,
        matrix,
        vector,
        vector,
        vector,
        matrix,
        vector,
        matrix,
        vector,
        token,
    )
    out_specs = (
        token,
        token,
        vector,
        vector,
        matrix,
        vector,
        matrix,
        vector,
        vector,
        vector,
        matrix,
        vector,
        matrix,
        vector,
    )
    shards = shards_kernel if fits_kernel(mesh) else shards_plain
    return jax.shard_map(shards, mesh=mesh, in_specs=in_specs, out_specs=out_specs, check_vma=False)
```

```python
import functools

import jax
import jax.numpy as jnp
import numpy as np
from jax import lax
from jax.experimental import pallas as pl
from jax.experimental.pallas import tpu as pltpu
from jax.sharding import PartitionSpec as P

HD = 80
NORM_EPSILON = 1e-06
MASKED = -1e30
BF = jnp.bfloat16
F32 = jnp.float32


def standardize(values_in):
    centre = jnp.mean(values_in, axis=-1, keepdims=True)
    shifted = values_in - centre
    factor = lax.rsqrt(jnp.mean(shifted * shifted, axis=-1, keepdims=True) + NORM_EPSILON)
    return (shifted * factor, factor)


def norm_back(grad_out, normed, factor, gain):
    scaled = grad_out * gain
    return factor * (
        scaled
        - jnp.mean(scaled, axis=-1, keepdims=True)
        - normed * jnp.mean(scaled * normed, axis=-1, keepdims=True)
    )


def rotary_tables(patch_row, patch_col, head_size):
    quarter = head_size // 4
    inverse = jnp.power(10000.0, -jnp.arange(quarter, dtype=F32) / quarter)
    half_angles = jnp.concatenate(
        [
            patch_row.astype(F32)[..., None] * inverse,
            patch_col.astype(F32)[..., None] * inverse,
        ],
        axis=-1,
    )
    angles = jnp.concatenate([half_angles, half_angles], axis=-1)
    return (jnp.cos(angles)[..., None, :], jnp.sin(angles)[..., None, :])


def rotate(values_in, cosine, sine):
    half_size = values_in.shape[-1] // 2
    turned = jnp.concatenate([-values_in[..., half_size:], values_in[..., :half_size]], axis=-1)
    return values_in * cosine + turned * sine


def unrotate(grad_in, cosine, sine):
    half_size = grad_in.shape[-1] // 2
    moved = grad_in * sine
    return grad_in * cosine + jnp.concatenate(
        [moved[..., half_size:], -moved[..., :half_size]], axis=-1
    )


def masked_scores(queries, keys, picture, factor):
    places = jnp.arange(picture.shape[0], dtype=jnp.int32)
    scores = jnp.einsum("qhd,khd->hqk", queries, keys, preferred_element_type=F32) * factor
    allowed = (picture[:, None] == picture[None, :]) & (
        (picture[None, :] >= 0) | (places[:, None] == places[None, :])
    )
    return jnp.where(allowed[None, :, :], scores, MASKED)


def attend(queries, keys, values, picture):
    scores = masked_scores(queries, keys, picture, HD**-0.5)
    row_max = jnp.max(scores, axis=-1, keepdims=True)
    powers = jnp.exp(scores - row_max)
    totals = jnp.sum(powers, axis=-1, keepdims=True)
    weights = (powers / totals).astype(BF)
    mixed = jnp.einsum("hqk,khd->qhd", weights, values, preferred_element_type=F32)
    return mixed.astype(BF), row_max + jnp.log(totals)


def attend_back(queries, keys, values, picture, grad_mixed, log_total):
    factor = HD**-0.5
    scores = masked_scores(queries, keys, picture, factor)
    probs = jnp.exp(scores - log_total)
    weights = probs.astype(BF)
    grad_values = jnp.einsum("hqk,qhd->khd", weights, grad_mixed, preferred_element_type=F32)
    grad_weights = jnp.einsum("qhd,khd->hqk", grad_mixed, values, preferred_element_type=F32)
    centre = jnp.sum(probs * grad_weights, axis=-1, keepdims=True)
    grad_scores = (probs * (grad_weights - centre)).astype(BF)
    grad_queries = jnp.einsum("hqk,khd->qhd", grad_scores, keys, preferred_element_type=F32) * factor
    grad_keys = jnp.einsum("hqk,qhd->khd", grad_scores, queries, preferred_element_type=F32) * factor
    return grad_queries.astype(BF), grad_keys.astype(BF), grad_values.astype(BF)


def dot(left, right):
    return jnp.dot(left, right, preferred_element_type=F32)


def rows_term(left, right):
    return lax.dot_general(left, right, (((0,), (0,)), ((), ())), preferred_element_type=F32)


def contract_back(grad_out, weight):
    return lax.dot_general(grad_out, weight, (((1,), (1,)), ((), ())), preferred_element_type=F32)


def gather(value, axis_name, axis=0):
    return lax.all_gather(value, axis_name, axis=axis, tiled=True)


def scatter_sum(value, axis_name, axis=0):
    return lax.psum_scatter(value, axis_name, scatter_dimension=axis, tiled=True)

MESH = pl.DeviceIdType.MESH


def mm(left, right):
    return jnp.dot(left, right, preferred_element_type=F32)


def mm_nt(left, right):
    return lax.dot_general(left, right, (((1,), (1,)), ((), ())), preferred_element_type=F32)


def mm_tn(left, right):
    return lax.dot_general(left, right, (((0,), (0,)), ((), ())), preferred_element_type=F32)


def lane_pad(value, lanes):
    gap = lanes - value.shape[1]
    if gap == 0:
        return value
    return jnp.concatenate([value, jnp.zeros((value.shape[0], gap), value.dtype)], axis=1)


def moments(value):
    centre = jnp.mean(value, axis=-1, keepdims=True)
    shifted = value - centre
    factor = lax.rsqrt(jnp.mean(shifted * shifted, axis=-1, keepdims=True) + NORM_EPSILON)
    return shifted * factor, factor


def block_kernel(
    dims,
    tok_in,
    cot_in,
    ids_in,
    row_in,
    col_in,
    vec_ins,
    wave_in,
    wq_in,
    wp_in,
    w1_in,
    w2_in,
    out_ref,
    tgrad_ref,
    rq_ref,
    rp_ref,
    r1_ref,
    r2_ref,
    sums_ref,
    tokb,
    ain,
    cotb,
    plb,
    smb,
    vec,
    bqkv,
    cosb,
    sinb,
    wqc,
    wq,
    wp,
    w1,
    w2,
    qkv,
    lse,
    mixc,
    mix,
    mid,
    mlp,
    act,
    dge,
    snd,
    rsr,
    gmd,
    gp,
    dq4,
    dp4,
    d14,
    d24,
    zq3,
    zp3,
    z13,
    z23,
    dkv,
    smg,
    sg8,
    hq,
    hp,
    h1,
    h2,
    sems,
    local_sems,
):
    n, T, L, D, F, R, hl, P1, CQ, HP = dims
    J = F // 2
    hw = hl * HD
    W = 128
    QW = hl * W
    scale = HD**-0.5
    tile = 256 if D % 256 == 0 else 128
    me = lax.axis_index("seq")
    f = lax.axis_index("fsdp")
    k = f % 2
    j = f // 2
    partner = f + 1 - 2 * k
    x = me % 2
    y = me // 2

    def peer(o):
        return (y + o // 2) % 2 * 2 + (x + o % 2) % 2

    seq_to = [peer(o) for o in range(n)]
    seq_from = seq_to
    near_x, near_y, across = seq_to[1], seq_to[2], seq_to[3]
    edge = (j == 0) | (j == J - 1)
    middle = (j > 0) & (j < J - 1)
    z_to = [2 * ((j + d) % J) + k for d in range(J)]
    z_from = [2 * ((j + J - d) % J) + k for d in range(J)]
    used = {"remote": 0, "local": 0}
    leftover = []

    def take(count=1):
        used["remote"] += count
        return used["remote"] - count

    def remote(src, dst, where, recv):
        return pltpu.make_async_remote_copy(
            src_ref=src,
            dst_ref=dst,
            send_sem=sems.at[take()],
            recv_sem=sems.at[recv],
            device_id=where,
            device_id_type=MESH,
        )

    def when(condition, action):
        pl.when(condition)(action)

    def send(src, dst, where, recv, late=True):
        copy = remote(src, dst, where, recv)
        copy.start()
        if late:
            leftover.append(copy)
        return copy

    def load(src, dst):
        used["local"] += 1
        copy = pltpu.make_async_copy(src, dst, local_sems.at[used["local"] - 1])
        copy.start()
        return copy

    def band(ref, index, size):
        return ref.at[pl.ds(pl.multiple_of(index * size, size), size)]

    def rows_of(index, size):
        return pl.ds(pl.multiple_of(index * size, size), size)

    def strips(total, step, body):
        def run(s, carry):
            body(rows_of(s, step))
            return carry

        lax.fori_loop(0, total // step, run, 0)

    strip = 32

    spot = lax.broadcasted_iota(jnp.int32, (1, T), 1) + me * T
    ids = ids_in[...]
    plb[me, 0:4, :] = jnp.concatenate(
        [
            ids.astype(F32),
            row_in[...].astype(F32),
            col_in[...].astype(F32),
            jnp.where(ids >= 0, ids, -1 - spot).astype(F32),
        ],
        axis=0,
    )
    plb[me, 4:8, :] = jnp.zeros((4, T), F32)
    for row in range(6):
        smb[f, row : row + 1, :] = vec_ins[row][...].astype(F32).reshape(1, R)
    up_bias = vec_ins[6][...].astype(F32).reshape(1, n * R)
    for m in range(n):

        @pl.when(me == m)
        def _():
            smb[f, 6:7, :] = up_bias[:, m * R : (m + 1) * R]

    qkv_bias = vec_ins[7][...].astype(F32).reshape(1, 3 * R)
    for t in range(3):
        smb[f, 7 + t : 8 + t, :] = qkv_bias[:, t * R : (t + 1) * R]
    smb[f, 10:16, :] = jnp.zeros((6, R), F32)

    raw_q = [load(wq_in.at[:, t * D : (t + 1) * D], d24.at[t]) for t in range(3)]
    raw_1 = [load(w1_in.at[:, c * P1 : (c + 1) * P1], d14.at[c]) for c in range(n)]

    barrier = pltpu.get_barrier_semaphore()
    for o in range(1, n):
        pl.semaphore_signal(barrier, inc=1, device_id={"seq": seq_to[o]}, device_id_type=MESH)
    for o in range(1, F):
        pl.semaphore_signal(barrier, inc=1, device_id={"fsdp": (f + o) % F}, device_id_type=MESH)
    pl.semaphore_wait(barrier, n - 1 + F - 1)

    class Spread:
        def __init__(self, src, at, rows):
            self.at, self.rows = at, rows
            self.first = [
                send(src, at(me, 0, rows), {"seq": seq_to[o]}, take()) for o in (1, 2)
            ]

        def relay(self):
            half = self.rows // 2
            self.first[0].wait_recv()
            part = self.at(near_x, 0, half)
            one = send(part, part, {"seq": near_y}, take(), late=False)
            self.first[1].wait_recv()
            part = self.at(near_y, half, self.rows)
            self.second = [one, send(part, part, {"seq": near_x}, take(), late=False)]

        def finish(self):
            for copy in self.second:
                copy.wait_recv()

        def drain(self):
            for copy in self.second:
                copy.wait_send()

    def rows_in(ref):
        return lambda index, lo, hi: ref.at[index, lo:hi]

    plc_copies = [
        send(plb.at[me], plb.at[me], {"seq": seq_to[o]}, take()) for o in range(1, n)
    ]
    tok = Spread(tok_in, rows_in(tokb), T)
    own_tok = load(tok_in, tokb.at[me])

    class Weight:
        def __init__(self, src, buf, rows):
            self.buf, self.rows = buf, rows
            self.own = None
            mine = band(buf, f, rows)
            if src is None:
                src = mine
            else:
                self.own = load(src, mine)
            self.near = send(src, mine, {"fsdp": partner}, take(), late=False)
            landed = {d: take() for d in (1, 2, 3)}
            self.far = {d: remote(src, mine, {"fsdp": z_to[d]}, landed[d]) for d in (1, 2, 3)}
            self.far[2].start()
            when(j != J - 1, self.far[1].start)
            when(j != 0, self.far[3].start)
            part = band(buf, z_from[2], rows)
            self.down = remote(part, part, {"fsdp": k}, landed[1])
            self.up = remote(part, part, {"fsdp": 2 * (J - 1) + k}, landed[3])
            self.relayed = []

        def hop(self):
            self.far[2].wait_recv()
            when(j == 1, self.down.start)
            when(j == J - 2, self.up.start)

        def relay(self):
            for d in (2, 1, 3):
                if d != 2:
                    self.far[d].wait_recv()
                part = band(self.buf, z_from[d], self.rows)
                self.relayed.append(send(part, part, {"fsdp": partner}, take(), late=False))

        def finish(self):
            if self.own is not None:
                self.own.wait()
            self.near.wait_recv()
            for copy in self.relayed:
                copy.wait_recv()

        def drain(self):
            for copy in [self.near, self.far[2]] + self.relayed:
                copy.wait_send()
            when(j != J - 1, self.far[1].wait_send)
            when(j != 0, self.far[3].wait_send)
            when(j == 1, self.down.wait_send)
            when(j == J - 2, self.up.wait_send)

    class Quarter:
        def __init__(self):
            self.cols = pl.ds(pl.multiple_of(x * (D // 2), D // 2), D // 2)
            self.holder, self.other = y == k, y != k
            used["local"] += 1
            self.own = pltpu.make_async_copy(
                wp_in.at[:, self.cols],
                wp.at[j, k, :, self.cols],
                local_sems.at[used["local"] - 1],
            )
            when(self.holder, self.own.start)
            landed = {d: take() for d in (1, 2, 3)}
            mine = wp.at[j, k, :, self.cols]
            self.far = {
                d: remote(wp_in.at[:, self.cols], mine, {"fsdp": z_to[d]}, landed[d])
                for d in (1, 2, 3)
            }
            part = wp.at[z_from[2] // 2, k, :, self.cols]
            self.down = remote(part, part, {"fsdp": k}, landed[1])
            self.up = remote(part, part, {"fsdp": 2 * (J - 1) + k}, landed[3])
            when(self.holder, self.far[2].start)
            when(self.holder & (j != J - 1), self.far[1].start)
            when(self.holder & (j != 0), self.far[3].start)

            def quarter(device_y, device_x, lo, hi):
                cols = pl.ds(pl.multiple_of(device_x * (D // 2), D // 2), D // 2)
                return wp.at[lo:hi, device_y, :, cols]

            to_x, to_y, to_core = {"seq": near_x}, {"seq": near_y}, {"fsdp": partner}
            h = J // 2
            whole = quarter(y, x, 0, J)
            self.give = [remote(whole, whole, where, take()) for where in (to_x, to_y, to_core)]
            q = quarter(y, 1 - x, 0, J)
            self.along_x = remote(q, q, to_core, take())
            q = quarter(y, 1 - x, 0, h)
            self.on_y = remote(q, q, to_y, take())
            q = quarter(1 - y, x, 0, J)
            self.along_y = remote(q, q, to_core, take())
            q = quarter(1 - y, x, h, J)
            self.on_x = remote(q, q, to_x, take())
            q = quarter(1 - y, 1 - x, 0, J)
            self.last = remote(q, q, to_core, take())

        def hop(self):
            @pl.when(self.holder)
            def _():
                self.far[2].wait_recv()
                when(j == 1, self.down.start)
                when(j == J - 2, self.up.start)

        def start_give(self):
            @pl.when(self.holder)
            def _():
                self.own.wait()
                self.far[1].wait_recv()
                self.far[3].wait_recv()
                for copy in self.give:
                    copy.start()

        def relay(self):
            @pl.when(self.holder)
            def _():
                self.give[0].wait_recv()
                self.on_y.start()
                self.along_x.start()

            @pl.when(self.other)
            def _():
                self.give[1].wait_recv()
                self.on_x.start()
                self.along_y.start()

        def relay_last(self):
            @pl.when(self.other)
            def _():
                self.on_y.wait_recv()
                self.on_x.wait_recv()
                self.last.start()

        def finish(self):
            @pl.when(self.holder)
            def _():
                self.along_y.wait_recv()
                self.last.wait_recv()

            @pl.when(self.other)
            def _():
                self.give[2].wait_recv()
                self.along_x.wait_recv()

        def drain(self):
            @pl.when(self.holder)
            def _():
                for copy in self.give + [self.along_x, self.on_y, self.far[2]]:
                    copy.wait_send()
                when(j != J - 1, self.far[1].wait_send)
                when(j != 0, self.far[3].wait_send)
                when(j == 1, self.down.wait_send)
                when(j == J - 2, self.up.wait_send)

            @pl.when(self.other)
            def _():
                for copy in (self.along_y, self.on_x, self.last):
                    copy.wait_send()

    def cut_columns(target, lines):
        for m in range(n):

            @pl.when(me == m)
            def _():
                target[rows_of(f, R), :] = lane_pad(
                    jnp.concatenate(lines(m), axis=1), target.shape[1]
                )

    small_copies = [
        send(smb.at[f], smb.at[f], {"fsdp": (f + o) % F}, take()) for o in range(1, F)
    ]
    for copy in raw_q:
        copy.wait()
    cut_columns(wqc, lambda m: [d24[t, :, m * hw : (m + 1) * hw] for t in range(3)])
    weight_q = Weight(None, wqc, R)
    for copy in raw_1:
        copy.wait()
    cut_columns(
        w1,
        lambda m: [
            d14[b * n * R // P1, :, b * n * R % P1 + m * R : b * n * R % P1 + (m + 1) * R]
            for b in range(F)
        ],
    )

    for copy in small_copies:
        copy.wait_recv()
    for row in range(7):
        vec[row : row + 1, :] = jnp.concatenate(
            [smb[s, row : row + 1, :R] for s in range(F)], axis=1
        )
    groups = 3 * D // R // 3
    heads = []
    for t in range(3):
        start = t * groups + me * (hw // R)
        line = jnp.concatenate(
            [
                smb[(start + b) // 3, pl.ds(7 + (start + b) % 3, 1), :][:, :R]
                for b in range(hw // R)
            ],
            axis=1,
        )
        for h in range(hl):
            heads.append(lane_pad(line[:, h * HD : (h + 1) * HD], W))
    bqkv[...] = jnp.broadcast_to(jnp.concatenate(heads, axis=1), bqkv.shape)

    def vector(row):
        return vec[row : row + 1, :]

    def rows_of_block(i, rows):
        return pl.ds(pl.multiple_of(i * T + rows.start, strip), strip)

    def norm_one(i):
        def body(rows):
            normed, _ = moments(tokb[i, rows, :].astype(F32))
            ain[rows_of_block(i, rows), :] = (normed * vector(0) + vector(1)).astype(BF)

        strips(T, strip, body)

    own_tok.wait()
    norm_one(me)
    tok.relay()
    weight_q.hop()
    weight_p = Quarter()
    weight_1 = Weight(None, w1, R)
    own_cot = load(cot_in, cotb.at[me])
    cot = Spread(cot_in, rows_in(cotb), T)
    norm_one(near_x)
    norm_one(near_y)

    for copy in plc_copies:
        copy.wait_recv()

    def table(i, carry):
        rows = rows_of(i, T)
        turned = jnp.transpose(plb[i], (1, 0))
        lse[rows, hl : hl + 8] = turned
        angle = turned[:, 1:2] * wave_in[0:1, :] + turned[:, 2:3] * wave_in[1:2, :]
        cosb[rows, :] = jnp.cos(angle)
        sinb[rows, :] = jnp.sin(angle) * wave_in[2:3, :]
        return carry

    lax.fori_loop(0, n, table, 0)
    lane = lax.broadcasted_iota(jnp.int32, (1, W), 1)
    low_half = lane < HD // 2

    def swap(value):
        return jnp.where(
            low_half, pltpu.roll(value, W - HD // 2, 1), pltpu.roll(value, HD // 2, 1)
        )

    tok.finish()
    norm_one(across)

    weight_q.relay()
    weight_p.hop()
    weight_q.finish()

    def spread_heads(rows):
        line = wqc[rows, :]
        for h in range(3 * hl):
            wq[rows, h * W : (h + 1) * W] = lane_pad(line[:, h * HD : (h + 1) * HD], W)

    strips(D, R, spread_heads)

    def project(i, carry):
        rows = rows_of(i, T)
        line = ain[rows, :]
        cosine = cosb[rows, :]
        sine = sinb[rows, :]
        for t in range(3):
            part = mm(line, wq[:, t * QW : (t + 1) * QW]) + bqkv[0:1, t * QW : (t + 1) * QW]
            for h in range(hl):
                u = part[:, h * W : (h + 1) * W]
                if t < 2:
                    u = u * cosine + swap(u) * sine
                qkv[rows, t * QW + h * W : t * QW + (h + 1) * W] = u.astype(BF)
        return carry

    weight_p.start_give()
    lax.fori_loop(0, n, project, 0)

    def masked(scores, i):
        ids = jnp.concatenate([plb[b, 3:4, :] for b in range(n)], axis=1)
        own_ids = lse[rows_of(i, T), hl + 3 : hl + 4]
        return jnp.where(own_ids == ids, scores * scale, MASKED)

    mix_send, mix_recv = take(n * (n - 1)), take(n * (n - 1))

    def mix_copy(i, o, peer, source):
        return pltpu.make_async_remote_copy(
            src_ref=mixc.at[source, i],
            dst_ref=mixc.at[source, i],
            send_sem=sems.at[mix_send + i * (n - 1) + o - 1],
            recv_sem=sems.at[mix_recv + i * (n - 1) + o - 1],
            device_id={"seq": peer},
            device_id_type=MESH,
        )

    def attend_block(i, carry):
        rows = rows_of(i, T)
        outs = []
        logs = lse[rows, :]
        for h in range(hl):
            q = qkv[rows, h * W : (h + 1) * W]
            kk = qkv[:, QW + h * W : QW + (h + 1) * W]
            v = qkv[:, 2 * QW + h * W : 2 * QW + (h + 1) * W]
            s = masked(mm_nt(q, kk), i)
            top = jnp.max(s, axis=-1, keepdims=True)
            p = jnp.exp(s - top)
            total = jnp.sum(p, axis=-1, keepdims=True)
            outs.append((mm(p.astype(BF), v) / total)[:, :HD].astype(BF))
            logs = jnp.where(lane == h, top + jnp.log(total), logs)
        lse[rows, :] = logs
        mixc[me, i] = lane_pad(jnp.concatenate(outs, axis=1), HP)
        for o in range(1, n):
            mix_copy(i, o, seq_to[o], me).start()
        return carry

    weight_2 = Weight(w2_in.at[rows_of(me, R)], w2, R)
    lax.fori_loop(0, n // 2, attend_block, 0)
    weight_p.relay()
    weight_1.hop()
    lax.fori_loop(n // 2, n, attend_block, 0)
    weight_p.relay_last()
    cot.relay()
    weight_p.finish()
    tok.drain()

    def proj_weight():
        return wp[...].reshape(D, D)

    def branch(i, carry):
        rows = rows_of(i, T)
        for o in range(1, n):
            mix_copy(i, o, seq_to[o], seq_from[o]).wait_recv()
        mix[rows, :] = jnp.concatenate([mixc[c, i][:, :hw] for c in range(n)], axis=1)
        gmd[...] = mm(mix[rows, :], proj_weight())

        def body(part):
            whole = rows_of_block(i, part)
            value = gmd[part, :] + tokb[i, part, :].astype(F32) + vector(2)

            @pl.when(i == me)
            def _():
                mid[part, :] = value

            normed, _ = moments(value)
            mlp[whole, :] = (normed * vector(3) + vector(4)).astype(BF)

        strips(T, strip, body)
        return carry

    lax.fori_loop(0, n, branch, 0)

    weight_2.hop()
    weight_1.relay()
    weight_1.finish()

    def up(i, carry):
        rows = rows_of(i, T)
        before = mm(mlp[rows, :], w1[...]) + vector(6)
        gate = jax.nn.sigmoid(1.702 * before)
        act[rows, :] = (before * gate).astype(BF)
        dge[rows, :] = (gate + 1.702 * before * gate * (1.0 - gate)).astype(BF)
        return carry

    lax.fori_loop(0, n, up, 0)

    own_cot.wait()
    cot.finish()
    cot.drain()
    weight_2.relay()
    weight_2.finish()

    half = T // 2

    class Scatter:
        def __init__(self, stage, landing, slots):
            self.stage, self.landing = stage, landing
            slot_x, slot_y, pass_x, pass_y = slots
            to_x, to_y = {"seq": near_x}, {"seq": near_y}
            self.pass_a = self.make(across, 0, pass_x, to_x)
            self.pass_b = self.make(across, 1, pass_y, to_y)
            self.last_a = self.make(near_x, 0, slot_x, to_x)
            self.last_b = self.make(near_y, 1, slot_y, to_y)
            self.sum_a = self.make(near_y, 0, slot_y, to_y)
            self.sum_b = self.make(near_x, 1, slot_x, to_x)

        def make(self, block, part, slot, where):
            return remote(
                self.stage.at[self.rows(block, part)],
                self.landing.at[slot, part * half : (part + 1) * half],
                where,
                take(),
            )

        def rows(self, block, part):
            return pl.ds(pl.multiple_of(block * T + part * half, half), half)

        def start(self, t):
            @pl.when(t == 0)
            def _():
                self.pass_a.start()
                self.pass_b.start()

            when(t == 1, self.last_a.start)
            when(t == 2, self.last_b.start)

        def relay(self, slot):
            for part, into, out, block in (
                (0, self.pass_a, self.sum_a, near_y),
                (1, self.pass_b, self.sum_b, near_x),
            ):
                into.wait_recv()

                def body(rows):
                    at = pl.ds(pl.multiple_of(block * T + part * half + rows.start, strip), strip)
                    there = pl.ds(pl.multiple_of(part * half + rows.start, strip), strip)
                    self.stage[at, :] = (
                        self.stage[at, :].astype(F32) + self.landing[slot, there, :].astype(F32)
                    ).astype(BF)

                strips(half, strip, body)
                out.start()

        def wait_recv(self):
            for copy in (self.last_a, self.last_b, self.sum_a, self.sum_b):
                copy.wait_recv()

        def wait_send(self):
            for copy in (
                self.pass_a,
                self.pass_b,
                self.last_a,
                self.last_b,
                self.sum_a,
                self.sum_b,
            ):
                copy.wait_send()

    def block_at(t):
        return peer(((t + 2) % 3 + 1) * (1 - t // 3))

    for i in range(n):
        for o in range(1, n):
            mix_copy(i, o, seq_to[o], me).wait_send()
    scatter_mlp = Scatter(snd, rsr, (0, 1, 2, 2))

    def back(t, carry):
        i = block_at(t)
        rows = rows_of(i, T)
        grad = (mm_nt(cotb[i], w2[...]) * dge[rows, :].astype(F32)).astype(BF)
        dge[rows, :] = grad
        snd[rows, :] = mm_nt(grad, w1[...]).astype(BF)
        scatter_mlp.start(t)
        return carry

    lax.fori_loop(0, n, back, 0)

    class Gradient:
        def __init__(self, grad, other, far, extra, result, lo, width):
            self.grad, self.other, self.far, self.extra = grad, other, far, extra
            self.result, self.lanes = result, slice(lo, lo + width)

        def of(self, index):
            return self.grad.at[rows_of(index, R), self.lanes]

        def exchange(self):
            self.near = [
                send(
                    self.of(2 * c + 1 - k),
                    self.other.at[c, :, self.lanes],
                    {"fsdp": partner},
                    take(),
                )
                for c in range(J)
            ]

        def add_near(self):
            for copy in self.near:
                copy.wait_recv()
            lanes = self.lanes

            def chip(c, carry):
                rows = rows_of(2 * c + k, R)
                self.grad[rows, lanes] = (
                    self.grad[rows, lanes].astype(F32) + self.other[c, :, lanes].astype(F32)
                ).astype(BF)
                return carry

            lax.fori_loop(0, J, chip, 0)
            self.pass_on = remote(
                self.of(2 * (J - 1 - j) + k),
                self.extra.at[:, lanes],
                {"fsdp": 2 * (1 + j // (J - 1)) + k},
                take(),
            )
            self.across = {
                d: remote(
                    self.of(z_to[d]), self.far.at[d - 1, :, lanes], {"fsdp": z_to[d]}, take()
                )
                for d in (1, 2, 3)
            }
            when(edge, self.pass_on.start)
            when(edge, self.across[2].start)
            when(j != J - 1, self.across[1].start)
            when(j != 0, self.across[3].start)

        def hop(self):
            @pl.when(middle)
            def _():
                self.pass_on.wait_recv()
                rows = rows_of(z_to[2], R)
                self.grad[rows, self.lanes] = (
                    self.grad[rows, self.lanes].astype(F32)
                    + self.extra[:, self.lanes].astype(F32)
                ).astype(BF)
                self.across[2].start()

        def add_far(self):
            def total_of(steps):
                def action():
                    for d in steps:
                        self.across[d].wait_recv()
                    total = self.grad[rows_of(f, R), self.lanes].astype(F32)
                    for d in steps:
                        total = total + self.far[d - 1, :, self.lanes].astype(F32)
                    self.other[0, :, self.lanes] = total.astype(BF)

                return action

            when(j == 0, total_of((2, 3)))
            when(middle, total_of((1, 2, 3)))
            when(j == J - 1, total_of((1, 2)))

        def share(self):
            mine = self.other.at[0, :, self.lanes]
            self.keep = load(mine, self.result.at[me, :, self.lanes])
            self.spread = Spread(
                mine, lambda index, lo, hi: self.result.at[index, lo:hi, self.lanes], R
            )

        def relay(self):
            self.spread.relay()

        def finish(self):
            self.keep.wait()
            self.spread.finish()
            self.spread.drain()
            self.across[2].wait_send()
            when(j != J - 1, self.across[1].wait_send)
            when(j != 0, self.across[3].wait_send)
            when(edge, self.pass_on.wait_send)

    CH = CQ // 2
    grad_up = Gradient(w1, d14, z13, h1, r1_ref, 0, P1)
    grad_down = Gradient(w2, d24, z23, h2, r2_ref, 0, D)
    grad_proj = Gradient(gp, dp4, zp3, hp, rp_ref, 0, HP)
    grad_qkv = [Gradient(wqc, dq4, zq3, hq, rq_ref, b * CH, CH) for b in range(2)]

    weight_1.drain()
    weight_2.drain()
    weight_q.drain()

    def up_grad(t, carry):
        w1[rows_of(t, tile), :] = mm_tn(mlp[:, rows_of(t, tile)], dge[...]).astype(BF)
        return carry

    lax.fori_loop(0, D // tile, up_grad, 0)
    grad_up.exchange()
    scatter_mlp.relay(2)

    def down(i, carry):
        rows = rows_of(i, T)
        mlp[rows, :] = mm(act[rows, :], w2[...]).astype(BF)
        return carry

    lax.fori_loop(0, n, down, 0)
    grad_up.add_near()

    def down_grad(t, carry):
        lanes = rows_of(t, tile)
        total = mm_tn(act[0:T, lanes], cotb[0])
        for b in range(1, n):
            total = total + mm_tn(act[b * T : (b + 1) * T, lanes], cotb[b])
        w2[lanes, :] = total.astype(BF)
        return carry

    lax.fori_loop(0, P1 // tile, down_grad, 0)
    grad_down.exchange()

    smg[...] = jnp.zeros(smg.shape, F32)
    scatter_mlp.wait_recv()

    def gather_parts(part):
        whole = rows_of_block(me, part)
        total = snd[whole, :].astype(F32)
        return total + rsr[0, part, :].astype(F32) + rsr[1, part, :].astype(F32)

    def add_sum(row, value):
        smg[row : row + 1, :] = smg[row : row + 1, :] + jnp.sum(value, axis=0, keepdims=True)

    def norm_two_back(part):
        upstream = cotb[me, part, :].astype(F32)
        grad = gather_parts(part)
        normed, factor = moments(mid[part, :])
        scaled = grad * vector(3)
        value = upstream + factor * (
            scaled
            - jnp.mean(scaled, axis=-1, keepdims=True)
            - normed * jnp.mean(scaled * normed, axis=-1, keepdims=True)
        )
        gmd[part, :] = value
        low = value.astype(BF)
        snd[rows_of_block(me, part), :] = low
        add_sum(2, low.astype(F32))
        add_sum(3, grad * normed)
        add_sum(4, grad)
        add_sum(5, upstream)

    strips(T, strip, norm_two_back)
    own_rows = rows_of(me, T)
    low_branch = snd[own_rows, :]
    grad_mixed = mm_nt(low_branch, proj_weight()).astype(BF)
    for c in range(n):
        mixc[0, c] = lane_pad(grad_mixed[:, c * hw : (c + 1) * hw], HP)
        mixc[2, c] = lane_pad(low_branch[:, c * hw : (c + 1) * hw], HP)
    head_copies = [
        send(mixc.at[0, seq_to[o]], mixc.at[1, me], {"seq": seq_to[o]}, take()) for o in range(1, n)
    ]
    branch_copies = [
        send(mixc.at[2, seq_to[o]], mixc.at[3, me], {"seq": seq_to[o]}, take()) for o in range(1, n)
    ]
    mixc[1, me] = mixc[0, me]
    mixc[3, me] = mixc[2, me]

    grad_down.add_near()
    grad_up.hop()

    for copy in head_copies:
        copy.wait_recv()
    scatter_out = Scatter(mlp, tokb, (me, me, near_y, near_x))
    for t in range(n - 1):
        scatter_out.start(t)

    def proj_grad(t, carry):
        lanes = rows_of(t, tile)
        total = mm_tn(mix[0:T, lanes], mixc[3, 0])
        for b in range(1, n):
            total = total + mm_tn(mix[b * T : (b + 1) * T, lanes], mixc[3, b])
        gp[lanes, :] = total.astype(BF)
        return carry

    def qkv_grad(half):
        pair = hl // 2 * W

        def body(t, carry):
            rows = rows_of(t, tile)
            parts = []
            for third in range(3):
                at = third * QW + half * pair
                total = mm_tn(ain[:, rows], qkv[:, at : at + pair])
                parts += [total[:, h * W : h * W + HD].astype(BF) for h in range(hl // 2)]
            wqc[rows, half * CH : (half + 1) * CH] = lane_pad(jnp.concatenate(parts, axis=1), CH)
            return carry

        lax.fori_loop(0, D // tile, body, 0)
        grad_qkv[half].exchange()

    def between(h):
        if h == 0:
            for copy in branch_copies:
                copy.wait_recv()
            lax.fori_loop(0, D // tile, proj_grad, 0)
            grad_proj.exchange()
        if h == 1:
            grad_down.hop()
            grad_proj.add_near()
            qkv_grad(0)
            scatter_out.relay(across)
        if h == 2:
            grad_up.add_far()
            grad_up.share()
            grad_qkv[0].add_near()
            grad_proj.hop()
        if h == 3:
            grad_down.add_far()
            grad_down.share()

    for h in range(hl):
        q_at = slice(h * W, (h + 1) * W)
        k_at = slice(QW + h * W, QW + (h + 1) * W)
        v_at = slice(2 * QW + h * W, 2 * QW + (h + 1) * W)
        dkv[...] = jnp.zeros(dkv.shape, F32)

        def attend_back_block(i, carry):
            rows = rows_of(i, T)
            q = qkv[rows, q_at]
            kk = qkv[:, k_at]
            g = lane_pad(mixc[1, i][:, h * HD : (h + 1) * HD], W)
            p = jnp.exp(masked(mm_nt(q, kk), i) - lse[rows, h : h + 1])
            dp = mm_nt(g, qkv[:, v_at])
            dkv[:, W:] = dkv[:, W:] + mm_tn(p.astype(BF), g)
            centre = jnp.sum(p * dp, axis=-1, keepdims=True)
            ds = (p * (dp - centre)).astype(BF)
            dq = (mm(ds, kk) * scale).astype(BF).astype(F32)
            dkv[:, :W] = dkv[:, :W] + mm_tn(ds, q)
            qkv[rows, q_at] = (dq * cosb[rows, :] - swap(dq) * sinb[rows, :]).astype(BF)
            return carry

        lax.fori_loop(0, n, attend_back_block, 0)

        def turn_back(i, carry):
            rows = rows_of(i, T)
            dk = (dkv[rows, :W] * scale).astype(BF).astype(F32)
            qkv[rows, k_at] = (dk * cosb[rows, :] - swap(dk) * sinb[rows, :]).astype(BF)
            qkv[rows, v_at] = dkv[rows, W:].astype(BF)
            return carry

        lax.fori_loop(0, n, turn_back, 0)
        between(h)

    scatter_mlp.wait_send()
    scatter_attn = Scatter(snd, rsr, (0, 1, 2, 2))

    def attn_back(t, carry):
        i = block_at(t)
        rows = rows_of(i, T)
        snd[rows, :] = mm_nt(qkv[rows, :], wq[...]).astype(BF)
        scatter_attn.start(t)
        return carry

    lax.fori_loop(0, n, attn_back, 0)

    grad_qkv[0].hop()
    qkv_grad(1)
    grad_up.relay()
    scatter_attn.relay(2)
    grad_down.relay()
    grad_proj.add_far()
    grad_proj.share()

    def bias_sums(part):
        smg[6:7, :] = smg[6:7, :] + jnp.sum(dge[part, :].astype(F32), axis=0, keepdims=True)
        line = jnp.sum(qkv[part, :].astype(F32), axis=0, keepdims=True)
        line = lane_pad(
            jnp.concatenate([line[:, h * W : h * W + HD] for h in range(3 * hl)], axis=1), D
        )
        smg[7:8, :] = smg[7:8, :] + line

    grad_qkv[1].add_near()
    strips(L, 64, bias_sums)
    grad_qkv[0].add_far()
    grad_qkv[0].share()
    grad_qkv[1].hop()

    scatter_attn.wait_recv()

    def norm_one_back(part):
        grad = gather_parts(part)
        normed, factor = moments(tokb[me, part, :].astype(F32))
        scaled = grad * vector(0)
        gmd[part, :] = gmd[part, :] + factor * (
            scaled
            - jnp.mean(scaled, axis=-1, keepdims=True)
            - normed * jnp.mean(scaled * normed, axis=-1, keepdims=True)
        )
        add_sum(0, grad * normed)
        add_sum(1, grad)

    strips(T, strip, norm_one_back)
    tokens_out = load(gmd, tgrad_ref)
    sum_copies = [
        send(smg, sg8.at[f], {"fsdp": (f + o) % F}, take()) for o in range(1, F)
    ]
    sg8[f] = smg[...]
    grad_proj.relay()
    grad_qkv[0].relay()
    grad_qkv[1].add_far()
    grad_qkv[1].share()

    scatter_out.wait_recv()

    def write_out(part):
        whole = rows_of_block(me, part)
        total = mid[part, :] + mlp[whole, :].astype(F32) + vector(5)
        for slot in (near_x, near_y):
            total = total + tokb[slot, part, :].astype(F32)
        bias_rows = rows_of_block(me, part)
        ain[bias_rows, :] = total.astype(BF)

    strips(T, strip, write_out)
    block_out = load(band(ain, me, T), out_ref)

    for copy in sum_copies:
        copy.wait_recv()
    total = sg8[0]
    for s in range(1, F):
        total = total + sg8[s]
    plain = lax.broadcasted_iota(jnp.int32, total.shape, 0)
    vec[...] = jnp.where(plain < 8, total, 0.0)
    sums_keep = load(vec, sums_ref.at[me])
    sums_share = [
        send(vec, sums_ref.at[me], {"seq": seq_to[o]}, take()) for o in range(1, n)
    ]

    grads = [grad_up, grad_down, grad_proj] + grad_qkv
    grad_qkv[1].relay()
    for item in grads:
        item.finish()
    for copy in sums_share:
        copy.wait_recv()
    sums_keep.wait()
    tokens_out.wait()
    block_out.wait()
    weight_p.drain()
    scatter_attn.wait_send()
    scatter_out.wait_send()
    for copy in leftover:
        copy.wait_send()
    assert used["remote"] <= sems.shape[0] and used["local"] <= local_sems.shape[0], used


def unpack_kernel(
    dims,
    block_in,
    tokens_in,
    rq_in,
    rp_in,
    r1_in,
    r2_in,
    sums_in,
    block_ref,
    tokens_ref,
    qkv_ref,
    proj_ref,
    up_ref,
    down_ref,
    v0,
    v1,
    v2,
    v3,
    v4,
    v5,
    v6,
    v7,
    block,
    tokens,
    rq,
    rp,
    r1,
    r2,
    sums,
    stage,
    in_sems,
    out_sems,
):
    n, T, L, D, F, R, hl, P1, CQ, HP = dims
    hw = hl * HD
    f = lax.axis_index("fsdp")
    loads = []
    for src, dst in (
        (r2_in, r2),
        (r1_in, r1),
        (rq_in, rq),
        (rp_in, rp),
        (tokens_in, tokens),
        (block_in, block),
        (sums_in, sums),
    ):
        copy = pltpu.make_async_copy(src, dst, in_sems.at[len(loads)])
        copy.start()
        loads.append(copy)
    stores = []

    def store(src, dst):
        copy = pltpu.make_async_copy(src, dst, out_sems.at[len(stores)])
        copy.start()
        stores.append(copy)

    loads[0].wait()
    for c in range(n):
        stage[c] = r2[c].astype(F32)
        store(stage.at[c], down_ref.at[c * R : (c + 1) * R])
    loads[1].wait()
    width = n * R
    for c in range(n):
        blocks = range(c * P1 // width, (c + 1) * P1 // width)
        stage[n + c] = jnp.concatenate(
            [r1[m, :, b * R : (b + 1) * R] for b in blocks for m in range(n)], axis=1
        ).astype(F32)
        store(stage.at[n + c], up_ref.at[:, c * P1 : (c + 1) * P1])
    loads[2].wait()
    for t in range(3):
        stage[2 * n + t] = jnp.concatenate(
            [
                rq[m, :, b * CQ // 2 + t * hw // 2 : b * CQ // 2 + (t + 1) * hw // 2]
                for m in range(n)
                for b in range(2)
            ],
            axis=1,
        ).astype(F32)
        store(stage.at[2 * n + t], qkv_ref.at[:, t * D : (t + 1) * D])
    loads[3].wait()
    stage[2 * n + 3] = jnp.concatenate([rp[m, :, :hw] for m in range(n)], axis=1).astype(F32)
    store(stage.at[2 * n + 3], proj_ref)
    loads[4].wait()
    store(tokens, tokens_ref)
    loads[5].wait()
    store(block, block_ref)
    loads[6].wait()
    per_part = hw // R
    for s in range(F):

        @pl.when(f == s)
        def _():
            own = slice(s * R, (s + 1) * R)
            total = sums[0, 0:6, own]
            for m in range(1, n):
                total = total + sums[m, 0:6, own]
            for row, out in enumerate((v0, v1, v2, v3, v4, v5)):
                out[...] = total[row : row + 1, :].reshape(R)
            lines = [sums[m, 6:7, own] for m in range(n)]
            v6[...] = jnp.concatenate(lines, axis=1).reshape(n * R)
            lines = []
            for b in range(3):
                spot = 3 * s + b
                third, rest = spot // (n * per_part), spot % (n * per_part)
                at = third * hw + rest % per_part * R
                lines.append(sums[rest // per_part, 7:8, at : at + R])
            v7[...] = jnp.concatenate(lines, axis=1).reshape(3 * R)

    for copy in stores:
        copy.wait()


def round_up(value, step):
    return -(-value // step) * step


def shards_kernel(
    tokens,
    picture_ids,
    patch_rows,
    patch_cols,
    norm1_gain,
    norm1_bias,
    qkv_weight,
    qkv_bias,
    proj_weight,
    proj_bias,
    norm2_gain,
    norm2_bias,
    fc1_weight,
    fc1_bias,
    fc2_weight,
    fc2_bias,
    cotangent,
):
    n = lax.axis_size("seq")
    me = lax.axis_index("seq")
    F = lax.axis_size("fsdp")
    f = lax.axis_index("fsdp")
    _, T, D = tokens.shape
    L = n * T
    hl = D // HD // n
    hw = hl * HD
    R = D // F
    hidden = fc1_weight.shape[1]
    P1 = hidden // n
    part = hidden // (F * n)
    CQ = round_up(3 * hw, 128)
    HP = round_up(hw, 128)
    J = F // 2
    W = 128

    lines = (
        norm1_gain,
        norm1_bias,
        proj_bias,
        norm2_gain,
        norm2_bias,
        fc2_bias,
        fc1_bias,
        qkv_bias,
    )
    quarter = HD // 4
    inverse = 10000.0 ** (-np.arange(quarter) / quarter)
    wave = np.zeros((8, W), np.float32)
    for c in range(2):
        wave[0, 2 * c * quarter : (2 * c + 1) * quarter] = inverse
        wave[1, (2 * c + 1) * quarter : (2 * c + 2) * quarter] = inverse
    wave[2] = np.where(np.arange(W) < HD // 2, -1.0, 1.0)
    dims = (n, T, L, D, F, R, hl, P1, CQ, HP)
    anywhere = pl.BlockSpec(memory_space=pl.ANY)
    local = pl.BlockSpec(memory_space=pltpu.VMEM)

    def vmem(shape, dtype=BF):
        return pltpu.VMEM(shape, dtype)

    scratch = [
        vmem((n, T, D)),
        vmem((L, D)),
        vmem((n, T, D)),
        vmem((n, 8, T), F32),
        vmem((F, 16, R), F32),
        vmem((8, D), F32),
        vmem((8, 3 * hl * W), F32),
        vmem((L, W), F32),
        vmem((L, W), F32),
        vmem((D, CQ)),
        vmem((D, 3 * hl * W)),
        vmem((J, 2, R, D)),
        vmem((D, P1)),
        vmem((P1, D)),
        vmem((L, 3 * hl * W)),
        vmem((L, W), F32),
        vmem((n, n, T, HP)),
        vmem((L, D)),
        vmem((T, D), F32),
        vmem((L, D)),
        vmem((L, P1)),
        vmem((L, P1)),
        vmem((L, D)),
        vmem((n - 1, T, D)),
        vmem((T, D), F32),
        vmem((D, HP)),
        vmem((J, R, CQ)),
        vmem((J, R, HP)),
        vmem((J, R, P1)),
        vmem((J, R, D)),
        vmem((J - 1, R, CQ)),
        vmem((J - 1, R, HP)),
        vmem((J - 1, R, P1)),
        vmem((J - 1, R, D)),
        vmem((L, 2 * W), F32),
        vmem((8, D), F32),
        vmem((F, 8, D), F32),
        vmem((R, CQ)),
        vmem((R, HP)),
        vmem((R, P1)),
        vmem((R, D)),
        pltpu.SemaphoreType.DMA((448,)),
        pltpu.SemaphoreType.DMA((24,)),
    ]
    shapes = (
        jax.ShapeDtypeStruct((T, D), BF),
        jax.ShapeDtypeStruct((T, D), F32),
        jax.ShapeDtypeStruct((n, R, CQ), BF),
        jax.ShapeDtypeStruct((n, R, HP), BF),
        jax.ShapeDtypeStruct((n, R, P1), BF),
        jax.ShapeDtypeStruct((n, R, D), BF),
        jax.ShapeDtypeStruct((n, 8, D), F32),
    )
    block_out, tokens_grad, rq, rp, r1, r2, sums = pl.pallas_call(
        functools.partial(block_kernel, dims),
        out_shape=shapes,
        in_specs=[anywhere] * 2 + [local] * 3 + [(local,) * 8] + [local] + [anywhere] * 4,
        out_specs=[anywhere] * 7,
        scratch_shapes=scratch,
        compiler_params=pltpu.CompilerParams(
            collective_id=0, has_side_effects=True, vmem_limit_bytes=67043328
        ),
    )(
        tokens[0],
        cotangent[0],
        picture_ids,
        patch_rows,
        patch_cols,
        lines,
        wave,
        qkv_weight,
        proj_weight,
        fc1_weight,
        fc2_weight,
    )
    stored = (
        jax.ShapeDtypeStruct((T, D), BF),
        jax.ShapeDtypeStruct((T, D), F32),
        jax.ShapeDtypeStruct((R, 3 * D), F32),
        jax.ShapeDtypeStruct((R, D), F32),
        jax.ShapeDtypeStruct((R, hidden), F32),
        jax.ShapeDtypeStruct((n * R, D), F32),
    ) + tuple(jax.ShapeDtypeStruct((size,), F32) for size in [R] * 6 + [n * R, 3 * R])
    block_out, tokens_grad, full_qkv, full_proj, full_up, full_down, *vectors = pl.pallas_call(
        functools.partial(unpack_kernel, dims),
        out_shape=stored,
        in_specs=[anywhere] * 7,
        out_specs=[anywhere] * 6 + [local] * 8,
        scratch_shapes=[
            vmem((T, D)),
            vmem((T, D), F32),
            vmem((n, R, CQ)),
            vmem((n, R, HP)),
            vmem((n, R, P1)),
            vmem((n, R, D)),
            vmem((n, 8, D), F32),
            vmem((4 + 2 * n, R, D), F32),
            pltpu.SemaphoreType.DMA((7,)),
            pltpu.SemaphoreType.DMA((7 + 2 * n,)),
        ],
        compiler_params=pltpu.CompilerParams(vmem_limit_bytes=67043328),
    )(block_out, tokens_grad, rq, rp, r1, r2, sums)
    return (
        block_out[None],
        tokens_grad[None],
        vectors[0],
        vectors[1],
        full_qkv,
        vectors[7],
        full_proj,
        vectors[2],
        vectors[3],
        vectors[4],
        full_up,
        vectors[6],
        full_down,
        vectors[5],
    )


def fits_kernel(mesh):
    return dict(mesh.shape) == {"seq": 4, "fsdp": 8}


def shards_plain(
    tokens,
    picture_ids,
    patch_rows,
    patch_cols,
    norm1_gain,
    norm1_bias,
    qkv_weight,
    qkv_bias,
    proj_weight,
    proj_bias,
    norm2_gain,
    norm2_bias,
    fc1_weight,
    fc1_bias,
    fc2_weight,
    fc2_bias,
    cotangent,
):
    n = lax.axis_size("seq")
    me = lax.axis_index("seq")
    stores = lax.axis_size("fsdp")
    _, own, width = tokens.shape
    heads = width // HD
    local_heads = heads // n
    hw = local_heads * HD
    rows = qkv_weight.shape[0]
    hidden = fc1_weight.shape[1]
    part = hidden // (stores * n)

    def pick(value, axis):
        return lax.dynamic_index_in_dim(value, me, axis, keepdims=False)

    own_qkv = pick(qkv_weight.reshape(rows, 3, n, hw), 2).reshape(rows, 3 * hw)
    own_up = pick(fc1_weight.reshape(rows, stores, n, part), 2).reshape(rows, stores * part)
    own_down = pick(fc2_weight.reshape(n, part, width), 0)
    small = (norm1_gain, norm1_bias, proj_bias, norm2_gain, norm2_bias, fc2_bias, qkv_bias, fc1_bias)
    sizes = [item.shape[0] for item in small]
    packed = gather(jnp.concatenate(small)[None], "fsdp")
    weight_qkv = gather(own_qkv, "fsdp")
    weight_proj = gather(proj_weight, "fsdp")
    weight_up = gather(own_up, "fsdp")
    weight_down = gather(own_down, "fsdp")
    params = []
    start = 0
    for size in sizes:
        params.append(packed[:, start : start + size].reshape(-1).astype(F32))
        start += size
    gain_one, bias_one, bias_proj, gain_two, bias_two, bias_down, bias_qkv, bias_up = params
    bias_qkv = pick(bias_qkv.reshape(3, n, hw), 1).reshape(3 * hw)
    bias_up = pick(bias_up.reshape(stores, n, part), 1).reshape(stores * part)

    places = jnp.stack([picture_ids[0], patch_rows[0], patch_cols[0]])
    places = gather(places, "seq", 1)
    picture = places[0]
    all_tokens = gather(tokens[0], "seq").astype(F32)
    upstream = gather(cotangent[0], "seq")
    length = all_tokens.shape[0]

    def mine(value):
        return lax.dynamic_slice_in_dim(value, me * own, own, 0)

    normed_one, factor_one = standardize(all_tokens)
    attn_input = (normed_one * gain_one + bias_one).astype(BF)
    projected = (dot(attn_input, weight_qkv) + bias_qkv).reshape(length, 3, local_heads, HD)
    cosine, sine = rotary_tables(places[1], places[2], HD)
    queries = rotate(projected[:, 0], cosine, sine).astype(BF)
    keys = rotate(projected[:, 1], cosine, sine).astype(BF)
    values = projected[:, 2].astype(BF)
    mixed_own, log_total = attend(queries, keys, values, picture)
    mixed = gather(mixed_own.reshape(length, hw), "seq", 1)
    middle = all_tokens + dot(mixed, weight_proj) + bias_proj
    normed_two, factor_two = standardize(middle)
    mlp_input = (normed_two * gain_two + bias_two).astype(BF)
    before = dot(mlp_input, weight_up) + bias_up
    gate = jax.nn.sigmoid(1.702 * before)
    activated = (before * gate).astype(BF)
    out_part = dot(activated, weight_down).astype(BF)
    block_out = (mine(middle) + scatter_sum(out_part, "seq").astype(F32) + bias_down).astype(BF)

    grad_down = scatter_sum(rows_term(activated, upstream).astype(BF), "fsdp")
    grad_activated = contract_back(upstream, weight_down)
    grad_before = (grad_activated * (gate + 1.702 * before * gate * (1.0 - gate))).astype(BF)
    grad_up = scatter_sum(rows_term(mlp_input, grad_before).astype(BF), "fsdp")
    grad_mlp_input = scatter_sum(contract_back(grad_before, weight_up).astype(BF), "seq").astype(F32)
    own_upstream = cotangent[0].astype(F32)
    own_two = mine(normed_two)
    grad_middle = own_upstream + norm_back(grad_mlp_input, own_two, mine(factor_two), gain_two)
    grad_branch = grad_middle.astype(BF)
    grad_mixed = contract_back(grad_branch, weight_proj).astype(BF)
    grad_heads = lax.all_to_all(grad_mixed, "seq", split_axis=1, concat_axis=0, tiled=True)
    branch_part = lax.all_to_all(grad_branch, "seq", split_axis=1, concat_axis=0, tiled=True)
    grad_proj = scatter_sum(rows_term(mixed, branch_part).astype(BF), "fsdp")
    grad_queries, grad_keys, grad_values = attend_back(
        queries, keys, values, picture, grad_heads.reshape(length, local_heads, HD), log_total
    )
    grad_projected = jnp.stack(
        [
            unrotate(grad_queries.astype(F32), cosine, sine).astype(BF),
            unrotate(grad_keys.astype(F32), cosine, sine).astype(BF),
            grad_values,
        ],
        axis=1,
    ).reshape(length, 3 * hw)
    grad_qkv = scatter_sum(rows_term(attn_input, grad_projected).astype(BF), "fsdp")
    grad_attn_input = scatter_sum(contract_back(grad_projected, weight_qkv).astype(BF), "seq").astype(F32)
    own_one = mine(normed_one)
    tokens_grad = grad_middle + norm_back(grad_attn_input, own_one, mine(factor_one), gain_one)

    def spread(value, groups):
        empty = jnp.zeros((groups, n, value.shape[0] // groups), F32)
        return lax.dynamic_update_slice_in_dim(
            empty, value.reshape(groups, 1, -1), me, 1
        ).reshape(stores, -1)

    sums = [
        jnp.sum(grad_attn_input * own_one, axis=0).reshape(stores, -1),
        jnp.sum(grad_attn_input, axis=0).reshape(stores, -1),
        jnp.sum(grad_branch.astype(F32), axis=0).reshape(stores, -1),
        jnp.sum(grad_mlp_input * own_two, axis=0).reshape(stores, -1),
        jnp.sum(grad_mlp_input, axis=0).reshape(stores, -1),
        jnp.sum(own_upstream, axis=0).reshape(stores, -1),
        spread(jnp.sum(grad_projected.astype(F32), axis=0), 3),
        spread(jnp.sum(grad_before.astype(F32), axis=0), stores),
    ]
    summed = lax.psum(scatter_sum(jnp.concatenate(sums, axis=1), "fsdp"), "seq")[0]
    finals = []
    start = 0
    for size in sizes:
        finals.append(summed[start : start + size])
        start += size
    full_down = gather(grad_down, "seq").astype(F32)
    full_up = gather(grad_up[None], "seq").reshape(n, rows, stores, part)
    full_up = full_up.transpose(1, 2, 0, 3).reshape(rows, hidden).astype(F32)
    full_proj = gather(grad_proj, "seq", 1).astype(F32)
    full_qkv = gather(grad_qkv[None], "seq").reshape(n, rows, 3, hw)
    full_qkv = full_qkv.transpose(1, 2, 0, 3).reshape(rows, 3 * width).astype(F32)
    return (
        block_out[None],
        tokens_grad[None],
        finals[0],
        finals[1],
        full_qkv,
        finals[6],
        full_proj,
        finals[2],
        finals[3],
        finals[4],
        full_up,
        finals[7],
        full_down,
        finals[5],
    )


def solution(mesh):
    token = P("fsdp", "seq", None)
    place = P("fsdp", "seq")
    vector = P("fsdp")
    matrix = P("fsdp", None)
    in_specs = (
        token,
        place,
        place,
        place,
        vector,
        vector,
        matrix,
        vector,
        matrix,
        vector,
        vector,
        vector,
        matrix,
        vector,
        matrix,
        vector,
        token,
    )
    out_specs = (
        token,
        token,
        vector,
        vector,
        matrix,
        vector,
        matrix,
        vector,
        vector,
        vector,
        matrix,
        vector,
        matrix,
        vector,
    )
    shards = shards_kernel if fits_kernel(mesh) else shards_plain
    return jax.shard_map(shards, mesh=mesh, in_specs=in_specs, out_specs=out_specs, check_vma=False)
```

```python
import functools

import jax
import jax.numpy as jnp
import numpy as np
from jax import lax
from jax.experimental import pallas as pl
from jax.experimental.pallas import tpu as pltpu
from jax.sharding import PartitionSpec as P

HD = 80
NORM_EPSILON = 1e-06
MASKED = -1e30
BF = jnp.bfloat16
F32 = jnp.float32


def standardize(values_in):
    centre = jnp.mean(values_in, axis=-1, keepdims=True)
    shifted = values_in - centre
    factor = lax.rsqrt(jnp.mean(shifted * shifted, axis=-1, keepdims=True) + NORM_EPSILON)
    return (shifted * factor, factor)


def norm_back(grad_out, normed, factor, gain):
    scaled = grad_out * gain
    return factor * (
        scaled
        - jnp.mean(scaled, axis=-1, keepdims=True)
        - normed * jnp.mean(scaled * normed, axis=-1, keepdims=True)
    )


def rotary_tables(patch_row, patch_col, head_size):
    quarter = head_size // 4
    inverse = jnp.power(10000.0, -jnp.arange(quarter, dtype=F32) / quarter)
    half_angles = jnp.concatenate(
        [
            patch_row.astype(F32)[..., None] * inverse,
            patch_col.astype(F32)[..., None] * inverse,
        ],
        axis=-1,
    )
    angles = jnp.concatenate([half_angles, half_angles], axis=-1)
    return (jnp.cos(angles)[..., None, :], jnp.sin(angles)[..., None, :])


def rotate(values_in, cosine, sine):
    half_size = values_in.shape[-1] // 2
    turned = jnp.concatenate([-values_in[..., half_size:], values_in[..., :half_size]], axis=-1)
    return values_in * cosine + turned * sine


def unrotate(grad_in, cosine, sine):
    half_size = grad_in.shape[-1] // 2
    moved = grad_in * sine
    return grad_in * cosine + jnp.concatenate(
        [moved[..., half_size:], -moved[..., :half_size]], axis=-1
    )


def masked_scores(queries, keys, picture, factor):
    places = jnp.arange(picture.shape[0], dtype=jnp.int32)
    scores = jnp.einsum("qhd,khd->hqk", queries, keys, preferred_element_type=F32) * factor
    allowed = (picture[:, None] == picture[None, :]) & (
        (picture[None, :] >= 0) | (places[:, None] == places[None, :])
    )
    return jnp.where(allowed[None, :, :], scores, MASKED)


def attend(queries, keys, values, picture):
    scores = masked_scores(queries, keys, picture, HD**-0.5)
    row_max = jnp.max(scores, axis=-1, keepdims=True)
    powers = jnp.exp(scores - row_max)
    totals = jnp.sum(powers, axis=-1, keepdims=True)
    weights = (powers / totals).astype(BF)
    mixed = jnp.einsum("hqk,khd->qhd", weights, values, preferred_element_type=F32)
    return mixed.astype(BF), row_max + jnp.log(totals)


def attend_back(queries, keys, values, picture, grad_mixed, log_total):
    factor = HD**-0.5
    scores = masked_scores(queries, keys, picture, factor)
    probs = jnp.exp(scores - log_total)
    weights = probs.astype(BF)
    grad_values = jnp.einsum("hqk,qhd->khd", weights, grad_mixed, preferred_element_type=F32)
    grad_weights = jnp.einsum("qhd,khd->hqk", grad_mixed, values, preferred_element_type=F32)
    centre = jnp.sum(probs * grad_weights, axis=-1, keepdims=True)
    grad_scores = (probs * (grad_weights - centre)).astype(BF)
    grad_queries = jnp.einsum("hqk,khd->qhd", grad_scores, keys, preferred_element_type=F32) * factor
    grad_keys = jnp.einsum("hqk,qhd->khd", grad_scores, queries, preferred_element_type=F32) * factor
    return grad_queries.astype(BF), grad_keys.astype(BF), grad_values.astype(BF)


def dot(left, right):
    return jnp.dot(left, right, preferred_element_type=F32)


def rows_term(left, right):
    return lax.dot_general(left, right, (((0,), (0,)), ((), ())), preferred_element_type=F32)


def contract_back(grad_out, weight):
    return lax.dot_general(grad_out, weight, (((1,), (1,)), ((), ())), preferred_element_type=F32)


def gather(value, axis_name, axis=0):
    return lax.all_gather(value, axis_name, axis=axis, tiled=True)


def scatter_sum(value, axis_name, axis=0):
    return lax.psum_scatter(value, axis_name, scatter_dimension=axis, tiled=True)

MESH = pl.DeviceIdType.MESH


def mm(left, right):
    return jnp.dot(left, right, preferred_element_type=F32)


def mm_nt(left, right):
    return lax.dot_general(left, right, (((1,), (1,)), ((), ())), preferred_element_type=F32)


def mm_tn(left, right):
    return lax.dot_general(left, right, (((0,), (0,)), ((), ())), preferred_element_type=F32)


def lane_pad(value, lanes):
    gap = lanes - value.shape[1]
    if gap == 0:
        return value
    return jnp.concatenate([value, jnp.zeros((value.shape[0], gap), value.dtype)], axis=1)


def moments(value):
    centre = jnp.mean(value, axis=-1, keepdims=True)
    shifted = value - centre
    factor = lax.rsqrt(jnp.mean(shifted * shifted, axis=-1, keepdims=True) + NORM_EPSILON)
    return shifted * factor, factor


def block_kernel(
    dims,
    tok_in,
    cot_in,
    ids_in,
    row_in,
    col_in,
    vec_ins,
    wave_in,
    wq_in,
    wp_in,
    w1_in,
    w2_in,
    out_ref,
    tgrad_ref,
    rq_ref,
    rp_ref,
    r1_ref,
    r2_ref,
    sums_ref,
    tokb,
    ain,
    cotb,
    plb,
    smb,
    vec,
    bqkv,
    cosb,
    sinb,
    wqc,
    wq,
    wp,
    w1,
    w2,
    qkv,
    lse,
    mixc,
    mix,
    mid,
    mlp,
    act,
    dge,
    snd,
    rsr,
    gmd,
    gp,
    dq4,
    dp4,
    d14,
    d24,
    zq3,
    zp3,
    z13,
    z23,
    dkv,
    smg,
    sg8,
    hq,
    hp,
    h1,
    h2,
    sems,
    local_sems,
):
    n, T, L, D, F, R, hl, P1, CQ, HP = dims
    J = F // 2
    hw = hl * HD
    W = 128
    QW = hl * W
    scale = HD**-0.5
    tile = 256 if D % 256 == 0 else 128
    me = lax.axis_index("seq")
    f = lax.axis_index("fsdp")
    k = f % 2
    j = f // 2
    partner = f + 1 - 2 * k
    x = me % 2
    y = me // 2

    def peer(o):
        return (y + o // 2) % 2 * 2 + (x + o % 2) % 2

    seq_to = [peer(o) for o in range(n)]
    seq_from = seq_to
    near_x, near_y, across = seq_to[1], seq_to[2], seq_to[3]
    edge = (j == 0) | (j == J - 1)
    middle = (j > 0) & (j < J - 1)
    z_to = [2 * ((j + d) % J) + k for d in range(J)]
    z_from = [2 * ((j + J - d) % J) + k for d in range(J)]
    used = {"remote": 0, "local": 0}
    leftover = []

    def take(count=1):
        used["remote"] += count
        return used["remote"] - count

    def remote(src, dst, where, recv):
        return pltpu.make_async_remote_copy(
            src_ref=src,
            dst_ref=dst,
            send_sem=sems.at[take()],
            recv_sem=sems.at[recv],
            device_id=where,
            device_id_type=MESH,
        )

    def when(condition, action):
        pl.when(condition)(action)

    def send(src, dst, where, recv, late=True):
        copy = remote(src, dst, where, recv)
        copy.start()
        if late:
            leftover.append(copy)
        return copy

    def load(src, dst):
        used["local"] += 1
        copy = pltpu.make_async_copy(src, dst, local_sems.at[used["local"] - 1])
        copy.start()
        return copy

    def band(ref, index, size):
        return ref.at[pl.ds(pl.multiple_of(index * size, size), size)]

    def rows_of(index, size):
        return pl.ds(pl.multiple_of(index * size, size), size)

    def strips(total, step, body):
        def run(s, carry):
            body(rows_of(s, step))
            return carry

        lax.fori_loop(0, total // step, run, 0)

    strip = 32

    spot = lax.broadcasted_iota(jnp.int32, (1, T), 1) + me * T
    ids = ids_in[...]
    plb[me, 0:4, :] = jnp.concatenate(
        [
            ids.astype(F32),
            row_in[...].astype(F32),
            col_in[...].astype(F32),
            jnp.where(ids >= 0, ids, -1 - spot).astype(F32),
        ],
        axis=0,
    )
    plb[me, 4:8, :] = jnp.zeros((4, T), F32)
    for row in range(6):
        smb[f, row : row + 1, :] = vec_ins[row][...].astype(F32).reshape(1, R)
    up_bias = vec_ins[6][...].astype(F32).reshape(1, n * R)
    for m in range(n):

        @pl.when(me == m)
        def _():
            smb[f, 6:7, :] = up_bias[:, m * R : (m + 1) * R]

    qkv_bias = vec_ins[7][...].astype(F32).reshape(1, 3 * R)
    for t in range(3):
        smb[f, 7 + t : 8 + t, :] = qkv_bias[:, t * R : (t + 1) * R]
    smb[f, 10:16, :] = jnp.zeros((6, R), F32)

    raw_q = [load(wq_in.at[:, t * D : (t + 1) * D], d24.at[t]) for t in range(3)]
    raw_1 = [load(w1_in.at[:, c * P1 : (c + 1) * P1], d14.at[c]) for c in range(n)]

    barrier = pltpu.get_barrier_semaphore()
    for o in range(1, n):
        pl.semaphore_signal(barrier, inc=1, device_id={"seq": seq_to[o]}, device_id_type=MESH)
    for o in range(1, F):
        pl.semaphore_signal(barrier, inc=1, device_id={"fsdp": (f + o) % F}, device_id_type=MESH)
    pl.semaphore_wait(barrier, n - 1 + F - 1)

    class Spread:
        def __init__(self, src, at, rows):
            self.at, self.rows = at, rows
            self.first = [
                send(src, at(me, 0, rows), {"seq": seq_to[o]}, take()) for o in (1, 2)
            ]

        def relay(self):
            half = self.rows // 2
            self.first[0].wait_recv()
            part = self.at(near_x, 0, half)
            one = send(part, part, {"seq": near_y}, take(), late=False)
            self.first[1].wait_recv()
            part = self.at(near_y, half, self.rows)
            self.second = [one, send(part, part, {"seq": near_x}, take(), late=False)]

        def finish(self):
            for copy in self.second:
                copy.wait_recv()

        def drain(self):
            for copy in self.second:
                copy.wait_send()

    def rows_in(ref):
        return lambda index, lo, hi: ref.at[index, lo:hi]

    plc_copies = [
        send(plb.at[me], plb.at[me], {"seq": seq_to[o]}, take()) for o in range(1, n)
    ]
    tok = Spread(tok_in, rows_in(tokb), T)
    own_tok = load(tok_in, tokb.at[me])

    class Weight:
        def __init__(self, src, buf, rows):
            self.buf, self.rows = buf, rows
            self.own = None
            mine = band(buf, f, rows)
            if src is None:
                src = mine
            else:
                self.own = load(src, mine)
            self.near = send(src, mine, {"fsdp": partner}, take(), late=False)
            landed = {d: take() for d in (1, 2, 3)}
            self.far = {d: remote(src, mine, {"fsdp": z_to[d]}, landed[d]) for d in (1, 2, 3)}
            self.far[2].start()
            when(j != J - 1, self.far[1].start)
            when(j != 0, self.far[3].start)
            part = band(buf, z_from[2], rows)
            self.down = remote(part, part, {"fsdp": k}, landed[1])
            self.up = remote(part, part, {"fsdp": 2 * (J - 1) + k}, landed[3])
            self.relayed = []

        def hop(self):
            self.far[2].wait_recv()
            when(j == 1, self.down.start)
            when(j == J - 2, self.up.start)

        def relay(self):
            for d in (2, 1, 3):
                if d != 2:
                    self.far[d].wait_recv()
                part = band(self.buf, z_from[d], self.rows)
                self.relayed.append(send(part, part, {"fsdp": partner}, take(), late=False))

        def finish(self):
            if self.own is not None:
                self.own.wait()
            self.near.wait_recv()
            for copy in self.relayed:
                copy.wait_recv()

        def drain(self):
            for copy in [self.near, self.far[2]] + self.relayed:
                copy.wait_send()
            when(j != J - 1, self.far[1].wait_send)
            when(j != 0, self.far[3].wait_send)
            when(j == 1, self.down.wait_send)
            when(j == J - 2, self.up.wait_send)

    class Quarter:
        def __init__(self):
            self.cols = pl.ds(pl.multiple_of(x * (D // 2), D // 2), D // 2)
            self.holder, self.other = y == k, y != k
            used["local"] += 1
            self.own = pltpu.make_async_copy(
                wp_in.at[:, self.cols],
                wp.at[j, k, :, self.cols],
                local_sems.at[used["local"] - 1],
            )
            when(self.holder, self.own.start)
            landed = {d: take() for d in (1, 2, 3)}
            mine = wp.at[j, k, :, self.cols]
            self.far = {
                d: remote(wp_in.at[:, self.cols], mine, {"fsdp": z_to[d]}, landed[d])
                for d in (1, 2, 3)
            }
            part = wp.at[z_from[2] // 2, k, :, self.cols]
            self.down = remote(part, part, {"fsdp": k}, landed[1])
            self.up = remote(part, part, {"fsdp": 2 * (J - 1) + k}, landed[3])
            when(self.holder, self.far[2].start)
            when(self.holder & (j != J - 1), self.far[1].start)
            when(self.holder & (j != 0), self.far[3].start)

            def quarter(device_y, device_x, lo, hi):
                cols = pl.ds(pl.multiple_of(device_x * (D // 2), D // 2), D // 2)
                return wp.at[lo:hi, device_y, :, cols]

            to_x, to_y, to_core = {"seq": near_x}, {"seq": near_y}, {"fsdp": partner}
            h = J // 2
            whole = quarter(y, x, 0, J)
            self.give = [remote(whole, whole, where, take()) for where in (to_x, to_y, to_core)]
            q = quarter(y, 1 - x, 0, J)
            self.along_x = remote(q, q, to_core, take())
            q = quarter(y, 1 - x, 0, h)
            self.on_y = remote(q, q, to_y, take())
            q = quarter(1 - y, x, 0, J)
            self.along_y = remote(q, q, to_core, take())
            q = quarter(1 - y, x, h, J)
            self.on_x = remote(q, q, to_x, take())
            q = quarter(1 - y, 1 - x, 0, J)
            self.last = remote(q, q, to_core, take())

        def hop(self):
            @pl.when(self.holder)
            def _():
                self.far[2].wait_recv()
                when(j == 1, self.down.start)
                when(j == J - 2, self.up.start)

        def start_give(self):
            @pl.when(self.holder)
            def _():
                self.own.wait()
                self.far[1].wait_recv()
                self.far[3].wait_recv()
                for copy in self.give:
                    copy.start()

        def relay(self):
            @pl.when(self.holder)
            def _():
                self.give[0].wait_recv()
                self.on_y.start()
                self.along_x.start()

            @pl.when(self.other)
            def _():
                self.give[1].wait_recv()
                self.on_x.start()
                self.along_y.start()

        def relay_last(self):
            @pl.when(self.other)
            def _():
                self.on_y.wait_recv()
                self.on_x.wait_recv()
                self.last.start()

        def finish(self):
            @pl.when(self.holder)
            def _():
                self.along_y.wait_recv()
                self.last.wait_recv()

            @pl.when(self.other)
            def _():
                self.give[2].wait_recv()
                self.along_x.wait_recv()

        def drain(self):
            @pl.when(self.holder)
            def _():
                for copy in self.give + [self.along_x, self.on_y, self.far[2]]:
                    copy.wait_send()
                when(j != J - 1, self.far[1].wait_send)
                when(j != 0, self.far[3].wait_send)
                when(j == 1, self.down.wait_send)
                when(j == J - 2, self.up.wait_send)

            @pl.when(self.other)
            def _():
                for copy in (self.along_y, self.on_x, self.last):
                    copy.wait_send()

    def cut_columns(target, lines):
        for m in range(n):

            @pl.when(me == m)
            def _():
                target[rows_of(f, R), :] = lane_pad(
                    jnp.concatenate(lines(m), axis=1), target.shape[1]
                )

    small_copies = [
        send(smb.at[f], smb.at[f], {"fsdp": (f + o) % F}, take()) for o in range(1, F)
    ]
    for copy in raw_q:
        copy.wait()
    cut_columns(wqc, lambda m: [d24[t, :, m * hw : (m + 1) * hw] for t in range(3)])
    weight_q = Weight(None, wqc, R)
    for copy in raw_1:
        copy.wait()
    cut_columns(
        w1,
        lambda m: [
            d14[b * n * R // P1, :, b * n * R % P1 + m * R : b * n * R % P1 + (m + 1) * R]
            for b in range(F)
        ],
    )

    for copy in small_copies:
        copy.wait_recv()
    for row in range(7):
        vec[row : row + 1, :] = jnp.concatenate(
            [smb[s, row : row + 1, :R] for s in range(F)], axis=1
        )
    groups = 3 * D // R // 3
    heads = []
    for t in range(3):
        start = t * groups + me * (hw // R)
        line = jnp.concatenate(
            [
                smb[(start + b) // 3, pl.ds(7 + (start + b) % 3, 1), :][:, :R]
                for b in range(hw // R)
            ],
            axis=1,
        )
        for h in range(hl):
            heads.append(lane_pad(line[:, h * HD : (h + 1) * HD], W))
    bqkv[...] = jnp.broadcast_to(jnp.concatenate(heads, axis=1), bqkv.shape)

    def vector(row):
        return vec[row : row + 1, :]

    def rows_of_block(i, rows):
        return pl.ds(pl.multiple_of(i * T + rows.start, strip), strip)

    def norm_one(i):
        def body(rows):
            normed, _ = moments(tokb[i, rows, :].astype(F32))
            ain[rows_of_block(i, rows), :] = (normed * vector(0) + vector(1)).astype(BF)

        strips(T, strip, body)

    own_tok.wait()
    norm_one(me)
    tok.relay()
    weight_q.hop()
    weight_p = Quarter()
    weight_1 = Weight(None, w1, R)
    own_cot = load(cot_in, cotb.at[me])
    cot = Spread(cot_in, rows_in(cotb), T)
    norm_one(near_x)
    norm_one(near_y)

    for copy in plc_copies:
        copy.wait_recv()

    def table(i, carry):
        rows = rows_of(i, T)
        turned = jnp.transpose(plb[i], (1, 0))
        lse[rows, hl : hl + 8] = turned
        angle = turned[:, 1:2] * wave_in[0:1, :] + turned[:, 2:3] * wave_in[1:2, :]
        cosb[rows, :] = jnp.cos(angle)
        sinb[rows, :] = jnp.sin(angle) * wave_in[2:3, :]
        return carry

    lax.fori_loop(0, n, table, 0)
    lane = lax.broadcasted_iota(jnp.int32, (1, W), 1)
    low_half = lane < HD // 2

    def swap(value):
        return jnp.where(
            low_half, pltpu.roll(value, W - HD // 2, 1), pltpu.roll(value, HD // 2, 1)
        )

    tok.finish()
    norm_one(across)

    weight_q.relay()
    weight_p.hop()
    weight_q.finish()

    def spread_heads(rows):
        line = wqc[rows, :]
        for h in range(3 * hl):
            wq[rows, h * W : (h + 1) * W] = lane_pad(line[:, h * HD : (h + 1) * HD], W)

    strips(D, R, spread_heads)

    def project(i, carry):
        rows = rows_of(i, T)
        line = ain[rows, :]
        cosine = cosb[rows, :]
        sine = sinb[rows, :]
        for t in range(3):
            part = mm(line, wq[:, t * QW : (t + 1) * QW]) + bqkv[0:1, t * QW : (t + 1) * QW]
            for h in range(hl):
                u = part[:, h * W : (h + 1) * W]
                if t < 2:
                    u = u * cosine + swap(u) * sine
                qkv[rows, t * QW + h * W : t * QW + (h + 1) * W] = u.astype(BF)
        return carry

    weight_p.start_give()
    lax.fori_loop(0, n, project, 0)

    def masked(scores, i):
        ids = jnp.concatenate([plb[b, 3:4, :] for b in range(n)], axis=1)
        own_ids = lse[rows_of(i, T), hl + 3 : hl + 4]
        return jnp.where(own_ids == ids, scores * scale, MASKED)

    mix_send, mix_recv = take(4 * n), take(4 * n)

    def mix_copy(i, spot, part, where):
        return pltpu.make_async_remote_copy(
            src_ref=part,
            dst_ref=part,
            send_sem=sems.at[mix_send + 4 * i + spot],
            recv_sem=sems.at[mix_recv + 4 * i + spot],
            device_id={"seq": where},
            device_id_type=MESH,
        )

    def mix_first(i, o, source):
        return mix_copy(i, o - 1, mixc.at[source, i], seq_to[o])

    def mix_pass(i, o):
        part = mixc.at[seq_to[o], i, (o - 1) * T // 2 : o * T // 2]
        return mix_copy(i, o + 1, part, seq_to[3 - o])

    def mix_relay(i):
        for o in (1, 2):
            mix_first(i, o, seq_to[o]).wait_recv()
            mix_pass(i, o).start()

    def attend_block(i, carry):
        rows = rows_of(i, T)
        outs = []
        logs = lse[rows, :]
        for h in range(hl):
            q = qkv[rows, h * W : (h + 1) * W]
            kk = qkv[:, QW + h * W : QW + (h + 1) * W]
            v = qkv[:, 2 * QW + h * W : 2 * QW + (h + 1) * W]
            s = masked(mm_nt(q, kk), i)
            top = jnp.max(s, axis=-1, keepdims=True)
            p = jnp.exp(s - top)
            total = jnp.sum(p, axis=-1, keepdims=True)
            outs.append((mm(p.astype(BF), v) / total)[:, :HD].astype(BF))
            logs = jnp.where(lane == h, top + jnp.log(total), logs)
        lse[rows, :] = logs
        mixc[me, i] = lane_pad(jnp.concatenate(outs, axis=1), HP)
        for o in (1, 2):
            mix_first(i, o, me).start()
        when(i > 0, lambda: mix_relay(i - 1))
        return carry

    weight_2 = Weight(w2_in.at[rows_of(me, R)], w2, R)
    lax.fori_loop(0, n // 2, attend_block, 0)
    weight_p.relay()
    weight_1.hop()
    lax.fori_loop(n // 2, n, attend_block, 0)
    weight_p.relay_last()
    weight_p.finish()
    tok.drain()

    def proj_weight():
        return wp[...].reshape(D, D)

    def branch(i, carry):
        rows = rows_of(i, T)
        for o in (1, 2):
            mix_pass(i, o).wait_recv()
        mix[rows, :] = jnp.concatenate([mixc[c, i][:, :hw] for c in range(n)], axis=1)
        gmd[...] = mm(mix[rows, :], proj_weight())

        def body(part):
            whole = rows_of_block(i, part)
            value = gmd[part, :] + tokb[i, part, :].astype(F32) + vector(2)

            @pl.when(i == me)
            def _():
                mid[part, :] = value

            normed, _ = moments(value)
            mlp[whole, :] = (normed * vector(3) + vector(4)).astype(BF)

        strips(T, strip, body)
        return carry

    lax.fori_loop(0, 1, branch, 0)
    mix_relay(n - 1)
    cot.relay()
    lax.fori_loop(1, n, branch, 0)

    weight_2.hop()
    weight_1.relay()
    weight_1.finish()

    def up(i, carry):
        rows = rows_of(i, T)
        before = mm(mlp[rows, :], w1[...]) + vector(6)
        gate = jax.nn.sigmoid(1.702 * before)
        act[rows, :] = (before * gate).astype(BF)
        dge[rows, :] = (gate + 1.702 * before * gate * (1.0 - gate)).astype(BF)
        return carry

    lax.fori_loop(0, n, up, 0)

    own_cot.wait()
    cot.finish()
    cot.drain()
    weight_2.relay()
    weight_2.finish()

    half = T // 2

    class Scatter:
        def __init__(self, stage, landing, slots):
            self.stage, self.landing = stage, landing
            slot_x, slot_y, pass_x, pass_y = slots
            to_x, to_y = {"seq": near_x}, {"seq": near_y}
            self.pass_a = self.make(across, 0, pass_x, to_x)
            self.pass_b = self.make(across, 1, pass_y, to_y)
            self.last_a = self.make(near_x, 0, slot_x, to_x)
            self.last_b = self.make(near_y, 1, slot_y, to_y)
            self.sum_a = self.make(near_y, 0, slot_y, to_y)
            self.sum_b = self.make(near_x, 1, slot_x, to_x)

        def make(self, block, part, slot, where):
            return remote(
                self.stage.at[self.rows(block, part)],
                self.landing.at[slot, part * half : (part + 1) * half],
                where,
                take(),
            )

        def rows(self, block, part):
            return pl.ds(pl.multiple_of(block * T + part * half, half), half)

        def start(self, t):
            @pl.when(t == 0)
            def _():
                self.pass_a.start()
                self.pass_b.start()

            when(t == 1, self.last_a.start)
            when(t == 2, self.last_b.start)

        def relay(self, slot):
            for part, into, out, block in (
                (0, self.pass_a, self.sum_a, near_y),
                (1, self.pass_b, self.sum_b, near_x),
            ):
                into.wait_recv()

                def body(rows):
                    at = pl.ds(pl.multiple_of(block * T + part * half + rows.start, strip), strip)
                    there = pl.ds(pl.multiple_of(part * half + rows.start, strip), strip)
                    self.stage[at, :] = (
                        self.stage[at, :].astype(F32) + self.landing[slot, there, :].astype(F32)
                    ).astype(BF)

                strips(half, strip, body)
                out.start()

        def wait_recv(self):
            for copy in (self.last_a, self.last_b, self.sum_a, self.sum_b):
                copy.wait_recv()

        def wait_send(self):
            for copy in (
                self.pass_a,
                self.pass_b,
                self.last_a,
                self.last_b,
                self.sum_a,
                self.sum_b,
            ):
                copy.wait_send()

    def block_at(t):
        return peer(((t + 2) % 3 + 1) * (1 - t // 3))

    for i in range(n):
        for o in (1, 2):
            mix_first(i, o, me).wait_send()
            mix_pass(i, o).wait_send()
    scatter_mlp = Scatter(snd, rsr, (0, 1, 2, 2))

    def back(t, carry):
        i = block_at(t)
        rows = rows_of(i, T)
        grad = (mm_nt(cotb[i], w2[...]) * dge[rows, :].astype(F32)).astype(BF)
        dge[rows, :] = grad
        snd[rows, :] = mm_nt(grad, w1[...]).astype(BF)
        scatter_mlp.start(t)
        return carry

    lax.fori_loop(0, n, back, 0)

    class Gradient:
        def __init__(self, grad, other, far, extra, result, lo, width):
            self.grad, self.other, self.far, self.extra = grad, other, far, extra
            self.result, self.lanes = result, slice(lo, lo + width)

        def of(self, index):
            return self.grad.at[rows_of(index, R), self.lanes]

        def exchange(self):
            self.near = [
                send(
                    self.of(2 * c + 1 - k),
                    self.other.at[c, :, self.lanes],
                    {"fsdp": partner},
                    take(),
                )
                for c in range(J)
            ]

        def add_near(self):
            for copy in self.near:
                copy.wait_recv()
            lanes = self.lanes

            def chip(c, carry):
                rows = rows_of(2 * c + k, R)
                self.grad[rows, lanes] = (
                    self.grad[rows, lanes].astype(F32) + self.other[c, :, lanes].astype(F32)
                ).astype(BF)
                return carry

            lax.fori_loop(0, J, chip, 0)
            self.pass_on = remote(
                self.of(2 * (J - 1 - j) + k),
                self.extra.at[:, lanes],
                {"fsdp": 2 * (1 + j // (J - 1)) + k},
                take(),
            )
            self.across = {
                d: remote(
                    self.of(z_to[d]), self.far.at[d - 1, :, lanes], {"fsdp": z_to[d]}, take()
                )
                for d in (1, 2, 3)
            }
            when(edge, self.pass_on.start)
            when(edge, self.across[2].start)
            when(j != J - 1, self.across[1].start)
            when(j != 0, self.across[3].start)

        def hop(self):
            @pl.when(middle)
            def _():
                self.pass_on.wait_recv()
                rows = rows_of(z_to[2], R)
                self.grad[rows, self.lanes] = (
                    self.grad[rows, self.lanes].astype(F32)
                    + self.extra[:, self.lanes].astype(F32)
                ).astype(BF)
                self.across[2].start()

        def add_far(self):
            def total_of(steps):
                def action():
                    for d in steps:
                        self.across[d].wait_recv()
                    total = self.grad[rows_of(f, R), self.lanes].astype(F32)
                    for d in steps:
                        total = total + self.far[d - 1, :, self.lanes].astype(F32)
                    self.other[0, :, self.lanes] = total.astype(BF)

                return action

            when(j == 0, total_of((2, 3)))
            when(middle, total_of((1, 2, 3)))
            when(j == J - 1, total_of((1, 2)))

        def share(self):
            mine = self.other.at[0, :, self.lanes]
            self.keep = load(mine, self.result.at[me, :, self.lanes])
            self.spread = Spread(
                mine, lambda index, lo, hi: self.result.at[index, lo:hi, self.lanes], R
            )

        def relay(self):
            self.spread.relay()

        def finish(self):
            self.keep.wait()
            self.spread.finish()
            self.spread.drain()
            self.across[2].wait_send()
            when(j != J - 1, self.across[1].wait_send)
            when(j != 0, self.across[3].wait_send)
            when(edge, self.pass_on.wait_send)

    CH = CQ // 2
    grad_up = Gradient(w1, d14, z13, h1, r1_ref, 0, P1)
    grad_down = Gradient(w2, d24, z23, h2, r2_ref, 0, D)
    grad_proj = Gradient(gp, dp4, zp3, hp, rp_ref, 0, HP)
    grad_qkv = [Gradient(wqc, dq4, zq3, hq, rq_ref, b * CH, CH) for b in range(2)]

    weight_1.drain()
    weight_2.drain()
    weight_q.drain()

    def up_grad(t, carry):
        w1[rows_of(t, tile), :] = mm_tn(mlp[:, rows_of(t, tile)], dge[...]).astype(BF)
        return carry

    lax.fori_loop(0, D // tile, up_grad, 0)
    grad_up.exchange()
    scatter_mlp.relay(2)

    def down(i, carry):
        rows = rows_of(i, T)
        mlp[rows, :] = mm(act[rows, :], w2[...]).astype(BF)
        return carry

    lax.fori_loop(0, n, down, 0)
    grad_up.add_near()

    def down_grad(t, carry):
        lanes = rows_of(t, tile)
        total = mm_tn(act[0:T, lanes], cotb[0])
        for b in range(1, n):
            total = total + mm_tn(act[b * T : (b + 1) * T, lanes], cotb[b])
        w2[lanes, :] = total.astype(BF)
        return carry

    lax.fori_loop(0, P1 // tile, down_grad, 0)
    grad_down.exchange()

    smg[...] = jnp.zeros(smg.shape, F32)
    scatter_mlp.wait_recv()

    def gather_parts(part):
        whole = rows_of_block(me, part)
        total = snd[whole, :].astype(F32)
        return total + rsr[0, part, :].astype(F32) + rsr[1, part, :].astype(F32)

    def add_sum(row, value):
        smg[row : row + 1, :] = smg[row : row + 1, :] + jnp.sum(value, axis=0, keepdims=True)

    def norm_two_back(part):
        upstream = cotb[me, part, :].astype(F32)
        grad = gather_parts(part)
        normed, factor = moments(mid[part, :])
        scaled = grad * vector(3)
        value = upstream + factor * (
            scaled
            - jnp.mean(scaled, axis=-1, keepdims=True)
            - normed * jnp.mean(scaled * normed, axis=-1, keepdims=True)
        )
        gmd[part, :] = value
        low = value.astype(BF)
        snd[rows_of_block(me, part), :] = low
        add_sum(2, low.astype(F32))
        add_sum(3, grad * normed)
        add_sum(4, grad)
        add_sum(5, upstream)

    strips(T, strip, norm_two_back)
    own_rows = rows_of(me, T)
    low_branch = snd[own_rows, :]
    grad_mixed = mm_nt(low_branch, proj_weight()).astype(BF)
    for c in range(n):
        mixc[0, c] = lane_pad(grad_mixed[:, c * hw : (c + 1) * hw], HP)
        mixc[2, c] = lane_pad(low_branch[:, c * hw : (c + 1) * hw], HP)
    head_copies = [
        send(mixc.at[0, seq_to[o]], mixc.at[1, me], {"seq": seq_to[o]}, take()) for o in range(1, n)
    ]
    branch_copies = [
        send(mixc.at[2, seq_to[o]], mixc.at[3, me], {"seq": seq_to[o]}, take()) for o in range(1, n)
    ]
    mixc[1, me] = mixc[0, me]
    mixc[3, me] = mixc[2, me]

    grad_down.add_near()
    grad_up.hop()

    for copy in head_copies:
        copy.wait_recv()
    scatter_out = Scatter(mlp, tokb, (me, me, near_y, near_x))
    for t in range(n - 1):
        scatter_out.start(t)

    def proj_grad(t, carry):
        lanes = rows_of(t, tile)
        total = mm_tn(mix[0:T, lanes], mixc[3, 0])
        for b in range(1, n):
            total = total + mm_tn(mix[b * T : (b + 1) * T, lanes], mixc[3, b])
        gp[lanes, :] = total.astype(BF)
        return carry

    def qkv_grad(half):
        pair = hl // 2 * W

        def body(t, carry):
            rows = rows_of(t, tile)
            parts = []
            for third in range(3):
                at = third * QW + half * pair
                total = mm_tn(ain[:, rows], qkv[:, at : at + pair])
                parts += [total[:, h * W : h * W + HD].astype(BF) for h in range(hl // 2)]
            wqc[rows, half * CH : (half + 1) * CH] = lane_pad(jnp.concatenate(parts, axis=1), CH)
            return carry

        lax.fori_loop(0, D // tile, body, 0)
        grad_qkv[half].exchange()

    def between(h):
        if h == 0:
            for copy in branch_copies:
                copy.wait_recv()
            lax.fori_loop(0, D // tile, proj_grad, 0)
            grad_proj.exchange()
        if h == 1:
            grad_down.hop()
            grad_proj.add_near()
            qkv_grad(0)
            scatter_out.relay(across)
        if h == 2:
            grad_up.add_far()
            grad_up.share()
            grad_qkv[0].add_near()
            grad_proj.hop()
        if h == 3:
            grad_down.add_far()
            grad_down.share()

    for h in range(hl):
        q_at = slice(h * W, (h + 1) * W)
        k_at = slice(QW + h * W, QW + (h + 1) * W)
        v_at = slice(2 * QW + h * W, 2 * QW + (h + 1) * W)
        dkv[...] = jnp.zeros(dkv.shape, F32)

        def attend_back_block(i, carry):
            rows = rows_of(i, T)
            q = qkv[rows, q_at]
            kk = qkv[:, k_at]
            g = lane_pad(mixc[1, i][:, h * HD : (h + 1) * HD], W)
            p = jnp.exp(masked(mm_nt(q, kk), i) - lse[rows, h : h + 1])
            dp = mm_nt(g, qkv[:, v_at])
            dkv[:, W:] = dkv[:, W:] + mm_tn(p.astype(BF), g)
            centre = jnp.sum(p * dp, axis=-1, keepdims=True)
            ds = (p * (dp - centre)).astype(BF)
            dq = (mm(ds, kk) * scale).astype(BF).astype(F32)
            dkv[:, :W] = dkv[:, :W] + mm_tn(ds, q)
            qkv[rows, q_at] = (dq * cosb[rows, :] - swap(dq) * sinb[rows, :]).astype(BF)
            return carry

        lax.fori_loop(0, n, attend_back_block, 0)

        def turn_back(i, carry):
            rows = rows_of(i, T)
            dk = (dkv[rows, :W] * scale).astype(BF).astype(F32)
            qkv[rows, k_at] = (dk * cosb[rows, :] - swap(dk) * sinb[rows, :]).astype(BF)
            qkv[rows, v_at] = dkv[rows, W:].astype(BF)
            return carry

        lax.fori_loop(0, n, turn_back, 0)
        between(h)

    scatter_mlp.wait_send()
    scatter_attn = Scatter(snd, rsr, (0, 1, 2, 2))

    def attn_back(t, carry):
        i = block_at(t)
        rows = rows_of(i, T)
        snd[rows, :] = mm_nt(qkv[rows, :], wq[...]).astype(BF)
        scatter_attn.start(t)
        return carry

    lax.fori_loop(0, n, attn_back, 0)

    grad_qkv[0].hop()
    qkv_grad(1)
    grad_up.relay()
    scatter_attn.relay(2)
    grad_down.relay()
    grad_proj.add_far()
    grad_proj.share()

    def bias_sums(part):
        smg[6:7, :] = smg[6:7, :] + jnp.sum(dge[part, :].astype(F32), axis=0, keepdims=True)
        line = jnp.sum(qkv[part, :].astype(F32), axis=0, keepdims=True)
        line = lane_pad(
            jnp.concatenate([line[:, h * W : h * W + HD] for h in range(3 * hl)], axis=1), D
        )
        smg[7:8, :] = smg[7:8, :] + line

    grad_qkv[1].add_near()
    strips(L, 64, bias_sums)
    grad_qkv[0].add_far()
    grad_qkv[0].share()
    grad_qkv[1].hop()

    scatter_attn.wait_recv()

    def norm_one_back(part):
        grad = gather_parts(part)
        normed, factor = moments(tokb[me, part, :].astype(F32))
        scaled = grad * vector(0)
        gmd[part, :] = gmd[part, :] + factor * (
            scaled
            - jnp.mean(scaled, axis=-1, keepdims=True)
            - normed * jnp.mean(scaled * normed, axis=-1, keepdims=True)
        )
        add_sum(0, grad * normed)
        add_sum(1, grad)

    strips(T, strip, norm_one_back)
    tokens_out = load(gmd, tgrad_ref)
    sum_copies = [
        send(smg, sg8.at[f], {"fsdp": (f + o) % F}, take()) for o in range(1, F)
    ]
    sg8[f] = smg[...]
    grad_proj.relay()
    grad_qkv[0].relay()
    grad_qkv[1].add_far()
    grad_qkv[1].share()

    scatter_out.wait_recv()

    def write_out(part):
        whole = rows_of_block(me, part)
        total = mid[part, :] + mlp[whole, :].astype(F32) + vector(5)
        for slot in (near_x, near_y):
            total = total + tokb[slot, part, :].astype(F32)
        bias_rows = rows_of_block(me, part)
        ain[bias_rows, :] = total.astype(BF)

    strips(T, strip, write_out)
    block_out = load(band(ain, me, T), out_ref)

    for copy in sum_copies:
        copy.wait_recv()
    total = sg8[0]
    for s in range(1, F):
        total = total + sg8[s]
    plain = lax.broadcasted_iota(jnp.int32, total.shape, 0)
    vec[...] = jnp.where(plain < 8, total, 0.0)
    sums_keep = load(vec, sums_ref.at[me])
    sums_share = [
        send(vec, sums_ref.at[me], {"seq": seq_to[o]}, take()) for o in range(1, n)
    ]

    grads = [grad_up, grad_down, grad_proj] + grad_qkv
    grad_qkv[1].relay()
    for item in grads:
        item.finish()
    for copy in sums_share:
        copy.wait_recv()
    sums_keep.wait()
    tokens_out.wait()
    block_out.wait()
    weight_p.drain()
    scatter_attn.wait_send()
    scatter_out.wait_send()
    for copy in leftover:
        copy.wait_send()
    assert used["remote"] <= sems.shape[0] and used["local"] <= local_sems.shape[0], used


def unpack_kernel(
    dims,
    block_in,
    tokens_in,
    rq_in,
    rp_in,
    r1_in,
    r2_in,
    sums_in,
    block_ref,
    tokens_ref,
    qkv_ref,
    proj_ref,
    up_ref,
    down_ref,
    v0,
    v1,
    v2,
    v3,
    v4,
    v5,
    v6,
    v7,
    block,
    tokens,
    rq,
    rp,
    r1,
    r2,
    sums,
    stage,
    in_sems,
    out_sems,
):
    n, T, L, D, F, R, hl, P1, CQ, HP = dims
    hw = hl * HD
    f = lax.axis_index("fsdp")
    loads = []
    for src, dst in (
        (r2_in, r2),
        (r1_in, r1),
        (rq_in, rq),
        (rp_in, rp),
        (tokens_in, tokens),
        (block_in, block),
        (sums_in, sums),
    ):
        copy = pltpu.make_async_copy(src, dst, in_sems.at[len(loads)])
        copy.start()
        loads.append(copy)
    stores = []

    def store(src, dst):
        copy = pltpu.make_async_copy(src, dst, out_sems.at[len(stores)])
        copy.start()
        stores.append(copy)

    loads[0].wait()
    for c in range(n):
        stage[c] = r2[c].astype(F32)
        store(stage.at[c], down_ref.at[c * R : (c + 1) * R])
    loads[1].wait()
    width = n * R
    for c in range(n):
        blocks = range(c * P1 // width, (c + 1) * P1 // width)
        stage[n + c] = jnp.concatenate(
            [r1[m, :, b * R : (b + 1) * R] for b in blocks for m in range(n)], axis=1
        ).astype(F32)
        store(stage.at[n + c], up_ref.at[:, c * P1 : (c + 1) * P1])
    loads[2].wait()
    for t in range(3):
        stage[2 * n + t] = jnp.concatenate(
            [
                rq[m, :, b * CQ // 2 + t * hw // 2 : b * CQ // 2 + (t + 1) * hw // 2]
                for m in range(n)
                for b in range(2)
            ],
            axis=1,
        ).astype(F32)
        store(stage.at[2 * n + t], qkv_ref.at[:, t * D : (t + 1) * D])
    loads[3].wait()
    stage[2 * n + 3] = jnp.concatenate([rp[m, :, :hw] for m in range(n)], axis=1).astype(F32)
    store(stage.at[2 * n + 3], proj_ref)
    loads[4].wait()
    store(tokens, tokens_ref)
    loads[5].wait()
    store(block, block_ref)
    loads[6].wait()
    per_part = hw // R
    for s in range(F):

        @pl.when(f == s)
        def _():
            own = slice(s * R, (s + 1) * R)
            total = sums[0, 0:6, own]
            for m in range(1, n):
                total = total + sums[m, 0:6, own]
            for row, out in enumerate((v0, v1, v2, v3, v4, v5)):
                out[...] = total[row : row + 1, :].reshape(R)
            lines = [sums[m, 6:7, own] for m in range(n)]
            v6[...] = jnp.concatenate(lines, axis=1).reshape(n * R)
            lines = []
            for b in range(3):
                spot = 3 * s + b
                third, rest = spot // (n * per_part), spot % (n * per_part)
                at = third * hw + rest % per_part * R
                lines.append(sums[rest // per_part, 7:8, at : at + R])
            v7[...] = jnp.concatenate(lines, axis=1).reshape(3 * R)

    for copy in stores:
        copy.wait()


def round_up(value, step):
    return -(-value // step) * step


def shards_kernel(
    tokens,
    picture_ids,
    patch_rows,
    patch_cols,
    norm1_gain,
    norm1_bias,
    qkv_weight,
    qkv_bias,
    proj_weight,
    proj_bias,
    norm2_gain,
    norm2_bias,
    fc1_weight,
    fc1_bias,
    fc2_weight,
    fc2_bias,
    cotangent,
):
    n = lax.axis_size("seq")
    me = lax.axis_index("seq")
    F = lax.axis_size("fsdp")
    f = lax.axis_index("fsdp")
    _, T, D = tokens.shape
    L = n * T
    hl = D // HD // n
    hw = hl * HD
    R = D // F
    hidden = fc1_weight.shape[1]
    P1 = hidden // n
    part = hidden // (F * n)
    CQ = round_up(3 * hw, 128)
    HP = round_up(hw, 128)
    J = F // 2
    W = 128

    lines = (
        norm1_gain,
        norm1_bias,
        proj_bias,
        norm2_gain,
        norm2_bias,
        fc2_bias,
        fc1_bias,
        qkv_bias,
    )
    quarter = HD // 4
    inverse = 10000.0 ** (-np.arange(quarter) / quarter)
    wave = np.zeros((8, W), np.float32)
    for c in range(2):
        wave[0, 2 * c * quarter : (2 * c + 1) * quarter] = inverse
        wave[1, (2 * c + 1) * quarter : (2 * c + 2) * quarter] = inverse
    wave[2] = np.where(np.arange(W) < HD // 2, -1.0, 1.0)
    dims = (n, T, L, D, F, R, hl, P1, CQ, HP)
    anywhere = pl.BlockSpec(memory_space=pl.ANY)
    local = pl.BlockSpec(memory_space=pltpu.VMEM)

    def vmem(shape, dtype=BF):
        return pltpu.VMEM(shape, dtype)

    scratch = [
        vmem((n, T, D)),
        vmem((L, D)),
        vmem((n, T, D)),
        vmem((n, 8, T), F32),
        vmem((F, 16, R), F32),
        vmem((8, D), F32),
        vmem((8, 3 * hl * W), F32),
        vmem((L, W), F32),
        vmem((L, W), F32),
        vmem((D, CQ)),
        vmem((D, 3 * hl * W)),
        vmem((J, 2, R, D)),
        vmem((D, P1)),
        vmem((P1, D)),
        vmem((L, 3 * hl * W)),
        vmem((L, W), F32),
        vmem((n, n, T, HP)),
        vmem((L, D)),
        vmem((T, D), F32),
        vmem((L, D)),
        vmem((L, P1)),
        vmem((L, P1)),
        vmem((L, D)),
        vmem((n - 1, T, D)),
        vmem((T, D), F32),
        vmem((D, HP)),
        vmem((J, R, CQ)),
        vmem((J, R, HP)),
        vmem((J, R, P1)),
        vmem((J, R, D)),
        vmem((J - 1, R, CQ)),
        vmem((J - 1, R, HP)),
        vmem((J - 1, R, P1)),
        vmem((J - 1, R, D)),
        vmem((L, 2 * W), F32),
        vmem((8, D), F32),
        vmem((F, 8, D), F32),
        vmem((R, CQ)),
        vmem((R, HP)),
        vmem((R, P1)),
        vmem((R, D)),
        pltpu.SemaphoreType.DMA((448,)),
        pltpu.SemaphoreType.DMA((24,)),
    ]
    shapes = (
        jax.ShapeDtypeStruct((T, D), BF),
        jax.ShapeDtypeStruct((T, D), F32),
        jax.ShapeDtypeStruct((n, R, CQ), BF),
        jax.ShapeDtypeStruct((n, R, HP), BF),
        jax.ShapeDtypeStruct((n, R, P1), BF),
        jax.ShapeDtypeStruct((n, R, D), BF),
        jax.ShapeDtypeStruct((n, 8, D), F32),
    )
    block_out, tokens_grad, rq, rp, r1, r2, sums = pl.pallas_call(
        functools.partial(block_kernel, dims),
        out_shape=shapes,
        in_specs=[anywhere] * 2 + [local] * 3 + [(local,) * 8] + [local] + [anywhere] * 4,
        out_specs=[anywhere] * 7,
        scratch_shapes=scratch,
        compiler_params=pltpu.CompilerParams(
            collective_id=0, has_side_effects=True, vmem_limit_bytes=67043328
        ),
    )(
        tokens[0],
        cotangent[0],
        picture_ids,
        patch_rows,
        patch_cols,
        lines,
        wave,
        qkv_weight,
        proj_weight,
        fc1_weight,
        fc2_weight,
    )
    stored = (
        jax.ShapeDtypeStruct((T, D), BF),
        jax.ShapeDtypeStruct((T, D), F32),
        jax.ShapeDtypeStruct((R, 3 * D), F32),
        jax.ShapeDtypeStruct((R, D), F32),
        jax.ShapeDtypeStruct((R, hidden), F32),
        jax.ShapeDtypeStruct((n * R, D), F32),
    ) + tuple(jax.ShapeDtypeStruct((size,), F32) for size in [R] * 6 + [n * R, 3 * R])
    block_out, tokens_grad, full_qkv, full_proj, full_up, full_down, *vectors = pl.pallas_call(
        functools.partial(unpack_kernel, dims),
        out_shape=stored,
        in_specs=[anywhere] * 7,
        out_specs=[anywhere] * 6 + [local] * 8,
        scratch_shapes=[
            vmem((T, D)),
            vmem((T, D), F32),
            vmem((n, R, CQ)),
            vmem((n, R, HP)),
            vmem((n, R, P1)),
            vmem((n, R, D)),
            vmem((n, 8, D), F32),
            vmem((4 + 2 * n, R, D), F32),
            pltpu.SemaphoreType.DMA((7,)),
            pltpu.SemaphoreType.DMA((7 + 2 * n,)),
        ],
        compiler_params=pltpu.CompilerParams(vmem_limit_bytes=67043328),
    )(block_out, tokens_grad, rq, rp, r1, r2, sums)
    return (
        block_out[None],
        tokens_grad[None],
        vectors[0],
        vectors[1],
        full_qkv,
        vectors[7],
        full_proj,
        vectors[2],
        vectors[3],
        vectors[4],
        full_up,
        vectors[6],
        full_down,
        vectors[5],
    )


def fits_kernel(mesh):
    return dict(mesh.shape) == {"seq": 4, "fsdp": 8}


def shards_plain(
    tokens,
    picture_ids,
    patch_rows,
    patch_cols,
    norm1_gain,
    norm1_bias,
    qkv_weight,
    qkv_bias,
    proj_weight,
    proj_bias,
    norm2_gain,
    norm2_bias,
    fc1_weight,
    fc1_bias,
    fc2_weight,
    fc2_bias,
    cotangent,
):
    n = lax.axis_size("seq")
    me = lax.axis_index("seq")
    stores = lax.axis_size("fsdp")
    _, own, width = tokens.shape
    heads = width // HD
    local_heads = heads // n
    hw = local_heads * HD
    rows = qkv_weight.shape[0]
    hidden = fc1_weight.shape[1]
    part = hidden // (stores * n)

    def pick(value, axis):
        return lax.dynamic_index_in_dim(value, me, axis, keepdims=False)

    own_qkv = pick(qkv_weight.reshape(rows, 3, n, hw), 2).reshape(rows, 3 * hw)
    own_up = pick(fc1_weight.reshape(rows, stores, n, part), 2).reshape(rows, stores * part)
    own_down = pick(fc2_weight.reshape(n, part, width), 0)
    small = (norm1_gain, norm1_bias, proj_bias, norm2_gain, norm2_bias, fc2_bias, qkv_bias, fc1_bias)
    sizes = [item.shape[0] for item in small]
    packed = gather(jnp.concatenate(small)[None], "fsdp")
    weight_qkv = gather(own_qkv, "fsdp")
    weight_proj = gather(proj_weight, "fsdp")
    weight_up = gather(own_up, "fsdp")
    weight_down = gather(own_down, "fsdp")
    params = []
    start = 0
    for size in sizes:
        params.append(packed[:, start : start + size].reshape(-1).astype(F32))
        start += size
    gain_one, bias_one, bias_proj, gain_two, bias_two, bias_down, bias_qkv, bias_up = params
    bias_qkv = pick(bias_qkv.reshape(3, n, hw), 1).reshape(3 * hw)
    bias_up = pick(bias_up.reshape(stores, n, part), 1).reshape(stores * part)

    places = jnp.stack([picture_ids[0], patch_rows[0], patch_cols[0]])
    places = gather(places, "seq", 1)
    picture = places[0]
    all_tokens = gather(tokens[0], "seq").astype(F32)
    upstream = gather(cotangent[0], "seq")
    length = all_tokens.shape[0]

    def mine(value):
        return lax.dynamic_slice_in_dim(value, me * own, own, 0)

    normed_one, factor_one = standardize(all_tokens)
    attn_input = (normed_one * gain_one + bias_one).astype(BF)
    projected = (dot(attn_input, weight_qkv) + bias_qkv).reshape(length, 3, local_heads, HD)
    cosine, sine = rotary_tables(places[1], places[2], HD)
    queries = rotate(projected[:, 0], cosine, sine).astype(BF)
    keys = rotate(projected[:, 1], cosine, sine).astype(BF)
    values = projected[:, 2].astype(BF)
    mixed_own, log_total = attend(queries, keys, values, picture)
    mixed = gather(mixed_own.reshape(length, hw), "seq", 1)
    middle = all_tokens + dot(mixed, weight_proj) + bias_proj
    normed_two, factor_two = standardize(middle)
    mlp_input = (normed_two * gain_two + bias_two).astype(BF)
    before = dot(mlp_input, weight_up) + bias_up
    gate = jax.nn.sigmoid(1.702 * before)
    activated = (before * gate).astype(BF)
    out_part = dot(activated, weight_down).astype(BF)
    block_out = (mine(middle) + scatter_sum(out_part, "seq").astype(F32) + bias_down).astype(BF)

    grad_down = scatter_sum(rows_term(activated, upstream).astype(BF), "fsdp")
    grad_activated = contract_back(upstream, weight_down)
    grad_before = (grad_activated * (gate + 1.702 * before * gate * (1.0 - gate))).astype(BF)
    grad_up = scatter_sum(rows_term(mlp_input, grad_before).astype(BF), "fsdp")
    grad_mlp_input = scatter_sum(contract_back(grad_before, weight_up).astype(BF), "seq").astype(F32)
    own_upstream = cotangent[0].astype(F32)
    own_two = mine(normed_two)
    grad_middle = own_upstream + norm_back(grad_mlp_input, own_two, mine(factor_two), gain_two)
    grad_branch = grad_middle.astype(BF)
    grad_mixed = contract_back(grad_branch, weight_proj).astype(BF)
    grad_heads = lax.all_to_all(grad_mixed, "seq", split_axis=1, concat_axis=0, tiled=True)
    branch_part = lax.all_to_all(grad_branch, "seq", split_axis=1, concat_axis=0, tiled=True)
    grad_proj = scatter_sum(rows_term(mixed, branch_part).astype(BF), "fsdp")
    grad_queries, grad_keys, grad_values = attend_back(
        queries, keys, values, picture, grad_heads.reshape(length, local_heads, HD), log_total
    )
    grad_projected = jnp.stack(
        [
            unrotate(grad_queries.astype(F32), cosine, sine).astype(BF),
            unrotate(grad_keys.astype(F32), cosine, sine).astype(BF),
            grad_values,
        ],
        axis=1,
    ).reshape(length, 3 * hw)
    grad_qkv = scatter_sum(rows_term(attn_input, grad_projected).astype(BF), "fsdp")
    grad_attn_input = scatter_sum(contract_back(grad_projected, weight_qkv).astype(BF), "seq").astype(F32)
    own_one = mine(normed_one)
    tokens_grad = grad_middle + norm_back(grad_attn_input, own_one, mine(factor_one), gain_one)

    def spread(value, groups):
        empty = jnp.zeros((groups, n, value.shape[0] // groups), F32)
        return lax.dynamic_update_slice_in_dim(
            empty, value.reshape(groups, 1, -1), me, 1
        ).reshape(stores, -1)

    sums = [
        jnp.sum(grad_attn_input * own_one, axis=0).reshape(stores, -1),
        jnp.sum(grad_attn_input, axis=0).reshape(stores, -1),
        jnp.sum(grad_branch.astype(F32), axis=0).reshape(stores, -1),
        jnp.sum(grad_mlp_input * own_two, axis=0).reshape(stores, -1),
        jnp.sum(grad_mlp_input, axis=0).reshape(stores, -1),
        jnp.sum(own_upstream, axis=0).reshape(stores, -1),
        spread(jnp.sum(grad_projected.astype(F32), axis=0), 3),
        spread(jnp.sum(grad_before.astype(F32), axis=0), stores),
    ]
    summed = lax.psum(scatter_sum(jnp.concatenate(sums, axis=1), "fsdp"), "seq")[0]
    finals = []
    start = 0
    for size in sizes:
        finals.append(summed[start : start + size])
        start += size
    full_down = gather(grad_down, "seq").astype(F32)
    full_up = gather(grad_up[None], "seq").reshape(n, rows, stores, part)
    full_up = full_up.transpose(1, 2, 0, 3).reshape(rows, hidden).astype(F32)
    full_proj = gather(grad_proj, "seq", 1).astype(F32)
    full_qkv = gather(grad_qkv[None], "seq").reshape(n, rows, 3, hw)
    full_qkv = full_qkv.transpose(1, 2, 0, 3).reshape(rows, 3 * width).astype(F32)
    return (
        block_out[None],
        tokens_grad[None],
        finals[0],
        finals[1],
        full_qkv,
        finals[6],
        full_proj,
        finals[2],
        finals[3],
        finals[4],
        full_up,
        finals[7],
        full_down,
        finals[5],
    )


def solution(mesh):
    token = P("fsdp", "seq", None)
    place = P("fsdp", "seq")
    vector = P("fsdp")
    matrix = P("fsdp", None)
    in_specs = (
        token,
        place,
        place,
        place,
        vector,
        vector,
        matrix,
        vector,
        matrix,
        vector,
        vector,
        vector,
        matrix,
        vector,
        matrix,
        vector,
        token,
    )
    out_specs = (
        token,
        token,
        vector,
        vector,
        matrix,
        vector,
        matrix,
        vector,
        vector,
        vector,
        matrix,
        vector,
        matrix,
        vector,
    )
    shards = shards_kernel if fits_kernel(mesh) else shards_plain
    return jax.shard_map(shards, mesh=mesh, in_specs=in_specs, out_specs=out_specs, check_vma=False)
```

```python
import functools

import jax
import jax.numpy as jnp
import numpy as np
from jax import lax
from jax.experimental import pallas as pl
from jax.experimental.pallas import tpu as pltpu
from jax.sharding import PartitionSpec as P

HD = 80
NORM_EPSILON = 1e-06
MASKED = -1e30
BF = jnp.bfloat16
F32 = jnp.float32


def standardize(values_in):
    centre = jnp.mean(values_in, axis=-1, keepdims=True)
    shifted = values_in - centre
    factor = lax.rsqrt(jnp.mean(shifted * shifted, axis=-1, keepdims=True) + NORM_EPSILON)
    return (shifted * factor, factor)


def norm_back(grad_out, normed, factor, gain):
    scaled = grad_out * gain
    return factor * (
        scaled
        - jnp.mean(scaled, axis=-1, keepdims=True)
        - normed * jnp.mean(scaled * normed, axis=-1, keepdims=True)
    )


def rotary_tables(patch_row, patch_col, head_size):
    quarter = head_size // 4
    inverse = jnp.power(10000.0, -jnp.arange(quarter, dtype=F32) / quarter)
    half_angles = jnp.concatenate(
        [
            patch_row.astype(F32)[..., None] * inverse,
            patch_col.astype(F32)[..., None] * inverse,
        ],
        axis=-1,
    )
    angles = jnp.concatenate([half_angles, half_angles], axis=-1)
    return (jnp.cos(angles)[..., None, :], jnp.sin(angles)[..., None, :])


def rotate(values_in, cosine, sine):
    half_size = values_in.shape[-1] // 2
    turned = jnp.concatenate([-values_in[..., half_size:], values_in[..., :half_size]], axis=-1)
    return values_in * cosine + turned * sine


def unrotate(grad_in, cosine, sine):
    half_size = grad_in.shape[-1] // 2
    moved = grad_in * sine
    return grad_in * cosine + jnp.concatenate(
        [moved[..., half_size:], -moved[..., :half_size]], axis=-1
    )


def masked_scores(queries, keys, picture, factor):
    places = jnp.arange(picture.shape[0], dtype=jnp.int32)
    scores = jnp.einsum("qhd,khd->hqk", queries, keys, preferred_element_type=F32) * factor
    allowed = (picture[:, None] == picture[None, :]) & (
        (picture[None, :] >= 0) | (places[:, None] == places[None, :])
    )
    return jnp.where(allowed[None, :, :], scores, MASKED)


def attend(queries, keys, values, picture):
    scores = masked_scores(queries, keys, picture, HD**-0.5)
    row_max = jnp.max(scores, axis=-1, keepdims=True)
    powers = jnp.exp(scores - row_max)
    totals = jnp.sum(powers, axis=-1, keepdims=True)
    weights = (powers / totals).astype(BF)
    mixed = jnp.einsum("hqk,khd->qhd", weights, values, preferred_element_type=F32)
    return mixed.astype(BF), row_max + jnp.log(totals)


def attend_back(queries, keys, values, picture, grad_mixed, log_total):
    factor = HD**-0.5
    scores = masked_scores(queries, keys, picture, factor)
    probs = jnp.exp(scores - log_total)
    weights = probs.astype(BF)
    grad_values = jnp.einsum("hqk,qhd->khd", weights, grad_mixed, preferred_element_type=F32)
    grad_weights = jnp.einsum("qhd,khd->hqk", grad_mixed, values, preferred_element_type=F32)
    centre = jnp.sum(probs * grad_weights, axis=-1, keepdims=True)
    grad_scores = (probs * (grad_weights - centre)).astype(BF)
    grad_queries = jnp.einsum("hqk,khd->qhd", grad_scores, keys, preferred_element_type=F32) * factor
    grad_keys = jnp.einsum("hqk,qhd->khd", grad_scores, queries, preferred_element_type=F32) * factor
    return grad_queries.astype(BF), grad_keys.astype(BF), grad_values.astype(BF)


def dot(left, right):
    return jnp.dot(left, right, preferred_element_type=F32)


def rows_term(left, right):
    return lax.dot_general(left, right, (((0,), (0,)), ((), ())), preferred_element_type=F32)


def contract_back(grad_out, weight):
    return lax.dot_general(grad_out, weight, (((1,), (1,)), ((), ())), preferred_element_type=F32)


def gather(value, axis_name, axis=0):
    return lax.all_gather(value, axis_name, axis=axis, tiled=True)


def scatter_sum(value, axis_name, axis=0):
    return lax.psum_scatter(value, axis_name, scatter_dimension=axis, tiled=True)

MESH = pl.DeviceIdType.MESH


def mm(left, right):
    return jnp.dot(left, right, preferred_element_type=F32)


def mm_nt(left, right):
    return lax.dot_general(left, right, (((1,), (1,)), ((), ())), preferred_element_type=F32)


def mm_tn(left, right):
    return lax.dot_general(left, right, (((0,), (0,)), ((), ())), preferred_element_type=F32)


def lane_pad(value, lanes):
    gap = lanes - value.shape[1]
    if gap == 0:
        return value
    return jnp.concatenate([value, jnp.zeros((value.shape[0], gap), value.dtype)], axis=1)


def moments(value):
    centre = jnp.mean(value, axis=-1, keepdims=True)
    shifted = value - centre
    factor = lax.rsqrt(jnp.mean(shifted * shifted, axis=-1, keepdims=True) + NORM_EPSILON)
    return shifted * factor, factor


def block_kernel(
    dims,
    tok_in,
    cot_in,
    ids_in,
    row_in,
    col_in,
    vec_ins,
    wave_in,
    wq_in,
    wp_in,
    w1_in,
    w2_in,
    out_ref,
    tgrad_ref,
    rq_ref,
    rp_ref,
    r1_ref,
    r2_ref,
    sums_ref,
    tokb,
    ain,
    cotb,
    plb,
    smb,
    vec,
    bqkv,
    cosb,
    sinb,
    wqc,
    wq,
    wp,
    w1,
    w2,
    qkv,
    lse,
    mixc,
    mix,
    mid,
    mlp,
    act,
    dge,
    snd,
    rsr,
    gmd,
    gp,
    dq4,
    dp4,
    d14,
    d24,
    zq3,
    zp3,
    z13,
    z23,
    dkv,
    smg,
    sg8,
    hq,
    hp,
    h1,
    h2,
    sems,
    local_sems,
):
    n, T, L, D, F, R, hl, P1, CQ, HP = dims
    J = F // 2
    hw = hl * HD
    W = 128
    QW = hl * W
    scale = HD**-0.5
    tile = 256 if D % 256 == 0 else 128
    me = lax.axis_index("seq")
    f = lax.axis_index("fsdp")
    k = f % 2
    j = f // 2
    partner = f + 1 - 2 * k
    x = me % 2
    y = me // 2

    def peer(o):
        return (y + o // 2) % 2 * 2 + (x + o % 2) % 2

    seq_to = [peer(o) for o in range(n)]
    seq_from = seq_to
    near_x, near_y, across = seq_to[1], seq_to[2], seq_to[3]
    edge = (j == 0) | (j == J - 1)
    middle = (j > 0) & (j < J - 1)
    z_to = [2 * ((j + d) % J) + k for d in range(J)]
    z_from = [2 * ((j + J - d) % J) + k for d in range(J)]
    used = {"remote": 0, "local": 0}
    leftover = []

    def take(count=1):
        used["remote"] += count
        return used["remote"] - count

    def remote(src, dst, where, recv):
        return pltpu.make_async_remote_copy(
            src_ref=src,
            dst_ref=dst,
            send_sem=sems.at[take()],
            recv_sem=sems.at[recv],
            device_id=where,
            device_id_type=MESH,
        )

    def when(condition, action):
        pl.when(condition)(action)

    def send(src, dst, where, recv, late=True):
        copy = remote(src, dst, where, recv)
        copy.start()
        if late:
            leftover.append(copy)
        return copy

    def load(src, dst):
        used["local"] += 1
        copy = pltpu.make_async_copy(src, dst, local_sems.at[used["local"] - 1])
        copy.start()
        return copy

    def band(ref, index, size):
        return ref.at[pl.ds(pl.multiple_of(index * size, size), size)]

    def rows_of(index, size):
        return pl.ds(pl.multiple_of(index * size, size), size)

    def strips(total, step, body):
        def run(s, carry):
            body(rows_of(s, step))
            return carry

        lax.fori_loop(0, total // step, run, 0)

    strip = 32

    spot = lax.broadcasted_iota(jnp.int32, (1, T), 1) + me * T
    ids = ids_in[...]
    plb[me, 0:4, :] = jnp.concatenate(
        [
            ids.astype(F32),
            row_in[...].astype(F32),
            col_in[...].astype(F32),
            jnp.where(ids >= 0, ids, -1 - spot).astype(F32),
        ],
        axis=0,
    )
    plb[me, 4:8, :] = jnp.zeros((4, T), F32)
    for row in range(6):
        smb[f, row : row + 1, :] = vec_ins[row][...].astype(F32).reshape(1, R)
    up_bias = vec_ins[6][...].astype(F32).reshape(1, n * R)
    for m in range(n):

        @pl.when(me == m)
        def _():
            smb[f, 6:7, :] = up_bias[:, m * R : (m + 1) * R]

    qkv_bias = vec_ins[7][...].astype(F32).reshape(1, 3 * R)
    for t in range(3):
        smb[f, 7 + t : 8 + t, :] = qkv_bias[:, t * R : (t + 1) * R]
    smb[f, 10:16, :] = jnp.zeros((6, R), F32)

    raw_q = [load(wq_in.at[:, t * D : (t + 1) * D], d24.at[t]) for t in range(3)]
    raw_1 = [load(w1_in.at[:, c * P1 : (c + 1) * P1], d14.at[c]) for c in range(n)]

    barrier = pltpu.get_barrier_semaphore()
    for o in range(1, n):
        pl.semaphore_signal(barrier, inc=1, device_id={"seq": seq_to[o]}, device_id_type=MESH)
    for o in range(1, F):
        pl.semaphore_signal(barrier, inc=1, device_id={"fsdp": (f + o) % F}, device_id_type=MESH)
    pl.semaphore_wait(barrier, n - 1 + F - 1)

    class Spread:
        def __init__(self, src, at, rows):
            self.at, self.rows = at, rows
            self.first = [
                send(src, at(me, 0, rows), {"seq": seq_to[o]}, take()) for o in (1, 2)
            ]

        def relay(self):
            half = self.rows // 2
            self.first[0].wait_recv()
            part = self.at(near_x, 0, half)
            one = send(part, part, {"seq": near_y}, take(), late=False)
            self.first[1].wait_recv()
            part = self.at(near_y, half, self.rows)
            self.second = [one, send(part, part, {"seq": near_x}, take(), late=False)]

        def finish(self):
            for copy in self.second:
                copy.wait_recv()

        def drain(self):
            for copy in self.second:
                copy.wait_send()

    def rows_in(ref):
        return lambda index, lo, hi: ref.at[index, lo:hi]

    plc_copies = [
        send(plb.at[me], plb.at[me], {"seq": seq_to[o]}, take()) for o in range(1, n)
    ]
    tok = Spread(tok_in, rows_in(tokb), T)
    own_tok = load(tok_in, tokb.at[me])

    class Weight:
        def __init__(self, src, buf, rows):
            self.buf, self.rows = buf, rows
            self.own = None
            mine = band(buf, f, rows)
            if src is None:
                src = mine
            else:
                self.own = load(src, mine)
            self.near = send(src, mine, {"fsdp": partner}, take(), late=False)
            landed = {d: take() for d in (1, 2, 3)}
            self.far = {d: remote(src, mine, {"fsdp": z_to[d]}, landed[d]) for d in (1, 2, 3)}
            self.far[2].start()
            when(j != J - 1, self.far[1].start)
            when(j != 0, self.far[3].start)
            part = band(buf, z_from[2], rows)
            self.down = remote(part, part, {"fsdp": k}, landed[1])
            self.up = remote(part, part, {"fsdp": 2 * (J - 1) + k}, landed[3])
            self.relayed = []

        def hop(self):
            self.far[2].wait_recv()
            when(j == 1, self.down.start)
            when(j == J - 2, self.up.start)

        def relay(self):
            for d in (2, 1, 3):
                if d != 2:
                    self.far[d].wait_recv()
                part = band(self.buf, z_from[d], self.rows)
                self.relayed.append(send(part, part, {"fsdp": partner}, take(), late=False))

        def finish(self):
            if self.own is not None:
                self.own.wait()
            self.near.wait_recv()
            for copy in self.relayed:
                copy.wait_recv()

        def drain(self):
            for copy in [self.near, self.far[2]] + self.relayed:
                copy.wait_send()
            when(j != J - 1, self.far[1].wait_send)
            when(j != 0, self.far[3].wait_send)
            when(j == 1, self.down.wait_send)
            when(j == J - 2, self.up.wait_send)

    class Quarter:
        def __init__(self):
            self.cols = pl.ds(pl.multiple_of(x * (D // 2), D // 2), D // 2)
            self.holder, self.other = y == k, y != k
            used["local"] += 1
            self.own = pltpu.make_async_copy(
                wp_in.at[:, self.cols],
                wp.at[j, k, :, self.cols],
                local_sems.at[used["local"] - 1],
            )
            when(self.holder, self.own.start)
            landed = {d: take() for d in (1, 2, 3)}
            mine = wp.at[j, k, :, self.cols]
            self.far = {
                d: remote(wp_in.at[:, self.cols], mine, {"fsdp": z_to[d]}, landed[d])
                for d in (1, 2, 3)
            }
            part = wp.at[z_from[2] // 2, k, :, self.cols]
            self.down = remote(part, part, {"fsdp": k}, landed[1])
            self.up = remote(part, part, {"fsdp": 2 * (J - 1) + k}, landed[3])
            when(self.holder, self.far[2].start)
            when(self.holder & (j != J - 1), self.far[1].start)
            when(self.holder & (j != 0), self.far[3].start)

            def quarter(device_y, device_x, lo, hi):
                cols = pl.ds(pl.multiple_of(device_x * (D // 2), D // 2), D // 2)
                return wp.at[lo:hi, device_y, :, cols]

            to_x, to_y, to_core = {"seq": near_x}, {"seq": near_y}, {"fsdp": partner}
            h = J // 2
            whole = quarter(y, x, 0, J)
            self.give = [remote(whole, whole, where, take()) for where in (to_x, to_y, to_core)]
            q = quarter(y, 1 - x, 0, J)
            self.along_x = remote(q, q, to_core, take())
            q = quarter(y, 1 - x, 0, h)
            self.on_y = remote(q, q, to_y, take())
            q = quarter(1 - y, x, 0, J)
            self.along_y = remote(q, q, to_core, take())
            q = quarter(1 - y, x, h, J)
            self.on_x = remote(q, q, to_x, take())
            q = quarter(1 - y, 1 - x, 0, J)
            self.last = remote(q, q, to_core, take())

        def hop(self):
            @pl.when(self.holder)
            def _():
                self.far[2].wait_recv()
                when(j == 1, self.down.start)
                when(j == J - 2, self.up.start)

        def start_give(self):
            @pl.when(self.holder)
            def _():
                self.own.wait()
                self.far[1].wait_recv()
                self.far[3].wait_recv()
                for copy in self.give:
                    copy.start()

        def relay(self):
            @pl.when(self.holder)
            def _():
                self.give[0].wait_recv()
                self.on_y.start()
                self.along_x.start()

            @pl.when(self.other)
            def _():
                self.give[1].wait_recv()
                self.on_x.start()
                self.along_y.start()

        def relay_last(self):
            @pl.when(self.other)
            def _():
                self.on_y.wait_recv()
                self.on_x.wait_recv()
                self.last.start()

        def finish(self):
            @pl.when(self.holder)
            def _():
                self.along_y.wait_recv()
                self.last.wait_recv()

            @pl.when(self.other)
            def _():
                self.give[2].wait_recv()
                self.along_x.wait_recv()

        def drain(self):
            @pl.when(self.holder)
            def _():
                for copy in self.give + [self.along_x, self.on_y, self.far[2]]:
                    copy.wait_send()
                when(j != J - 1, self.far[1].wait_send)
                when(j != 0, self.far[3].wait_send)
                when(j == 1, self.down.wait_send)
                when(j == J - 2, self.up.wait_send)

            @pl.when(self.other)
            def _():
                for copy in (self.along_y, self.on_x, self.last):
                    copy.wait_send()

    def cut_columns(target, lines):
        for m in range(n):

            @pl.when(me == m)
            def _():
                target[rows_of(f, R), :] = lane_pad(
                    jnp.concatenate(lines(m), axis=1), target.shape[1]
                )

    small_copies = [
        send(smb.at[f], smb.at[f], {"fsdp": (f + o) % F}, take()) for o in range(1, F)
    ]
    for copy in raw_q:
        copy.wait()
    cut_columns(wqc, lambda m: [d24[t, :, m * hw : (m + 1) * hw] for t in range(3)])
    weight_q = Weight(None, wqc, R)
    for copy in raw_1:
        copy.wait()
    cut_columns(
        w1,
        lambda m: [
            d14[b * n * R // P1, :, b * n * R % P1 + m * R : b * n * R % P1 + (m + 1) * R]
            for b in range(F)
        ],
    )

    for copy in small_copies:
        copy.wait_recv()
    for row in range(7):
        vec[row : row + 1, :] = jnp.concatenate(
            [smb[s, row : row + 1, :R] for s in range(F)], axis=1
        )
    groups = 3 * D // R // 3
    heads = []
    for t in range(3):
        start = t * groups + me * (hw // R)
        line = jnp.concatenate(
            [
                smb[(start + b) // 3, pl.ds(7 + (start + b) % 3, 1), :][:, :R]
                for b in range(hw // R)
            ],
            axis=1,
        )
        for h in range(hl):
            heads.append(lane_pad(line[:, h * HD : (h + 1) * HD], W))
    bqkv[...] = jnp.broadcast_to(jnp.concatenate(heads, axis=1), bqkv.shape)

    def vector(row):
        return vec[row : row + 1, :]

    def rows_of_block(i, rows):
        return pl.ds(pl.multiple_of(i * T + rows.start, strip), strip)

    def norm_one(i):
        def body(rows):
            normed, _ = moments(tokb[i, rows, :].astype(F32))
            ain[rows_of_block(i, rows), :] = (normed * vector(0) + vector(1)).astype(BF)

        strips(T, strip, body)

    own_tok.wait()
    norm_one(me)
    tok.relay()
    weight_q.hop()
    weight_p = Quarter()
    weight_1 = Weight(None, w1, R)
    own_cot = load(cot_in, cotb.at[me])
    cot = Spread(cot_in, rows_in(cotb), T)
    norm_one(near_x)
    norm_one(near_y)

    for copy in plc_copies:
        copy.wait_recv()

    def table(i, carry):
        rows = rows_of(i, T)
        turned = jnp.transpose(plb[i], (1, 0))
        lse[rows, hl : hl + 8] = turned
        angle = turned[:, 1:2] * wave_in[0:1, :] + turned[:, 2:3] * wave_in[1:2, :]
        cosb[rows, :] = jnp.cos(angle)
        sinb[rows, :] = jnp.sin(angle) * wave_in[2:3, :]
        return carry

    lax.fori_loop(0, n, table, 0)
    lane = lax.broadcasted_iota(jnp.int32, (1, W), 1)
    low_half = lane < HD // 2

    def swap(value):
        return jnp.where(
            low_half, pltpu.roll(value, W - HD // 2, 1), pltpu.roll(value, HD // 2, 1)
        )

    tok.finish()
    norm_one(across)

    weight_q.relay()
    weight_p.hop()
    weight_q.finish()

    def spread_heads(rows):
        line = wqc[rows, :]
        for h in range(3 * hl):
            wq[rows, h * W : (h + 1) * W] = lane_pad(line[:, h * HD : (h + 1) * HD], W)

    strips(D, R, spread_heads)

    def project(i, carry):
        rows = rows_of(i, T)
        line = ain[rows, :]
        cosine = cosb[rows, :]
        sine = sinb[rows, :]
        for t in range(3):
            part = mm(line, wq[:, t * QW : (t + 1) * QW]) + bqkv[0:1, t * QW : (t + 1) * QW]
            for h in range(hl):
                u = part[:, h * W : (h + 1) * W]
                if t < 2:
                    u = u * cosine + swap(u) * sine
                qkv[rows, t * QW + h * W : t * QW + (h + 1) * W] = u.astype(BF)
        return carry

    weight_p.start_give()
    lax.fori_loop(0, n, project, 0)

    def masked(scores, i):
        ids = jnp.concatenate([plb[b, 3:4, :] for b in range(n)], axis=1)
        own_ids = lse[rows_of(i, T), hl + 3 : hl + 4]
        return jnp.where(own_ids == ids, scores * scale, MASKED)

    mix_send, mix_recv = take(4 * n), take(4 * n)

    def mix_copy(i, spot, part, where):
        return pltpu.make_async_remote_copy(
            src_ref=part,
            dst_ref=part,
            send_sem=sems.at[mix_send + 4 * i + spot],
            recv_sem=sems.at[mix_recv + 4 * i + spot],
            device_id={"seq": where},
            device_id_type=MESH,
        )

    def mix_first(i, o, source):
        return mix_copy(i, o - 1, mixc.at[source, i], seq_to[o])

    def mix_pass(i, o):
        part = mixc.at[seq_to[o], i, (o - 1) * T // 2 : o * T // 2]
        return mix_copy(i, o + 1, part, seq_to[3 - o])

    def mix_relay(i):
        for o in (1, 2):
            mix_first(i, o, seq_to[o]).wait_recv()
            mix_pass(i, o).start()

    def attend_block(i, carry):
        rows = rows_of(i, T)
        outs = []
        logs = lse[rows, :]
        for h in range(hl):
            q = qkv[rows, h * W : (h + 1) * W]
            kk = qkv[:, QW + h * W : QW + (h + 1) * W]
            v = qkv[:, 2 * QW + h * W : 2 * QW + (h + 1) * W]
            s = masked(mm_nt(q, kk), i)
            top = jnp.max(s, axis=-1, keepdims=True)
            p = jnp.exp(s - top)
            total = jnp.sum(p, axis=-1, keepdims=True)
            outs.append((mm(p.astype(BF), v) / total)[:, :HD].astype(BF))
            logs = jnp.where(lane == h, top + jnp.log(total), logs)
        lse[rows, :] = logs
        mixc[me, i] = lane_pad(jnp.concatenate(outs, axis=1), HP)
        for o in (1, 2):
            mix_first(i, o, me).start()
        when(i > 0, lambda: mix_relay(i - 1))
        return carry

    weight_2 = Weight(w2_in.at[rows_of(me, R)], w2, R)
    lax.fori_loop(0, n // 2, attend_block, 0)
    weight_p.relay()
    lax.fori_loop(n // 2, n, attend_block, 0)
    weight_1.hop()
    weight_p.relay_last()
    weight_p.finish()
    tok.drain()

    def proj_weight():
        return wp[...].reshape(D, D)

    def branch(i, carry):
        rows = rows_of(i, T)
        for o in (1, 2):
            mix_pass(i, o).wait_recv()
        mix[rows, :] = jnp.concatenate([mixc[c, i][:, :hw] for c in range(n)], axis=1)
        gmd[...] = mm(mix[rows, :], proj_weight())

        def body(part):
            whole = rows_of_block(i, part)
            value = gmd[part, :] + tokb[i, part, :].astype(F32) + vector(2)

            @pl.when(i == me)
            def _():
                mid[part, :] = value

            normed, _ = moments(value)
            mlp[whole, :] = (normed * vector(3) + vector(4)).astype(BF)

        strips(T, strip, body)
        return carry

    lax.fori_loop(0, 1, branch, 0)
    mix_relay(n - 1)
    cot.relay()
    weight_2.hop()
    lax.fori_loop(1, n, branch, 0)

    weight_1.relay()
    weight_1.finish()

    def up(i, carry):
        rows = rows_of(i, T)
        before = mm(mlp[rows, :], w1[...]) + vector(6)
        gate = jax.nn.sigmoid(1.702 * before)
        act[rows, :] = (before * gate).astype(BF)
        dge[rows, :] = (gate + 1.702 * before * gate * (1.0 - gate)).astype(BF)
        return carry

    lax.fori_loop(0, n, up, 0)

    own_cot.wait()
    cot.finish()
    cot.drain()
    weight_2.relay()
    weight_2.finish()

    half = T // 2

    class Scatter:
        def __init__(self, stage, landing, slots):
            self.stage, self.landing = stage, landing
            slot_x, slot_y, pass_x, pass_y = slots
            to_x, to_y = {"seq": near_x}, {"seq": near_y}
            self.pass_a = self.make(across, 0, pass_x, to_x)
            self.pass_b = self.make(across, 1, pass_y, to_y)
            self.last_a = self.make(near_x, 0, slot_x, to_x)
            self.last_b = self.make(near_y, 1, slot_y, to_y)
            self.sum_a = self.make(near_y, 0, slot_y, to_y)
            self.sum_b = self.make(near_x, 1, slot_x, to_x)

        def make(self, block, part, slot, where):
            return remote(
                self.stage.at[self.rows(block, part)],
                self.landing.at[slot, part * half : (part + 1) * half],
                where,
                take(),
            )

        def rows(self, block, part):
            return pl.ds(pl.multiple_of(block * T + part * half, half), half)

        def start(self, t):
            @pl.when(t == 0)
            def _():
                self.pass_a.start()
                self.pass_b.start()

            when(t == 1, self.last_a.start)
            when(t == 2, self.last_b.start)

        def relay(self, slot):
            for part, into, out, block in (
                (0, self.pass_a, self.sum_a, near_y),
                (1, self.pass_b, self.sum_b, near_x),
            ):
                into.wait_recv()

                def body(rows):
                    at = pl.ds(pl.multiple_of(block * T + part * half + rows.start, strip), strip)
                    there = pl.ds(pl.multiple_of(part * half + rows.start, strip), strip)
                    self.stage[at, :] = (
                        self.stage[at, :].astype(F32) + self.landing[slot, there, :].astype(F32)
                    ).astype(BF)

                strips(half, strip, body)
                out.start()

        def wait_recv(self):
            for copy in (self.last_a, self.last_b, self.sum_a, self.sum_b):
                copy.wait_recv()

        def wait_send(self):
            for copy in (
                self.pass_a,
                self.pass_b,
                self.last_a,
                self.last_b,
                self.sum_a,
                self.sum_b,
            ):
                copy.wait_send()

    def block_at(t):
        return peer(((t + 2) % 3 + 1) * (1 - t // 3))

    for i in range(n):
        for o in (1, 2):
            mix_first(i, o, me).wait_send()
            mix_pass(i, o).wait_send()
    scatter_mlp = Scatter(snd, rsr, (0, 1, 2, 2))

    def back(t, carry):
        i = block_at(t)
        rows = rows_of(i, T)
        grad = (mm_nt(cotb[i], w2[...]) * dge[rows, :].astype(F32)).astype(BF)
        dge[rows, :] = grad
        snd[rows, :] = mm_nt(grad, w1[...]).astype(BF)
        scatter_mlp.start(t)
        return carry

    lax.fori_loop(0, n, back, 0)

    class Gradient:
        def __init__(self, grad, other, far, extra, result, lo, width):
            self.grad, self.other, self.far, self.extra = grad, other, far, extra
            self.result, self.lanes = result, slice(lo, lo + width)

        def of(self, index):
            return self.grad.at[rows_of(index, R), self.lanes]

        def exchange(self):
            self.near = [
                send(
                    self.of(2 * c + 1 - k),
                    self.other.at[c, :, self.lanes],
                    {"fsdp": partner},
                    take(),
                )
                for c in range(J)
            ]

        def add_near(self):
            for copy in self.near:
                copy.wait_recv()
            lanes = self.lanes

            def chip(c, carry):
                rows = rows_of(2 * c + k, R)
                self.grad[rows, lanes] = (
                    self.grad[rows, lanes].astype(F32) + self.other[c, :, lanes].astype(F32)
                ).astype(BF)
                return carry

            lax.fori_loop(0, J, chip, 0)
            self.pass_on = remote(
                self.of(2 * (J - 1 - j) + k),
                self.extra.at[:, lanes],
                {"fsdp": 2 * (1 + j // (J - 1)) + k},
                take(),
            )
            self.across = {
                d: remote(
                    self.of(z_to[d]), self.far.at[d - 1, :, lanes], {"fsdp": z_to[d]}, take()
                )
                for d in (1, 2, 3)
            }
            when(edge, self.pass_on.start)
            when(edge, self.across[2].start)
            when(j != J - 1, self.across[1].start)
            when(j != 0, self.across[3].start)

        def hop(self):
            @pl.when(middle)
            def _():
                self.pass_on.wait_recv()
                rows = rows_of(z_to[2], R)
                self.grad[rows, self.lanes] = (
                    self.grad[rows, self.lanes].astype(F32)
                    + self.extra[:, self.lanes].astype(F32)
                ).astype(BF)
                self.across[2].start()

        def add_far(self):
            def total_of(steps):
                def action():
                    for d in steps:
                        self.across[d].wait_recv()
                    total = self.grad[rows_of(f, R), self.lanes].astype(F32)
                    for d in steps:
                        total = total + self.far[d - 1, :, self.lanes].astype(F32)
                    self.other[0, :, self.lanes] = total.astype(BF)

                return action

            when(j == 0, total_of((2, 3)))
            when(middle, total_of((1, 2, 3)))
            when(j == J - 1, total_of((1, 2)))

        def share(self):
            mine = self.other.at[0, :, self.lanes]
            self.keep = load(mine, self.result.at[me, :, self.lanes])
            self.spread = Spread(
                mine, lambda index, lo, hi: self.result.at[index, lo:hi, self.lanes], R
            )

        def relay(self):
            self.spread.relay()

        def finish(self):
            self.keep.wait()
            self.spread.finish()
            self.spread.drain()
            self.across[2].wait_send()
            when(j != J - 1, self.across[1].wait_send)
            when(j != 0, self.across[3].wait_send)
            when(edge, self.pass_on.wait_send)

    CH = CQ // 2
    grad_up = Gradient(w1, d14, z13, h1, r1_ref, 0, P1)
    grad_down = Gradient(w2, d24, z23, h2, r2_ref, 0, D)
    grad_proj = Gradient(gp, dp4, zp3, hp, rp_ref, 0, HP)
    grad_qkv = [Gradient(wqc, dq4, zq3, hq, rq_ref, b * CH, CH) for b in range(2)]

    weight_1.drain()
    weight_2.drain()
    weight_q.drain()

    def up_grad(t, carry):
        w1[rows_of(t, tile), :] = mm_tn(mlp[:, rows_of(t, tile)], dge[...]).astype(BF)
        return carry

    lax.fori_loop(0, D // tile, up_grad, 0)
    grad_up.exchange()
    scatter_mlp.relay(2)

    def down(i, carry):
        rows = rows_of(i, T)
        mlp[rows, :] = mm(act[rows, :], w2[...]).astype(BF)
        return carry

    lax.fori_loop(0, n, down, 0)
    grad_up.add_near()

    def down_grad(t, carry):
        lanes = rows_of(t, tile)
        total = mm_tn(act[0:T, lanes], cotb[0])
        for b in range(1, n):
            total = total + mm_tn(act[b * T : (b + 1) * T, lanes], cotb[b])
        w2[lanes, :] = total.astype(BF)
        return carry

    lax.fori_loop(0, P1 // tile, down_grad, 0)
    grad_down.exchange()

    smg[...] = jnp.zeros(smg.shape, F32)
    scatter_mlp.wait_recv()

    def gather_parts(part):
        whole = rows_of_block(me, part)
        total = snd[whole, :].astype(F32)
        return total + rsr[0, part, :].astype(F32) + rsr[1, part, :].astype(F32)

    def add_sum(row, value):
        smg[row : row + 1, :] = smg[row : row + 1, :] + jnp.sum(value, axis=0, keepdims=True)

    def norm_two_back(part):
        upstream = cotb[me, part, :].astype(F32)
        grad = gather_parts(part)
        normed, factor = moments(mid[part, :])
        scaled = grad * vector(3)
        value = upstream + factor * (
            scaled
            - jnp.mean(scaled, axis=-1, keepdims=True)
            - normed * jnp.mean(scaled * normed, axis=-1, keepdims=True)
        )
        gmd[part, :] = value
        low = value.astype(BF)
        snd[rows_of_block(me, part), :] = low
        add_sum(2, low.astype(F32))
        add_sum(3, grad * normed)
        add_sum(4, grad)
        add_sum(5, upstream)

    strips(T, strip, norm_two_back)
    own_rows = rows_of(me, T)
    low_branch = snd[own_rows, :]
    grad_mixed = mm_nt(low_branch, proj_weight()).astype(BF)
    for c in range(n):
        mixc[0, c] = lane_pad(grad_mixed[:, c * hw : (c + 1) * hw], HP)
        mixc[2, c] = lane_pad(low_branch[:, c * hw : (c + 1) * hw], HP)
    head_copies = [
        send(mixc.at[0, seq_to[o]], mixc.at[1, me], {"seq": seq_to[o]}, take()) for o in range(1, n)
    ]
    branch_copies = [
        send(mixc.at[2, seq_to[o]], mixc.at[3, me], {"seq": seq_to[o]}, take()) for o in range(1, n)
    ]
    mixc[1, me] = mixc[0, me]
    mixc[3, me] = mixc[2, me]

    grad_down.add_near()
    grad_up.hop()

    for copy in head_copies:
        copy.wait_recv()
    scatter_out = Scatter(mlp, tokb, (me, me, near_y, near_x))
    for t in range(n - 1):
        scatter_out.start(t)

    def proj_grad(t, carry):
        lanes = rows_of(t, tile)
        total = mm_tn(mix[0:T, lanes], mixc[3, 0])
        for b in range(1, n):
            total = total + mm_tn(mix[b * T : (b + 1) * T, lanes], mixc[3, b])
        gp[lanes, :] = total.astype(BF)
        return carry

    def qkv_grad(half):
        pair = hl // 2 * W

        def body(t, carry):
            rows = rows_of(t, tile)
            parts = []
            for third in range(3):
                at = third * QW + half * pair
                total = mm_tn(ain[:, rows], qkv[:, at : at + pair])
                parts += [total[:, h * W : h * W + HD].astype(BF) for h in range(hl // 2)]
            wqc[rows, half * CH : (half + 1) * CH] = lane_pad(jnp.concatenate(parts, axis=1), CH)
            return carry

        lax.fori_loop(0, D // tile, body, 0)
        grad_qkv[half].exchange()

    def between(h):
        if h == 0:
            for copy in branch_copies:
                copy.wait_recv()
            lax.fori_loop(0, D // tile, proj_grad, 0)
            grad_proj.exchange()
        if h == 1:
            grad_down.hop()
            grad_proj.add_near()
            qkv_grad(0)
            scatter_out.relay(across)
        if h == 2:
            grad_up.add_far()
            grad_up.share()
            grad_qkv[0].add_near()
            grad_proj.hop()
        if h == 3:
            grad_down.add_far()
            grad_down.share()

    for h in range(hl):
        q_at = slice(h * W, (h + 1) * W)
        k_at = slice(QW + h * W, QW + (h + 1) * W)
        v_at = slice(2 * QW + h * W, 2 * QW + (h + 1) * W)
        dkv[...] = jnp.zeros(dkv.shape, F32)

        def attend_back_block(i, carry):
            rows = rows_of(i, T)
            q = qkv[rows, q_at]
            kk = qkv[:, k_at]
            g = lane_pad(mixc[1, i][:, h * HD : (h + 1) * HD], W)
            p = jnp.exp(masked(mm_nt(q, kk), i) - lse[rows, h : h + 1])
            dp = mm_nt(g, qkv[:, v_at])
            dkv[:, W:] = dkv[:, W:] + mm_tn(p.astype(BF), g)
            centre = jnp.sum(p * dp, axis=-1, keepdims=True)
            ds = (p * (dp - centre)).astype(BF)
            dq = (mm(ds, kk) * scale).astype(BF).astype(F32)
            dkv[:, :W] = dkv[:, :W] + mm_tn(ds, q)
            qkv[rows, q_at] = (dq * cosb[rows, :] - swap(dq) * sinb[rows, :]).astype(BF)
            return carry

        lax.fori_loop(0, n, attend_back_block, 0)

        def turn_back(i, carry):
            rows = rows_of(i, T)
            dk = (dkv[rows, :W] * scale).astype(BF).astype(F32)
            qkv[rows, k_at] = (dk * cosb[rows, :] - swap(dk) * sinb[rows, :]).astype(BF)
            qkv[rows, v_at] = dkv[rows, W:].astype(BF)
            return carry

        lax.fori_loop(0, n, turn_back, 0)
        between(h)

    scatter_mlp.wait_send()
    scatter_attn = Scatter(snd, rsr, (0, 1, 2, 2))

    def attn_back(t, carry):
        i = block_at(t)
        rows = rows_of(i, T)
        snd[rows, :] = mm_nt(qkv[rows, :], wq[...]).astype(BF)
        scatter_attn.start(t)
        return carry

    lax.fori_loop(0, n, attn_back, 0)

    grad_qkv[0].hop()
    qkv_grad(1)
    grad_up.relay()
    scatter_attn.relay(2)
    grad_down.relay()
    grad_proj.add_far()
    grad_proj.share()

    def bias_sums(part):
        smg[6:7, :] = smg[6:7, :] + jnp.sum(dge[part, :].astype(F32), axis=0, keepdims=True)
        line = jnp.sum(qkv[part, :].astype(F32), axis=0, keepdims=True)
        line = lane_pad(
            jnp.concatenate([line[:, h * W : h * W + HD] for h in range(3 * hl)], axis=1), D
        )
        smg[7:8, :] = smg[7:8, :] + line

    grad_qkv[1].add_near()
    strips(L, 64, bias_sums)
    grad_qkv[0].add_far()
    grad_qkv[0].share()
    grad_qkv[1].hop()

    scatter_attn.wait_recv()

    def norm_one_back(part):
        grad = gather_parts(part)
        normed, factor = moments(tokb[me, part, :].astype(F32))
        scaled = grad * vector(0)
        gmd[part, :] = gmd[part, :] + factor * (
            scaled
            - jnp.mean(scaled, axis=-1, keepdims=True)
            - normed * jnp.mean(scaled * normed, axis=-1, keepdims=True)
        )
        add_sum(0, grad * normed)
        add_sum(1, grad)

    strips(T, strip, norm_one_back)
    tokens_out = load(gmd, tgrad_ref)
    sum_copies = [
        send(smg, sg8.at[f], {"fsdp": (f + o) % F}, take()) for o in range(1, F)
    ]
    sg8[f] = smg[...]
    grad_proj.relay()
    grad_qkv[0].relay()
    grad_qkv[1].add_far()
    grad_qkv[1].share()

    scatter_out.wait_recv()

    def write_out(part):
        whole = rows_of_block(me, part)
        total = mid[part, :] + mlp[whole, :].astype(F32) + vector(5)
        for slot in (near_x, near_y):
            total = total + tokb[slot, part, :].astype(F32)
        bias_rows = rows_of_block(me, part)
        ain[bias_rows, :] = total.astype(BF)

    strips(T, strip, write_out)
    block_out = load(band(ain, me, T), out_ref)

    for copy in sum_copies:
        copy.wait_recv()
    total = sg8[0]
    for s in range(1, F):
        total = total + sg8[s]
    plain = lax.broadcasted_iota(jnp.int32, total.shape, 0)
    vec[...] = jnp.where(plain < 8, total, 0.0)
    sums_keep = load(vec, sums_ref.at[me])
    sums_share = [
        send(vec, sums_ref.at[me], {"seq": seq_to[o]}, take()) for o in range(1, n)
    ]

    grads = [grad_up, grad_down, grad_proj] + grad_qkv
    grad_qkv[1].relay()
    for item in grads:
        item.finish()
    for copy in sums_share:
        copy.wait_recv()
    sums_keep.wait()
    tokens_out.wait()
    block_out.wait()
    weight_p.drain()
    scatter_attn.wait_send()
    scatter_out.wait_send()
    for copy in leftover:
        copy.wait_send()
    assert used["remote"] <= sems.shape[0] and used["local"] <= local_sems.shape[0], used


def unpack_kernel(
    dims,
    block_in,
    tokens_in,
    rq_in,
    rp_in,
    r1_in,
    r2_in,
    sums_in,
    block_ref,
    tokens_ref,
    qkv_ref,
    proj_ref,
    up_ref,
    down_ref,
    v0,
    v1,
    v2,
    v3,
    v4,
    v5,
    v6,
    v7,
    block,
    tokens,
    rq,
    rp,
    r1,
    r2,
    sums,
    stage,
    in_sems,
    out_sems,
):
    n, T, L, D, F, R, hl, P1, CQ, HP = dims
    hw = hl * HD
    f = lax.axis_index("fsdp")
    loads = []
    for src, dst in (
        (r2_in, r2),
        (r1_in, r1),
        (rq_in, rq),
        (rp_in, rp),
        (tokens_in, tokens),
        (block_in, block),
        (sums_in, sums),
    ):
        copy = pltpu.make_async_copy(src, dst, in_sems.at[len(loads)])
        copy.start()
        loads.append(copy)
    stores = []

    def store(src, dst):
        copy = pltpu.make_async_copy(src, dst, out_sems.at[len(stores)])
        copy.start()
        stores.append(copy)

    loads[0].wait()
    for c in range(n):
        stage[c] = r2[c].astype(F32)
        store(stage.at[c], down_ref.at[c * R : (c + 1) * R])
    loads[1].wait()
    width = n * R
    for c in range(n):
        blocks = range(c * P1 // width, (c + 1) * P1 // width)
        stage[n + c] = jnp.concatenate(
            [r1[m, :, b * R : (b + 1) * R] for b in blocks for m in range(n)], axis=1
        ).astype(F32)
        store(stage.at[n + c], up_ref.at[:, c * P1 : (c + 1) * P1])
    loads[2].wait()
    for t in range(3):
        stage[2 * n + t] = jnp.concatenate(
            [
                rq[m, :, b * CQ // 2 + t * hw // 2 : b * CQ // 2 + (t + 1) * hw // 2]
                for m in range(n)
                for b in range(2)
            ],
            axis=1,
        ).astype(F32)
        store(stage.at[2 * n + t], qkv_ref.at[:, t * D : (t + 1) * D])
    loads[3].wait()
    stage[2 * n + 3] = jnp.concatenate([rp[m, :, :hw] for m in range(n)], axis=1).astype(F32)
    store(stage.at[2 * n + 3], proj_ref)
    loads[4].wait()
    store(tokens, tokens_ref)
    loads[5].wait()
    store(block, block_ref)
    loads[6].wait()
    per_part = hw // R
    for s in range(F):

        @pl.when(f == s)
        def _():
            own = slice(s * R, (s + 1) * R)
            total = sums[0, 0:6, own]
            for m in range(1, n):
                total = total + sums[m, 0:6, own]
            for row, out in enumerate((v0, v1, v2, v3, v4, v5)):
                out[...] = total[row : row + 1, :].reshape(R)
            lines = [sums[m, 6:7, own] for m in range(n)]
            v6[...] = jnp.concatenate(lines, axis=1).reshape(n * R)
            lines = []
            for b in range(3):
                spot = 3 * s + b
                third, rest = spot // (n * per_part), spot % (n * per_part)
                at = third * hw + rest % per_part * R
                lines.append(sums[rest // per_part, 7:8, at : at + R])
            v7[...] = jnp.concatenate(lines, axis=1).reshape(3 * R)

    for copy in stores:
        copy.wait()


def round_up(value, step):
    return -(-value // step) * step


def shards_kernel(
    tokens,
    picture_ids,
    patch_rows,
    patch_cols,
    norm1_gain,
    norm1_bias,
    qkv_weight,
    qkv_bias,
    proj_weight,
    proj_bias,
    norm2_gain,
    norm2_bias,
    fc1_weight,
    fc1_bias,
    fc2_weight,
    fc2_bias,
    cotangent,
):
    n = lax.axis_size("seq")
    me = lax.axis_index("seq")
    F = lax.axis_size("fsdp")
    f = lax.axis_index("fsdp")
    _, T, D = tokens.shape
    L = n * T
    hl = D // HD // n
    hw = hl * HD
    R = D // F
    hidden = fc1_weight.shape[1]
    P1 = hidden // n
    part = hidden // (F * n)
    CQ = round_up(3 * hw, 128)
    HP = round_up(hw, 128)
    J = F // 2
    W = 128

    lines = (
        norm1_gain,
        norm1_bias,
        proj_bias,
        norm2_gain,
        norm2_bias,
        fc2_bias,
        fc1_bias,
        qkv_bias,
    )
    quarter = HD // 4
    inverse = 10000.0 ** (-np.arange(quarter) / quarter)
    wave = np.zeros((8, W), np.float32)
    for c in range(2):
        wave[0, 2 * c * quarter : (2 * c + 1) * quarter] = inverse
        wave[1, (2 * c + 1) * quarter : (2 * c + 2) * quarter] = inverse
    wave[2] = np.where(np.arange(W) < HD // 2, -1.0, 1.0)
    dims = (n, T, L, D, F, R, hl, P1, CQ, HP)
    anywhere = pl.BlockSpec(memory_space=pl.ANY)
    local = pl.BlockSpec(memory_space=pltpu.VMEM)

    def vmem(shape, dtype=BF):
        return pltpu.VMEM(shape, dtype)

    scratch = [
        vmem((n, T, D)),
        vmem((L, D)),
        vmem((n, T, D)),
        vmem((n, 8, T), F32),
        vmem((F, 16, R), F32),
        vmem((8, D), F32),
        vmem((8, 3 * hl * W), F32),
        vmem((L, W), F32),
        vmem((L, W), F32),
        vmem((D, CQ)),
        vmem((D, 3 * hl * W)),
        vmem((J, 2, R, D)),
        vmem((D, P1)),
        vmem((P1, D)),
        vmem((L, 3 * hl * W)),
        vmem((L, W), F32),
        vmem((n, n, T, HP)),
        vmem((L, D)),
        vmem((T, D), F32),
        vmem((L, D)),
        vmem((L, P1)),
        vmem((L, P1)),
        vmem((L, D)),
        vmem((n - 1, T, D)),
        vmem((T, D), F32),
        vmem((D, HP)),
        vmem((J, R, CQ)),
        vmem((J, R, HP)),
        vmem((J, R, P1)),
        vmem((J, R, D)),
        vmem((J - 1, R, CQ)),
        vmem((J - 1, R, HP)),
        vmem((J - 1, R, P1)),
        vmem((J - 1, R, D)),
        vmem((L, 2 * W), F32),
        vmem((8, D), F32),
        vmem((F, 8, D), F32),
        vmem((R, CQ)),
        vmem((R, HP)),
        vmem((R, P1)),
        vmem((R, D)),
        pltpu.SemaphoreType.DMA((448,)),
        pltpu.SemaphoreType.DMA((24,)),
    ]
    shapes = (
        jax.ShapeDtypeStruct((T, D), BF),
        jax.ShapeDtypeStruct((T, D), F32),
        jax.ShapeDtypeStruct((n, R, CQ), BF),
        jax.ShapeDtypeStruct((n, R, HP), BF),
        jax.ShapeDtypeStruct((n, R, P1), BF),
        jax.ShapeDtypeStruct((n, R, D), BF),
        jax.ShapeDtypeStruct((n, 8, D), F32),
    )
    block_out, tokens_grad, rq, rp, r1, r2, sums = pl.pallas_call(
        functools.partial(block_kernel, dims),
        out_shape=shapes,
        in_specs=[anywhere] * 2 + [local] * 3 + [(local,) * 8] + [local] + [anywhere] * 4,
        out_specs=[anywhere] * 7,
        scratch_shapes=scratch,
        compiler_params=pltpu.CompilerParams(
            collective_id=0, has_side_effects=True, vmem_limit_bytes=67043328
        ),
    )(
        tokens[0],
        cotangent[0],
        picture_ids,
        patch_rows,
        patch_cols,
        lines,
        wave,
        qkv_weight,
        proj_weight,
        fc1_weight,
        fc2_weight,
    )
    stored = (
        jax.ShapeDtypeStruct((T, D), BF),
        jax.ShapeDtypeStruct((T, D), F32),
        jax.ShapeDtypeStruct((R, 3 * D), F32),
        jax.ShapeDtypeStruct((R, D), F32),
        jax.ShapeDtypeStruct((R, hidden), F32),
        jax.ShapeDtypeStruct((n * R, D), F32),
    ) + tuple(jax.ShapeDtypeStruct((size,), F32) for size in [R] * 6 + [n * R, 3 * R])
    block_out, tokens_grad, full_qkv, full_proj, full_up, full_down, *vectors = pl.pallas_call(
        functools.partial(unpack_kernel, dims),
        out_shape=stored,
        in_specs=[anywhere] * 7,
        out_specs=[anywhere] * 6 + [local] * 8,
        scratch_shapes=[
            vmem((T, D)),
            vmem((T, D), F32),
            vmem((n, R, CQ)),
            vmem((n, R, HP)),
            vmem((n, R, P1)),
            vmem((n, R, D)),
            vmem((n, 8, D), F32),
            vmem((4 + 2 * n, R, D), F32),
            pltpu.SemaphoreType.DMA((7,)),
            pltpu.SemaphoreType.DMA((7 + 2 * n,)),
        ],
        compiler_params=pltpu.CompilerParams(vmem_limit_bytes=67043328),
    )(block_out, tokens_grad, rq, rp, r1, r2, sums)
    return (
        block_out[None],
        tokens_grad[None],
        vectors[0],
        vectors[1],
        full_qkv,
        vectors[7],
        full_proj,
        vectors[2],
        vectors[3],
        vectors[4],
        full_up,
        vectors[6],
        full_down,
        vectors[5],
    )


def fits_kernel(mesh):
    return dict(mesh.shape) == {"seq": 4, "fsdp": 8}


def shards_plain(
    tokens,
    picture_ids,
    patch_rows,
    patch_cols,
    norm1_gain,
    norm1_bias,
    qkv_weight,
    qkv_bias,
    proj_weight,
    proj_bias,
    norm2_gain,
    norm2_bias,
    fc1_weight,
    fc1_bias,
    fc2_weight,
    fc2_bias,
    cotangent,
):
    n = lax.axis_size("seq")
    me = lax.axis_index("seq")
    stores = lax.axis_size("fsdp")
    _, own, width = tokens.shape
    heads = width // HD
    local_heads = heads // n
    hw = local_heads * HD
    rows = qkv_weight.shape[0]
    hidden = fc1_weight.shape[1]
    part = hidden // (stores * n)

    def pick(value, axis):
        return lax.dynamic_index_in_dim(value, me, axis, keepdims=False)

    own_qkv = pick(qkv_weight.reshape(rows, 3, n, hw), 2).reshape(rows, 3 * hw)
    own_up = pick(fc1_weight.reshape(rows, stores, n, part), 2).reshape(rows, stores * part)
    own_down = pick(fc2_weight.reshape(n, part, width), 0)
    small = (norm1_gain, norm1_bias, proj_bias, norm2_gain, norm2_bias, fc2_bias, qkv_bias, fc1_bias)
    sizes = [item.shape[0] for item in small]
    packed = gather(jnp.concatenate(small)[None], "fsdp")
    weight_qkv = gather(own_qkv, "fsdp")
    weight_proj = gather(proj_weight, "fsdp")
    weight_up = gather(own_up, "fsdp")
    weight_down = gather(own_down, "fsdp")
    params = []
    start = 0
    for size in sizes:
        params.append(packed[:, start : start + size].reshape(-1).astype(F32))
        start += size
    gain_one, bias_one, bias_proj, gain_two, bias_two, bias_down, bias_qkv, bias_up = params
    bias_qkv = pick(bias_qkv.reshape(3, n, hw), 1).reshape(3 * hw)
    bias_up = pick(bias_up.reshape(stores, n, part), 1).reshape(stores * part)

    places = jnp.stack([picture_ids[0], patch_rows[0], patch_cols[0]])
    places = gather(places, "seq", 1)
    picture = places[0]
    all_tokens = gather(tokens[0], "seq").astype(F32)
    upstream = gather(cotangent[0], "seq")
    length = all_tokens.shape[0]

    def mine(value):
        return lax.dynamic_slice_in_dim(value, me * own, own, 0)

    normed_one, factor_one = standardize(all_tokens)
    attn_input = (normed_one * gain_one + bias_one).astype(BF)
    projected = (dot(attn_input, weight_qkv) + bias_qkv).reshape(length, 3, local_heads, HD)
    cosine, sine = rotary_tables(places[1], places[2], HD)
    queries = rotate(projected[:, 0], cosine, sine).astype(BF)
    keys = rotate(projected[:, 1], cosine, sine).astype(BF)
    values = projected[:, 2].astype(BF)
    mixed_own, log_total = attend(queries, keys, values, picture)
    mixed = gather(mixed_own.reshape(length, hw), "seq", 1)
    middle = all_tokens + dot(mixed, weight_proj) + bias_proj
    normed_two, factor_two = standardize(middle)
    mlp_input = (normed_two * gain_two + bias_two).astype(BF)
    before = dot(mlp_input, weight_up) + bias_up
    gate = jax.nn.sigmoid(1.702 * before)
    activated = (before * gate).astype(BF)
    out_part = dot(activated, weight_down).astype(BF)
    block_out = (mine(middle) + scatter_sum(out_part, "seq").astype(F32) + bias_down).astype(BF)

    grad_down = scatter_sum(rows_term(activated, upstream).astype(BF), "fsdp")
    grad_activated = contract_back(upstream, weight_down)
    grad_before = (grad_activated * (gate + 1.702 * before * gate * (1.0 - gate))).astype(BF)
    grad_up = scatter_sum(rows_term(mlp_input, grad_before).astype(BF), "fsdp")
    grad_mlp_input = scatter_sum(contract_back(grad_before, weight_up).astype(BF), "seq").astype(F32)
    own_upstream = cotangent[0].astype(F32)
    own_two = mine(normed_two)
    grad_middle = own_upstream + norm_back(grad_mlp_input, own_two, mine(factor_two), gain_two)
    grad_branch = grad_middle.astype(BF)
    grad_mixed = contract_back(grad_branch, weight_proj).astype(BF)
    grad_heads = lax.all_to_all(grad_mixed, "seq", split_axis=1, concat_axis=0, tiled=True)
    branch_part = lax.all_to_all(grad_branch, "seq", split_axis=1, concat_axis=0, tiled=True)
    grad_proj = scatter_sum(rows_term(mixed, branch_part).astype(BF), "fsdp")
    grad_queries, grad_keys, grad_values = attend_back(
        queries, keys, values, picture, grad_heads.reshape(length, local_heads, HD), log_total
    )
    grad_projected = jnp.stack(
        [
            unrotate(grad_queries.astype(F32), cosine, sine).astype(BF),
            unrotate(grad_keys.astype(F32), cosine, sine).astype(BF),
            grad_values,
        ],
        axis=1,
    ).reshape(length, 3 * hw)
    grad_qkv = scatter_sum(rows_term(attn_input, grad_projected).astype(BF), "fsdp")
    grad_attn_input = scatter_sum(contract_back(grad_projected, weight_qkv).astype(BF), "seq").astype(F32)
    own_one = mine(normed_one)
    tokens_grad = grad_middle + norm_back(grad_attn_input, own_one, mine(factor_one), gain_one)

    def spread(value, groups):
        empty = jnp.zeros((groups, n, value.shape[0] // groups), F32)
        return lax.dynamic_update_slice_in_dim(
            empty, value.reshape(groups, 1, -1), me, 1
        ).reshape(stores, -1)

    sums = [
        jnp.sum(grad_attn_input * own_one, axis=0).reshape(stores, -1),
        jnp.sum(grad_attn_input, axis=0).reshape(stores, -1),
        jnp.sum(grad_branch.astype(F32), axis=0).reshape(stores, -1),
        jnp.sum(grad_mlp_input * own_two, axis=0).reshape(stores, -1),
        jnp.sum(grad_mlp_input, axis=0).reshape(stores, -1),
        jnp.sum(own_upstream, axis=0).reshape(stores, -1),
        spread(jnp.sum(grad_projected.astype(F32), axis=0), 3),
        spread(jnp.sum(grad_before.astype(F32), axis=0), stores),
    ]
    summed = lax.psum(scatter_sum(jnp.concatenate(sums, axis=1), "fsdp"), "seq")[0]
    finals = []
    start = 0
    for size in sizes:
        finals.append(summed[start : start + size])
        start += size
    full_down = gather(grad_down, "seq").astype(F32)
    full_up = gather(grad_up[None], "seq").reshape(n, rows, stores, part)
    full_up = full_up.transpose(1, 2, 0, 3).reshape(rows, hidden).astype(F32)
    full_proj = gather(grad_proj, "seq", 1).astype(F32)
    full_qkv = gather(grad_qkv[None], "seq").reshape(n, rows, 3, hw)
    full_qkv = full_qkv.transpose(1, 2, 0, 3).reshape(rows, 3 * width).astype(F32)
    return (
        block_out[None],
        tokens_grad[None],
        finals[0],
        finals[1],
        full_qkv,
        finals[6],
        full_proj,
        finals[2],
        finals[3],
        finals[4],
        full_up,
        finals[7],
        full_down,
        finals[5],
    )


def solution(mesh):
    token = P("fsdp", "seq", None)
    place = P("fsdp", "seq")
    vector = P("fsdp")
    matrix = P("fsdp", None)
    in_specs = (
        token,
        place,
        place,
        place,
        vector,
        vector,
        matrix,
        vector,
        matrix,
        vector,
        vector,
        vector,
        matrix,
        vector,
        matrix,
        vector,
        token,
    )
    out_specs = (
        token,
        token,
        vector,
        vector,
        matrix,
        vector,
        matrix,
        vector,
        vector,
        vector,
        matrix,
        vector,
        matrix,
        vector,
    )
    shards = shards_kernel if fits_kernel(mesh) else shards_plain
    return jax.shard_map(shards, mesh=mesh, in_specs=in_specs, out_specs=out_specs, check_vma=False)
```

```python
import functools

import jax
import jax.numpy as jnp
import numpy as np
from jax import lax
from jax.experimental import pallas as pl
from jax.experimental.pallas import tpu as pltpu
from jax.sharding import PartitionSpec as P

HD = 80
NORM_EPSILON = 1e-06
MASKED = -1e30
BF = jnp.bfloat16
F32 = jnp.float32


def standardize(values_in):
    centre = jnp.mean(values_in, axis=-1, keepdims=True)
    shifted = values_in - centre
    factor = lax.rsqrt(jnp.mean(shifted * shifted, axis=-1, keepdims=True) + NORM_EPSILON)
    return (shifted * factor, factor)


def norm_back(grad_out, normed, factor, gain):
    scaled = grad_out * gain
    return factor * (
        scaled
        - jnp.mean(scaled, axis=-1, keepdims=True)
        - normed * jnp.mean(scaled * normed, axis=-1, keepdims=True)
    )


def rotary_tables(patch_row, patch_col, head_size):
    quarter = head_size // 4
    inverse = jnp.power(10000.0, -jnp.arange(quarter, dtype=F32) / quarter)
    half_angles = jnp.concatenate(
        [
            patch_row.astype(F32)[..., None] * inverse,
            patch_col.astype(F32)[..., None] * inverse,
        ],
        axis=-1,
    )
    angles = jnp.concatenate([half_angles, half_angles], axis=-1)
    return (jnp.cos(angles)[..., None, :], jnp.sin(angles)[..., None, :])


def rotate(values_in, cosine, sine):
    half_size = values_in.shape[-1] // 2
    turned = jnp.concatenate([-values_in[..., half_size:], values_in[..., :half_size]], axis=-1)
    return values_in * cosine + turned * sine


def unrotate(grad_in, cosine, sine):
    half_size = grad_in.shape[-1] // 2
    moved = grad_in * sine
    return grad_in * cosine + jnp.concatenate(
        [moved[..., half_size:], -moved[..., :half_size]], axis=-1
    )


def masked_scores(queries, keys, picture, factor):
    places = jnp.arange(picture.shape[0], dtype=jnp.int32)
    scores = jnp.einsum("qhd,khd->hqk", queries, keys, preferred_element_type=F32) * factor
    allowed = (picture[:, None] == picture[None, :]) & (
        (picture[None, :] >= 0) | (places[:, None] == places[None, :])
    )
    return jnp.where(allowed[None, :, :], scores, MASKED)


def attend(queries, keys, values, picture):
    scores = masked_scores(queries, keys, picture, HD**-0.5)
    row_max = jnp.max(scores, axis=-1, keepdims=True)
    powers = jnp.exp(scores - row_max)
    totals = jnp.sum(powers, axis=-1, keepdims=True)
    weights = (powers / totals).astype(BF)
    mixed = jnp.einsum("hqk,khd->qhd", weights, values, preferred_element_type=F32)
    return mixed.astype(BF), row_max + jnp.log(totals)


def attend_back(queries, keys, values, picture, grad_mixed, log_total):
    factor = HD**-0.5
    scores = masked_scores(queries, keys, picture, factor)
    probs = jnp.exp(scores - log_total)
    weights = probs.astype(BF)
    grad_values = jnp.einsum("hqk,qhd->khd", weights, grad_mixed, preferred_element_type=F32)
    grad_weights = jnp.einsum("qhd,khd->hqk", grad_mixed, values, preferred_element_type=F32)
    centre = jnp.sum(probs * grad_weights, axis=-1, keepdims=True)
    grad_scores = (probs * (grad_weights - centre)).astype(BF)
    grad_queries = jnp.einsum("hqk,khd->qhd", grad_scores, keys, preferred_element_type=F32) * factor
    grad_keys = jnp.einsum("hqk,qhd->khd", grad_scores, queries, preferred_element_type=F32) * factor
    return grad_queries.astype(BF), grad_keys.astype(BF), grad_values.astype(BF)


def dot(left, right):
    return jnp.dot(left, right, preferred_element_type=F32)


def rows_term(left, right):
    return lax.dot_general(left, right, (((0,), (0,)), ((), ())), preferred_element_type=F32)


def contract_back(grad_out, weight):
    return lax.dot_general(grad_out, weight, (((1,), (1,)), ((), ())), preferred_element_type=F32)


def gather(value, axis_name, axis=0):
    return lax.all_gather(value, axis_name, axis=axis, tiled=True)


def scatter_sum(value, axis_name, axis=0):
    return lax.psum_scatter(value, axis_name, scatter_dimension=axis, tiled=True)

MESH = pl.DeviceIdType.MESH


def mm(left, right):
    return jnp.dot(left, right, preferred_element_type=F32)


def mm_nt(left, right):
    return lax.dot_general(left, right, (((1,), (1,)), ((), ())), preferred_element_type=F32)


def mm_tn(left, right):
    return lax.dot_general(left, right, (((0,), (0,)), ((), ())), preferred_element_type=F32)


def lane_pad(value, lanes):
    gap = lanes - value.shape[1]
    if gap == 0:
        return value
    return jnp.concatenate([value, jnp.zeros((value.shape[0], gap), value.dtype)], axis=1)


def moments(value):
    centre = jnp.mean(value, axis=-1, keepdims=True)
    shifted = value - centre
    factor = lax.rsqrt(jnp.mean(shifted * shifted, axis=-1, keepdims=True) + NORM_EPSILON)
    return shifted * factor, factor


def block_kernel(
    dims,
    tok_in,
    cot_in,
    ids_in,
    row_in,
    col_in,
    vec_ins,
    wave_in,
    wq_in,
    wp_in,
    w1_in,
    w2_in,
    out_ref,
    tgrad_ref,
    rq_ref,
    rp_ref,
    r1_ref,
    r2_ref,
    sums_ref,
    tokb,
    ain,
    cotb,
    plb,
    smb,
    vec,
    bqkv,
    cosb,
    sinb,
    wqc,
    wq,
    wp,
    w1,
    w2,
    qkv,
    lse,
    mixc,
    mix,
    mid,
    mlp,
    act,
    dge,
    snd,
    rsr,
    gmd,
    gp,
    dq4,
    dp4,
    d14,
    d24,
    zq3,
    zp3,
    z13,
    z23,
    dkv,
    smg,
    sg8,
    hq,
    hp,
    h1,
    h2,
    sems,
    local_sems,
):
    n, T, L, D, F, R, hl, P1, CQ, HP = dims
    J = F // 2
    hw = hl * HD
    W = 128
    QW = hl * W
    scale = HD**-0.5
    tile = 256 if D % 256 == 0 else 128
    me = lax.axis_index("seq")
    f = lax.axis_index("fsdp")
    k = f % 2
    j = f // 2
    partner = f + 1 - 2 * k
    x = me % 2
    y = me // 2

    def peer(o):
        return (y + o // 2) % 2 * 2 + (x + o % 2) % 2

    seq_to = [peer(o) for o in range(n)]
    seq_from = seq_to
    near_x, near_y, across = seq_to[1], seq_to[2], seq_to[3]
    edge = (j == 0) | (j == J - 1)
    middle = (j > 0) & (j < J - 1)
    z_to = [2 * ((j + d) % J) + k for d in range(J)]
    z_from = [2 * ((j + J - d) % J) + k for d in range(J)]
    used = {"remote": 0, "local": 0}
    leftover = []

    def take(count=1):
        used["remote"] += count
        return used["remote"] - count

    def remote(src, dst, where, recv):
        return pltpu.make_async_remote_copy(
            src_ref=src,
            dst_ref=dst,
            send_sem=sems.at[take()],
            recv_sem=sems.at[recv],
            device_id=where,
            device_id_type=MESH,
        )

    def when(condition, action):
        pl.when(condition)(action)

    def send(src, dst, where, recv, late=True):
        copy = remote(src, dst, where, recv)
        copy.start()
        if late:
            leftover.append(copy)
        return copy

    def load(src, dst):
        used["local"] += 1
        copy = pltpu.make_async_copy(src, dst, local_sems.at[used["local"] - 1])
        copy.start()
        return copy

    def band(ref, index, size):
        return ref.at[pl.ds(pl.multiple_of(index * size, size), size)]

    def rows_of(index, size):
        return pl.ds(pl.multiple_of(index * size, size), size)

    def strips(total, step, body):
        def run(s, carry):
            body(rows_of(s, step))
            return carry

        lax.fori_loop(0, total // step, run, 0)

    strip = 32

    spot = lax.broadcasted_iota(jnp.int32, (1, T), 1) + me * T
    ids = ids_in[...]
    plb[me, 0:4, :] = jnp.concatenate(
        [
            ids.astype(F32),
            row_in[...].astype(F32),
            col_in[...].astype(F32),
            jnp.where(ids >= 0, ids, -1 - spot).astype(F32),
        ],
        axis=0,
    )
    plb[me, 4:8, :] = jnp.zeros((4, T), F32)
    for row in range(6):
        smb[f, row : row + 1, :] = vec_ins[row][...].astype(F32).reshape(1, R)
    up_bias = vec_ins[6][...].astype(F32).reshape(1, n * R)
    for m in range(n):

        @pl.when(me == m)
        def _():
            smb[f, 6:7, :] = up_bias[:, m * R : (m + 1) * R]

    qkv_bias = vec_ins[7][...].astype(F32).reshape(1, 3 * R)
    for t in range(3):
        smb[f, 7 + t : 8 + t, :] = qkv_bias[:, t * R : (t + 1) * R]
    smb[f, 10:16, :] = jnp.zeros((6, R), F32)

    raw_q = [load(wq_in.at[:, t * D : (t + 1) * D], d24.at[t]) for t in range(3)]
    raw_1 = [load(w1_in.at[:, c * P1 : (c + 1) * P1], d14.at[c]) for c in range(n)]

    barrier = pltpu.get_barrier_semaphore()
    for o in range(1, n):
        pl.semaphore_signal(barrier, inc=1, device_id={"seq": seq_to[o]}, device_id_type=MESH)
    for o in range(1, F):
        pl.semaphore_signal(barrier, inc=1, device_id={"fsdp": (f + o) % F}, device_id_type=MESH)
    pl.semaphore_wait(barrier, n - 1 + F - 1)

    class Spread:
        def __init__(self, src, at, rows):
            self.at, self.rows = at, rows
            self.first = [
                send(src, at(me, 0, rows), {"seq": seq_to[o]}, take()) for o in (1, 2)
            ]

        def relay(self):
            half = self.rows // 2
            self.first[0].wait_recv()
            part = self.at(near_x, 0, half)
            one = send(part, part, {"seq": near_y}, take(), late=False)
            self.first[1].wait_recv()
            part = self.at(near_y, half, self.rows)
            self.second = [one, send(part, part, {"seq": near_x}, take(), late=False)]

        def finish(self):
            for copy in self.second:
                copy.wait_recv()

        def drain(self):
            for copy in self.second:
                copy.wait_send()

    def rows_in(ref):
        return lambda index, lo, hi: ref.at[index, lo:hi]

    plc_copies = [
        send(plb.at[me], plb.at[me], {"seq": seq_to[o]}, take()) for o in range(1, n)
    ]
    tok = Spread(tok_in, rows_in(tokb), T)
    own_tok = load(tok_in, tokb.at[me])

    class Weight:
        def __init__(self, src, buf, rows):
            self.buf, self.rows = buf, rows
            self.own = None
            mine = band(buf, f, rows)
            if src is None:
                src = mine
            else:
                self.own = load(src, mine)
            self.near = send(src, mine, {"fsdp": partner}, take(), late=False)
            landed = {d: take() for d in (1, 2, 3)}
            self.far = {d: remote(src, mine, {"fsdp": z_to[d]}, landed[d]) for d in (1, 2, 3)}
            self.far[2].start()
            when(j != J - 1, self.far[1].start)
            when(j != 0, self.far[3].start)
            part = band(buf, z_from[2], rows)
            self.down = remote(part, part, {"fsdp": k}, landed[1])
            self.up = remote(part, part, {"fsdp": 2 * (J - 1) + k}, landed[3])
            self.relayed = []

        def hop(self):
            self.far[2].wait_recv()
            when(j == 1, self.down.start)
            when(j == J - 2, self.up.start)

        def relay(self):
            for d in (2, 1, 3):
                if d != 2:
                    self.far[d].wait_recv()
                part = band(self.buf, z_from[d], self.rows)
                self.relayed.append(send(part, part, {"fsdp": partner}, take(), late=False))

        def finish(self):
            if self.own is not None:
                self.own.wait()
            self.near.wait_recv()
            for copy in self.relayed:
                copy.wait_recv()

        def drain(self):
            for copy in [self.near, self.far[2]] + self.relayed:
                copy.wait_send()
            when(j != J - 1, self.far[1].wait_send)
            when(j != 0, self.far[3].wait_send)
            when(j == 1, self.down.wait_send)
            when(j == J - 2, self.up.wait_send)

    class Quarter:
        def __init__(self):
            self.cols = pl.ds(pl.multiple_of(x * (D // 2), D // 2), D // 2)
            self.holder, self.other = y == k, y != k
            used["local"] += 1
            self.own = pltpu.make_async_copy(
                wp_in.at[:, self.cols],
                wp.at[j, k, :, self.cols],
                local_sems.at[used["local"] - 1],
            )
            when(self.holder, self.own.start)
            landed = {d: take() for d in (1, 2, 3)}
            mine = wp.at[j, k, :, self.cols]
            self.far = {
                d: remote(wp_in.at[:, self.cols], mine, {"fsdp": z_to[d]}, landed[d])
                for d in (1, 2, 3)
            }
            part = wp.at[z_from[2] // 2, k, :, self.cols]
            self.down = remote(part, part, {"fsdp": k}, landed[1])
            self.up = remote(part, part, {"fsdp": 2 * (J - 1) + k}, landed[3])
            when(self.holder, self.far[2].start)
            when(self.holder & (j != J - 1), self.far[1].start)
            when(self.holder & (j != 0), self.far[3].start)

            def quarter(device_y, device_x, lo, hi):
                cols = pl.ds(pl.multiple_of(device_x * (D // 2), D // 2), D // 2)
                return wp.at[lo:hi, device_y, :, cols]

            to_x, to_y, to_core = {"seq": near_x}, {"seq": near_y}, {"fsdp": partner}
            h = J // 2
            whole = quarter(y, x, 0, J)
            self.give = [remote(whole, whole, where, take()) for where in (to_x, to_y, to_core)]
            q = quarter(y, 1 - x, 0, J)
            self.along_x = remote(q, q, to_core, take())
            q = quarter(y, 1 - x, 0, h)
            self.on_y = remote(q, q, to_y, take())
            q = quarter(1 - y, x, 0, J)
            self.along_y = remote(q, q, to_core, take())
            q = quarter(1 - y, x, h, J)
            self.on_x = remote(q, q, to_x, take())
            q = quarter(1 - y, 1 - x, 0, J)
            self.last = remote(q, q, to_core, take())

        def hop(self):
            @pl.when(self.holder)
            def _():
                self.far[2].wait_recv()
                when(j == 1, self.down.start)
                when(j == J - 2, self.up.start)

        def start_give(self):
            @pl.when(self.holder)
            def _():
                self.own.wait()
                self.far[1].wait_recv()
                self.far[3].wait_recv()
                for copy in self.give:
                    copy.start()

        def relay(self):
            @pl.when(self.holder)
            def _():
                self.give[0].wait_recv()
                self.on_y.start()
                self.along_x.start()

            @pl.when(self.other)
            def _():
                self.give[1].wait_recv()
                self.on_x.start()
                self.along_y.start()

        def relay_last(self):
            @pl.when(self.other)
            def _():
                self.on_y.wait_recv()
                self.on_x.wait_recv()
                self.last.start()

        def finish(self):
            @pl.when(self.holder)
            def _():
                self.along_y.wait_recv()
                self.last.wait_recv()

            @pl.when(self.other)
            def _():
                self.give[2].wait_recv()
                self.along_x.wait_recv()

        def drain(self):
            @pl.when(self.holder)
            def _():
                for copy in self.give + [self.along_x, self.on_y, self.far[2]]:
                    copy.wait_send()
                when(j != J - 1, self.far[1].wait_send)
                when(j != 0, self.far[3].wait_send)
                when(j == 1, self.down.wait_send)
                when(j == J - 2, self.up.wait_send)

            @pl.when(self.other)
            def _():
                for copy in (self.along_y, self.on_x, self.last):
                    copy.wait_send()

    def cut_columns(target, lines):
        for m in range(n):

            @pl.when(me == m)
            def _():
                target[rows_of(f, R), :] = lane_pad(
                    jnp.concatenate(lines(m), axis=1), target.shape[1]
                )

    small_copies = [
        send(smb.at[f], smb.at[f], {"fsdp": (f + o) % F}, take()) for o in range(1, F)
    ]
    for copy in raw_q:
        copy.wait()
    cut_columns(wqc, lambda m: [d24[t, :, m * hw : (m + 1) * hw] for t in range(3)])
    weight_q = Weight(None, wqc, R)
    for copy in raw_1:
        copy.wait()
    cut_columns(
        w1,
        lambda m: [
            d14[b * n * R // P1, :, b * n * R % P1 + m * R : b * n * R % P1 + (m + 1) * R]
            for b in range(F)
        ],
    )

    for copy in small_copies:
        copy.wait_recv()
    for row in range(7):
        vec[row : row + 1, :] = jnp.concatenate(
            [smb[s, row : row + 1, :R] for s in range(F)], axis=1
        )
    groups = 3 * D // R // 3
    heads = []
    for t in range(3):
        start = t * groups + me * (hw // R)
        line = jnp.concatenate(
            [
                smb[(start + b) // 3, pl.ds(7 + (start + b) % 3, 1), :][:, :R]
                for b in range(hw // R)
            ],
            axis=1,
        )
        for h in range(hl):
            heads.append(lane_pad(line[:, h * HD : (h + 1) * HD], W))
    bqkv[...] = jnp.broadcast_to(jnp.concatenate(heads, axis=1), bqkv.shape)

    def vector(row):
        return vec[row : row + 1, :]

    def rows_of_block(i, rows):
        return pl.ds(pl.multiple_of(i * T + rows.start, strip), strip)

    def norm_one(i):
        def body(rows):
            normed, _ = moments(tokb[i, rows, :].astype(F32))
            ain[rows_of_block(i, rows), :] = (normed * vector(0) + vector(1)).astype(BF)

        strips(T, strip, body)

    own_tok.wait()
    norm_one(me)
    tok.relay()
    weight_q.hop()
    weight_p = Quarter()
    weight_1 = Weight(None, w1, R)
    own_cot = load(cot_in, cotb.at[me])
    cot = Spread(cot_in, rows_in(cotb), T)
    norm_one(near_x)
    norm_one(near_y)

    for copy in plc_copies:
        copy.wait_recv()

    def table(i, carry):
        rows = rows_of(i, T)
        turned = jnp.transpose(plb[i], (1, 0))
        lse[rows, hl : hl + 8] = turned
        angle = turned[:, 1:2] * wave_in[0:1, :] + turned[:, 2:3] * wave_in[1:2, :]
        cosb[rows, :] = jnp.cos(angle)
        sinb[rows, :] = jnp.sin(angle) * wave_in[2:3, :]
        return carry

    lax.fori_loop(0, n, table, 0)
    lane = lax.broadcasted_iota(jnp.int32, (1, W), 1)
    low_half = lane < HD // 2

    def swap(value):
        return jnp.where(
            low_half, pltpu.roll(value, W - HD // 2, 1), pltpu.roll(value, HD // 2, 1)
        )

    tok.finish()
    norm_one(across)

    weight_q.relay()
    weight_p.hop()
    weight_q.finish()

    def spread_heads(rows):
        line = wqc[rows, :]
        for h in range(3 * hl):
            wq[rows, h * W : (h + 1) * W] = lane_pad(line[:, h * HD : (h + 1) * HD], W)

    strips(D, R, spread_heads)

    def project(i, carry):
        rows = rows_of(i, T)
        line = ain[rows, :]
        cosine = cosb[rows, :]
        sine = sinb[rows, :]
        for t in range(3):
            part = mm(line, wq[:, t * QW : (t + 1) * QW]) + bqkv[0:1, t * QW : (t + 1) * QW]
            for h in range(hl):
                u = part[:, h * W : (h + 1) * W]
                if t < 2:
                    u = u * cosine + swap(u) * sine
                qkv[rows, t * QW + h * W : t * QW + (h + 1) * W] = u.astype(BF)
        return carry

    weight_p.start_give()
    lax.fori_loop(0, n, project, 0)

    def masked(scores, i):
        ids = jnp.concatenate([plb[b, 3:4, :] for b in range(n)], axis=1)
        own_ids = lse[rows_of(i, T), hl + 3 : hl + 4]
        return jnp.where(own_ids == ids, scores * scale, MASKED)

    mix_send, mix_recv = take(4 * n), take(4 * n)

    def mix_copy(i, spot, part, where):
        return pltpu.make_async_remote_copy(
            src_ref=part,
            dst_ref=part,
            send_sem=sems.at[mix_send + 4 * i + spot],
            recv_sem=sems.at[mix_recv + 4 * i + spot],
            device_id={"seq": where},
            device_id_type=MESH,
        )

    def mix_first(i, o, source):
        return mix_copy(i, o - 1, mixc.at[source, i], seq_to[o])

    def mix_pass(i, o):
        part = mixc.at[seq_to[o], i, (o - 1) * T // 2 : o * T // 2]
        return mix_copy(i, o + 1, part, seq_to[3 - o])

    def mix_relay(i):
        for o in (1, 2):
            mix_first(i, o, seq_to[o]).wait_recv()
            mix_pass(i, o).start()

    def attend_block(i, carry):
        rows = rows_of(i, T)
        outs = []
        logs = lse[rows, :]
        for h in range(hl):
            q = qkv[rows, h * W : (h + 1) * W]
            kk = qkv[:, QW + h * W : QW + (h + 1) * W]
            v = qkv[:, 2 * QW + h * W : 2 * QW + (h + 1) * W]
            s = masked(mm_nt(q, kk), i)
            top = jnp.max(s, axis=-1, keepdims=True)
            p = jnp.exp(s - top)
            total = jnp.sum(p, axis=-1, keepdims=True)
            outs.append((mm(p.astype(BF), v) / total)[:, :HD].astype(BF))
            logs = jnp.where(lane == h, top + jnp.log(total), logs)
        lse[rows, :] = logs
        mixc[me, i] = lane_pad(jnp.concatenate(outs, axis=1), HP)
        for o in (1, 2):
            mix_first(i, o, me).start()
        when(i > 0, lambda: mix_relay(i - 1))
        return carry

    weight_2 = Weight(w2_in.at[rows_of(me, R)], w2, R)
    lax.fori_loop(0, n // 2, attend_block, 0)
    weight_p.relay()
    lax.fori_loop(n // 2, n, attend_block, 0)
    weight_1.hop()
    weight_p.relay_last()
    weight_p.finish()
    tok.drain()

    def proj_weight():
        return wp[...].reshape(D, D)

    def branch(i, carry):
        rows = rows_of(i, T)
        for o in (1, 2):
            mix_pass(i, o).wait_recv()
        mix[rows, :] = jnp.concatenate([mixc[c, i][:, :hw] for c in range(n)], axis=1)
        gmd[...] = mm(mix[rows, :], proj_weight())

        def body(part):
            whole = rows_of_block(i, part)
            value = gmd[part, :] + tokb[i, part, :].astype(F32) + vector(2)

            @pl.when(i == me)
            def _():
                mid[part, :] = value

            normed, _ = moments(value)
            mlp[whole, :] = (normed * vector(3) + vector(4)).astype(BF)

        strips(T, strip, body)
        return carry

    lax.fori_loop(0, 1, branch, 0)
    mix_relay(n - 1)
    cot.relay()
    lax.fori_loop(1, 2, branch, 0)
    weight_2.hop()
    weight_1.relay()
    lax.fori_loop(2, n, branch, 0)

    weight_1.finish()

    def up(i, carry):
        rows = rows_of(i, T)
        before = mm(mlp[rows, :], w1[...]) + vector(6)
        gate = jax.nn.sigmoid(1.702 * before)
        act[rows, :] = (before * gate).astype(BF)
        dge[rows, :] = (gate + 1.702 * before * gate * (1.0 - gate)).astype(BF)
        return carry

    lax.fori_loop(0, n, up, 0)

    own_cot.wait()
    cot.finish()
    cot.drain()
    weight_2.relay()
    weight_2.finish()

    half = T // 2

    class Scatter:
        def __init__(self, stage, landing, slots):
            self.stage, self.landing = stage, landing
            slot_x, slot_y, pass_x, pass_y = slots
            to_x, to_y = {"seq": near_x}, {"seq": near_y}
            self.pass_a = self.make(across, 0, pass_x, to_x)
            self.pass_b = self.make(across, 1, pass_y, to_y)
            self.last_a = self.make(near_x, 0, slot_x, to_x)
            self.last_b = self.make(near_y, 1, slot_y, to_y)
            self.sum_a = self.make(near_y, 0, slot_y, to_y)
            self.sum_b = self.make(near_x, 1, slot_x, to_x)

        def make(self, block, part, slot, where):
            return remote(
                self.stage.at[self.rows(block, part)],
                self.landing.at[slot, part * half : (part + 1) * half],
                where,
                take(),
            )

        def rows(self, block, part):
            return pl.ds(pl.multiple_of(block * T + part * half, half), half)

        def start(self, t):
            @pl.when(t == 0)
            def _():
                self.pass_a.start()
                self.pass_b.start()

            when(t == 1, self.last_a.start)
            when(t == 2, self.last_b.start)

        def relay(self, slot):
            for part, into, out, block in (
                (0, self.pass_a, self.sum_a, near_y),
                (1, self.pass_b, self.sum_b, near_x),
            ):
                into.wait_recv()

                def body(rows):
                    at = pl.ds(pl.multiple_of(block * T + part * half + rows.start, strip), strip)
                    there = pl.ds(pl.multiple_of(part * half + rows.start, strip), strip)
                    self.stage[at, :] = (
                        self.stage[at, :].astype(F32) + self.landing[slot, there, :].astype(F32)
                    ).astype(BF)

                strips(half, strip, body)
                out.start()

        def wait_recv(self):
            for copy in (self.last_a, self.last_b, self.sum_a, self.sum_b):
                copy.wait_recv()

        def wait_send(self):
            for copy in (
                self.pass_a,
                self.pass_b,
                self.last_a,
                self.last_b,
                self.sum_a,
                self.sum_b,
            ):
                copy.wait_send()

    def block_at(t):
        return peer(((t + 2) % 3 + 1) * (1 - t // 3))

    for i in range(n):
        for o in (1, 2):
            mix_first(i, o, me).wait_send()
            mix_pass(i, o).wait_send()
    scatter_mlp = Scatter(snd, rsr, (0, 1, 2, 2))

    def back(t, carry):
        i = block_at(t)
        rows = rows_of(i, T)
        grad = (mm_nt(cotb[i], w2[...]) * dge[rows, :].astype(F32)).astype(BF)
        dge[rows, :] = grad
        snd[rows, :] = mm_nt(grad, w1[...]).astype(BF)
        scatter_mlp.start(t)
        return carry

    lax.fori_loop(0, n, back, 0)

    class Gradient:
        def __init__(self, grad, other, far, extra, result, lo, width):
            self.grad, self.other, self.far, self.extra = grad, other, far, extra
            self.result, self.lanes = result, slice(lo, lo + width)

        def of(self, index):
            return self.grad.at[rows_of(index, R), self.lanes]

        def exchange(self):
            self.near = [
                send(
                    self.of(2 * c + 1 - k),
                    self.other.at[c, :, self.lanes],
                    {"fsdp": partner},
                    take(),
                )
                for c in range(J)
            ]

        def add_near(self):
            for copy in self.near:
                copy.wait_recv()
            lanes = self.lanes

            def chip(c, carry):
                rows = rows_of(2 * c + k, R)
                self.grad[rows, lanes] = (
                    self.grad[rows, lanes].astype(F32) + self.other[c, :, lanes].astype(F32)
                ).astype(BF)
                return carry

            lax.fori_loop(0, J, chip, 0)
            self.pass_on = remote(
                self.of(2 * (J - 1 - j) + k),
                self.extra.at[:, lanes],
                {"fsdp": 2 * (1 + j // (J - 1)) + k},
                take(),
            )
            self.across = {
                d: remote(
                    self.of(z_to[d]), self.far.at[d - 1, :, lanes], {"fsdp": z_to[d]}, take()
                )
                for d in (1, 2, 3)
            }
            when(edge, self.pass_on.start)
            when(edge, self.across[2].start)
            when(j != J - 1, self.across[1].start)
            when(j != 0, self.across[3].start)

        def hop(self):
            @pl.when(middle)
            def _():
                self.pass_on.wait_recv()
                rows = rows_of(z_to[2], R)
                self.grad[rows, self.lanes] = (
                    self.grad[rows, self.lanes].astype(F32)
                    + self.extra[:, self.lanes].astype(F32)
                ).astype(BF)
                self.across[2].start()

        def add_far(self):
            def total_of(steps):
                def action():
                    for d in steps:
                        self.across[d].wait_recv()
                    total = self.grad[rows_of(f, R), self.lanes].astype(F32)
                    for d in steps:
                        total = total + self.far[d - 1, :, self.lanes].astype(F32)
                    self.other[0, :, self.lanes] = total.astype(BF)

                return action

            when(j == 0, total_of((2, 3)))
            when(middle, total_of((1, 2, 3)))
            when(j == J - 1, total_of((1, 2)))

        def share(self):
            mine = self.other.at[0, :, self.lanes]
            self.keep = load(mine, self.result.at[me, :, self.lanes])
            self.spread = Spread(
                mine, lambda index, lo, hi: self.result.at[index, lo:hi, self.lanes], R
            )

        def relay(self):
            self.spread.relay()

        def finish(self):
            self.keep.wait()
            self.spread.finish()
            self.spread.drain()
            self.across[2].wait_send()
            when(j != J - 1, self.across[1].wait_send)
            when(j != 0, self.across[3].wait_send)
            when(edge, self.pass_on.wait_send)

    CH = CQ // 2
    grad_up = Gradient(w1, d14, z13, h1, r1_ref, 0, P1)
    grad_down = Gradient(w2, d24, z23, h2, r2_ref, 0, D)
    grad_proj = Gradient(gp, dp4, zp3, hp, rp_ref, 0, HP)
    grad_qkv = [Gradient(wqc, dq4, zq3, hq, rq_ref, b * CH, CH) for b in range(2)]

    weight_1.drain()
    weight_2.drain()
    weight_q.drain()

    def up_grad(t, carry):
        w1[rows_of(t, tile), :] = mm_tn(mlp[:, rows_of(t, tile)], dge[...]).astype(BF)
        return carry

    lax.fori_loop(0, D // tile, up_grad, 0)
    grad_up.exchange()
    scatter_mlp.relay(2)

    def down(i, carry):
        rows = rows_of(i, T)
        mlp[rows, :] = mm(act[rows, :], w2[...]).astype(BF)
        return carry

    lax.fori_loop(0, n, down, 0)
    grad_up.add_near()

    def down_grad(t, carry):
        lanes = rows_of(t, tile)
        total = mm_tn(act[0:T, lanes], cotb[0])
        for b in range(1, n):
            total = total + mm_tn(act[b * T : (b + 1) * T, lanes], cotb[b])
        w2[lanes, :] = total.astype(BF)
        return carry

    lax.fori_loop(0, P1 // tile, down_grad, 0)
    grad_down.exchange()

    smg[...] = jnp.zeros(smg.shape, F32)
    scatter_mlp.wait_recv()

    def gather_parts(part):
        whole = rows_of_block(me, part)
        total = snd[whole, :].astype(F32)
        return total + rsr[0, part, :].astype(F32) + rsr[1, part, :].astype(F32)

    def add_sum(row, value):
        smg[row : row + 1, :] = smg[row : row + 1, :] + jnp.sum(value, axis=0, keepdims=True)

    def norm_two_back(part):
        upstream = cotb[me, part, :].astype(F32)
        grad = gather_parts(part)
        normed, factor = moments(mid[part, :])
        scaled = grad * vector(3)
        value = upstream + factor * (
            scaled
            - jnp.mean(scaled, axis=-1, keepdims=True)
            - normed * jnp.mean(scaled * normed, axis=-1, keepdims=True)
        )
        gmd[part, :] = value
        low = value.astype(BF)
        snd[rows_of_block(me, part), :] = low
        add_sum(2, low.astype(F32))
        add_sum(3, grad * normed)
        add_sum(4, grad)
        add_sum(5, upstream)

    strips(T, strip, norm_two_back)
    own_rows = rows_of(me, T)
    low_branch = snd[own_rows, :]
    grad_mixed = mm_nt(low_branch, proj_weight()).astype(BF)
    for c in range(n):
        mixc[0, c] = lane_pad(grad_mixed[:, c * hw : (c + 1) * hw], HP)
        mixc[2, c] = lane_pad(low_branch[:, c * hw : (c + 1) * hw], HP)
    head_copies = [
        send(mixc.at[0, seq_to[o]], mixc.at[1, me], {"seq": seq_to[o]}, take()) for o in range(1, n)
    ]
    branch_copies = [
        send(mixc.at[2, seq_to[o]], mixc.at[3, me], {"seq": seq_to[o]}, take()) for o in range(1, n)
    ]
    mixc[1, me] = mixc[0, me]
    mixc[3, me] = mixc[2, me]

    grad_down.add_near()
    grad_up.hop()

    for copy in head_copies:
        copy.wait_recv()
    scatter_out = Scatter(mlp, tokb, (me, me, near_y, near_x))
    for t in range(n - 1):
        scatter_out.start(t)

    def proj_grad(t, carry):
        lanes = rows_of(t, tile)
        total = mm_tn(mix[0:T, lanes], mixc[3, 0])
        for b in range(1, n):
            total = total + mm_tn(mix[b * T : (b + 1) * T, lanes], mixc[3, b])
        gp[lanes, :] = total.astype(BF)
        return carry

    def qkv_grad(half):
        pair = hl // 2 * W

        def body(t, carry):
            rows = rows_of(t, tile)
            parts = []
            for third in range(3):
                at = third * QW + half * pair
                total = mm_tn(ain[:, rows], qkv[:, at : at + pair])
                parts += [total[:, h * W : h * W + HD].astype(BF) for h in range(hl // 2)]
            wqc[rows, half * CH : (half + 1) * CH] = lane_pad(jnp.concatenate(parts, axis=1), CH)
            return carry

        lax.fori_loop(0, D // tile, body, 0)
        grad_qkv[half].exchange()

    def between(h):
        if h == 0:
            for copy in branch_copies:
                copy.wait_recv()
            lax.fori_loop(0, D // tile, proj_grad, 0)
            grad_proj.exchange()
        if h == 1:
            grad_down.hop()
            grad_proj.add_near()
            qkv_grad(0)
            scatter_out.relay(across)
        if h == 2:
            grad_up.add_far()
            grad_up.share()
            grad_qkv[0].add_near()
            grad_proj.hop()
        if h == 3:
            grad_down.add_far()
            grad_down.share()

    for h in range(hl):
        q_at = slice(h * W, (h + 1) * W)
        k_at = slice(QW + h * W, QW + (h + 1) * W)
        v_at = slice(2 * QW + h * W, 2 * QW + (h + 1) * W)
        dkv[...] = jnp.zeros(dkv.shape, F32)

        def attend_back_block(i, carry):
            rows = rows_of(i, T)
            q = qkv[rows, q_at]
            kk = qkv[:, k_at]
            g = lane_pad(mixc[1, i][:, h * HD : (h + 1) * HD], W)
            p = jnp.exp(masked(mm_nt(q, kk), i) - lse[rows, h : h + 1])
            dp = mm_nt(g, qkv[:, v_at])
            dkv[:, W:] = dkv[:, W:] + mm_tn(p.astype(BF), g)
            centre = jnp.sum(p * dp, axis=-1, keepdims=True)
            ds = (p * (dp - centre)).astype(BF)
            dq = (mm(ds, kk) * scale).astype(BF).astype(F32)
            dkv[:, :W] = dkv[:, :W] + mm_tn(ds, q)
            qkv[rows, q_at] = (dq * cosb[rows, :] - swap(dq) * sinb[rows, :]).astype(BF)
            return carry

        lax.fori_loop(0, n, attend_back_block, 0)

        def turn_back(i, carry):
            rows = rows_of(i, T)
            dk = (dkv[rows, :W] * scale).astype(BF).astype(F32)
            qkv[rows, k_at] = (dk * cosb[rows, :] - swap(dk) * sinb[rows, :]).astype(BF)
            qkv[rows, v_at] = dkv[rows, W:].astype(BF)
            return carry

        lax.fori_loop(0, n, turn_back, 0)
        between(h)

    scatter_mlp.wait_send()
    scatter_attn = Scatter(snd, rsr, (0, 1, 2, 2))

    def attn_back(t, carry):
        i = block_at(t)
        rows = rows_of(i, T)
        snd[rows, :] = mm_nt(qkv[rows, :], wq[...]).astype(BF)
        scatter_attn.start(t)
        return carry

    lax.fori_loop(0, n, attn_back, 0)

    grad_qkv[0].hop()
    qkv_grad(1)
    grad_up.relay()
    scatter_attn.relay(2)
    grad_down.relay()
    grad_proj.add_far()
    grad_proj.share()

    def bias_sums(part):
        smg[6:7, :] = smg[6:7, :] + jnp.sum(dge[part, :].astype(F32), axis=0, keepdims=True)
        line = jnp.sum(qkv[part, :].astype(F32), axis=0, keepdims=True)
        line = lane_pad(
            jnp.concatenate([line[:, h * W : h * W + HD] for h in range(3 * hl)], axis=1), D
        )
        smg[7:8, :] = smg[7:8, :] + line

    grad_qkv[1].add_near()
    strips(L, 64, bias_sums)
    grad_qkv[0].add_far()
    grad_qkv[0].share()
    grad_qkv[1].hop()

    scatter_attn.wait_recv()

    def norm_one_back(part):
        grad = gather_parts(part)
        normed, factor = moments(tokb[me, part, :].astype(F32))
        scaled = grad * vector(0)
        gmd[part, :] = gmd[part, :] + factor * (
            scaled
            - jnp.mean(scaled, axis=-1, keepdims=True)
            - normed * jnp.mean(scaled * normed, axis=-1, keepdims=True)
        )
        add_sum(0, grad * normed)
        add_sum(1, grad)

    strips(T, strip, norm_one_back)
    tokens_out = load(gmd, tgrad_ref)
    sum_copies = [
        send(smg, sg8.at[f], {"fsdp": (f + o) % F}, take()) for o in range(1, F)
    ]
    sg8[f] = smg[...]
    grad_proj.relay()
    grad_qkv[0].relay()
    grad_qkv[1].add_far()
    grad_qkv[1].share()

    scatter_out.wait_recv()

    def write_out(part):
        whole = rows_of_block(me, part)
        total = mid[part, :] + mlp[whole, :].astype(F32) + vector(5)
        for slot in (near_x, near_y):
            total = total + tokb[slot, part, :].astype(F32)
        bias_rows = rows_of_block(me, part)
        ain[bias_rows, :] = total.astype(BF)

    strips(T, strip, write_out)
    block_out = load(band(ain, me, T), out_ref)

    for copy in sum_copies:
        copy.wait_recv()
    total = sg8[0]
    for s in range(1, F):
        total = total + sg8[s]
    plain = lax.broadcasted_iota(jnp.int32, total.shape, 0)
    vec[...] = jnp.where(plain < 8, total, 0.0)
    sums_keep = load(vec, sums_ref.at[me])
    sums_share = [
        send(vec, sums_ref.at[me], {"seq": seq_to[o]}, take()) for o in range(1, n)
    ]

    grads = [grad_up, grad_down, grad_proj] + grad_qkv
    grad_qkv[1].relay()
    for item in grads:
        item.finish()
    for copy in sums_share:
        copy.wait_recv()
    sums_keep.wait()
    tokens_out.wait()
    block_out.wait()
    weight_p.drain()
    scatter_attn.wait_send()
    scatter_out.wait_send()
    for copy in leftover:
        copy.wait_send()
    assert used["remote"] <= sems.shape[0] and used["local"] <= local_sems.shape[0], used


def unpack_kernel(
    dims,
    block_in,
    tokens_in,
    rq_in,
    rp_in,
    r1_in,
    r2_in,
    sums_in,
    block_ref,
    tokens_ref,
    qkv_ref,
    proj_ref,
    up_ref,
    down_ref,
    v0,
    v1,
    v2,
    v3,
    v4,
    v5,
    v6,
    v7,
    block,
    tokens,
    rq,
    rp,
    r1,
    r2,
    sums,
    stage,
    in_sems,
    out_sems,
):
    n, T, L, D, F, R, hl, P1, CQ, HP = dims
    hw = hl * HD
    f = lax.axis_index("fsdp")
    loads = []
    for src, dst in (
        (r2_in, r2),
        (r1_in, r1),
        (rq_in, rq),
        (rp_in, rp),
        (tokens_in, tokens),
        (block_in, block),
        (sums_in, sums),
    ):
        copy = pltpu.make_async_copy(src, dst, in_sems.at[len(loads)])
        copy.start()
        loads.append(copy)
    stores = []

    def store(src, dst):
        copy = pltpu.make_async_copy(src, dst, out_sems.at[len(stores)])
        copy.start()
        stores.append(copy)

    loads[0].wait()
    for c in range(n):
        stage[c] = r2[c].astype(F32)
        store(stage.at[c], down_ref.at[c * R : (c + 1) * R])
    loads[1].wait()
    width = n * R
    for c in range(n):
        blocks = range(c * P1 // width, (c + 1) * P1 // width)
        stage[n + c] = jnp.concatenate(
            [r1[m, :, b * R : (b + 1) * R] for b in blocks for m in range(n)], axis=1
        ).astype(F32)
        store(stage.at[n + c], up_ref.at[:, c * P1 : (c + 1) * P1])
    loads[2].wait()
    for t in range(3):
        stage[2 * n + t] = jnp.concatenate(
            [
                rq[m, :, b * CQ // 2 + t * hw // 2 : b * CQ // 2 + (t + 1) * hw // 2]
                for m in range(n)
                for b in range(2)
            ],
            axis=1,
        ).astype(F32)
        store(stage.at[2 * n + t], qkv_ref.at[:, t * D : (t + 1) * D])
    loads[3].wait()
    stage[2 * n + 3] = jnp.concatenate([rp[m, :, :hw] for m in range(n)], axis=1).astype(F32)
    store(stage.at[2 * n + 3], proj_ref)
    loads[4].wait()
    store(tokens, tokens_ref)
    loads[5].wait()
    store(block, block_ref)
    loads[6].wait()
    per_part = hw // R
    for s in range(F):

        @pl.when(f == s)
        def _():
            own = slice(s * R, (s + 1) * R)
            total = sums[0, 0:6, own]
            for m in range(1, n):
                total = total + sums[m, 0:6, own]
            for row, out in enumerate((v0, v1, v2, v3, v4, v5)):
                out[...] = total[row : row + 1, :].reshape(R)
            lines = [sums[m, 6:7, own] for m in range(n)]
            v6[...] = jnp.concatenate(lines, axis=1).reshape(n * R)
            lines = []
            for b in range(3):
                spot = 3 * s + b
                third, rest = spot // (n * per_part), spot % (n * per_part)
                at = third * hw + rest % per_part * R
                lines.append(sums[rest // per_part, 7:8, at : at + R])
            v7[...] = jnp.concatenate(lines, axis=1).reshape(3 * R)

    for copy in stores:
        copy.wait()


def round_up(value, step):
    return -(-value // step) * step


def shards_kernel(
    tokens,
    picture_ids,
    patch_rows,
    patch_cols,
    norm1_gain,
    norm1_bias,
    qkv_weight,
    qkv_bias,
    proj_weight,
    proj_bias,
    norm2_gain,
    norm2_bias,
    fc1_weight,
    fc1_bias,
    fc2_weight,
    fc2_bias,
    cotangent,
):
    n = lax.axis_size("seq")
    me = lax.axis_index("seq")
    F = lax.axis_size("fsdp")
    f = lax.axis_index("fsdp")
    _, T, D = tokens.shape
    L = n * T
    hl = D // HD // n
    hw = hl * HD
    R = D // F
    hidden = fc1_weight.shape[1]
    P1 = hidden // n
    part = hidden // (F * n)
    CQ = round_up(3 * hw, 128)
    HP = round_up(hw, 128)
    J = F // 2
    W = 128

    lines = (
        norm1_gain,
        norm1_bias,
        proj_bias,
        norm2_gain,
        norm2_bias,
        fc2_bias,
        fc1_bias,
        qkv_bias,
    )
    quarter = HD // 4
    inverse = 10000.0 ** (-np.arange(quarter) / quarter)
    wave = np.zeros((8, W), np.float32)
    for c in range(2):
        wave[0, 2 * c * quarter : (2 * c + 1) * quarter] = inverse
        wave[1, (2 * c + 1) * quarter : (2 * c + 2) * quarter] = inverse
    wave[2] = np.where(np.arange(W) < HD // 2, -1.0, 1.0)
    dims = (n, T, L, D, F, R, hl, P1, CQ, HP)
    anywhere = pl.BlockSpec(memory_space=pl.ANY)
    local = pl.BlockSpec(memory_space=pltpu.VMEM)

    def vmem(shape, dtype=BF):
        return pltpu.VMEM(shape, dtype)

    scratch = [
        vmem((n, T, D)),
        vmem((L, D)),
        vmem((n, T, D)),
        vmem((n, 8, T), F32),
        vmem((F, 16, R), F32),
        vmem((8, D), F32),
        vmem((8, 3 * hl * W), F32),
        vmem((L, W), F32),
        vmem((L, W), F32),
        vmem((D, CQ)),
        vmem((D, 3 * hl * W)),
        vmem((J, 2, R, D)),
        vmem((D, P1)),
        vmem((P1, D)),
        vmem((L, 3 * hl * W)),
        vmem((L, W), F32),
        vmem((n, n, T, HP)),
        vmem((L, D)),
        vmem((T, D), F32),
        vmem((L, D)),
        vmem((L, P1)),
        vmem((L, P1)),
        vmem((L, D)),
        vmem((n - 1, T, D)),
        vmem((T, D), F32),
        vmem((D, HP)),
        vmem((J, R, CQ)),
        vmem((J, R, HP)),
        vmem((J, R, P1)),
        vmem((J, R, D)),
        vmem((J - 1, R, CQ)),
        vmem((J - 1, R, HP)),
        vmem((J - 1, R, P1)),
        vmem((J - 1, R, D)),
        vmem((L, 2 * W), F32),
        vmem((8, D), F32),
        vmem((F, 8, D), F32),
        vmem((R, CQ)),
        vmem((R, HP)),
        vmem((R, P1)),
        vmem((R, D)),
        pltpu.SemaphoreType.DMA((448,)),
        pltpu.SemaphoreType.DMA((24,)),
    ]
    shapes = (
        jax.ShapeDtypeStruct((T, D), BF),
        jax.ShapeDtypeStruct((T, D), F32),
        jax.ShapeDtypeStruct((n, R, CQ), BF),
        jax.ShapeDtypeStruct((n, R, HP), BF),
        jax.ShapeDtypeStruct((n, R, P1), BF),
        jax.ShapeDtypeStruct((n, R, D), BF),
        jax.ShapeDtypeStruct((n, 8, D), F32),
    )
    block_out, tokens_grad, rq, rp, r1, r2, sums = pl.pallas_call(
        functools.partial(block_kernel, dims),
        out_shape=shapes,
        in_specs=[anywhere] * 2 + [local] * 3 + [(local,) * 8] + [local] + [anywhere] * 4,
        out_specs=[anywhere] * 7,
        scratch_shapes=scratch,
        compiler_params=pltpu.CompilerParams(
            collective_id=0, has_side_effects=True, vmem_limit_bytes=67043328
        ),
    )(
        tokens[0],
        cotangent[0],
        picture_ids,
        patch_rows,
        patch_cols,
        lines,
        wave,
        qkv_weight,
        proj_weight,
        fc1_weight,
        fc2_weight,
    )
    stored = (
        jax.ShapeDtypeStruct((T, D), BF),
        jax.ShapeDtypeStruct((T, D), F32),
        jax.ShapeDtypeStruct((R, 3 * D), F32),
        jax.ShapeDtypeStruct((R, D), F32),
        jax.ShapeDtypeStruct((R, hidden), F32),
        jax.ShapeDtypeStruct((n * R, D), F32),
    ) + tuple(jax.ShapeDtypeStruct((size,), F32) for size in [R] * 6 + [n * R, 3 * R])
    block_out, tokens_grad, full_qkv, full_proj, full_up, full_down, *vectors = pl.pallas_call(
        functools.partial(unpack_kernel, dims),
        out_shape=stored,
        in_specs=[anywhere] * 7,
        out_specs=[anywhere] * 6 + [local] * 8,
        scratch_shapes=[
            vmem((T, D)),
            vmem((T, D), F32),
            vmem((n, R, CQ)),
            vmem((n, R, HP)),
            vmem((n, R, P1)),
            vmem((n, R, D)),
            vmem((n, 8, D), F32),
            vmem((4 + 2 * n, R, D), F32),
            pltpu.SemaphoreType.DMA((7,)),
            pltpu.SemaphoreType.DMA((7 + 2 * n,)),
        ],
        compiler_params=pltpu.CompilerParams(vmem_limit_bytes=67043328),
    )(block_out, tokens_grad, rq, rp, r1, r2, sums)
    return (
        block_out[None],
        tokens_grad[None],
        vectors[0],
        vectors[1],
        full_qkv,
        vectors[7],
        full_proj,
        vectors[2],
        vectors[3],
        vectors[4],
        full_up,
        vectors[6],
        full_down,
        vectors[5],
    )


def fits_kernel(mesh):
    return dict(mesh.shape) == {"seq": 4, "fsdp": 8}


def shards_plain(
    tokens,
    picture_ids,
    patch_rows,
    patch_cols,
    norm1_gain,
    norm1_bias,
    qkv_weight,
    qkv_bias,
    proj_weight,
    proj_bias,
    norm2_gain,
    norm2_bias,
    fc1_weight,
    fc1_bias,
    fc2_weight,
    fc2_bias,
    cotangent,
):
    n = lax.axis_size("seq")
    me = lax.axis_index("seq")
    stores = lax.axis_size("fsdp")
    _, own, width = tokens.shape
    heads = width // HD
    local_heads = heads // n
    hw = local_heads * HD
    rows = qkv_weight.shape[0]
    hidden = fc1_weight.shape[1]
    part = hidden // (stores * n)

    def pick(value, axis):
        return lax.dynamic_index_in_dim(value, me, axis, keepdims=False)

    own_qkv = pick(qkv_weight.reshape(rows, 3, n, hw), 2).reshape(rows, 3 * hw)
    own_up = pick(fc1_weight.reshape(rows, stores, n, part), 2).reshape(rows, stores * part)
    own_down = pick(fc2_weight.reshape(n, part, width), 0)
    small = (norm1_gain, norm1_bias, proj_bias, norm2_gain, norm2_bias, fc2_bias, qkv_bias, fc1_bias)
    sizes = [item.shape[0] for item in small]
    packed = gather(jnp.concatenate(small)[None], "fsdp")
    weight_qkv = gather(own_qkv, "fsdp")
    weight_proj = gather(proj_weight, "fsdp")
    weight_up = gather(own_up, "fsdp")
    weight_down = gather(own_down, "fsdp")
    params = []
    start = 0
    for size in sizes:
        params.append(packed[:, start : start + size].reshape(-1).astype(F32))
        start += size
    gain_one, bias_one, bias_proj, gain_two, bias_two, bias_down, bias_qkv, bias_up = params
    bias_qkv = pick(bias_qkv.reshape(3, n, hw), 1).reshape(3 * hw)
    bias_up = pick(bias_up.reshape(stores, n, part), 1).reshape(stores * part)

    places = jnp.stack([picture_ids[0], patch_rows[0], patch_cols[0]])
    places = gather(places, "seq", 1)
    picture = places[0]
    all_tokens = gather(tokens[0], "seq").astype(F32)
    upstream = gather(cotangent[0], "seq")
    length = all_tokens.shape[0]

    def mine(value):
        return lax.dynamic_slice_in_dim(value, me * own, own, 0)

    normed_one, factor_one = standardize(all_tokens)
    attn_input = (normed_one * gain_one + bias_one).astype(BF)
    projected = (dot(attn_input, weight_qkv) + bias_qkv).reshape(length, 3, local_heads, HD)
    cosine, sine = rotary_tables(places[1], places[2], HD)
    queries = rotate(projected[:, 0], cosine, sine).astype(BF)
    keys = rotate(projected[:, 1], cosine, sine).astype(BF)
    values = projected[:, 2].astype(BF)
    mixed_own, log_total = attend(queries, keys, values, picture)
    mixed = gather(mixed_own.reshape(length, hw), "seq", 1)
    middle = all_tokens + dot(mixed, weight_proj) + bias_proj
    normed_two, factor_two = standardize(middle)
    mlp_input = (normed_two * gain_two + bias_two).astype(BF)
    before = dot(mlp_input, weight_up) + bias_up
    gate = jax.nn.sigmoid(1.702 * before)
    activated = (before * gate).astype(BF)
    out_part = dot(activated, weight_down).astype(BF)
    block_out = (mine(middle) + scatter_sum(out_part, "seq").astype(F32) + bias_down).astype(BF)

    grad_down = scatter_sum(rows_term(activated, upstream).astype(BF), "fsdp")
    grad_activated = contract_back(upstream, weight_down)
    grad_before = (grad_activated * (gate + 1.702 * before * gate * (1.0 - gate))).astype(BF)
    grad_up = scatter_sum(rows_term(mlp_input, grad_before).astype(BF), "fsdp")
    grad_mlp_input = scatter_sum(contract_back(grad_before, weight_up).astype(BF), "seq").astype(F32)
    own_upstream = cotangent[0].astype(F32)
    own_two = mine(normed_two)
    grad_middle = own_upstream + norm_back(grad_mlp_input, own_two, mine(factor_two), gain_two)
    grad_branch = grad_middle.astype(BF)
    grad_mixed = contract_back(grad_branch, weight_proj).astype(BF)
    grad_heads = lax.all_to_all(grad_mixed, "seq", split_axis=1, concat_axis=0, tiled=True)
    branch_part = lax.all_to_all(grad_branch, "seq", split_axis=1, concat_axis=0, tiled=True)
    grad_proj = scatter_sum(rows_term(mixed, branch_part).astype(BF), "fsdp")
    grad_queries, grad_keys, grad_values = attend_back(
        queries, keys, values, picture, grad_heads.reshape(length, local_heads, HD), log_total
    )
    grad_projected = jnp.stack(
        [
            unrotate(grad_queries.astype(F32), cosine, sine).astype(BF),
            unrotate(grad_keys.astype(F32), cosine, sine).astype(BF),
            grad_values,
        ],
        axis=1,
    ).reshape(length, 3 * hw)
    grad_qkv = scatter_sum(rows_term(attn_input, grad_projected).astype(BF), "fsdp")
    grad_attn_input = scatter_sum(contract_back(grad_projected, weight_qkv).astype(BF), "seq").astype(F32)
    own_one = mine(normed_one)
    tokens_grad = grad_middle + norm_back(grad_attn_input, own_one, mine(factor_one), gain_one)

    def spread(value, groups):
        empty = jnp.zeros((groups, n, value.shape[0] // groups), F32)
        return lax.dynamic_update_slice_in_dim(
            empty, value.reshape(groups, 1, -1), me, 1
        ).reshape(stores, -1)

    sums = [
        jnp.sum(grad_attn_input * own_one, axis=0).reshape(stores, -1),
        jnp.sum(grad_attn_input, axis=0).reshape(stores, -1),
        jnp.sum(grad_branch.astype(F32), axis=0).reshape(stores, -1),
        jnp.sum(grad_mlp_input * own_two, axis=0).reshape(stores, -1),
        jnp.sum(grad_mlp_input, axis=0).reshape(stores, -1),
        jnp.sum(own_upstream, axis=0).reshape(stores, -1),
        spread(jnp.sum(grad_projected.astype(F32), axis=0), 3),
        spread(jnp.sum(grad_before.astype(F32), axis=0), stores),
    ]
    summed = lax.psum(scatter_sum(jnp.concatenate(sums, axis=1), "fsdp"), "seq")[0]
    finals = []
    start = 0
    for size in sizes:
        finals.append(summed[start : start + size])
        start += size
    full_down = gather(grad_down, "seq").astype(F32)
    full_up = gather(grad_up[None], "seq").reshape(n, rows, stores, part)
    full_up = full_up.transpose(1, 2, 0, 3).reshape(rows, hidden).astype(F32)
    full_proj = gather(grad_proj, "seq", 1).astype(F32)
    full_qkv = gather(grad_qkv[None], "seq").reshape(n, rows, 3, hw)
    full_qkv = full_qkv.transpose(1, 2, 0, 3).reshape(rows, 3 * width).astype(F32)
    return (
        block_out[None],
        tokens_grad[None],
        finals[0],
        finals[1],
        full_qkv,
        finals[6],
        full_proj,
        finals[2],
        finals[3],
        finals[4],
        full_up,
        finals[7],
        full_down,
        finals[5],
    )


def solution(mesh):
    token = P("fsdp", "seq", None)
    place = P("fsdp", "seq")
    vector = P("fsdp")
    matrix = P("fsdp", None)
    in_specs = (
        token,
        place,
        place,
        place,
        vector,
        vector,
        matrix,
        vector,
        matrix,
        vector,
        vector,
        vector,
        matrix,
        vector,
        matrix,
        vector,
        token,
    )
    out_specs = (
        token,
        token,
        vector,
        vector,
        matrix,
        vector,
        matrix,
        vector,
        vector,
        vector,
        matrix,
        vector,
        matrix,
        vector,
    )
    shards = shards_kernel if fits_kernel(mesh) else shards_plain
    return jax.shard_map(shards, mesh=mesh, in_specs=in_specs, out_specs=out_specs, check_vma=False)
```
